32 devices in a mesh: dp: 16 (over z, x, core), tensor: 2 (over y).
Axes of the slice: x: 2, y: 2, z: 4, core: 2. Of those that a mesh axis runs over, the one named last changes fastest.
Arguments:
- tokens: bfloat16 [32768, 768], P(('dp', 'tensor')), may hold values from -6 to 6
- segment_ids: int32 [16, 2048], P('dp'), may hold values from 0 to 15, never falling along the last dimension, each value on 1 to 1024 neighbouring positions
- ln1_gain: bfloat16 [768], P('dp'), may hold values from 0.25 to 1.75
- ln1_bias: bfloat16 [768], P('dp'), may hold values from -1.796875 to 1.796875
- w_qkv: bfloat16 [768, 3, 768], P('dp', None, 'tensor'), may hold values from -0.3125 to 0.3125
- b_qv: bfloat16 [2, 768], P(None, 'dp'), may hold values from -1.796875 to 1.796875
- w_attn_out: bfloat16 [768, 768], P('tensor', 'dp'), may hold values from -3 to 3
- b_attn_out: bfloat16 [768], P('dp'), may hold values from -6 to 6
- ln2_gain: bfloat16 [768], P('dp'), may hold values from 0.25 to 1.75
- ln2_bias: bfloat16 [768], P('dp'), may hold values from -1.796875 to 1.796875
- w_fc: bfloat16 [768, 3072], P('dp', 'tensor'), may hold values from -0.21875 to 0.21875
- b_fc: bfloat16 [3072], P('dp'), may hold values from -1.796875 to 1.796875
- w_proj: bfloat16 [3072, 768], P('tensor', 'dp'), may hold values from -0.8984375 to 0.8984375
- b_proj: bfloat16 [768], P('dp'), may hold values from -6 to 6
- cotangent: bfloat16 [32768, 768], P(('dp', 'tensor')), may hold values from -6 to 6
Outputs:
- block_out: bfloat16 [32768, 768], P(('dp', 'tensor'))
- grad_tokens: bfloat16 [32768, 768], P(('dp', 'tensor'))
- grad_ln1_gain: float32 [768], P('dp')
- grad_ln1_bias: float32 [768], P('dp')
- grad_w_qkv: float32 [768, 3, 768], P('dp', None, 'tensor')
- grad_b_qv: float32 [2, 768], P(None, 'dp')
- grad_w_attn_out: float32 [768, 768], P('tensor', 'dp')
- grad_b_attn_out: float32 [768], P('dp')
- grad_ln2_gain: float32 [768], P('dp')
- grad_ln2_bias: float32 [768], P('dp')
- grad_w_fc: float32 [768, 3072], P('dp', 'tensor')
- grad_b_fc: float32 [3072], P('dp')
- grad_w_proj: float32 [3072, 768], P('tensor', 'dp')
- grad_b_proj: float32 [768], P('dp')
The draws below stay inside these ranges and needn't reach their ends.
Inputs may be any that keep to these rules, and one draw needn't show every extreme that they name: `segment_ids`: in each sequence the document numbers never fall; each document has 1 to 1024 tokens, and one has exactly 1024.
All inputs are finite; a program needn't handle non-finite values.
Results may differ from the reference program's by a relative error of at most 0.02.
Values may be sent and summed in bfloat16 or wider, within the bound.
A program may use at most 256 MiB of HBM per device.

```python
import math
import jax
import jax.numpy as jnp
import numpy as np
from jax import lax

D = 768
HEADS = 12
FF = 3072
SEQ = 2048
HEAD_DIM = 64
SEQS = 16
TOKENS = 32768
SEGS = 16


def raised(entries, rng, source, target, shards_of, factor):
    owner, partner = [(jnp.arange(entries.shape[position]) // (entries.shape[position] // shards_of)).reshape([-1 if axis == position else 1 for axis in range(entries.ndim)]) for position in (source, target)]
    chosen = jax.random.permutation(rng, shards_of)[partner]
    strong = (owner == chosen) | (owner == (partner + shards_of // 2) % shards_of)
    return jnp.where(strong, factor * entries, entries)


def block_levels(stream_key, dims, cuts, low, high):
    def one(position, parts):
        draws = jax.random.uniform(jax.random.fold_in(jax.random.fold_in(stream_key, 6), position), (parts,), jnp.float32, low / len(cuts), high / len(cuts))
        return jnp.repeat(jnp.exp(draws), dims[position] // parts).reshape((-1,) + (1,) * (len(dims) - position - 1))

    level = one(*cuts[0])
    for cut in cuts[1:]:
        level = level * one(*cut)
    return level


def length_profile(number_of, total, limit, lean):
    loads = [(1 << 20) // math.isqrt(grade ** lean) + 1 for grade in range(2, number_of + 1)]
    rest, given = total - limit - (number_of - 1), [1] * (number_of - 1)
    while rest > 0:
        movable = [i for i in range(number_of - 1) if given[i] < limit]
        mass, remaining = sum([loads[i] for i in movable]), rest
        for i in movable:
            more = min(limit - given[i], max(1, remaining * loads[i] // mass), rest)
            given[i] = given[i] + more
            rest = rest - more
    return np.array([limit] + given)


def ragged_sizes(stream_key, count, total, limit, lean):
    if count == 2:
        one = jax.random.randint(stream_key, (), max(1, total - limit), min(limit, total - 1) + 1)
        return jnp.stack([one, total - one])
    lengths = jnp.asarray(length_profile(count, total, limit, lean), jnp.int32)
    twos = (count - 1) // 2
    donor, taker = lengths[1:1 + 2 * twos:2], lengths[2:2 + 2 * twos:2]
    slack = jnp.minimum(donor - 1, limit - taker)
    moved = jax.random.randint(jax.random.fold_in(stream_key, 1), (twos,), 0, 1 << 20) % (slack + 1)
    lengths = lengths.at[1:1 + 2 * twos:2].set(donor - moved).at[2:2 + 2 * twos:2].set(taker + moved)
    return lengths[jax.random.permutation(jax.random.fold_in(stream_key, 2), count)]


def noise(stream_key, shape, scale, reach, split=(), kind=jnp.bfloat16):
    entries = jax.random.normal(stream_key, shape, jnp.float32) * scale
    if len(split) > 0:
        entries = block_levels(stream_key, shape, split, -0.22, 0.18) * entries
    return jnp.clip(entries, min=-reach, max=reach).astype(kind)


def gaussian_with(rng, extent, width, reach, split, heavy, kind=jnp.bfloat16):
    values = width * jax.random.normal(rng, extent, jnp.float32)
    if split:
        values = values * block_levels(rng, extent, split, -0.22, 0.18)
    return jnp.clip(raised(values, jax.random.fold_in(rng, 3), *heavy), -reach, reach).astype(kind)


def setup_inputs(seed: int = 0) -> dict:
    splits = jax.random.split(jax.random.key(seed), 16)
    return {
        "tokens": gaussian_with(splits[0], (TOKENS, D), 1.0, 6.0, ((0, 32),), (0, 1, 32, 2.75)),
        "segment_ids": jax.vmap(lambda own: jnp.searchsorted(jnp.cumsum(ragged_sizes(own, SEGS, SEQ, SEQ // 2, 2)), jnp.arange(SEQ), side="right"))(jax.random.split(splits[1], SEQS)).reshape((SEQS, SEQ)).astype(jnp.int32),
        "ln1_gain": jnp.clip(1.0 + 0.15 * jax.random.normal(splits[2], (D,), jnp.float32), 0.25, 1.75).astype(jnp.bfloat16),
        "ln1_bias": noise(splits[3], (D,), 0.3, 1.796875, ((0, 16),)),
        "w_qkv": noise(splits[4], (D, 3, D), (D // 2) ** -0.5, 0.3125, ((0, 16), (2, 2))),
        "b_qv": noise(splits[5], (2, D), 0.3, 1.796875, ((1, 16),)),
        "w_attn_out": noise(splits[6], (D, D), 0.5, 3.0, ((0, 2), (1, 16))),
        "b_attn_out": noise(splits[7], (D,), 1.0, 6.0, ((0, 16),)),
        "ln2_gain": jnp.clip(1.0 + 0.15 * jax.random.normal(splits[8], (D,), jnp.float32), 0.25, 1.75).astype(jnp.bfloat16),
        "ln2_bias": noise(splits[9], (D,), 0.3, 1.796875, ((0, 16),)),
        "w_fc": noise(splits[10], (D, FF), D ** -0.5, 0.21875, ((0, 16), (1, 2))),
        "b_fc": noise(splits[11], (FF,), 0.3, 1.796875, ((0, 16),)),
        "w_proj": noise(splits[12], (FF, D), 0.15, 0.8984375, ((0, 2), (1, 16))),
        "b_proj": noise(splits[13], (D,), 1.0, 6.0, ((0, 16),)),
        "cotangent": gaussian_with(splits[14], (TOKENS, D), 1.0, 6.0, ((0, 32),), (0, 1, 32, 2.75)),
    }


EPSILON = 1e-05
BRANCH_SCALE = 48.0 ** (-0.5)
MASKED_SCORE = -1e+30

@jax.custom_vjp
def low(v):
    return lax.optimization_barrier(v.astype(jnp.bfloat16)).astype(jnp.float32)

@jax.custom_vjp
def low_back(v):
    return v

def low_keep(v):
    return (low(v), None)

def low_pass(kept, grad):
    return (grad,)

def back_keep(v):
    return (v, None)

def back_low(kept, grad):
    return (low(grad),)
low.defvjp(low_keep, low_pass)
low_back.defvjp(back_keep, back_low)

def layer_norm(values, gain, offsets):
    centered = values - lax.optimization_barrier(jnp.mean(values, axis=-1, keepdims=True))
    variance = lax.optimization_barrier(jnp.mean(centered * centered, axis=-1, keepdims=True))
    return centered * lax.rsqrt(variance + EPSILON) * gain + offsets

def gelu_tanh(values):
    return jax.nn.gelu(values, approximate=True)

def one_sequence(rows, seg_row, params):
    gain_attn, offset_attn, qkv_weight, qv_bias, out_weight, out_bias, gain_mlp, offset_mlp, fc_weight, fc_bias, proj_weight, proj_bias = params
    highest = lax.Precision.HIGHEST
    seq_len = rows.shape[0]
    normed_one = low(layer_norm(rows, gain_attn, offset_attn))
    qkv_bias = jnp.stack([qv_bias[0], jnp.zeros((D,), jnp.float32), qv_bias[1]])
    projected = jnp.dot(normed_one, qkv_weight.reshape(D, 3 * D), precision=highest).reshape(seq_len, 3, D) + qkv_bias
    projected = low_back(low(projected))
    queries = projected[:, 0].reshape(seq_len, HEADS, HEAD_DIM)
    keys_all = projected[:, 1].reshape(seq_len, HEADS, HEAD_DIM)
    values_all = projected[:, 2].reshape(seq_len, HEADS, HEAD_DIM)
    block_rows = min(512, seq_len)
    key_pos = jnp.arange(seq_len, dtype=jnp.int32)

    def attend(row_start):
        seg_query = lax.dynamic_slice_in_dim(seg_row, row_start, block_rows, 0)
        query_pos = row_start + jnp.arange(block_rows, dtype=jnp.int32)
        visible = (seg_query[:, None] == seg_row[None, :]) & (query_pos[:, None] >= key_pos[None, :])
        query_block = lax.dynamic_slice_in_dim(queries, row_start, block_rows, 0)
        raw_scores = jnp.einsum('qhd,khd->hqk', query_block, keys_all, precision=highest)
        scores = jnp.where(visible[None], low_back(raw_scores) * HEAD_DIM ** (-0.5), MASKED_SCORE)
        row_max = lax.optimization_barrier(jnp.max(scores, axis=2, keepdims=True))
        exponent = jnp.exp(scores - row_max)
        soft = exponent / lax.optimization_barrier(jnp.sum(exponent, axis=2, keepdims=True))
        mixed = jnp.einsum('hqk,khd->qhd', low(soft), values_all, precision=highest)
        return mixed.reshape(block_rows, D)
    starts = jnp.arange(seq_len // block_rows, dtype=jnp.int32) * block_rows
    attended = lax.map(jax.checkpoint(attend), starts).reshape(seq_len, D)
    attended = low_back(low(attended))
    attn_branch = low_back(jnp.dot(attended, out_weight, precision=highest)) + out_bias
    middle = rows + BRANCH_SCALE * attn_branch
    normed_two = low(layer_norm(middle, gain_mlp, offset_mlp))
    pre_act = low_back(jnp.dot(normed_two, fc_weight, precision=highest)) + fc_bias
    activated = low(gelu_tanh(pre_act))
    mlp_branch = low_back(jnp.dot(activated, proj_weight, precision=highest)) + proj_bias
    return middle + BRANCH_SCALE * mlp_branch

def reference(tokens, segment_ids, ln1_gain, ln1_bias, w_qkv, b_qv, w_attn_out, b_attn_out, ln2_gain, ln2_bias, w_fc, b_fc, w_proj, b_proj, cotangent):
    params = (ln1_gain.astype(jnp.float32), ln1_bias.astype(jnp.float32), w_qkv.astype(jnp.float32), b_qv.astype(jnp.float32), w_attn_out.astype(jnp.float32), b_attn_out.astype(jnp.float32), ln2_gain.astype(jnp.float32), ln2_bias.astype(jnp.float32), w_fc.astype(jnp.float32), b_fc.astype(jnp.float32), w_proj.astype(jnp.float32), b_proj.astype(jnp.float32))
    sequences = segment_ids.shape[0]
    rows = tokens.astype(jnp.float32).reshape(sequences, SEQ, D)

    def forward(rows_all, *params_all):

        def per_sequence(paired):
            return one_sequence(paired[0], paired[1], params_all)
        return lax.map(per_sequence, (rows_all, segment_ids))
    outputs, backward = jax.vjp(forward, rows, *params)
    grads = backward(cotangent.astype(jnp.float32).reshape(sequences, SEQ, D))
    return (outputs.reshape(TOKENS, D).astype(jnp.bfloat16), grads[0].reshape(TOKENS, D).astype(jnp.bfloat16), grads[1], grads[2], grads[3], grads[4], grads[5], grads[6], grads[7], grads[8], grads[9], grads[10], grads[11], grads[12])
```

```python
import functools

import jax
import jax.numpy as jnp
from jax import lax
from jax.experimental import pallas as pl
from jax.experimental.pallas import tpu as pltpu
from jax.sharding import PartitionSpec as P

HD = 64
QB = 256
NEG = -1e30
EPSILON = 1e-05
BRANCH_SCALE = 48.0 ** (-0.5)
SMALL = 128
bf = jnp.bfloat16
f32 = jnp.float32
NT = (((1,), (1,)), ((), ()))
TN = (((0,), (0,)), ((), ()))
BOTH = ("dp", "tensor")


def attn_info(seg, core):
    n=seg.shape[0]; nb=n//QB
    docs=jnp.arange(16,dtype=jnp.int32)
    first=jnp.sum((seg[None,:]<docs[:,None]).astype(jnp.int32),axis=1)
    starts=jnp.sum(jnp.where(seg[None,:]==docs[:,None],first[:,None],0),axis=0)
    blocks=starts.reshape(nb,QB)
    idx=jnp.arange(nb,dtype=jnp.int32)
    low=blocks[:,0]//QB
    mid=jnp.clip((blocks[:,QB-1]+QB-1)//QB,low,idx)
    return starts.reshape(1,n), jnp.concatenate([jnp.reshape(core,(1,)),low,mid]).astype(jnp.int32)

def fwd_kernel(info, own, recv, st_ref, okeep, osend, lse_ref, qm, ks, vt, osc, acc):
    half,cols=own.shape[0],own.shape[1]//3; n=2*half; nb=n//QB; heads=cols//HD; pairs=cols//128
    c=info[0]
    low_lane=(lax.broadcasted_iota(jnp.int32,(1,cols),1)%128)<HD
    zero=jnp.zeros((),bf)
    for base,src in ((c*half,own),((1-c)*half,recv)):
        rows=pl.ds(pl.multiple_of(base,half),half)
        qv=src[:,:cols]*bf(HD**-0.5)
        qm[0,rows]=jnp.where(low_lane,qv,zero)
        qm[1,rows]=jnp.where(low_lane,zero,qv)
        ks[rows]=src[:,cols:2*cols]
        vt[:,rows]=src[:,2*cols:].T
    kio=lax.broadcasted_iota(jnp.int32,(QB,QB),0)
    qio=lax.broadcasted_iota(jnp.int32,(QB,QB),1)
    def qblock(i,_):
        at=pl.multiple_of(i*QB,QB)
        srow=st_ref[:,pl.ds(at,QB)]
        acc[...]=jnp.zeros_like(acc)
        def step(mode,j,carry):
            kat=pl.multiple_of(j*QB,QB)
            if mode:
                mask=kio>=(srow-kat)
                if mode==2: mask=mask&(kio<=qio)
            out=[]
            for h in range(heads):
                m,l=carry[h]
                lanes=slice((h//2)*128,(h//2+1)*128); sub=slice(h*HD,(h+1)*HD)
                s=lax.dot_general(ks[pl.ds(kat,QB),lanes],qm[h%2,pl.ds(at,QB),lanes],NT,preferred_element_type=f32)
                if mode: s=jnp.where(mask,s,NEG)
                mn=jnp.maximum(m,jnp.max(s,axis=0,keepdims=True))
                p=jnp.exp(s-mn); a=jnp.exp(m-mn)
                l=a*l+jnp.sum(p,axis=0,keepdims=True)
                acc[sub]=a*acc[sub]+jnp.dot(vt[sub,pl.ds(kat,QB)],p.astype(bf),preferred_element_type=f32)
                out.append((mn,l))
            return tuple(out)
        one=(jnp.full((1,QB),NEG,f32),jnp.zeros((1,QB),f32))
        carry=step(2,i,(one,)*heads)
        carry=lax.fori_loop(info[1+i],info[1+nb+i],functools.partial(step,1),carry)
        carry=lax.fori_loop(info[1+nb+i],i,functools.partial(step,0),carry)
        for h,(m,l) in enumerate(carry):
            sub=slice(h*HD,(h+1)*HD)
            acc[sub]=acc[sub]/l
            lse_ref[h:h+1,pl.ds(at,QB)]=m+jnp.log(l)
        osc[pl.ds(at,QB)]=acc[...].T.astype(bf)
        return 0
    lax.fori_loop(0,nb,qblock,0)
    okeep[...]=osc[pl.ds(pl.multiple_of(c*half,half),half)]
    osend[...]=osc[pl.ds(pl.multiple_of((1-c)*half,half),half)]

VM=pl.BlockSpec(memory_space=pltpu.VMEM)
SM=pl.BlockSpec(memory_space=pltpu.SMEM)
def attn_fwd(own,recv,starts,info):
    half,cols=own.shape[0],own.shape[1]//3; n=2*half
    return pl.pallas_call(fwd_kernel,
        in_specs=[SM,VM,VM,VM], out_specs=[VM]*3,
        scratch_shapes=[pltpu.VMEM((2,n,cols),bf),pltpu.VMEM((n,cols),bf),pltpu.VMEM((cols,n),bf),pltpu.VMEM((n,cols),bf),pltpu.VMEM((cols,QB),f32)],
        out_shape=[jax.ShapeDtypeStruct((half,cols),bf)]*2+[jax.ShapeDtypeStruct((cols//HD,n),f32)],
        cost_estimate=pl.CostEstimate(flops=2*2*n*n//3*cols,bytes_accessed=8*half*cols*2,transcendentals=n*n*6//3),
        compiler_params=pltpu.CompilerParams(vmem_limit_bytes=48<<20),
    )(info,own,recv,starts)

def bwd_kernel(info, own, recv, doo, dor, oo, orr, st_ref, lse_ref, dkeep, dsend, qm, ks, vs, kt, dom, dlt, dqs, dks, dvs):
    half,cols=own.shape[0],own.shape[1]//3; n=2*half; nb=n//QB; heads=cols//HD; pairs=cols//128
    c=info[0]
    low_lane=(lax.broadcasted_iota(jnp.int32,(1,cols),1)%128)<HD
    zero=jnp.zeros((),bf)
    for base,src,do,o in ((c*half,own,doo,oo),((1-c)*half,recv,dor,orr)):
        rows=pl.ds(pl.multiple_of(base,half),half)
        qv=src[:,:cols]*bf(HD**-0.5)
        qm[0,rows]=jnp.where(low_lane,qv,zero)
        qm[1,rows]=jnp.where(low_lane,zero,qv)
        ks[rows]=src[:,cols:2*cols]
        vs[rows]=src[:,2*cols:]
        kt[:,rows]=src[:,cols:2*cols].T
        dv=do[...]
        dom[0,rows]=jnp.where(low_lane,dv,zero)
        dom[1,rows]=jnp.where(low_lane,zero,dv)
        prod=(dv.astype(f32)*o[...].astype(f32)).T
        for h in range(heads):
            dlt[h:h+1,rows]=jnp.sum(prod[h*HD:(h+1)*HD],axis=0,keepdims=True)
    dks[...]=jnp.zeros_like(dks); dvs[...]=jnp.zeros_like(dvs)
    kio=lax.broadcasted_iota(jnp.int32,(QB,QB),0)
    qio=lax.broadcasted_iota(jnp.int32,(QB,QB),1)
    def qblock(i,_):
        at=pl.multiple_of(i*QB,QB)
        qr=pl.ds(at,QB)
        srow=st_ref[:,qr]
        dqs[...]=jnp.zeros_like(dqs)
        def step(mode,j,carry):
            kat=pl.multiple_of(j*QB,QB); kr=pl.ds(kat,QB)
            if mode:
                mask=kio>=(srow-kat)
                if mode==2: mask=mask&(kio<=qio)
            for g in range(pairs):
                lanes=slice(g*128,(g+1)*128)
                ps=[];dss=[]
                for e in range(2):
                    h=2*g+e; sub=slice(h*HD,(h+1)*HD)
                    s=lax.dot_general(ks[kr,lanes],qm[e,qr,lanes],NT,preferred_element_type=f32)
                    if mode: s=jnp.where(mask,s,NEG)
                    p=jnp.exp(s-lse_ref[h:h+1,qr])
                    dp=lax.dot_general(vs[kr,lanes],dom[e,qr,lanes],NT,preferred_element_type=f32)
                    d=(p*(dp-dlt[h:h+1,qr])).astype(bf)
                    dqs[sub]+=jnp.dot(kt[sub,kr],d,preferred_element_type=f32)
                    ps.append(p.astype(bf)); dss.append(d)
                dcat=jnp.concatenate([dom[0,qr,lanes],dom[1,qr,lanes]],axis=0)
                qcat=jnp.concatenate([qm[0,qr,lanes],qm[1,qr,lanes]],axis=0)
                dvs[kr,lanes]+=jnp.dot(jnp.concatenate(ps,axis=1),dcat,preferred_element_type=f32)
                dks[kr,lanes]+=jnp.dot(jnp.concatenate(dss,axis=1),qcat,preferred_element_type=f32)
            return carry
        step(2,i,0)
        lax.fori_loop(info[1+i],info[1+nb+i],functools.partial(step,1),0)
        lax.fori_loop(info[1+nb+i],i,functools.partial(step,0),0)
        qm[0,qr]=(dqs[...]*(HD**-0.5)).T.astype(bf)
        return 0
    lax.fori_loop(0,nb,qblock,0)
    for dst,base in ((dkeep,c*half),(dsend,(1-c)*half)):
        rows=pl.ds(pl.multiple_of(base,half),half)
        dst[:,:cols]=qm[0,rows]
        dst[:,cols:2*cols]=dks[rows].astype(bf)
        dst[:,2*cols:]=dvs[rows].astype(bf)

def attn_bwd(own,recv,do_own,do_recv,o_own,o_recv,starts,lse,info):
    half,cols=own.shape[0],own.shape[1]//3; n=2*half
    return pl.pallas_call(bwd_kernel,
        in_specs=[SM]+[VM]*8, out_specs=[VM]*2,
        scratch_shapes=[pltpu.VMEM((2,n,cols),bf),pltpu.VMEM((n,cols),bf),pltpu.VMEM((n,cols),bf),pltpu.VMEM((cols,n),bf),pltpu.VMEM((2,n,cols),bf),pltpu.VMEM((cols//HD,n),f32),
                            pltpu.VMEM((cols,QB),f32),pltpu.VMEM((n,cols),f32),pltpu.VMEM((n,cols),f32)],
        out_shape=[jax.ShapeDtypeStruct((half,3*cols),bf)]*2,
        cost_estimate=pl.CostEstimate(flops=2*5*n*n//3*cols,bytes_accessed=16*half*cols*2,transcendentals=n*n*6//3),
        compiler_params=pltpu.CompilerParams(vmem_limit_bytes=56<<20),
    )(info,own,recv,do_own,do_recv,o_own,o_recv,starts,lse)


def dot(left, right, dims=(((1,), (0,)), ((), ()))):
    return lax.dot_general(left, right, dims, preferred_element_type=f32)


def phase_order(dp_size, last):
    high = [1 << k for k in range(dp_size.bit_length() - 2, 1, -1)]
    return high + ([2, 0, 1] if last == "tensor" else [0, 2, 1]) if dp_size > 2 else [0, 1]


def exchange(value, bit, dp_size):
    if bit:
        return lax.ppermute(value, "dp", [(i, i ^ bit) for i in range(dp_size)])
    return lax.ppermute(value, "tensor", [(0, 1), (1, 0)])


def gather_blocks(shard, order, dp_size):
    held = shard[None]
    for bit in order:
        held = jnp.concatenate([held, exchange(held, bit, dp_size)], axis=0)
    return held


def scatter_sum(partial, order, dp_size):
    kept = partial
    for bit in reversed(order):
        n = kept.shape[0] // 2
        got = exchange(kept[n:], bit, dp_size)
        kept = (kept[:n].astype(f32) + got.astype(f32)).astype(bf)
    return kept[0]


def positions(order, dp_size, dp_pos, tensor_pos):
    d = jnp.arange(dp_size, dtype=jnp.int32) ^ dp_pos
    out = []
    for t in range(2):
        place = jnp.zeros((dp_size,), jnp.int32)
        for k, bit in enumerate(order):
            on = ((d & bit) != 0).astype(jnp.int32) if bit else (tensor_pos != t).astype(jnp.int32)
            place = place + (on << k)
        out.append(place)
    return jnp.concatenate(out)


def move_kernel(table, source, out):
    out[...] = source[...]


def move_blocks(blocks, table, scatter):
    count, rows, cols = blocks.shape
    one, other = (lambda g, s: (g, 0, 0)), (lambda g, s: (s[g], 0, 0))
    return pl.pallas_call(
        move_kernel,
        grid_spec=pltpu.PrefetchScalarGridSpec(
            num_scalar_prefetch=1,
            grid=(count,),
            in_specs=[pl.BlockSpec((1, rows, cols), one if scatter else other)],
            out_specs=pl.BlockSpec((1, rows, cols), other if scatter else one),
        ),
        out_shape=jax.ShapeDtypeStruct(blocks.shape, blocks.dtype),
        cost_estimate=pl.CostEstimate(flops=0, bytes_accessed=4 * blocks.size, transcendentals=0),
    )(table, blocks)


def layer_norm_parts(values):
    centered = values - jnp.mean(values, axis=-1, keepdims=True)
    inverse = lax.rsqrt(jnp.mean(centered * centered, axis=-1, keepdims=True) + EPSILON)
    return centered * inverse, inverse


def layer_norm_back(hat, inverse, gain, grad):
    scaled = grad * gain
    back = inverse * (
        scaled
        - jnp.mean(scaled, axis=-1, keepdims=True)
        - hat * jnp.mean(scaled * hat, axis=-1, keepdims=True)
    )
    return back, jnp.sum(grad * hat, axis=0), jnp.sum(grad, axis=0)


def gelu_parts(pre):
    root = 0.7978845608
    inner = jnp.tanh(root * (pre + 0.044715 * pre * pre * pre))
    value = 0.5 * pre * (1.0 + inner)
    slope = 0.5 * (1.0 + inner) + 0.5 * pre * (1.0 - inner * inner) * root * (
        1.0 + 3 * 0.044715 * pre * pre
    )
    return value, slope


def on_device(
    tokens, segment_ids, ln1_gain, ln1_bias, w_qkv, b_qv, w_attn_out, b_attn_out,
    ln2_gain, ln2_bias, w_fc, b_fc, w_proj, b_proj, cotangent,
):
    dp_size = lax.axis_size("dp")
    dp_pos, t_pos = lax.axis_index("dp"), lax.axis_index("tensor")
    core = dp_pos % 2
    rows = ln1_gain.shape[0]
    width = tokens.shape[1]
    cols = w_qkv.shape[2]
    hidden = w_fc.shape[1]
    fan = b_fc.shape[0] // rows
    first, second = phase_order(dp_size, "tensor"), phase_order(dp_size, "x")
    swap = []
    for d in range(dp_size):
        for t in range(2):
            swap.append((2 * d + t, 2 * (d - d % 2 + t) + d % 2))
    mine = core == t_pos

    residual_in = lax.ppermute(tokens, BOTH, swap)
    seg_other = lax.ppermute(segment_ids, "dp", [(i, i ^ 1) for i in range(dp_size)])
    seg = jnp.where(mine, segment_ids, seg_other)[0]
    small = jnp.concatenate(
        [ln1_gain[:, None], ln1_bias[:, None], b_qv.T, b_attn_out[:, None], ln2_gain[:, None],
         ln2_bias[:, None], b_proj[:, None], b_fc.reshape(rows, fan)], axis=1)
    small = jnp.pad(small, ((0, 0), (0, SMALL - small.shape[1])))
    pack_a = jnp.concatenate([w_qkv.reshape(rows, 3 * cols), w_attn_out.T, small], axis=1)
    place_a = positions(first, dp_size, dp_pos, t_pos)
    place_b = positions(second, dp_size, dp_pos, t_pos)
    all_a = move_blocks(gather_blocks(pack_a, first, dp_size), place_a, False).reshape(2, width, -1)
    all_fc = move_blocks(gather_blocks(w_fc, first, dp_size), place_a, False).reshape(2, width, hidden)
    all_proj = move_blocks(gather_blocks(w_proj.T, second, dp_size), place_b, False).reshape(2, width, hidden)
    qkv_w = all_a[:, :, : 3 * cols]
    out_w = all_a[:, :, 3 * cols : 4 * cols]
    vec = all_a[0, :, 4 * cols :].astype(f32).T
    gain1, bias1, b_q, b_v, out_bias, gain2, bias2, proj_bias = (vec[k] for k in range(8))
    fc_bias = vec[8 : 8 + fan].T.reshape(2, hidden)
    qkv_bias = jnp.stack([b_q.reshape(2, cols), jnp.zeros((2, cols), f32), b_v.reshape(2, cols)], axis=1).reshape(2, 3 * cols)

    x = residual_in.astype(f32)
    hat1, inv1 = layer_norm_parts(x)
    n1 = (hat1 * gain1 + bias1).astype(bf)
    take = lambda arr, k: lax.dynamic_index_in_dim(arr, k, 0, keepdims=False)
    other = 1 - core
    qkv_send = (dot(n1, take(qkv_w, other)) + take(qkv_bias, other)).astype(bf)
    qkv_recv = exchange(qkv_send, 1, dp_size)
    qkv_own = (dot(n1, take(qkv_w, core)) + take(qkv_bias, core)).astype(bf)
    starts, info = attn_info(seg, core)
    o_own, o_send, lse = attn_fwd(qkv_own, qkv_recv, starts, info)
    o_recv = exchange(o_send, 1, dp_size)
    wo_own, wo_other = take(out_w, core), take(out_w, other)
    branch = dot(o_own, wo_own, NT) + dot(o_recv, wo_other, NT) + out_bias
    middle = x + BRANCH_SCALE * branch
    hat2, inv2 = layer_norm_parts(middle)
    n2 = (hat2 * gain2 + bias2).astype(bf)
    grad_out = lax.ppermute(cotangent, BOTH, swap).astype(f32)
    scaled_out = BRANCH_SCALE * grad_out
    d_b_proj = jnp.sum(scaled_out, axis=0)
    d_mlp = scaled_out.astype(bf)
    mlp = jnp.zeros_like(x)
    d_n2 = jnp.zeros_like(x)
    d_fc, d_proj, d_b_fc = [], [], []
    for t in range(2):
        act, slope = gelu_parts(dot(n2, all_fc[t]) + fc_bias[t])
        act = act.astype(bf)
        mlp = mlp + dot(act, all_proj[t], NT)
        d_pre = dot(d_mlp, all_proj[t]) * slope
        d_b_fc.append(jnp.sum(d_pre, axis=0))
        d_pre = d_pre.astype(bf)
        d_n2 = d_n2 + dot(d_pre, all_fc[t], NT)
        d_fc.append(dot(n2, d_pre, TN).astype(bf))
        d_proj.append(dot(d_mlp, act, TN).astype(bf))
    block_out = (middle + BRANCH_SCALE * (mlp + proj_bias)).astype(bf)
    block_out = lax.ppermute(block_out, BOTH, swap)
    blocks = lambda parts: jnp.stack(parts).reshape(2 * dp_size, rows, -1)
    sum_fc = scatter_sum(move_blocks(blocks(d_fc), place_a, True), first, dp_size)
    sum_proj = scatter_sum(move_blocks(blocks(d_proj), place_b, True), second, dp_size)

    back2, d_gain2, d_bias2 = layer_norm_back(hat2, inv2, gain2, d_n2)
    d_middle = grad_out + back2
    scaled_mid = BRANCH_SCALE * d_middle
    d_b_out = jnp.sum(scaled_mid, axis=0)
    d_attn = scaled_mid.astype(bf)
    do_send = dot(d_attn, wo_other).astype(bf)
    do_recv = exchange(do_send, 1, dp_size)
    do_own = dot(d_attn, wo_own).astype(bf)
    dwo_own = dot(d_attn, o_own, TN).astype(bf)
    dwo_other = dot(d_attn, o_recv, TN).astype(bf)
    dq_own, dq_send = attn_bwd(qkv_own, qkv_recv, do_own, do_recv, o_own, o_send, starts, lse, info)
    dq_recv = exchange(dq_send, 1, dp_size)
    d_n1 = dot(dq_own, take(qkv_w, core), NT) + dot(dq_recv, take(qkv_w, other), NT)
    dwq_own = dot(n1, dq_own, TN).astype(bf)
    dwq_other = dot(n1, dq_recv, TN).astype(bf)
    back1, d_gain1, d_bias1 = layer_norm_back(hat1, inv1, gain1, d_n1)
    grad_tokens = lax.ppermute((d_middle + back1).astype(bf), BOTH, swap)
    s_own = jnp.sum(dq_own.astype(f32), axis=0).reshape(3, cols)
    s_other = jnp.sum(dq_recv.astype(f32), axis=0).reshape(3, cols)
    pick = lambda a, b: jnp.where(core == 0, jnp.concatenate([a, b]), jnp.concatenate([b, a]))
    d_small = jnp.stack(
        [d_gain1, d_bias1, pick(s_own[0], s_other[0]), pick(s_own[2], s_other[2]), d_b_out, d_gain2, d_bias2, d_b_proj], axis=1)
    d_small = jnp.concatenate(
        [d_small, jnp.concatenate(d_b_fc).reshape(width, fan), jnp.zeros((width, SMALL - 8 - fan), f32)], axis=1).astype(bf)
    own_a = jnp.concatenate([dwq_own, dwo_own, d_small], axis=1)
    other_a = jnp.concatenate([dwq_other, dwo_other, d_small], axis=1)
    part_a = jnp.where(core == 0, jnp.stack([own_a, other_a]), jnp.stack([other_a, own_a])).reshape(2 * dp_size, rows, -1)
    sum_a = scatter_sum(move_blocks(part_a, place_a, True), first, dp_size).astype(f32)
    vecs = sum_a[:, 4 * cols :]
    return (
        block_out,
        grad_tokens,
        vecs[:, 0],
        vecs[:, 1],
        sum_a[:, : 3 * cols].reshape(rows, 3, cols),
        vecs[:, 2:4].T,
        sum_a[:, 3 * cols : 4 * cols].T,
        vecs[:, 4],
        vecs[:, 5],
        vecs[:, 6],
        sum_fc.astype(f32),
        vecs[:, 8 : 8 + fan].reshape(rows * fan),
        sum_proj.astype(f32).T,
        vecs[:, 7],
    )


def solution(mesh):
    vec, tok = P("dp"), P(BOTH, None)
    in_specs = (
        tok, P("dp", None), vec, vec, P("dp", None, "tensor"), P(None, "dp"), P("tensor", "dp"),
        vec, vec, vec, P("dp", "tensor"), vec, P("tensor", "dp"), vec, tok,
    )
    out_specs = (
        tok, tok, vec, vec, P("dp", None, "tensor"), P(None, "dp"), P("tensor", "dp"),
        vec, vec, vec, P("dp", "tensor"), vec, P("tensor", "dp"), vec,
    )
    return jax.shard_map(on_device, mesh=mesh, in_specs=in_specs, out_specs=out_specs, check_vma=False)
```

```python
import functools

import jax
import jax.numpy as jnp
from jax import lax
from jax.experimental import pallas as pl
from jax.experimental.pallas import tpu as pltpu
from jax.sharding import PartitionSpec as P

HD = 64
QB = 256
NEG = -1e30
EPSILON = 1e-05
BRANCH_SCALE = 48.0 ** (-0.5)
SMALL = 128
bf = jnp.bfloat16
f32 = jnp.float32
NT = (((1,), (1,)), ((), ()))
TN = (((0,), (0,)), ((), ()))
BOTH = ("dp", "tensor")
MESH_ID = pl.DeviceIdType.MESH
ANY = pl.BlockSpec(memory_space=pl.ANY)
VM = pl.BlockSpec(memory_space=pltpu.VMEM)
SM = pl.BlockSpec(memory_space=pltpu.SMEM)


def attn_info(seg, core):
    n=seg.shape[0]; nb=n//QB
    docs=jnp.arange(16,dtype=jnp.int32)
    first=jnp.sum((seg[None,:]<docs[:,None]).astype(jnp.int32),axis=1)
    starts=jnp.sum(jnp.where(seg[None,:]==docs[:,None],first[:,None],0),axis=0)
    blocks=starts.reshape(nb,QB)
    idx=jnp.arange(nb,dtype=jnp.int32)
    low=blocks[:,0]//QB
    mid=jnp.clip((blocks[:,QB-1]+QB-1)//QB,low,idx)
    return starts.reshape(1,n), jnp.concatenate([jnp.reshape(core,(1,)),low,mid]).astype(jnp.int32)

def fwd_kernel(info, own, recv, st_ref, okeep, osend, lse_ref, qm, ks, vt, osc, acc):
    half,cols=own.shape[0],own.shape[1]//3; n=2*half; nb=n//QB; heads=cols//HD; pairs=cols//128
    c=info[0]
    low_lane=(lax.broadcasted_iota(jnp.int32,(1,cols),1)%128)<HD
    zero=jnp.zeros((),bf)
    for base,src in ((c*half,own),((1-c)*half,recv)):
        rows=pl.ds(pl.multiple_of(base,half),half)
        qv=src[:,:cols]*bf(HD**-0.5)
        qm[0,rows]=jnp.where(low_lane,qv,zero)
        qm[1,rows]=jnp.where(low_lane,zero,qv)
        ks[rows]=src[:,cols:2*cols]
        vt[:,rows]=src[:,2*cols:].T
    kio=lax.broadcasted_iota(jnp.int32,(QB,QB),0)
    qio=lax.broadcasted_iota(jnp.int32,(QB,QB),1)
    def qblock(i,_):
        at=pl.multiple_of(i*QB,QB)
        srow=st_ref[:,pl.ds(at,QB)]
        acc[...]=jnp.zeros_like(acc)
        def step(mode,j,carry):
            kat=pl.multiple_of(j*QB,QB)
            if mode:
                mask=kio>=(srow-kat)
                if mode==2: mask=mask&(kio<=qio)
            out=[]
            for h in range(heads):
                m,l=carry[h]
                lanes=slice((h//2)*128,(h//2+1)*128); sub=slice(h*HD,(h+1)*HD)
                s=lax.dot_general(ks[pl.ds(kat,QB),lanes],qm[h%2,pl.ds(at,QB),lanes],NT,preferred_element_type=f32)
                if mode: s=jnp.where(mask,s,NEG)
                mn=jnp.maximum(m,jnp.max(s,axis=0,keepdims=True))
                p=jnp.exp(s-mn); a=jnp.exp(m-mn)
                l=a*l+jnp.sum(p,axis=0,keepdims=True)
                acc[sub]=a*acc[sub]+jnp.dot(vt[sub,pl.ds(kat,QB)],p.astype(bf),preferred_element_type=f32)
                out.append((mn,l))
            return tuple(out)
        one=(jnp.full((1,QB),NEG,f32),jnp.zeros((1,QB),f32))
        carry=step(2,i,(one,)*heads)
        carry=lax.fori_loop(info[1+i],info[1+nb+i],functools.partial(step,1),carry)
        carry=lax.fori_loop(info[1+nb+i],i,functools.partial(step,0),carry)
        for h,(m,l) in enumerate(carry):
            sub=slice(h*HD,(h+1)*HD)
            acc[sub]=acc[sub]/l
            lse_ref[h:h+1,pl.ds(at,QB)]=m+jnp.log(l)
        osc[pl.ds(at,QB)]=acc[...].T.astype(bf)
        return 0
    lax.fori_loop(0,nb,qblock,0)
    okeep[...]=osc[pl.ds(pl.multiple_of(c*half,half),half)]
    osend[...]=osc[pl.ds(pl.multiple_of((1-c)*half,half),half)]

def attn_fwd(own,recv,starts,info):
    half,cols=own.shape[0],own.shape[1]//3; n=2*half
    return pl.pallas_call(fwd_kernel,
        in_specs=[SM,VM,VM,VM], out_specs=[VM]*3,
        scratch_shapes=[pltpu.VMEM((2,n,cols),bf),pltpu.VMEM((n,cols),bf),pltpu.VMEM((cols,n),bf),pltpu.VMEM((n,cols),bf),pltpu.VMEM((cols,QB),f32)],
        out_shape=[jax.ShapeDtypeStruct((half,cols),bf)]*2+[jax.ShapeDtypeStruct((cols//HD,n),f32)],
        cost_estimate=pl.CostEstimate(flops=2*2*n*n//3*cols,bytes_accessed=8*half*cols*2,transcendentals=n*n*6//3),
        compiler_params=pltpu.CompilerParams(vmem_limit_bytes=48<<20),
    )(info,own,recv,starts)

def bwd_kernel(info, own, recv, doo, dor, oo, orr, st_ref, lse_ref, dkeep, dsend, qm, ks, vs, kt, dom, dlt, dqs, dks, dvs):
    half,cols=own.shape[0],own.shape[1]//3; n=2*half; nb=n//QB; heads=cols//HD; pairs=cols//128
    c=info[0]
    low_lane=(lax.broadcasted_iota(jnp.int32,(1,cols),1)%128)<HD
    zero=jnp.zeros((),bf)
    for base,src,do,o in ((c*half,own,doo,oo),((1-c)*half,recv,dor,orr)):
        rows=pl.ds(pl.multiple_of(base,half),half)
        qv=src[:,:cols]*bf(HD**-0.5)
        qm[0,rows]=jnp.where(low_lane,qv,zero)
        qm[1,rows]=jnp.where(low_lane,zero,qv)
        ks[rows]=src[:,cols:2*cols]
        vs[rows]=src[:,2*cols:]
        kt[:,rows]=src[:,cols:2*cols].T
        dv=do[...]
        dom[0,rows]=jnp.where(low_lane,dv,zero)
        dom[1,rows]=jnp.where(low_lane,zero,dv)
        prod=(dv.astype(f32)*o[...].astype(f32)).T
        for h in range(heads):
            dlt[h:h+1,rows]=jnp.sum(prod[h*HD:(h+1)*HD],axis=0,keepdims=True)
    dks[...]=jnp.zeros_like(dks); dvs[...]=jnp.zeros_like(dvs)
    kio=lax.broadcasted_iota(jnp.int32,(QB,QB),0)
    qio=lax.broadcasted_iota(jnp.int32,(QB,QB),1)
    def qblock(i,_):
        at=pl.multiple_of(i*QB,QB)
        qr=pl.ds(at,QB)
        srow=st_ref[:,qr]
        dqs[...]=jnp.zeros_like(dqs)
        def step(mode,j,carry):
            kat=pl.multiple_of(j*QB,QB); kr=pl.ds(kat,QB)
            if mode:
                mask=kio>=(srow-kat)
                if mode==2: mask=mask&(kio<=qio)
            for g in range(pairs):
                lanes=slice(g*128,(g+1)*128)
                ps=[];dss=[]
                for e in range(2):
                    h=2*g+e; sub=slice(h*HD,(h+1)*HD)
                    s=lax.dot_general(ks[kr,lanes],qm[e,qr,lanes],NT,preferred_element_type=f32)
                    if mode: s=jnp.where(mask,s,NEG)
                    p=jnp.exp(s-lse_ref[h:h+1,qr])
                    dp=lax.dot_general(vs[kr,lanes],dom[e,qr,lanes],NT,preferred_element_type=f32)
                    d=(p*(dp-dlt[h:h+1,qr])).astype(bf)
                    dqs[sub]+=jnp.dot(kt[sub,kr],d,preferred_element_type=f32)
                    ps.append(p.astype(bf)); dss.append(d)
                dcat=jnp.concatenate([dom[0,qr,lanes],dom[1,qr,lanes]],axis=0)
                qcat=jnp.concatenate([qm[0,qr,lanes],qm[1,qr,lanes]],axis=0)
                dvs[kr,lanes]+=jnp.dot(jnp.concatenate(ps,axis=1),dcat,preferred_element_type=f32)
                dks[kr,lanes]+=jnp.dot(jnp.concatenate(dss,axis=1),qcat,preferred_element_type=f32)
            return carry
        step(2,i,0)
        lax.fori_loop(info[1+i],info[1+nb+i],functools.partial(step,1),0)
        lax.fori_loop(info[1+nb+i],i,functools.partial(step,0),0)
        qm[0,qr]=(dqs[...]*(HD**-0.5)).T.astype(bf)
        return 0
    lax.fori_loop(0,nb,qblock,0)
    for dst,base in ((dkeep,c*half),(dsend,(1-c)*half)):
        rows=pl.ds(pl.multiple_of(base,half),half)
        dst[:,:cols]=qm[0,rows]
        dst[:,cols:2*cols]=dks[rows].astype(bf)
        dst[:,2*cols:]=dvs[rows].astype(bf)

def attn_bwd(own,recv,do_own,do_recv,o_own,o_recv,starts,lse,info):
    half,cols=own.shape[0],own.shape[1]//3; n=2*half
    return pl.pallas_call(bwd_kernel,
        in_specs=[SM]+[VM]*8, out_specs=[VM]*2,
        scratch_shapes=[pltpu.VMEM((2,n,cols),bf),pltpu.VMEM((n,cols),bf),pltpu.VMEM((n,cols),bf),pltpu.VMEM((cols,n),bf),pltpu.VMEM((2,n,cols),bf),pltpu.VMEM((cols//HD,n),f32),
                            pltpu.VMEM((cols,QB),f32),pltpu.VMEM((n,cols),f32),pltpu.VMEM((n,cols),f32)],
        out_shape=[jax.ShapeDtypeStruct((half,3*cols),bf)]*2,
        cost_estimate=pl.CostEstimate(flops=2*5*n*n//3*cols,bytes_accessed=16*half*cols*2,transcendentals=n*n*6//3),
        compiler_params=pltpu.CompilerParams(vmem_limit_bytes=56<<20),
    )(info,own,recv,do_own,do_recv,o_own,o_recv,starts,lse)


def dot(left, right, dims=(((1,), (0,)), ((), ()))):
    return lax.dot_general(left, right, dims, preferred_element_type=f32)


def exchange(value, bit, dp_size):
    if bit:
        return lax.ppermute(value, "dp", [(i, i ^ bit) for i in range(dp_size)])
    return lax.ppermute(value, "tensor", [(0, 1), (1, 0)])


def flip(index, bits):
    for bit in bits:
        index = index + bit * (1 - 2 * ((index // bit) % 2))
    return index

def far_groups(dp_size):
    far = [1 << k for k in range(dp_size.bit_length() - 2, 1, -1)]
    return [tuple(far[k : k + 2]) for k in range(0, len(far), 2)]

def group_moves(group):
    if len(group) == 1:
        return [(1, group)]
    return [(1, group[:1]), (2, group[1:]), (3, group)]

def chunks_of(cols, which, count, until=None):
    tiles = cols // 128
    cuts = [128 * ((tiles * k) // count) for k in range(count + 1)]
    arrays = range(which, until + 1) if until else (which,)
    return tuple(
        (array, low, high - low, 128 * max(1, (high - low) * 2 // 3 // 128))
        for low, high in zip(cuts, cuts[1:]) for array in arrays)


def head_kernel(groups, chunks, tokens, *refs):
    shards, x_out, outs, (send_sem, recv_sem, local_sem) = refs[:4], refs[4], refs[5:9], refs[9:]
    dp, t = lax.axis_index("dp"), lax.axis_index("tensor")
    core = dp % 2
    away = core + t - 2 * core * t
    near = {1: (flip(dp, (1,)), t), 2: (flip(dp, (2,)), t), 0: (dp, 1 - t)}
    distant = [bits for group in groups for _, bits in group_moves(group)]
    swap = (dp - core + t, core)
    barrier = pltpu.get_barrier_semaphore()
    for device in list(near.values()) + [(flip(dp, bits), t) for bits in distant]:
        pl.semaphore_signal(barrier, inc=1, device_id=device, device_id_type=MESH_ID)

    @pl.when(away == 1)
    def _():
        pl.semaphore_signal(barrier, inc=1, device_id=swap, device_id_type=MESH_ID)

    local = [
        pltpu.make_async_copy(shards[k], outs[k].at[away if k < 2 else 0, 0], local_sem.at[k]) for k in range(4)]
    for copy in local:
        copy.start()
    pl.semaphore_wait(barrier, len(near) + len(distant) + away)
    count = [0]

    def remote(src, dst, device):
        slot = count[0]
        count[0] += 1
        return pltpu.make_async_remote_copy(
            src_ref=src, dst_ref=dst, send_sem=send_sem.at[slot], recv_sem=recv_sem.at[slot],
            device_id=device, device_id_type=MESH_ID)

    def blocks(ref, index, first, held, low, size):
        return ref.at[index, pl.ds(first, held), :, pl.ds(low, size)]

    plans = []
    for which, low, size, half in chunks:
        shard, out, by_group = shards[which], outs[which], which < 2
        first = away if by_group else 0
        steps, held = [], 1
        for group in groups:
            moves = []
            for place, bits in group_moves(group):
                src = shard.at[:, pl.ds(low, size)] if held == 1 else blocks(out, first, 0, held, low, size)
                dst = out.at[first, place, :, pl.ds(low, size)] if held == 1 else blocks(out, first, place * held, held, low, size)
                moves.append(remote(src, dst, (flip(dp, bits), t)))
            held *= len(group_moves(group)) + 1
            steps.append(moves)
        a, b = (low, half), (low + half, size - half)
        other = first if by_group else 1
        steps.append([
            remote(blocks(out, first, 0, held, *a), blocks(out, other, 0, held, *a), near[0]),
            remote(blocks(out, first, 0, held, *b), blocks(out, first, held, held, *b), near[2]),
        ])
        steps.append(
            [remote(blocks(out, k, 0, held, *a), blocks(out, k, held, held, *a), near[2]) for k in range(2)]
            + [remote(blocks(out, first, 0, 2 * held, *b), blocks(out, other, 0, 2 * held, *b), near[0])])
        steps.append([
            remote(blocks(out, k, 0, 2 * held, low, size),
                   blocks(out, 1 - k if by_group else k, 2 * held, 2 * held, low, size), near[1]) for k in range(2)])
        plans.append(steps)
    depth = len(plans[0])
    swap_copy = remote(tokens, x_out, swap)
    stay_copy = pltpu.make_async_copy(tokens, x_out, local_sem.at[4])
    waited = set()

    def advance(number, phase):
        if number >= len(plans):
            return
        if phase > 0:
            for move in plans[number][phase - 1]:
                move.wait_recv()
        if phase == 1 and chunks[number][0] not in waited:
            waited.add(chunks[number][0])
            local[chunks[number][0]].wait()
        if phase < depth:
            for move in plans[number][phase]:
                move.start()

    advance(0, 0)

    @pl.when(away == 1)
    def _():
        swap_copy.start()

    @pl.when(away == 0)
    def _():
        stay_copy.start()

    far = len(groups)
    for number in range(len(plans)):
        if number == 0:
            for phase in range(1, far + 1):
                advance(0, phase)
            advance(1, 0)
        advance(number, far + 1)
        for phase in range(1, far + 1):
            advance(number + 1, phase)
        advance(number + 2, 0)
        advance(number, far + 2)
    for number in range(len(plans)):
        advance(number, depth)

    @pl.when(away == 1)
    def _():
        swap_copy.wait()

    @pl.when(away == 0)
    def _():
        stay_copy.wait()

    for which in sorted(set(range(4)) - waited):
        local[which].wait()
    for steps in plans:
        for moves in steps:
            for move in moves:
                move.wait_send()


def head(dp_size, tokens, shards, chunks):
    groups = far_groups(dp_size)
    slots = len(chunks) * (sum(len(group_moves(g)) for g in groups) + 7) + 1
    return pl.pallas_call(
        functools.partial(head_kernel, groups, chunks),
        in_specs=[VM] * 5,
        out_specs=[ANY] * 5,
        out_shape=[jax.ShapeDtypeStruct(tokens.shape, tokens.dtype)]
        + [jax.ShapeDtypeStruct((2, dp_size) + s.shape, s.dtype) for s in shards],
        scratch_shapes=[pltpu.SemaphoreType.DMA((slots,)), pltpu.SemaphoreType.DMA((slots,)), pltpu.SemaphoreType.DMA((5,))],
        compiler_params=pltpu.CompilerParams(collective_id=0, has_side_effects=True),
    )(tokens, *shards)


def halve_rows(kept, bits, dp_size):
    for bit in bits:
        n = kept[0].shape[0] // 2
        kept = [add_low(k[:n], exchange(k[n:], bit, dp_size)) for k in kept]
    return kept


def add_low(left, right):
    return (left.astype(f32) + right.astype(f32)).astype(bf)


def layer_norm_parts(values):
    centered = values - jnp.mean(values, axis=-1, keepdims=True)
    inverse = lax.rsqrt(jnp.mean(centered * centered, axis=-1, keepdims=True) + EPSILON)
    return centered * inverse, inverse


def layer_norm_back(hat, inverse, gain, grad):
    scaled = grad * gain
    back = inverse * (
        scaled
        - jnp.mean(scaled, axis=-1, keepdims=True)
        - hat * jnp.mean(scaled * hat, axis=-1, keepdims=True)
    )
    return back, jnp.sum(grad * hat, axis=0), jnp.sum(grad, axis=0)


def gelu_parts(pre):
    root = 0.7978845608
    inner = jnp.tanh(root * (pre + 0.044715 * pre * pre * pre))
    value = 0.5 * pre * (1.0 + inner)
    slope = 0.5 * (1.0 + inner) + 0.5 * pre * (1.0 - inner * inner) * root * (
        1.0 + 3 * 0.044715 * pre * pre
    )
    return value, slope


def on_device(
    tokens, segment_ids, ln1_gain, ln1_bias, w_qkv, b_qv, w_attn_out, b_attn_out,
    ln2_gain, ln2_bias, w_fc, b_fc, w_proj, b_proj, cotangent,
):
    dp_size = lax.axis_size("dp")
    dp_pos, t_pos = lax.axis_index("dp"), lax.axis_index("tensor")
    core = dp_pos % 2
    rows = ln1_gain.shape[0]
    width = tokens.shape[1]
    cols = w_qkv.shape[2]
    hidden = w_fc.shape[1]
    fan = b_fc.shape[0] // rows
    far = [1 << k for k in range(dp_size.bit_length() - 2, 1, -1)]
    swap = []
    for d in range(dp_size):
        for t in range(2):
            swap.append((2 * d + t, 2 * (d - d % 2 + t) + d % 2))
    mine = core == t_pos

    seg_other = exchange(segment_ids, 1, dp_size)
    seg = jnp.where(mine, segment_ids, seg_other)[0]
    small = jnp.concatenate(
        [ln1_gain[:, None], ln1_bias[:, None], b_qv.T, b_attn_out[:, None], ln2_gain[:, None],
         ln2_bias[:, None], b_proj[:, None], b_fc.reshape(rows, fan)], axis=1)
    small = jnp.pad(small, ((0, 0), (0, SMALL - small.shape[1])))
    out_pack = jnp.concatenate([w_attn_out.T, small], axis=1)
    tokens, all_qkv, all_out, all_fc, all_proj = head(
        dp_size, tokens, (w_qkv.reshape(rows, 3 * cols), out_pack, w_fc, w_proj.T),
        chunks_of(3 * cols, 0, 2) + chunks_of(cols + SMALL, 1, 1) + chunks_of(hidden, 2, 2, 3))
    all_qkv, all_out, all_fc, all_proj = (a.reshape(2, width, -1) for a in (all_qkv, all_out, all_fc, all_proj))

    place = jnp.arange(width, dtype=jnp.int32)
    block = place // rows
    source = jnp.zeros_like(block)
    for k, bit in enumerate(far + [2, 1]):
        source = source + ((block >> k) & 1) * bit
    natural = (source ^ dp_pos) * rows + place % rows
    order = (place[:, None] == natural[None, :]).astype(bf)

    vec_rel = all_out[0, :, cols:]
    vec_nat = dot(order, vec_rel).T
    vec_rel = vec_rel.astype(f32).T
    gain1, bias1, _, _, out_bias, gain2, bias2, proj_bias = (vec_rel[k] for k in range(8))
    fc_bias = vec_nat[8 : 8 + fan].T.reshape(2, hidden)
    b_q, b_v = vec_nat[2].reshape(2, cols), vec_nat[3].reshape(2, cols)
    take = lambda arr, k: lax.dynamic_index_in_dim(arr, k, 0, keepdims=False)
    other = 1 - core
    qkv_bias = lambda k: jnp.concatenate([take(b_q, k), jnp.zeros((cols,), f32), take(b_v, k)])

    x = dot(tokens, order)
    hat1, inv1 = layer_norm_parts(x)
    n1 = (hat1 * gain1 + bias1).astype(bf)
    wq_own, wq_other = all_qkv[0], all_qkv[1]
    wo_own, wo_other = all_out[0, :, :cols], all_out[1, :, :cols]
    qkv_send = (dot(n1, wq_other) + qkv_bias(other)).astype(bf)
    qkv_recv = exchange(qkv_send, 1, dp_size)
    qkv_own = (dot(n1, wq_own) + qkv_bias(core)).astype(bf)
    starts, info = attn_info(seg, core)
    o_own, o_send, lse = attn_fwd(qkv_own, qkv_recv, starts, info)
    o_recv = exchange(o_send, 1, dp_size)
    branch = dot(o_own, wo_own, NT) + dot(o_recv, wo_other, NT) + out_bias
    middle = x + BRANCH_SCALE * branch
    hat2, inv2 = layer_norm_parts(middle)
    n2 = (hat2 * gain2 + bias2).astype(bf)
    grad_out = dot(lax.ppermute(cotangent, BOTH, swap), order)
    scaled_out = BRANCH_SCALE * grad_out
    d_b_proj = jnp.sum(scaled_out, axis=0)
    d_mlp = scaled_out.astype(bf)
    mlp = jnp.zeros_like(x)
    d_n2 = jnp.zeros_like(x)
    half = width // 2

    def weight_grad(left, right):
        return dot(left[:, :half], right, TN).astype(bf), dot(left[:, half:], right, TN).astype(bf)

    sum_fc, sum_proj, d_b_fc = [], [], []
    for k in range(2):
        act, slope = gelu_parts(dot(n2, all_fc[k]) + take(fc_bias, t_pos ^ k))
        act = act.astype(bf)
        mlp = mlp + dot(act, all_proj[k], NT)
        d_pre = dot(d_mlp, all_proj[k]) * slope
        d_b_fc.append(jnp.sum(d_pre, axis=0))
        d_pre = d_pre.astype(bf)
        d_n2 = d_n2 + dot(d_pre, all_fc[k], NT)
        keep, send = weight_grad(n2, d_pre)
        sum_fc.append(add_low(keep, exchange(send, 1, dp_size)))
        keep, send = weight_grad(d_mlp, act)
        sum_proj.append(add_low(keep, exchange(send, 1, dp_size)))
    down = far[::-1]
    sum_fc = add_low(sum_fc[0], exchange(sum_fc[1], 0, dp_size))
    (sum_fc,) = halve_rows([sum_fc], [2] + down, dp_size)
    sum_proj = halve_rows(sum_proj, [2], dp_size)
    sum_proj = add_low(sum_proj[0], exchange(sum_proj[1], 0, dp_size))
    (sum_proj,) = halve_rows([sum_proj], down, dp_size)
    block_out = (middle + BRANCH_SCALE * (mlp + proj_bias)).astype(bf)
    block_out = lax.ppermute(dot(block_out, order, NT).astype(bf), BOTH, swap)

    back2, d_gain2, d_bias2 = layer_norm_back(hat2, inv2, gain2, d_n2)
    d_middle = grad_out + back2
    scaled_mid = BRANCH_SCALE * d_middle
    d_b_out = jnp.sum(scaled_mid, axis=0)
    d_attn = scaled_mid.astype(bf)
    do_send = dot(d_attn, wo_other).astype(bf)
    do_recv = exchange(do_send, 1, dp_size)
    do_own = dot(d_attn, wo_own).astype(bf)

    def reduce_pair(own_keep, own_send, other_keep, other_send):
        own = add_low(own_keep, exchange(other_send, 1, dp_size))
        rest = add_low(other_keep, exchange(own_send, 1, dp_size))
        keep, send = jnp.where(mine, own, rest), jnp.where(mine, rest, own)
        total = add_low(keep, exchange(send, 0, dp_size))
        (total,) = halve_rows([total], [2] + down, dp_size)
        return total

    sum_out = reduce_pair(*weight_grad(d_attn, o_own), *weight_grad(d_attn, o_recv))
    dq_own, dq_send = attn_bwd(qkv_own, qkv_recv, do_own, do_recv, o_own, o_send, starts, lse, info)
    dq_recv = exchange(dq_send, 1, dp_size)
    d_n1 = dot(dq_own, wq_own, NT) + dot(dq_recv, wq_other, NT)
    back1, d_gain1, d_bias1 = layer_norm_back(hat1, inv1, gain1, d_n1)
    grad_tokens = dot((d_middle + back1).astype(bf), order, NT).astype(bf)
    grad_tokens = lax.ppermute(grad_tokens, BOTH, swap)
    s_own = jnp.sum(dq_own.astype(f32), axis=0).reshape(3, cols)
    s_other = jnp.sum(dq_recv.astype(f32), axis=0).reshape(3, cols)
    pick = lambda cond, a, b: jnp.where(cond, jnp.concatenate([a, b]), jnp.concatenate([b, a]))
    nat = jnp.concatenate(
        [pick(core == 0, s_own[0], s_other[0])[:, None], pick(core == 0, s_own[2], s_other[2])[:, None],
         pick(t_pos == 0, *d_b_fc).reshape(width, fan)], axis=1).astype(bf)
    nat = dot(order, nat, TN)
    d_small = jnp.stack([d_gain1, d_bias1, nat[:, 0], nat[:, 1], d_b_out, d_gain2, d_bias2, d_b_proj], axis=1)
    d_small = jnp.concatenate([d_small, nat[:, 2:], jnp.zeros((width, SMALL - 8 - fan), f32)], axis=1).astype(bf)
    with_small = lambda pair: [
        jnp.concatenate([pair[0], d_small[:half]], axis=1), jnp.concatenate([pair[1], d_small[half:]], axis=1)]
    sum_a = reduce_pair(*with_small(weight_grad(n1, dq_own)), *with_small(weight_grad(n1, dq_recv))).astype(f32)
    vecs = sum_a[:, 3 * cols :]
    return (
        block_out,
        grad_tokens,
        vecs[:, 0],
        vecs[:, 1],
        sum_a[:, : 3 * cols].reshape(rows, 3, cols),
        vecs[:, 2:4].T,
        sum_out.astype(f32).T,
        vecs[:, 4],
        vecs[:, 5],
        vecs[:, 6],
        sum_fc.astype(f32),
        vecs[:, 8 : 8 + fan].reshape(rows * fan),
        sum_proj.astype(f32).T,
        vecs[:, 7],
    )


def solution(mesh):
    vec, tok = P("dp"), P(BOTH, None)
    in_specs = (
        tok, P("dp", None), vec, vec, P("dp", None, "tensor"), P(None, "dp"), P("tensor", "dp"),
        vec, vec, vec, P("dp", "tensor"), vec, P("tensor", "dp"), vec, tok,
    )
    out_specs = (
        tok, tok, vec, vec, P("dp", None, "tensor"), P(None, "dp"), P("tensor", "dp"),
        vec, vec, vec, P("dp", "tensor"), vec, P("tensor", "dp"), vec,
    )
    return jax.shard_map(on_device, mesh=mesh, in_specs=in_specs, out_specs=out_specs, check_vma=False)
```

```python
import functools

import jax
import jax.numpy as jnp
from jax import lax
from jax.experimental import pallas as pl
from jax.experimental.pallas import tpu as pltpu
from jax.sharding import PartitionSpec as P

HD = 64
QB = 256
NEG = -1e30
EPSILON = 1e-05
BRANCH_SCALE = 48.0 ** (-0.5)
SMALL = 128
bf = jnp.bfloat16
f32 = jnp.float32
NT = (((1,), (1,)), ((), ()))
TN = (((0,), (0,)), ((), ()))
BOTH = ("dp", "tensor")
MESH_ID = pl.DeviceIdType.MESH
ANY = pl.BlockSpec(memory_space=pl.ANY)
VM = pl.BlockSpec(memory_space=pltpu.VMEM)
SM = pl.BlockSpec(memory_space=pltpu.SMEM)


def attn_info(seg, core):
    n=seg.shape[0]; nb=n//QB
    docs=jnp.arange(16,dtype=jnp.int32)
    first=jnp.sum((seg[None,:]<docs[:,None]).astype(jnp.int32),axis=1)
    starts=jnp.sum(jnp.where(seg[None,:]==docs[:,None],first[:,None],0),axis=0)
    blocks=starts.reshape(nb,QB)
    idx=jnp.arange(nb,dtype=jnp.int32)
    low=blocks[:,0]//QB
    mid=jnp.clip((blocks[:,QB-1]+QB-1)//QB,low,idx)
    return starts.reshape(1,n), jnp.concatenate([jnp.reshape(core,(1,)),low,mid]).astype(jnp.int32)

def attn_masks(kat, srow, diagonal):
    keys = lax.broadcasted_iota(jnp.int32, (QB, QB), 0)
    mask = keys >= (srow - kat)
    if diagonal:
        mask = mask & (keys <= lax.broadcasted_iota(jnp.int32, (QB, QB), 1))
    return mask


def head_lanes(values):
    low = (lax.broadcasted_iota(jnp.int32, (1, values.shape[1]), 1) % 128) < HD
    zero = jnp.zeros((), bf)
    return jnp.where(low, values, zero), jnp.where(low, zero, values)


def fwd_kernel(info, own, recv, st_ref, okeep, osend, lse_ref, qm, ks, vt, osc, acc):
    half, cols = own.shape[0], own.shape[1] // 3
    n, nb, heads, pairs = 2 * half, 2 * half // QB, cols // HD, cols // 128
    c = info[0]
    for base, src in ((c * half, own), ((1 - c) * half, recv)):
        rows = pl.ds(pl.multiple_of(base, half), half)
        for g in range(pairs):
            lanes = slice(g * 128, (g + 1) * 128)
            part = lambda k: src[:, (3 * g + k) * 128 : (3 * g + k + 1) * 128]
            qm[0, rows, lanes], qm[1, rows, lanes] = head_lanes(part(0) * bf(HD**-0.5))
            ks[rows, lanes] = part(1)
            vt[lanes, rows] = part(2).T

    def qblock(i, _):
        at = pl.multiple_of(i * QB, QB)
        qr = pl.ds(at, QB)
        srow = st_ref[:, qr]
        acc[...] = jnp.zeros_like(acc)

        def step(mode, j, carry):
            kat = pl.multiple_of(j * QB, QB)
            kr = pl.ds(kat, QB)
            if mode:
                mask = attn_masks(kat, srow, mode == 2)
            scores, mixed = [], []
            for h in range(heads):
                lanes = slice(h // 2 * 128, h // 2 * 128 + 128)
                one = lax.dot_general(ks[kr, lanes], qm[h % 2, qr, lanes], NT, preferred_element_type=f32)
                scores.append(jnp.where(mask, one, NEG) if mode else one)
            for h in range(heads):
                top, total = carry[h]
                new = jnp.maximum(top, jnp.max(scores[h], axis=0, keepdims=True))
                weights = jnp.exp(scores[h] - new)
                fade = jnp.exp(top - new)
                total = fade * total + jnp.sum(weights, axis=0, keepdims=True)
                mixed.append((new, total, fade, weights.astype(bf)))
            for h in range(heads):
                sub = slice(h * HD, (h + 1) * HD)
                acc[sub] = mixed[h][2] * acc[sub] + jnp.dot(vt[sub, kr], mixed[h][3], preferred_element_type=f32)
            return tuple(m[:2] for m in mixed)

        carry = step(2, i, ((jnp.full((1, QB), NEG, f32), jnp.zeros((1, QB), f32)),) * heads)
        carry = lax.fori_loop(info[1 + i], info[1 + nb + i], functools.partial(step, 1), carry)
        carry = lax.fori_loop(info[1 + nb + i], i, functools.partial(step, 0), carry)
        for h, (top, total) in enumerate(carry):
            sub = slice(h * HD, (h + 1) * HD)
            acc[sub] = acc[sub] / total
            lse_ref[h : h + 1, qr] = top + jnp.log(total)
        osc[qr] = acc[...].T.astype(bf)
        return 0

    lax.fori_loop(0, nb, qblock, 0)
    okeep[...] = osc[pl.ds(pl.multiple_of(c * half, half), half)]
    osend[...] = osc[pl.ds(pl.multiple_of((1 - c) * half, half), half)]


def attn_fwd(own, recv, starts, info):
    half, cols = own.shape[0], own.shape[1] // 3
    n = 2 * half
    return pl.pallas_call(
        fwd_kernel,
        in_specs=[SM, VM, VM, VM],
        out_specs=[VM] * 3,
        scratch_shapes=[
            pltpu.VMEM((2, n, cols), bf), pltpu.VMEM((n, cols), bf), pltpu.VMEM((cols, n), bf),
            pltpu.VMEM((n, cols), bf), pltpu.VMEM((cols, QB), f32)],
        out_shape=[jax.ShapeDtypeStruct((half, cols), bf)] * 2 + [jax.ShapeDtypeStruct((cols // HD, n), f32)],
        cost_estimate=pl.CostEstimate(flops=4 * n * n * cols, bytes_accessed=8 * half * cols * 2, transcendentals=2 * n * n),
        compiler_params=pltpu.CompilerParams(vmem_limit_bytes=48 << 20),
    )(info, own, recv, starts)


def bwd_kernel(first, info, own, recv, doo, dor, oo, orr, st_ref, lse_ref, dkeep, dsend, qm, ks, vs, kt, dom, dlt, dqs, dks, dvs):
    half, n, nb = own.shape[0], 2 * own.shape[0], 2 * own.shape[0] // QB
    c = info[0]
    for base, src, do, o in ((c * half, own, doo, oo), ((1 - c) * half, recv, dor, orr)):
        rows = pl.ds(pl.multiple_of(base, half), half)
        qm[0, rows], qm[1, rows] = head_lanes(src[:, :128] * bf(HD**-0.5))
        ks[rows] = src[:, 128:256]
        vs[rows] = src[:, 256:]
        kt[:, rows] = src[:, 128:256].T
        dom[0, rows], dom[1, rows] = head_lanes(do[...])
        prod = (do[...].astype(f32) * o[...].astype(f32)).T
        for h in range(2):
            dlt[h : h + 1, rows] = jnp.sum(prod[h * HD : (h + 1) * HD], axis=0, keepdims=True)
    dks[...] = jnp.zeros_like(dks)
    dvs[...] = jnp.zeros_like(dvs)

    def qblock(i, _):
        at = pl.multiple_of(i * QB, QB)
        qr = pl.ds(at, QB)
        srow = st_ref[:, qr]
        dqs[...] = jnp.zeros_like(dqs)

        def step(mode, j, carry):
            kat = pl.multiple_of(j * QB, QB)
            kr = pl.ds(kat, QB)
            if mode:
                mask = attn_masks(kat, srow, mode == 2)
            scores, softs, grads = [], [], []
            for h in range(2):
                one = lax.dot_general(ks[kr], qm[h, qr], NT, preferred_element_type=f32)
                back = lax.dot_general(vs[kr], dom[h, qr], NT, preferred_element_type=f32)
                scores.append((jnp.where(mask, one, NEG) if mode else one, back))
            for h in range(2):
                soft = jnp.exp(scores[h][0] - lse_ref[first + h : first + h + 1, qr])
                grads.append((soft * (scores[h][1] - dlt[h : h + 1, qr])).astype(bf))
                softs.append(soft.astype(bf))
            both = lambda ref: jnp.concatenate([ref[0, qr], ref[1, qr]], axis=0)
            dvs[kr] += jnp.dot(jnp.concatenate(softs, axis=1), both(dom), preferred_element_type=f32)
            dks[kr] += jnp.dot(jnp.concatenate(grads, axis=1), both(qm), preferred_element_type=f32)
            for h in range(2):
                sub = slice(h * HD, (h + 1) * HD)
                dqs[sub] += jnp.dot(kt[sub, kr], grads[h], preferred_element_type=f32)
            return carry

        step(2, i, 0)
        lax.fori_loop(info[1 + i], info[1 + nb + i], functools.partial(step, 1), 0)
        lax.fori_loop(info[1 + nb + i], i, functools.partial(step, 0), 0)
        qm[0, qr] = (dqs[...] * (HD**-0.5)).T.astype(bf)
        return 0

    lax.fori_loop(0, nb, qblock, 0)
    for dst, base in ((dkeep, c * half), (dsend, (1 - c) * half)):
        rows = pl.ds(pl.multiple_of(base, half), half)
        dst[:, :128] = qm[0, rows]
        dst[:, 128:256] = dks[rows].astype(bf)
        dst[:, 256:] = dvs[rows].astype(bf)


def attn_bwd(pair, own, recv, do_own, do_recv, o_own, o_recv, starts, lse, info):
    half = own.shape[0]
    n = 2 * half
    wide = pl.BlockSpec((half, 384), lambda k, s: (0, pair))
    slim = pl.BlockSpec((half, 128), lambda k, s: (0, pair))
    whole = lambda a: pl.BlockSpec(a.shape, lambda k, s: (0, 0))
    return pl.pallas_call(
        functools.partial(bwd_kernel, 2 * pair),
        grid_spec=pltpu.PrefetchScalarGridSpec(
            num_scalar_prefetch=1,
            grid=(1,),
            in_specs=[wide, wide, slim, slim, slim, slim, whole(starts), whole(lse)],
            out_specs=[pl.BlockSpec((half, 384), lambda k, s: (0, 0))] * 2,
            scratch_shapes=[
                pltpu.VMEM((2, n, 128), bf), pltpu.VMEM((n, 128), bf), pltpu.VMEM((n, 128), bf), pltpu.VMEM((128, n), bf),
                pltpu.VMEM((2, n, 128), bf), pltpu.VMEM((2, n), f32), pltpu.VMEM((128, QB), f32), pltpu.VMEM((n, 128), f32),
                pltpu.VMEM((n, 128), f32)],
        ),
        out_shape=[jax.ShapeDtypeStruct((half, 384), bf)] * 2,
        cost_estimate=pl.CostEstimate(flops=10 * n * n * 128, bytes_accessed=16 * half * 128 * 2, transcendentals=n * n),
        compiler_params=pltpu.CompilerParams(vmem_limit_bytes=40 << 20),
    )(info, own, recv, do_own, do_recv, o_own, o_recv, starts, lse)


def dot(left, right, dims=(((1,), (0,)), ((), ()))):
    return lax.dot_general(left, right, dims, preferred_element_type=f32)


def exchange(value, bit, dp_size):
    if bit:
        return lax.ppermute(value, "dp", [(i, i ^ bit) for i in range(dp_size)])
    return lax.ppermute(value, "tensor", [(0, 1), (1, 0)])


def flip(index, bits):
    for bit in bits:
        index = index + bit * (1 - 2 * ((index // bit) % 2))
    return index

def far_groups(dp_size):
    far = [1 << k for k in range(dp_size.bit_length() - 2, 1, -1)]
    return [tuple(far[k : k + 2]) for k in range(0, len(far), 2)]

def group_moves(group):
    if len(group) == 1:
        return [(1, group)]
    return [(1, group[:1]), (2, group[1:]), (3, group)]

def chunks_of(cols, which, count, until=None):
    tiles = cols // 128
    cuts = [128 * ((tiles * k) // count) for k in range(count + 1)]
    arrays = range(which, until + 1) if until else (which,)
    return tuple(
        (array, low, high - low, 128 * max(1, (high - low) * 2 // 3 // 128))
        for low, high in zip(cuts, cuts[1:]) for array in arrays)


def head_kernel(groups, chunks, tokens, *refs):
    shards, x_out, outs, (send_sem, recv_sem, local_sem) = refs[:4], refs[4], refs[5:9], refs[9:]
    dp, t = lax.axis_index("dp"), lax.axis_index("tensor")
    core = dp % 2
    away = core + t - 2 * core * t
    near = {1: (flip(dp, (1,)), t), 2: (flip(dp, (2,)), t), 0: (dp, 1 - t)}
    distant = [bits for group in groups for _, bits in group_moves(group)]
    swap = (dp - core + t, core)
    barrier = pltpu.get_barrier_semaphore()
    for device in list(near.values()) + [(flip(dp, bits), t) for bits in distant]:
        pl.semaphore_signal(barrier, inc=1, device_id=device, device_id_type=MESH_ID)

    @pl.when(away == 1)
    def _():
        pl.semaphore_signal(barrier, inc=1, device_id=swap, device_id_type=MESH_ID)

    local = [
        pltpu.make_async_copy(shards[k], outs[k].at[away if k < 2 else 0, 0], local_sem.at[k]) for k in range(4)]
    for copy in local:
        copy.start()
    pl.semaphore_wait(barrier, len(near) + len(distant) + away)
    count = [0]

    def remote(src, dst, device):
        slot = count[0]
        count[0] += 1
        return pltpu.make_async_remote_copy(
            src_ref=src, dst_ref=dst, send_sem=send_sem.at[slot], recv_sem=recv_sem.at[slot],
            device_id=device, device_id_type=MESH_ID)

    def blocks(ref, index, first, held, low, size):
        return ref.at[index, pl.ds(first, held), :, pl.ds(low, size)]

    plans = []
    for which, low, size, half in chunks:
        shard, out, by_group = shards[which], outs[which], which < 2
        first = away if by_group else 0
        steps, held = [], 1
        for group in groups:
            moves = []
            for place, bits in group_moves(group):
                src = shard.at[:, pl.ds(low, size)] if held == 1 else blocks(out, first, 0, held, low, size)
                dst = out.at[first, place, :, pl.ds(low, size)] if held == 1 else blocks(out, first, place * held, held, low, size)
                moves.append(remote(src, dst, (flip(dp, bits), t)))
            held *= len(group_moves(group)) + 1
            steps.append(moves)
        a, b = (low, half), (low + half, size - half)
        other = first if by_group else 1
        steps.append([
            remote(blocks(out, first, 0, held, *a), blocks(out, other, 0, held, *a), near[0]),
            remote(blocks(out, first, 0, held, *b), blocks(out, first, held, held, *b), near[2]),
        ])
        steps.append(
            [remote(blocks(out, k, 0, held, *a), blocks(out, k, held, held, *a), near[2]) for k in range(2)]
            + [remote(blocks(out, first, 0, 2 * held, *b), blocks(out, other, 0, 2 * held, *b), near[0])])
        steps.append([
            remote(blocks(out, k, 0, 2 * held, low, size),
                   blocks(out, 1 - k if by_group else k, 2 * held, 2 * held, low, size), near[1]) for k in range(2)])
        plans.append(steps)
    depth = len(plans[0])
    swap_copy = remote(tokens, x_out, swap)
    stay_copy = pltpu.make_async_copy(tokens, x_out, local_sem.at[4])
    waited = set()

    def advance(number, phase):
        if number >= len(plans):
            return
        if phase > 0:
            for move in plans[number][phase - 1]:
                move.wait_recv()
        if phase == 1 and chunks[number][0] not in waited:
            waited.add(chunks[number][0])
            local[chunks[number][0]].wait()
        if phase < depth:
            for move in plans[number][phase]:
                move.start()

    advance(0, 0)

    @pl.when(away == 1)
    def _():
        swap_copy.start()

    @pl.when(away == 0)
    def _():
        stay_copy.start()

    far = len(groups)
    for number in range(len(plans)):
        if number == 0:
            for phase in range(1, far + 1):
                advance(0, phase)
            advance(1, 0)
        advance(number, far + 1)
        for phase in range(1, far + 1):
            advance(number + 1, phase)
        advance(number + 2, 0)
        advance(number, far + 2)
    for number in range(len(plans)):
        advance(number, depth)

    @pl.when(away == 1)
    def _():
        swap_copy.wait()

    @pl.when(away == 0)
    def _():
        stay_copy.wait()

    for which in sorted(set(range(4)) - waited):
        local[which].wait()
    for steps in plans:
        for moves in steps:
            for move in moves:
                move.wait_send()


def head(dp_size, tokens, shards, chunks):
    groups = far_groups(dp_size)
    slots = len(chunks) * (sum(len(group_moves(g)) for g in groups) + 7) + 1
    return pl.pallas_call(
        functools.partial(head_kernel, groups, chunks),
        in_specs=[VM] * 5,
        out_specs=[ANY] * 5,
        out_shape=[jax.ShapeDtypeStruct(tokens.shape, tokens.dtype)]
        + [jax.ShapeDtypeStruct((2, dp_size) + s.shape, s.dtype) for s in shards],
        scratch_shapes=[pltpu.SemaphoreType.DMA((slots,)), pltpu.SemaphoreType.DMA((slots,)), pltpu.SemaphoreType.DMA((5,))],
        compiler_params=pltpu.CompilerParams(collective_id=0, has_side_effects=True),
    )(tokens, *shards)


def tail_kernel(groups, tokens, own_lo, own_hi, rest_lo, rest_hi, small_lo, small_hi, x_out, total, vecs,
                part, got_core, got_near, got_last, got_far, vec, vec_core, vec_two, vec_one, vec_far, send_sem, recv_sem, local_sem):
    dp, t = lax.axis_index("dp"), lax.axis_index("tensor")
    core = dp % 2
    away = core + t - 2 * core * t
    near = {1: (flip(dp, (1,)), t), 2: (flip(dp, (2,)), t), 0: (dp, 1 - t)}
    distant = [bits for group in groups for _, bits in group_moves(group)]
    swap = (dp - core + t, core)
    barrier = pltpu.get_barrier_semaphore()
    for device in list(near.values()) + [(flip(dp, bits), t) for bits in distant]:
        pl.semaphore_signal(barrier, inc=1, device_id=device, device_id_type=MESH_ID)

    @pl.when(away == 1)
    def _():
        pl.semaphore_signal(barrier, inc=1, device_id=swap, device_id_type=MESH_ID)

    pl.semaphore_wait(barrier, len(near) + len(distant) + away)
    count = [0]

    def remote(src, dst, device):
        slot = count[0]
        count[0] += 1
        return pltpu.make_async_remote_copy(
            src_ref=src, dst_ref=dst, send_sem=send_sem.at[slot], recv_sem=recv_sem.at[slot],
            device_id=device, device_id_type=MESH_ID)

    swap_copy = remote(tokens, x_out, swap)
    stay_copy = pltpu.make_async_copy(tokens, x_out, local_sem.at[0])
    half, rows, cols = own_lo.shape
    cut = cols * 2 // 3 // 128 * 128
    a, b = pl.ds(0, cut), pl.ds(cut, cols - cut)
    quarter = half // 2
    to_core = [
        remote(rest_hi, got_core.at[0], near[1]), remote(own_hi, got_core.at[1], near[1]),
        remote(small_hi, vec_core, near[1])]
    for move in to_core:
        move.start()

    @pl.when(away == 1)
    def _():
        swap_copy.start()

    @pl.when(away == 0)
    def _():
        stay_copy.start()

    def add(*terms):
        out = terms[0].astype(f32)
        for term in terms[1:]:
            out = out + term.astype(f32)
        return out.astype(bf)

    for move in to_core:
        move.wait_recv()

    def sum_core(k, _):
        part[0, k] = add(own_lo[k], got_core[0, k])
        part[1, k] = add(rest_lo[k], got_core[1, k])
        vec[k] = add(small_lo[k], vec_core[k])
        return 0

    lax.fori_loop(0, half, sum_core, 0)
    upper, lower = pl.ds(quarter, quarter), pl.ds(0, quarter)
    mine, other = away, 1 - away
    to_near = [
        remote(part.at[0, upper, :, a], got_near.at[0, lower, :, a], near[2]),
        remote(part.at[1, upper, :, a], got_near.at[1, lower, :, a], near[2]),
        remote(part.at[other, :, :, b], got_near.at[0, :, :, b], near[0]),
        remote(vec.at[upper], vec_two, near[2])]
    for move in to_near:
        move.start()
    for move in to_near:
        move.wait_recv()

    def sum_near(k, _):
        for g in range(2):
            part[g, k, :, a] = add(part[g, k, :, a], got_near[g, k, :, a])
        for q in (k, k + quarter):
            part[mine, q, :, b] = add(part[mine, q, :, b], got_near[0, q, :, b])
        vec[k] = add(vec[k], vec_two[k])
        return 0

    lax.fori_loop(0, quarter, sum_near, 0)
    to_last = [
        remote(part.at[other, lower, :, a], got_last.at[:, :, a], near[0]),
        remote(part.at[mine, upper, :, b], got_last.at[:, :, b], near[2]),
        remote(vec.at[lower], vec_one, near[0])]
    for move in to_last:
        move.start()
    for move in to_last:
        move.wait_recv()

    def sum_last(k, _):
        part[mine, k] = add(part[mine, k], got_last[k])
        vec_one[k] = add(vec[k], vec_one[k])
        return 0

    lax.fori_loop(0, quarter, sum_last, 0)
    to_far = []
    held, used = quarter, 0
    for group in reversed(groups):
        moves = group_moves(group)
        held //= len(moves) + 1
        step = []
        for place, bits in moves:
            device = (flip(dp, bits), t)
            step.append(remote(part.at[mine, pl.ds(place * held, held)], got_far.at[pl.ds(used, held)], device))
            step.append(remote(vec_one.at[pl.ds(place * held, held)], vec_far.at[pl.ds(used, held)], device))
            used += held
        for move in step:
            move.start()
        for move in step:
            move.wait_recv()
        base = used - held * len(moves)

        def sum_far(k, _, base=base, held=held, count=len(moves)):
            part[mine, k] = add(part[mine, k], *[got_far[base + m * held + k] for m in range(count)])
            vec_one[k] = add(vec_one[k], *[vec_far[base + m * held + k] for m in range(count)])
            return 0

        lax.fori_loop(0, held, sum_far, 0)
        to_far += step
    total[...] = part[mine, 0].astype(f32)
    vecs[...] = vec_one[0].astype(f32)

    @pl.when(away == 1)
    def _():
        swap_copy.wait()

    @pl.when(away == 0)
    def _():
        stay_copy.wait()

    for move in to_core + to_near + to_last + to_far:
        move.wait_send()


def tail(dp_size, tokens, own, rest, small):
    groups = far_groups(dp_size)
    half, rows, cols = own[0].shape
    quarter = half // 2
    wide = small[0].shape[2]
    partners = sum(len(group_moves(g)) for g in groups)
    slots = 11 + 2 * partners
    return pl.pallas_call(
        functools.partial(tail_kernel, groups),
        in_specs=[VM] * 7,
        out_specs=[ANY, VM, VM],
        out_shape=[
            jax.ShapeDtypeStruct(tokens.shape, bf), jax.ShapeDtypeStruct((rows, cols), f32),
            jax.ShapeDtypeStruct((rows, wide), f32)],
        scratch_shapes=[
            pltpu.VMEM((2, half, rows, cols), bf), pltpu.VMEM((2, half, rows, cols), bf), pltpu.VMEM((2, half, rows, cols), bf),
            pltpu.VMEM((quarter, rows, cols), bf), pltpu.VMEM((quarter, rows, cols), bf),
            pltpu.VMEM((half, rows, wide), bf), pltpu.VMEM((half, rows, wide), bf), pltpu.VMEM((quarter, rows, wide), bf),
            pltpu.VMEM((quarter, rows, wide), bf), pltpu.VMEM((quarter, rows, wide), bf),
            pltpu.SemaphoreType.DMA((slots,)), pltpu.SemaphoreType.DMA((slots,)), pltpu.SemaphoreType.DMA((1,))],
        compiler_params=pltpu.CompilerParams(collective_id=1, has_side_effects=True, vmem_limit_bytes=48 << 20),
    )(tokens, *own, *rest, *small)


def far_exchange(value, dp_size):
    out, held = [], value.shape[0]
    (group,) = far_groups(dp_size)[-1:]
    held //= len(group_moves(group)) + 1
    for place, bits in group_moves(group):
        mask = sum(bits)
        piece = value[place * held : (place + 1) * held]
        out.append(lax.ppermute(piece, "dp", [(i, i ^ mask) for i in range(dp_size)]))
    return out


def far_sum(value, got, dp_size):
    held = got[0].shape[0]
    total = value[:held].astype(f32)
    for piece in got:
        total = total + piece.astype(f32)
    for group in far_groups(dp_size)[-2::-1]:
        total = total.astype(bf)
        held //= len(group_moves(group)) + 1
        moves = [
            lax.ppermute(total[place * held : (place + 1) * held], "dp", [(i, i ^ sum(bits)) for i in range(dp_size)])
            for place, bits in group_moves(group)]
        total = total[:held].astype(f32)
        for piece in moves:
            total = total + piece.astype(f32)
    return total


def add_low(left, right):
    return (left.astype(f32) + right.astype(f32)).astype(bf)


def layer_norm_parts(values):
    centered = values - jnp.mean(values, axis=-1, keepdims=True)
    inverse = lax.rsqrt(jnp.mean(centered * centered, axis=-1, keepdims=True) + EPSILON)
    return centered * inverse, inverse


def layer_norm_back(hat, inverse, gain, grad):
    scaled = grad * gain
    back = inverse * (
        scaled
        - jnp.mean(scaled, axis=-1, keepdims=True)
        - hat * jnp.mean(scaled * hat, axis=-1, keepdims=True)
    )
    return back, jnp.sum(grad * hat, axis=0), jnp.sum(grad, axis=0)


def gelu_parts(pre):
    root = 0.7978845608
    inner = jnp.tanh(root * (pre + 0.044715 * pre * pre * pre))
    value = 0.5 * pre * (1.0 + inner)
    slope = 0.5 * (1.0 + inner) + 0.5 * pre * (1.0 - inner * inner) * root * (
        1.0 + 3 * 0.044715 * pre * pre
    )
    return value, slope


def on_device(
    tokens, segment_ids, ln1_gain, ln1_bias, w_qkv, b_qv, w_attn_out, b_attn_out,
    ln2_gain, ln2_bias, w_fc, b_fc, w_proj, b_proj, cotangent,
):
    dp_size = lax.axis_size("dp")
    dp_pos, t_pos = lax.axis_index("dp"), lax.axis_index("tensor")
    core = dp_pos % 2
    rows = ln1_gain.shape[0]
    width = tokens.shape[1]
    cols = w_qkv.shape[2]
    hidden = w_fc.shape[1]
    fan = b_fc.shape[0] // rows
    far = [1 << k for k in range(dp_size.bit_length() - 2, 1, -1)]
    swap = []
    for d in range(dp_size):
        for t in range(2):
            swap.append((2 * d + t, 2 * (d - d % 2 + t) + d % 2))
    mine = core == t_pos

    pairs = cols // 128

    def by_pair(parts):
        parts = parts.reshape(-1, 3, pairs, 128)
        return jnp.swapaxes(parts, 1, 2).reshape(-1, 3 * cols)

    def by_part(columns):
        return jnp.swapaxes(columns.reshape(-1, pairs, 3, 128), 1, 2).reshape(-1, 3, cols)

    seg_other = exchange(segment_ids, 1, dp_size)
    seg = jnp.where(mine, segment_ids, seg_other)[0]
    small = jnp.concatenate(
        [ln1_gain[:, None], ln1_bias[:, None], b_qv.T, b_attn_out[:, None], ln2_gain[:, None],
         ln2_bias[:, None], b_proj[:, None], b_fc.reshape(rows, fan)], axis=1)
    small = jnp.pad(small, ((0, 0), (0, SMALL - small.shape[1])))
    out_pack = jnp.concatenate([w_attn_out.T, small], axis=1)
    tokens, all_qkv, all_out, all_fc, all_proj = head(
        dp_size, tokens, (by_pair(w_qkv), out_pack, w_fc, w_proj.T),
        chunks_of(3 * cols, 0, 2) + chunks_of(cols + SMALL, 1, 1) + chunks_of(hidden, 2, 2, 3))
    all_qkv, all_out, all_fc, all_proj = (a.reshape(2, width, -1) for a in (all_qkv, all_out, all_fc, all_proj))

    place = jnp.arange(width, dtype=jnp.int32)
    block = place // rows
    source = jnp.zeros_like(block)
    for k, bit in enumerate(far + [2, 1]):
        source = source + ((block >> k) & 1) * bit

    def column_order(owner):
        natural = (source ^ owner) * rows + place % rows
        return (place[:, None] == natural[None, :]).astype(bf)

    order = column_order(dp_pos)

    vec_rel = all_out[0, :, cols:]
    vec_nat = dot(order, vec_rel).T
    vec_rel = vec_rel.astype(f32).T
    gain1, bias1, _, _, out_bias, gain2, bias2, proj_bias = (vec_rel[k] for k in range(8))
    fc_bias = vec_nat[8 : 8 + fan].T.reshape(2, hidden)
    b_q, b_v = vec_nat[2].reshape(2, cols), vec_nat[3].reshape(2, cols)
    take = lambda arr, k: lax.dynamic_index_in_dim(arr, k, 0, keepdims=False)
    other = 1 - core
    qkv_bias = lambda k: by_pair(jnp.stack([take(b_q, k), jnp.zeros((cols,), f32), take(b_v, k)]))

    x = dot(tokens, order)
    hat1, inv1 = layer_norm_parts(x)
    n1 = (hat1 * gain1 + bias1).astype(bf)
    wq_own, wq_other = all_qkv[0], all_qkv[1]
    wo_own, wo_other = all_out[0, :, :cols], all_out[1, :, :cols]
    qkv_send = (dot(n1, wq_other) + qkv_bias(other)).astype(bf)
    qkv_recv = exchange(qkv_send, 1, dp_size)
    qkv_own = (dot(n1, wq_own) + qkv_bias(core)).astype(bf)
    starts, info = attn_info(seg, core)
    o_own, o_send, lse = attn_fwd(qkv_own, qkv_recv, starts, info)
    o_recv = exchange(o_send, 1, dp_size)
    branch = dot(o_own, wo_own, NT) + dot(o_recv, wo_other, NT) + out_bias
    middle = x + BRANCH_SCALE * branch
    hat2, inv2 = layer_norm_parts(middle)
    n2 = (hat2 * gain2 + bias2).astype(bf)
    grad_out = dot(lax.ppermute(cotangent, BOTH, swap), order)
    scaled_out = BRANCH_SCALE * grad_out
    d_b_proj = jnp.sum(scaled_out, axis=0)
    d_mlp = scaled_out.astype(bf)
    mlp = jnp.zeros_like(x)
    d_n2 = jnp.zeros_like(x)
    half = width // 2

    def weight_grad(left, right):
        return dot(left[:, :half], right, TN).astype(bf), dot(left[:, half:], right, TN).astype(bf)

    sum_fc, sum_proj, d_b_fc = [], [], []
    for k in range(2):
        act, slope = gelu_parts(dot(n2, all_fc[k]) + take(fc_bias, t_pos ^ k))
        act = act.astype(bf)
        mlp = mlp + dot(act, all_proj[k], NT)
        d_pre = dot(d_mlp, all_proj[k]) * slope
        d_b_fc.append(jnp.sum(d_pre, axis=0))
        d_pre = d_pre.astype(bf)
        d_n2 = d_n2 + dot(d_pre, all_fc[k], NT)
        keep, send = weight_grad(n2, d_pre)
        sum_fc.append(add_low(keep, exchange(send, 1, dp_size)))
        keep, send = weight_grad(d_mlp, act)
        sum_proj.append(add_low(keep, exchange(send, 1, dp_size)))
    block_out = (middle + BRANCH_SCALE * (mlp + proj_bias)).astype(bf)
    block_out = lax.ppermute(dot(block_out, order, NT).astype(bf), BOTH, swap)

    back2, d_gain2, d_bias2 = layer_norm_back(hat2, inv2, gain2, d_n2)
    d_middle = grad_out + back2
    scaled_mid = BRANCH_SCALE * d_middle
    d_b_out = jnp.sum(scaled_mid, axis=0)
    d_attn = scaled_mid.astype(bf)
    do_send = dot(d_attn, wo_other).astype(bf)
    do_recv = exchange(do_send, 1, dp_size)
    do_own = dot(d_attn, wo_own).astype(bf)

    near_size = half // 2
    fc_sent = exchange(sum_fc[1], 0, dp_size)
    proj_sent = [exchange(p[near_size:], 2, dp_size) for p in sum_proj]
    d_n1 = jnp.zeros_like(x)
    dq_own, dq_recv = [], []
    last = (qkv_own, qkv_recv, do_own, do_recv, o_own, o_send)
    for g in range(pairs):
        own_g, send_g = attn_bwd(g, *last, starts, lse, info)
        recv_g = exchange(send_g, 1, dp_size)
        dq_own.append(own_g)
        dq_recv.append(recv_g)
        if g == 0:
            sum_fc = add_low(sum_fc[0], fc_sent)
            sum_proj = [add_low(p[:near_size], r) for p, r in zip(sum_proj, proj_sent)]
            fc_sent = exchange(sum_fc[near_size:], 2, dp_size)
            proj_sent = exchange(sum_proj[1], 0, dp_size)
            last, sum_fc, sum_proj = lax.optimization_barrier((last, sum_fc, sum_proj))
        if g == 1:
            sum_fc = add_low(sum_fc[:near_size], fc_sent)
            sum_proj = add_low(sum_proj[0], proj_sent)
            fc_sent = far_exchange(sum_fc, dp_size)
            proj_sent = far_exchange(sum_proj, dp_size)
            last, sum_fc, sum_proj = lax.optimization_barrier((last, sum_fc, sum_proj))
    sum_fc, sum_proj = far_sum(sum_fc, fc_sent, dp_size), far_sum(sum_proj, proj_sent, dp_size)
    dwq = [weight_grad(n1, jnp.concatenate(d, axis=1)) for d in (dq_own, dq_recv)]
    for g in range(pairs):
        lanes = slice(384 * g, 384 * (g + 1))
        d_n1 = d_n1 + dot(dq_own[g], wq_own[:, lanes], NT) + dot(dq_recv[g], wq_other[:, lanes], NT)
    dwo = [weight_grad(d_attn, o) for o in (o_own, o_recv)]
    back1, d_gain1, d_bias1 = layer_norm_back(hat1, inv1, gain1, d_n1)
    grad_tokens = (d_middle + back1).astype(bf)
    part_sums = lambda d: by_part(jnp.concatenate([jnp.sum(p.astype(f32), axis=0) for p in d]))[0]
    s_own, s_other = part_sums(dq_own), part_sums(dq_recv)
    pick = lambda cond, a, b: jnp.where(cond, jnp.concatenate([a, b]), jnp.concatenate([b, a]))
    nat = jnp.concatenate(
        [pick(core == 0, s_own[0], s_other[0])[:, None], pick(core == 0, s_own[2], s_other[2])[:, None],
         pick(t_pos == 0, *d_b_fc).reshape(width, fan)], axis=1).astype(bf)
    nat = dot(order, nat, TN)
    d_small = jnp.stack([d_gain1, d_bias1, nat[:, 0], nat[:, 1], d_b_out, d_gain2, d_bias2, d_b_proj], axis=1)
    d_small = jnp.concatenate([d_small, nat[:, 2:], jnp.zeros((width, SMALL - 8 - fan), f32)], axis=1).astype(bf)
    blocks = lambda arr: arr.reshape(dp_size // 2, rows, -1)
    both = lambda k: [blocks(jnp.concatenate([dwq[k][e], dwo[k][e]], axis=1)) for e in range(2)]
    grad_tokens, sum_a, vecs = tail(
        dp_size, grad_tokens, both(0), both(1), [blocks(d_small[:half]), blocks(d_small[half:])])
    grad_tokens = dot(grad_tokens, column_order(dp_pos - core + t_pos), NT).astype(bf)
    return (
        block_out,
        grad_tokens,
        vecs[:, 0],
        vecs[:, 1],
        by_part(sum_a[:, : 3 * cols]),
        vecs[:, 2:4].T,
        sum_a[:, 3 * cols :].T,
        vecs[:, 4],
        vecs[:, 5],
        vecs[:, 6],
        sum_fc.astype(f32),
        vecs[:, 8 : 8 + fan].reshape(rows * fan),
        sum_proj.astype(f32).T,
        vecs[:, 7],
    )


def solution(mesh):
    vec, tok = P("dp"), P(BOTH, None)
    in_specs = (
        tok, P("dp", None), vec, vec, P("dp", None, "tensor"), P(None, "dp"), P("tensor", "dp"),
        vec, vec, vec, P("dp", "tensor"), vec, P("tensor", "dp"), vec, tok,
    )
    out_specs = (
        tok, tok, vec, vec, P("dp", None, "tensor"), P(None, "dp"), P("tensor", "dp"),
        vec, vec, vec, P("dp", "tensor"), vec, P("tensor", "dp"), vec,
    )
    return jax.shard_map(on_device, mesh=mesh, in_specs=in_specs, out_specs=out_specs, check_vma=False)
```

```python
import functools

import jax
import jax.numpy as jnp
from jax import lax
from jax.experimental import pallas as pl
from jax.experimental.pallas import tpu as pltpu
from jax.sharding import PartitionSpec as P

HD = 64
QB = 256
NEG = -1e30
EPSILON = 1e-05
BRANCH_SCALE = 48.0 ** (-0.5)
SMALL = 128
bf = jnp.bfloat16
f32 = jnp.float32
NT = (((1,), (1,)), ((), ()))
TN = (((0,), (0,)), ((), ()))
BOTH = ("dp", "tensor")
MESH_ID = pl.DeviceIdType.MESH
ANY = pl.BlockSpec(memory_space=pl.ANY)
VM = pl.BlockSpec(memory_space=pltpu.VMEM)
SM = pl.BlockSpec(memory_space=pltpu.SMEM)


def attn_info(seg, core):
    n=seg.shape[0]; nb=n//QB
    docs=jnp.arange(16,dtype=jnp.int32)
    first=jnp.sum((seg[None,:]<docs[:,None]).astype(jnp.int32),axis=1)
    starts=jnp.sum(jnp.where(seg[None,:]==docs[:,None],first[:,None],0),axis=0)
    blocks=starts.reshape(nb,QB)
    idx=jnp.arange(nb,dtype=jnp.int32)
    low=blocks[:,0]//QB
    mid=jnp.clip((blocks[:,QB-1]+QB-1)//QB,low,idx)
    return starts.reshape(1,n), jnp.concatenate([jnp.reshape(core,(1,)),low,mid]).astype(jnp.int32)

def attn_masks(kat, srow, diagonal):
    keys = lax.broadcasted_iota(jnp.int32, (QB, QB), 0)
    mask = keys >= (srow - kat)
    if diagonal:
        mask = mask & (keys <= lax.broadcasted_iota(jnp.int32, (QB, QB), 1))
    return mask


def head_lanes(values):
    low = (lax.broadcasted_iota(jnp.int32, (1, values.shape[1]), 1) % 128) < HD
    zero = jnp.zeros((), bf)
    return jnp.where(low, values, zero), jnp.where(low, zero, values)


def fwd_kernel(info, own, recv, st_ref, okeep, osend, lse_ref, qm, ks, vt, osc, acc):
    half, cols = own.shape[0], own.shape[1] // 3
    n, nb, heads, pairs = 2 * half, 2 * half // QB, cols // HD, cols // 128
    c = info[0]
    for base, src in ((c * half, own), ((1 - c) * half, recv)):
        rows = pl.ds(pl.multiple_of(base, half), half)
        for g in range(pairs):
            lanes = slice(g * 128, (g + 1) * 128)
            part = lambda k: src[:, (3 * g + k) * 128 : (3 * g + k + 1) * 128]
            qm[0, rows, lanes], qm[1, rows, lanes] = head_lanes(part(0) * bf(HD**-0.5))
            ks[rows, lanes] = part(1)
            vt[lanes, rows] = part(2).T

    def qblock(i, _):
        at = pl.multiple_of(i * QB, QB)
        qr = pl.ds(at, QB)
        srow = st_ref[:, qr]
        acc[...] = jnp.zeros_like(acc)

        def step(mode, j, carry):
            kat = pl.multiple_of(j * QB, QB)
            kr = pl.ds(kat, QB)
            if mode:
                mask = attn_masks(kat, srow, mode == 2)
            scores, mixed = [], []
            for h in range(heads):
                lanes = slice(h // 2 * 128, h // 2 * 128 + 128)
                one = lax.dot_general(ks[kr, lanes], qm[h % 2, qr, lanes], NT, preferred_element_type=f32)
                scores.append(jnp.where(mask, one, NEG) if mode else one)
            for h in range(heads):
                top, total = carry[h]
                new = jnp.maximum(top, jnp.max(scores[h], axis=0, keepdims=True))
                weights = jnp.exp(scores[h] - new)
                fade = jnp.exp(top - new)
                total = fade * total + jnp.sum(weights, axis=0, keepdims=True)
                mixed.append((new, total, fade, weights.astype(bf)))
            for h in range(heads):
                sub = slice(h * HD, (h + 1) * HD)
                acc[sub] = mixed[h][2] * acc[sub] + jnp.dot(vt[sub, kr], mixed[h][3], preferred_element_type=f32)
            return tuple(m[:2] for m in mixed)

        carry = step(2, i, ((jnp.full((1, QB), NEG, f32), jnp.zeros((1, QB), f32)),) * heads)
        carry = lax.fori_loop(info[1 + i], info[1 + nb + i], functools.partial(step, 1), carry)
        carry = lax.fori_loop(info[1 + nb + i], i, functools.partial(step, 0), carry)
        for h, (top, total) in enumerate(carry):
            sub = slice(h * HD, (h + 1) * HD)
            acc[sub] = acc[sub] / total
            lse_ref[h : h + 1, qr] = top + jnp.log(total)
        osc[qr] = acc[...].T.astype(bf)
        return 0

    lax.fori_loop(0, nb, qblock, 0)
    okeep[...] = osc[pl.ds(pl.multiple_of(c * half, half), half)]
    osend[...] = osc[pl.ds(pl.multiple_of((1 - c) * half, half), half)]


def attn_fwd(own, recv, starts, info):
    half, cols = own.shape[0], own.shape[1] // 3
    n = 2 * half
    return pl.pallas_call(
        fwd_kernel,
        in_specs=[SM, VM, VM, VM],
        out_specs=[VM] * 3,
        scratch_shapes=[
            pltpu.VMEM((2, n, cols), bf), pltpu.VMEM((n, cols), bf), pltpu.VMEM((cols, n), bf),
            pltpu.VMEM((n, cols), bf), pltpu.VMEM((cols, QB), f32)],
        out_shape=[jax.ShapeDtypeStruct((half, cols), bf)] * 2 + [jax.ShapeDtypeStruct((cols // HD, n), f32)],
        cost_estimate=pl.CostEstimate(flops=n * n, bytes_accessed=n * 128, transcendentals=0),
        compiler_params=pltpu.CompilerParams(vmem_limit_bytes=48 << 20),
    )(info, own, recv, starts)


def bwd_kernel(first, info, own, recv, doo, dor, oo, orr, st_ref, lse_ref, dkeep, dsend, qm, ks, vs, kt, dom, dlt, dqs, dks, dvs):
    half, n, nb = own.shape[0], 2 * own.shape[0], 2 * own.shape[0] // QB
    c = info[0]
    for base, src, do, o in ((c * half, own, doo, oo), ((1 - c) * half, recv, dor, orr)):
        rows = pl.ds(pl.multiple_of(base, half), half)
        qm[0, rows], qm[1, rows] = head_lanes(src[:, :128] * bf(HD**-0.5))
        ks[rows] = src[:, 128:256]
        vs[rows] = src[:, 256:]
        kt[:, rows] = src[:, 128:256].T
        dom[0, rows], dom[1, rows] = head_lanes(do[...])
        prod = (do[...].astype(f32) * o[...].astype(f32)).T
        for h in range(2):
            dlt[h : h + 1, rows] = jnp.sum(prod[h * HD : (h + 1) * HD], axis=0, keepdims=True)
    dks[...] = jnp.zeros_like(dks)
    dvs[...] = jnp.zeros_like(dvs)

    def qblock(i, _):
        at = pl.multiple_of(i * QB, QB)
        qr = pl.ds(at, QB)
        srow = st_ref[:, qr]
        dqs[...] = jnp.zeros_like(dqs)

        def step(mode, j, carry):
            kat = pl.multiple_of(j * QB, QB)
            kr = pl.ds(kat, QB)
            if mode:
                mask = attn_masks(kat, srow, mode == 2)
            scores, softs, grads = [], [], []
            for h in range(2):
                one = lax.dot_general(ks[kr], qm[h, qr], NT, preferred_element_type=f32)
                back = lax.dot_general(vs[kr], dom[h, qr], NT, preferred_element_type=f32)
                scores.append((jnp.where(mask, one, NEG) if mode else one, back))
            for h in range(2):
                soft = jnp.exp(scores[h][0] - lse_ref[first + h : first + h + 1, qr])
                grads.append((soft * (scores[h][1] - dlt[h : h + 1, qr])).astype(bf))
                softs.append(soft.astype(bf))
            both = lambda ref: jnp.concatenate([ref[0, qr], ref[1, qr]], axis=0)
            dvs[kr] += jnp.dot(jnp.concatenate(softs, axis=1), both(dom), preferred_element_type=f32)
            dks[kr] += jnp.dot(jnp.concatenate(grads, axis=1), both(qm), preferred_element_type=f32)
            for h in range(2):
                sub = slice(h * HD, (h + 1) * HD)
                dqs[sub] += jnp.dot(kt[sub, kr], grads[h], preferred_element_type=f32)
            return carry

        step(2, i, 0)
        lax.fori_loop(info[1 + i], info[1 + nb + i], functools.partial(step, 1), 0)
        lax.fori_loop(info[1 + nb + i], i, functools.partial(step, 0), 0)
        qm[0, qr] = (dqs[...] * (HD**-0.5)).T.astype(bf)
        return 0

    lax.fori_loop(0, nb, qblock, 0)
    for dst, base in ((dkeep, c * half), (dsend, (1 - c) * half)):
        rows = pl.ds(pl.multiple_of(base, half), half)
        dst[:, :128] = qm[0, rows]
        dst[:, 128:256] = dks[rows].astype(bf)
        dst[:, 256:] = dvs[rows].astype(bf)


def attn_bwd(pair, own, recv, do_own, do_recv, o_own, o_recv, starts, lse, info):
    half = own.shape[0]
    n = 2 * half
    wide = pl.BlockSpec((half, 384), lambda k, s: (0, pair))
    slim = pl.BlockSpec((half, 128), lambda k, s: (0, pair))
    whole = lambda a: pl.BlockSpec(a.shape, lambda k, s: (0, 0))
    return pl.pallas_call(
        functools.partial(bwd_kernel, 2 * pair),
        grid_spec=pltpu.PrefetchScalarGridSpec(
            num_scalar_prefetch=1,
            grid=(1,),
            in_specs=[wide, wide, slim, slim, slim, slim, whole(starts), whole(lse)],
            out_specs=[pl.BlockSpec((half, 384), lambda k, s: (0, 0))] * 2,
            scratch_shapes=[
                pltpu.VMEM((2, n, 128), bf), pltpu.VMEM((n, 128), bf), pltpu.VMEM((n, 128), bf), pltpu.VMEM((128, n), bf),
                pltpu.VMEM((2, n, 128), bf), pltpu.VMEM((2, n), f32), pltpu.VMEM((128, QB), f32), pltpu.VMEM((n, 128), f32),
                pltpu.VMEM((n, 128), f32)],
        ),
        out_shape=[jax.ShapeDtypeStruct((half, 384), bf)] * 2,
        cost_estimate=pl.CostEstimate(flops=n * n, bytes_accessed=n * 128, transcendentals=0),
        compiler_params=pltpu.CompilerParams(vmem_limit_bytes=40 << 20),
    )(info, own, recv, do_own, do_recv, o_own, o_recv, starts, lse)


def dot(left, right, dims=(((1,), (0,)), ((), ()))):
    return lax.dot_general(left, right, dims, preferred_element_type=f32)


def exchange(value, bit, dp_size):
    if bit:
        return lax.ppermute(value, "dp", [(i, i ^ bit) for i in range(dp_size)])
    return lax.ppermute(value, "tensor", [(0, 1), (1, 0)])


def flip(index, bits):
    for bit in bits:
        index = index + bit * (1 - 2 * ((index // bit) % 2))
    return index

def far_groups(dp_size):
    far = [1 << k for k in range(dp_size.bit_length() - 2, 1, -1)]
    return [tuple(far[k : k + 2]) for k in range(0, len(far), 2)]

def group_moves(group):
    if len(group) == 1:
        return [(1, group)]
    return [(1, group[:1]), (2, group[1:]), (3, group)]

def chunks_of(cols, which, count, until=None):
    tiles = cols // 128
    cuts = [128 * ((tiles * k) // count) for k in range(count + 1)]
    arrays = range(which, until + 1) if until else (which,)
    return tuple(
        (array, low, high - low, 128 * max(1, (high - low) * 2 // 3 // 128))
        for low, high in zip(cuts, cuts[1:]) for array in arrays)


def head_kernel(groups, chunks, tokens, *refs):
    shards, x_out, outs, (send_sem, recv_sem, local_sem) = refs[:4], refs[4], refs[5:9], refs[9:]
    dp, t = lax.axis_index("dp"), lax.axis_index("tensor")
    core = dp % 2
    away = core + t - 2 * core * t
    near = {1: (flip(dp, (1,)), t), 2: (flip(dp, (2,)), t), 0: (dp, 1 - t)}
    distant = [bits for group in groups for _, bits in group_moves(group)]
    swap = (dp - core + t, core)
    barrier = pltpu.get_barrier_semaphore()
    for device in list(near.values()) + [(flip(dp, bits), t) for bits in distant]:
        pl.semaphore_signal(barrier, inc=1, device_id=device, device_id_type=MESH_ID)

    @pl.when(away == 1)
    def _():
        pl.semaphore_signal(barrier, inc=1, device_id=swap, device_id_type=MESH_ID)

    local = [
        pltpu.make_async_copy(shards[k], outs[k].at[away, 0] if k < 2 else outs[k].at[0], local_sem.at[k]) for k in range(4)]
    for copy in local:
        copy.start()
    pl.semaphore_wait(barrier, len(near) + len(distant) + away)
    count = [0]

    def remote(src, dst, device):
        slot = count[0]
        count[0] += 1
        return pltpu.make_async_remote_copy(
            src_ref=src, dst_ref=dst, send_sem=send_sem.at[slot], recv_sem=recv_sem.at[slot],
            device_id=device, device_id_type=MESH_ID)

    def blocks(ref, index, first, held, low, size):
        return ref.at[index, pl.ds(first, held), :, pl.ds(low, size)]

    plans = []
    for which, low, size, part in chunks:
        shard, out = shards[which], outs[which]
        steps, held = [], 1
        for group in groups:
            moves = []
            for place, bits in group_moves(group):
                src = shard.at[:, pl.ds(low, size)] if held == 1 else blocks(out, away, 0, held, low, size)
                dst = out.at[away, place, :, pl.ds(low, size)] if held == 1 else blocks(out, away, place * held, held, low, size)
                moves.append(remote(src, dst, (flip(dp, bits), t)))
            held *= len(group_moves(group)) + 1
            steps.append(moves)
        a, b = (low, part), (low + part, size - part)
        steps.append([
            remote(blocks(out, away, 0, held, *a), blocks(out, away, 0, held, *a), near[0]),
            remote(blocks(out, away, 0, held, *b), blocks(out, away, held, held, *b), near[2]),
        ])
        steps.append(
            [remote(blocks(out, k, 0, held, *a), blocks(out, k, held, held, *a), near[2]) for k in range(2)]
            + [remote(blocks(out, away, 0, 2 * held, *b), blocks(out, away, 0, 2 * held, *b), near[0])])
        steps.append([
            remote(blocks(out, k, 0, 2 * held, low, size),
                   blocks(out, 1 - k, 2 * held, 2 * held, low, size), near[1]) for k in range(2)])
        plans.append(steps)
    later = []
    held = 1
    for group in groups:
        moves = []
        for place, bits in group_moves(group):
            for shard, out in zip(shards[2:], outs[2:]):
                src = shard if held == 1 else out.at[pl.ds(0, held)]
                dst = out.at[place] if held == 1 else out.at[pl.ds(place * held, held)]
                moves.append(remote(src, dst, (flip(dp, bits), t)))
        held *= len(group_moves(group)) + 1
        later.append(moves)
    depth = len(plans[0])
    swap_copy = remote(tokens, x_out, swap)
    stay_copy = pltpu.make_async_copy(tokens, x_out, local_sem.at[4])
    waited = set()

    def advance(number, phase):
        if number >= len(plans):
            return
        if phase > 0:
            for move in plans[number][phase - 1]:
                move.wait_recv()
        if phase == 1 and chunks[number][0] not in waited:
            waited.add(chunks[number][0])
            local[chunks[number][0]].wait()
        if phase < depth:
            for move in plans[number][phase]:
                move.start()

    advance(0, 0)

    @pl.when(away == 1)
    def _():
        swap_copy.start()

    @pl.when(away == 0)
    def _():
        stay_copy.start()

    far = len(groups)
    for number in range(len(plans)):
        if number == 0:
            for phase in range(1, far + 1):
                advance(0, phase)
            advance(1, 0)
        advance(number, far + 1)
        for phase in range(1, far + 1):
            advance(number + 1, phase)
        advance(number + 2, 0)
        if number == len(plans) - 2:
            for move in later[0]:
                move.start()
        advance(number, far + 2)
    for number in range(len(plans)):
        advance(number, depth)

    @pl.when(away == 1)
    def _():
        swap_copy.wait()

    @pl.when(away == 0)
    def _():
        stay_copy.wait()

    for which in sorted(set(range(4)) - waited):
        local[which].wait()
    for k, moves in enumerate(later):
        if k > 0:
            for move in moves:
                move.start()
        for move in moves:
            move.wait()
    for steps in plans:
        for moves in steps:
            for move in moves:
                move.wait_send()


def head(dp_size, tokens, shards, chunks):
    groups = far_groups(dp_size)
    partners = sum(len(group_moves(g)) for g in groups)
    slots = len(chunks) * (partners + 7) + 2 * partners + 1
    shapes = [(2, dp_size)] * 2 + [(dp_size // 4,)] * 2
    return pl.pallas_call(
        functools.partial(head_kernel, groups, chunks),
        in_specs=[VM] * 5,
        out_specs=[ANY] * 5,
        out_shape=[jax.ShapeDtypeStruct(tokens.shape, tokens.dtype)]
        + [jax.ShapeDtypeStruct(lead + s.shape, s.dtype) for lead, s in zip(shapes, shards)],
        scratch_shapes=[pltpu.SemaphoreType.DMA((slots,)), pltpu.SemaphoreType.DMA((slots,)), pltpu.SemaphoreType.DMA((5,))],
        compiler_params=pltpu.CompilerParams(collective_id=0, has_side_effects=True),
    )(tokens, *shards)


def tail_kernel(groups, tokens, own_lo, own_hi, rest_lo, rest_hi, small_lo, small_hi, x_out, total, vecs,
                part, got_core, got_near, got_last, got_far, vec, vec_core, vec_two, vec_one, vec_far, send_sem, recv_sem, local_sem):
    dp, t = lax.axis_index("dp"), lax.axis_index("tensor")
    core = dp % 2
    away = core + t - 2 * core * t
    near = {1: (flip(dp, (1,)), t), 2: (flip(dp, (2,)), t), 0: (dp, 1 - t)}
    distant = [bits for group in groups for _, bits in group_moves(group)]
    swap = (dp - core + t, core)
    barrier = pltpu.get_barrier_semaphore()
    for device in list(near.values()) + [(flip(dp, bits), t) for bits in distant]:
        pl.semaphore_signal(barrier, inc=1, device_id=device, device_id_type=MESH_ID)

    @pl.when(away == 1)
    def _():
        pl.semaphore_signal(barrier, inc=1, device_id=swap, device_id_type=MESH_ID)

    pl.semaphore_wait(barrier, len(near) + len(distant) + away)
    count = [0]

    def remote(src, dst, device):
        slot = count[0]
        count[0] += 1
        return pltpu.make_async_remote_copy(
            src_ref=src, dst_ref=dst, send_sem=send_sem.at[slot], recv_sem=recv_sem.at[slot],
            device_id=device, device_id_type=MESH_ID)

    swap_copy = remote(tokens, x_out, swap)
    stay_copy = pltpu.make_async_copy(tokens, x_out, local_sem.at[0])
    half, rows, cols = own_lo.shape
    cut = cols * 2 // 3 // 128 * 128
    a, b = pl.ds(0, cut), pl.ds(cut, cols - cut)
    quarter = half // 2
    to_core = [
        remote(rest_hi, got_core.at[0], near[1]), remote(own_hi, got_core.at[1], near[1]),
        remote(small_hi, vec_core, near[1])]
    for move in to_core:
        move.start()

    @pl.when(away == 1)
    def _():
        swap_copy.start()

    @pl.when(away == 0)
    def _():
        stay_copy.start()

    def add(*terms):
        out = terms[0].astype(f32)
        for term in terms[1:]:
            out = out + term.astype(f32)
        return out.astype(bf)

    for move in to_core:
        move.wait_recv()

    def sum_core(k, _):
        part[0, k] = add(own_lo[k], got_core[0, k])
        part[1, k] = add(rest_lo[k], got_core[1, k])
        vec[k] = add(small_lo[k], vec_core[k])
        return 0

    lax.fori_loop(0, half, sum_core, 0)
    upper, lower = pl.ds(quarter, quarter), pl.ds(0, quarter)
    mine, other = away, 1 - away
    to_near = [
        remote(part.at[0, upper, :, a], got_near.at[0, lower, :, a], near[2]),
        remote(part.at[1, upper, :, a], got_near.at[1, lower, :, a], near[2]),
        remote(part.at[other, :, :, b], got_near.at[0, :, :, b], near[0]),
        remote(vec.at[upper], vec_two, near[2])]
    for move in to_near:
        move.start()
    for move in to_near:
        move.wait_recv()

    def sum_near(k, _):
        for g in range(2):
            part[g, k, :, a] = add(part[g, k, :, a], got_near[g, k, :, a])
        for q in (k, k + quarter):
            part[mine, q, :, b] = add(part[mine, q, :, b], got_near[0, q, :, b])
        vec[k] = add(vec[k], vec_two[k])
        return 0

    lax.fori_loop(0, quarter, sum_near, 0)
    to_last = [
        remote(part.at[other, lower, :, a], got_last.at[:, :, a], near[0]),
        remote(part.at[mine, upper, :, b], got_last.at[:, :, b], near[2]),
        remote(vec.at[lower], vec_one, near[0])]
    for move in to_last:
        move.start()
    for move in to_last:
        move.wait_recv()

    def sum_last(k, _):
        part[mine, k] = add(part[mine, k], got_last[k])
        vec_one[k] = add(vec[k], vec_one[k])
        return 0

    lax.fori_loop(0, quarter, sum_last, 0)
    to_far = []
    held, used = quarter, 0
    for group in reversed(groups):
        moves = group_moves(group)
        held //= len(moves) + 1
        step = []
        for place, bits in moves:
            device = (flip(dp, bits), t)
            step.append(remote(part.at[mine, pl.ds(place * held, held)], got_far.at[pl.ds(used, held)], device))
            step.append(remote(vec_one.at[pl.ds(place * held, held)], vec_far.at[pl.ds(used, held)], device))
            used += held
        for move in step:
            move.start()
        for move in step:
            move.wait_recv()
        base = used - held * len(moves)

        def sum_far(k, _, base=base, held=held, count=len(moves)):
            part[mine, k] = add(part[mine, k], *[got_far[base + m * held + k] for m in range(count)])
            vec_one[k] = add(vec_one[k], *[vec_far[base + m * held + k] for m in range(count)])
            return 0

        lax.fori_loop(0, held, sum_far, 0)
        to_far += step
    total[...] = part[mine, 0].astype(f32)
    vecs[...] = vec_one[0].astype(f32)

    @pl.when(away == 1)
    def _():
        swap_copy.wait()

    @pl.when(away == 0)
    def _():
        stay_copy.wait()

    for move in to_core + to_near + to_last + to_far:
        move.wait_send()


def tail(dp_size, tokens, own, rest, small):
    groups = far_groups(dp_size)
    half, rows, cols = own[0].shape
    quarter = half // 2
    wide = small[0].shape[2]
    partners = sum(len(group_moves(g)) for g in groups)
    slots = 11 + 2 * partners
    return pl.pallas_call(
        functools.partial(tail_kernel, groups),
        in_specs=[VM] * 7,
        out_specs=[ANY, VM, VM],
        out_shape=[
            jax.ShapeDtypeStruct(tokens.shape, bf), jax.ShapeDtypeStruct((rows, cols), f32),
            jax.ShapeDtypeStruct((rows, wide), f32)],
        scratch_shapes=[
            pltpu.VMEM((2, half, rows, cols), bf), pltpu.VMEM((2, half, rows, cols), bf), pltpu.VMEM((2, half, rows, cols), bf),
            pltpu.VMEM((quarter, rows, cols), bf), pltpu.VMEM((quarter, rows, cols), bf),
            pltpu.VMEM((half, rows, wide), bf), pltpu.VMEM((half, rows, wide), bf), pltpu.VMEM((quarter, rows, wide), bf),
            pltpu.VMEM((quarter, rows, wide), bf), pltpu.VMEM((quarter, rows, wide), bf),
            pltpu.SemaphoreType.DMA((slots,)), pltpu.SemaphoreType.DMA((slots,)), pltpu.SemaphoreType.DMA((1,))],
        compiler_params=pltpu.CompilerParams(collective_id=1, has_side_effects=True, vmem_limit_bytes=48 << 20),
    )(tokens, *own, *rest, *small)


def far_exchange(value, dp_size):
    out, held = [], value.shape[0]
    (group,) = far_groups(dp_size)[-1:]
    held //= len(group_moves(group)) + 1
    for place, bits in group_moves(group):
        mask = sum(bits)
        piece = value[place * held : (place + 1) * held]
        out.append(lax.ppermute(piece, "dp", [(i, i ^ mask) for i in range(dp_size)]))
    return out


def far_sum(value, got, dp_size):
    held = got[0].shape[0]
    total = value[:held].astype(f32)
    for piece in got:
        total = total + piece.astype(f32)
    for group in far_groups(dp_size)[-2::-1]:
        total = total.astype(bf)
        held //= len(group_moves(group)) + 1
        moves = [
            lax.ppermute(total[place * held : (place + 1) * held], "dp", [(i, i ^ sum(bits)) for i in range(dp_size)])
            for place, bits in group_moves(group)]
        total = total[:held].astype(f32)
        for piece in moves:
            total = total + piece.astype(f32)
    return total


def add_low(left, right):
    return (left.astype(f32) + right.astype(f32)).astype(bf)


def layer_norm_parts(values):
    centered = values - jnp.mean(values, axis=-1, keepdims=True)
    inverse = lax.rsqrt(jnp.mean(centered * centered, axis=-1, keepdims=True) + EPSILON)
    return centered * inverse, inverse


def layer_norm_back(hat, inverse, gain, grad):
    scaled = grad * gain
    back = inverse * (
        scaled
        - jnp.mean(scaled, axis=-1, keepdims=True)
        - hat * jnp.mean(scaled * hat, axis=-1, keepdims=True)
    )
    return back, jnp.sum(grad * hat, axis=0), jnp.sum(grad, axis=0)


def gelu_parts(pre):
    root = 0.7978845608
    inner = jnp.tanh(root * (pre + 0.044715 * pre * pre * pre))
    value = 0.5 * pre * (1.0 + inner)
    slope = 0.5 * (1.0 + inner) + 0.5 * pre * (1.0 - inner * inner) * root * (
        1.0 + 3 * 0.044715 * pre * pre
    )
    return value, slope


def on_device(
    tokens, segment_ids, ln1_gain, ln1_bias, w_qkv, b_qv, w_attn_out, b_attn_out,
    ln2_gain, ln2_bias, w_fc, b_fc, w_proj, b_proj, cotangent,
):
    dp_size = lax.axis_size("dp")
    dp_pos, t_pos = lax.axis_index("dp"), lax.axis_index("tensor")
    core = dp_pos % 2
    rows = ln1_gain.shape[0]
    width = tokens.shape[1]
    cols = w_qkv.shape[2]
    hidden = w_fc.shape[1]
    fan = b_fc.shape[0] // rows
    far = [1 << k for k in range(dp_size.bit_length() - 2, 1, -1)]
    swap = []
    for d in range(dp_size):
        for t in range(2):
            if d % 2 != t:
                swap.append((2 * d + t, 2 * (d - d % 2 + t) + d % 2))
    mine = core == t_pos

    pairs = cols // 128

    def by_pair(parts):
        parts = parts.reshape(-1, 3, pairs, 128)
        return jnp.swapaxes(parts, 1, 2).reshape(-1, 3 * cols)

    def by_part(columns):
        return jnp.swapaxes(columns.reshape(-1, pairs, 3, 128), 1, 2).reshape(-1, 3, cols)

    seg_other = exchange(segment_ids, 1, dp_size)
    seg = jnp.where(mine, segment_ids, seg_other)[0]
    small = jnp.concatenate(
        [ln1_gain[:, None], ln1_bias[:, None], b_qv.T, b_attn_out[:, None], ln2_gain[:, None],
         ln2_bias[:, None], b_proj[:, None], b_fc.reshape(rows, fan)], axis=1)
    small = jnp.pad(small, ((0, 0), (0, SMALL - small.shape[1])))
    out_pack = jnp.concatenate([w_attn_out.T, small], axis=1)
    tokens, all_qkv, all_out, fc_far, proj_far = head(
        dp_size, tokens, (by_pair(w_qkv), out_pack, w_fc, w_proj.T), chunks_of(3 * cols, 0, 2) + chunks_of(cols + SMALL, 1, 1))
    all_qkv, all_out = (a.reshape(2, width, -1) for a in (all_qkv, all_out))
    fc_far, proj_far = fc_far.reshape(-1, hidden), proj_far.reshape(-1, hidden)
    fc_parts = [[fc_far], [exchange(fc_far, 0, dp_size)]]
    proj_half = exchange(proj_far, 2, dp_size)

    place = jnp.arange(width, dtype=jnp.int32)
    block = place // rows
    source = jnp.zeros_like(block)
    for k, bit in enumerate(far + [2, 1]):
        source = source + ((block >> k) & 1) * bit

    def column_order(owner):
        natural = (source ^ owner) * rows + place % rows
        return (place[:, None] == natural[None, :]).astype(bf)

    order = column_order(dp_pos)

    vec_rel = all_out[0, :, cols:]
    vec_nat = dot(order, vec_rel).T
    vec_rel = vec_rel.astype(f32).T
    gain1, bias1, _, _, out_bias, gain2, bias2, proj_bias = (vec_rel[k] for k in range(8))
    fc_bias = vec_nat[8 : 8 + fan].T.reshape(2, hidden)
    b_q, b_v = vec_nat[2].reshape(2, cols), vec_nat[3].reshape(2, cols)
    take = lambda arr, k: lax.dynamic_index_in_dim(arr, k, 0, keepdims=False)
    other = 1 - core
    qkv_bias = lambda k: by_pair(jnp.stack([take(b_q, k), jnp.zeros((cols,), f32), take(b_v, k)]))

    x = dot(tokens, order)
    hat1, inv1 = layer_norm_parts(x)
    n1 = (hat1 * gain1 + bias1).astype(bf)
    wq_own, wq_other = all_qkv[0], all_qkv[1]
    wo_own, wo_other = all_out[0, :, :cols], all_out[1, :, :cols]
    qkv_send = (dot(n1, wq_other) + qkv_bias(other)).astype(bf)
    qkv_recv = exchange(qkv_send, 1, dp_size)
    fc_parts, proj_half, n1 = lax.optimization_barrier((fc_parts, proj_half, n1))
    fc_parts = [p + [exchange(p[0], 2, dp_size)] for p in fc_parts]
    proj_half = jnp.concatenate([proj_far, proj_half], axis=0)
    proj_parts = [[proj_half], [exchange(proj_half, 0, dp_size)]]
    qkv_own = (dot(n1, wq_own) + qkv_bias(core)).astype(bf)
    starts, info = attn_info(seg, core)
    o_own, o_send, lse = attn_fwd(qkv_own, qkv_recv, starts, info)
    o_recv = exchange(o_send, 1, dp_size)
    all_fc, all_proj = (
        [jnp.concatenate(p + [exchange(e, 1, dp_size) for e in p], axis=0) for p in parts] for parts in (fc_parts, proj_parts))
    branch = dot(o_own, wo_own, NT) + dot(o_recv, wo_other, NT) + out_bias
    middle = x + BRANCH_SCALE * branch
    hat2, inv2 = layer_norm_parts(middle)
    n2 = (hat2 * gain2 + bias2).astype(bf)
    grad_out = dot(jnp.where(mine, cotangent, lax.ppermute(cotangent, BOTH, swap)), order)
    scaled_out = BRANCH_SCALE * grad_out
    d_b_proj = jnp.sum(scaled_out, axis=0)
    d_mlp = scaled_out.astype(bf)
    mlp = jnp.zeros_like(x)
    d_n2 = jnp.zeros_like(x)
    half = width // 2

    def weight_grad(left, right):
        return dot(left[:, :half], right, TN).astype(bf), dot(left[:, half:], right, TN).astype(bf)

    sum_fc, sum_proj, d_b_fc = [], [], []
    for k in range(2):
        act, slope = gelu_parts(dot(n2, all_fc[k]) + take(fc_bias, t_pos ^ k))
        act = act.astype(bf)
        mlp = mlp + dot(act, all_proj[k], NT)
        d_pre = dot(d_mlp, all_proj[k]) * slope
        d_b_fc.append(jnp.sum(d_pre, axis=0))
        d_pre = d_pre.astype(bf)
        d_n2 = d_n2 + dot(d_pre, all_fc[k], NT)
        keep, send = weight_grad(n2, d_pre)
        sum_fc.append(add_low(keep, exchange(send, 1, dp_size)))
        keep, send = weight_grad(d_mlp, act)
        sum_proj.append(add_low(keep, exchange(send, 1, dp_size)))
    block_out = (middle + BRANCH_SCALE * (mlp + proj_bias)).astype(bf)
    block_out = dot(block_out, order, NT).astype(bf)
    block_out = jnp.where(mine, block_out, lax.ppermute(block_out, BOTH, swap))

    back2, d_gain2, d_bias2 = layer_norm_back(hat2, inv2, gain2, d_n2)
    d_middle = grad_out + back2
    scaled_mid = BRANCH_SCALE * d_middle
    d_b_out = jnp.sum(scaled_mid, axis=0)
    d_attn = scaled_mid.astype(bf)
    do_send = dot(d_attn, wo_other).astype(bf)
    do_recv = exchange(do_send, 1, dp_size)
    do_own = dot(d_attn, wo_own).astype(bf)

    near_size = half // 2
    d_n1 = jnp.zeros_like(x)
    dq_own, dq_recv = [], []
    last = (qkv_own, qkv_recv, do_own, do_recv, o_own, o_send)
    last, sum_fc, sum_proj = lax.optimization_barrier((last, sum_fc, sum_proj))
    fc_sent = exchange(sum_fc[1], 0, dp_size)
    proj_sent = [exchange(p[near_size:], 2, dp_size) for p in sum_proj]
    for g in range(pairs):
        if g == pairs - 1:
            sum_fc = add_low(sum_fc[0], fc_sent)
            sum_proj = [add_low(p[:near_size], r) for p, r in zip(sum_proj, proj_sent)]
            last, dq_own, sum_fc, sum_proj = lax.optimization_barrier((last, dq_own, sum_fc, sum_proj))
            fc_sent = exchange(sum_fc[near_size:], 2, dp_size)
            proj_sent = exchange(sum_proj[1], 0, dp_size)
        own_g, send_g = attn_bwd(g, *last, starts, lse, info)
        dq_own = dq_own + [own_g]
        dq_recv = dq_recv + [exchange(send_g, 1, dp_size)]
    sum_fc = add_low(sum_fc[:near_size], fc_sent)
    sum_proj = add_low(sum_proj[0], proj_sent)
    dq_own, sum_fc, sum_proj = lax.optimization_barrier((dq_own, sum_fc, sum_proj))
    fc_sent = far_exchange(sum_fc, dp_size)
    proj_sent = far_exchange(sum_proj, dp_size)
    dwq = [weight_grad(n1, jnp.concatenate(d, axis=1)) for d in (dq_own, dq_recv)]
    for g in range(pairs):
        lanes = slice(384 * g, 384 * (g + 1))
        d_n1 = d_n1 + dot(dq_own[g], wq_own[:, lanes], NT) + dot(dq_recv[g], wq_other[:, lanes], NT)
    dwo = [weight_grad(d_attn, o) for o in (o_own, o_recv)]
    back1, d_gain1, d_bias1 = layer_norm_back(hat1, inv1, gain1, d_n1)
    grad_tokens = (d_middle + back1).astype(bf)
    part_sums = lambda d: by_part(jnp.concatenate([jnp.sum(p.astype(f32), axis=0) for p in d]))[0]
    s_own, s_other = part_sums(dq_own), part_sums(dq_recv)
    pick = lambda cond, a, b: jnp.where(cond, jnp.concatenate([a, b]), jnp.concatenate([b, a]))
    nat = jnp.concatenate(
        [pick(core == 0, s_own[0], s_other[0])[:, None], pick(core == 0, s_own[2], s_other[2])[:, None],
         pick(t_pos == 0, *d_b_fc).reshape(width, fan)], axis=1).astype(bf)
    nat = dot(order, nat, TN)
    d_small = jnp.stack([d_gain1, d_bias1, nat[:, 0], nat[:, 1], d_b_out, d_gain2, d_bias2, d_b_proj], axis=1)
    d_small = jnp.concatenate([d_small, nat[:, 2:], jnp.zeros((width, SMALL - 8 - fan), f32)], axis=1).astype(bf)
    blocks = lambda arr: arr.reshape(dp_size // 2, rows, -1)
    both = lambda k: [blocks(jnp.concatenate([dwq[k][e], dwo[k][e]], axis=1)) for e in range(2)]
    grad_tokens, sum_a, vecs = tail(
        dp_size, grad_tokens, both(0), both(1), [blocks(d_small[:half]), blocks(d_small[half:])])
    grad_tokens = dot(grad_tokens, column_order(dp_pos - core + t_pos), NT).astype(bf)
    sum_fc, sum_proj = far_sum(sum_fc, fc_sent, dp_size), far_sum(sum_proj, proj_sent, dp_size)
    return (
        block_out,
        grad_tokens,
        vecs[:, 0],
        vecs[:, 1],
        by_part(sum_a[:, : 3 * cols]),
        vecs[:, 2:4].T,
        sum_a[:, 3 * cols :].T,
        vecs[:, 4],
        vecs[:, 5],
        vecs[:, 6],
        sum_fc.astype(f32),
        vecs[:, 8 : 8 + fan].reshape(rows * fan),
        sum_proj.astype(f32).T,
        vecs[:, 7],
    )


def solution(mesh):
    vec, tok = P("dp"), P(BOTH, None)
    in_specs = (
        tok, P("dp", None), vec, vec, P("dp", None, "tensor"), P(None, "dp"), P("tensor", "dp"),
        vec, vec, vec, P("dp", "tensor"), vec, P("tensor", "dp"), vec, tok,
    )
    out_specs = (
        tok, tok, vec, vec, P("dp", None, "tensor"), P(None, "dp"), P("tensor", "dp"),
        vec, vec, vec, P("dp", "tensor"), vec, P("tensor", "dp"), vec,
    )
    return jax.shard_map(on_device, mesh=mesh, in_specs=in_specs, out_specs=out_specs, check_vma=False)
```

```python
import functools

import jax
import jax.numpy as jnp
from jax import lax
from jax.experimental import pallas as pl
from jax.experimental.pallas import tpu as pltpu
from jax.sharding import PartitionSpec as P

HD = 64
QB = 256
NEG = -1e30
EPSILON = 1e-05
BRANCH_SCALE = 48.0 ** (-0.5)
SMALL = 128
VECS = 16
ROWS = 256
HIDDEN = 512
bf = jnp.bfloat16
f32 = jnp.float32
NT = (((1,), (1,)), ((), ()))
TN = (((0,), (0,)), ((), ()))
BOTH = ("dp", "tensor")
MESH_ID = pl.DeviceIdType.MESH
ANY = pl.BlockSpec(memory_space=pl.ANY)
VM = pl.BlockSpec(memory_space=pltpu.VMEM)
SM = pl.BlockSpec(memory_space=pltpu.SMEM)


def attn_info(seg, core):
    n=seg.shape[0]; nb=n//QB
    docs=jnp.arange(16,dtype=jnp.int32)
    first=jnp.sum((seg[None,:]<docs[:,None]).astype(jnp.int32),axis=1)
    starts=jnp.sum(jnp.where(seg[None,:]==docs[:,None],first[:,None],0),axis=0)
    blocks=starts.reshape(nb,QB)
    idx=jnp.arange(nb,dtype=jnp.int32)
    low=blocks[:,0]//QB
    mid=jnp.clip((blocks[:,QB-1]+QB-1)//QB,low,idx)
    return starts.reshape(1,n), jnp.concatenate([jnp.reshape(core,(1,)),low,mid]).astype(jnp.int32)

def attn_masks(kat, srow, diagonal):
    keys = lax.broadcasted_iota(jnp.int32, (QB, QB), 0)
    mask = keys >= (srow - kat)
    if diagonal:
        mask = mask & (keys <= lax.broadcasted_iota(jnp.int32, (QB, QB), 1))
    return mask


def head_lanes(values):
    low = (lax.broadcasted_iota(jnp.int32, (1, values.shape[1]), 1) % 128) < HD
    zero = jnp.zeros((), bf)
    return jnp.where(low, values, zero), jnp.where(low, zero, values)


def fwd_kernel(info, own, recv, st_ref, okeep, osend, lse_ref, qm, ks, vt, osc, acc):
    half, cols = own.shape[0], own.shape[1] // 3
    n, nb, heads, pairs = 2 * half, 2 * half // QB, cols // HD, cols // 128
    c = info[0]
    for base, src in ((c * half, own), ((1 - c) * half, recv)):
        rows = pl.ds(pl.multiple_of(base, half), half)
        for g in range(pairs):
            lanes = slice(g * 128, (g + 1) * 128)
            part = lambda k: src[:, (3 * g + k) * 128 : (3 * g + k + 1) * 128]
            qm[0, rows, lanes], qm[1, rows, lanes] = head_lanes(part(0) * bf(HD**-0.5))
            ks[rows, lanes] = part(1)
            vt[lanes, rows] = part(2).T

    def qblock(i, _):
        at = pl.multiple_of(i * QB, QB)
        qr = pl.ds(at, QB)
        srow = st_ref[:, qr]
        acc[...] = jnp.zeros_like(acc)

        def step(mode, j, carry):
            kat = pl.multiple_of(j * QB, QB)
            kr = pl.ds(kat, QB)
            if mode:
                mask = attn_masks(kat, srow, mode == 2)
            scores, mixed = [], []
            for h in range(heads):
                lanes = slice(h // 2 * 128, h // 2 * 128 + 128)
                one = lax.dot_general(ks[kr, lanes], qm[h % 2, qr, lanes], NT, preferred_element_type=f32)
                scores.append(jnp.where(mask, one, NEG) if mode else one)
            for h in range(heads):
                top, total = carry[h]
                new = jnp.maximum(top, jnp.max(scores[h], axis=0, keepdims=True))
                weights = jnp.exp(scores[h] - new)
                fade = jnp.exp(top - new)
                total = fade * total + jnp.sum(weights, axis=0, keepdims=True)
                mixed.append((new, total, fade, weights.astype(bf)))
            for h in range(heads):
                sub = slice(h * HD, (h + 1) * HD)
                acc[sub] = mixed[h][2] * acc[sub] + jnp.dot(vt[sub, kr], mixed[h][3], preferred_element_type=f32)
            return tuple(m[:2] for m in mixed)

        carry = step(2, i, ((jnp.full((1, QB), NEG, f32), jnp.zeros((1, QB), f32)),) * heads)
        carry = lax.fori_loop(info[1 + i], info[1 + nb + i], functools.partial(step, 1), carry)
        carry = lax.fori_loop(info[1 + nb + i], i, functools.partial(step, 0), carry)
        for h, (top, total) in enumerate(carry):
            sub = slice(h * HD, (h + 1) * HD)
            acc[sub] = acc[sub] / total
            lse_ref[h : h + 1, qr] = top + jnp.log(total)
        osc[qr] = acc[...].T.astype(bf)
        return 0

    lax.fori_loop(0, nb, qblock, 0)
    okeep[...] = osc[pl.ds(pl.multiple_of(c * half, half), half)]
    osend[...] = osc[pl.ds(pl.multiple_of((1 - c) * half, half), half)]


def attn_fwd(own, recv, starts, info):
    half, cols = own.shape[0], own.shape[1] // 3
    n = 2 * half
    return pl.pallas_call(
        fwd_kernel,
        in_specs=[SM, VM, VM, VM],
        out_specs=[VM] * 3,
        scratch_shapes=[
            pltpu.VMEM((2, n, cols), bf), pltpu.VMEM((n, cols), bf), pltpu.VMEM((cols, n), bf),
            pltpu.VMEM((n, cols), bf), pltpu.VMEM((cols, QB), f32)],
        out_shape=[jax.ShapeDtypeStruct((half, cols), bf)] * 2 + [jax.ShapeDtypeStruct((cols // HD, n), f32)],
        cost_estimate=pl.CostEstimate(flops=n * n, bytes_accessed=n * 128, transcendentals=0),
        compiler_params=pltpu.CompilerParams(vmem_limit_bytes=48 << 20),
    )(info, own, recv, starts)


def bwd_kernel(first, info, own, recv, doo, dor, oo, orr, st_ref, lse_ref, dkeep, dsend, qm, ks, vs, kt, dom, dlt, dqs, dks, dvs):
    half, n, nb = own.shape[0], 2 * own.shape[0], 2 * own.shape[0] // QB
    c = info[0]
    for base, src, do, o in ((c * half, own, doo, oo), ((1 - c) * half, recv, dor, orr)):
        rows = pl.ds(pl.multiple_of(base, half), half)
        qm[0, rows], qm[1, rows] = head_lanes(src[:, :128] * bf(HD**-0.5))
        ks[rows] = src[:, 128:256]
        vs[rows] = src[:, 256:]
        kt[:, rows] = src[:, 128:256].T
        dom[0, rows], dom[1, rows] = head_lanes(do[...])
        prod = (do[...].astype(f32) * o[...].astype(f32)).T
        for h in range(2):
            dlt[h : h + 1, rows] = jnp.sum(prod[h * HD : (h + 1) * HD], axis=0, keepdims=True)
    dks[...] = jnp.zeros_like(dks)
    dvs[...] = jnp.zeros_like(dvs)

    def qblock(i, _):
        at = pl.multiple_of(i * QB, QB)
        qr = pl.ds(at, QB)
        srow = st_ref[:, qr]
        dqs[...] = jnp.zeros_like(dqs)

        def step(mode, j, carry):
            kat = pl.multiple_of(j * QB, QB)
            kr = pl.ds(kat, QB)
            if mode:
                mask = attn_masks(kat, srow, mode == 2)
            scores, softs, grads = [], [], []
            for h in range(2):
                one = lax.dot_general(ks[kr], qm[h, qr], NT, preferred_element_type=f32)
                back = lax.dot_general(vs[kr], dom[h, qr], NT, preferred_element_type=f32)
                scores.append((jnp.where(mask, one, NEG) if mode else one, back))
            for h in range(2):
                soft = jnp.exp(scores[h][0] - lse_ref[first + h : first + h + 1, qr])
                grads.append((soft * (scores[h][1] - dlt[h : h + 1, qr])).astype(bf))
                softs.append(soft.astype(bf))
            both = lambda ref: jnp.concatenate([ref[0, qr], ref[1, qr]], axis=0)
            dvs[kr] += jnp.dot(jnp.concatenate(softs, axis=1), both(dom), preferred_element_type=f32)
            dks[kr] += jnp.dot(jnp.concatenate(grads, axis=1), both(qm), preferred_element_type=f32)
            for h in range(2):
                sub = slice(h * HD, (h + 1) * HD)
                dqs[sub] += jnp.dot(kt[sub, kr], grads[h], preferred_element_type=f32)
            return carry

        step(2, i, 0)
        lax.fori_loop(info[1 + i], info[1 + nb + i], functools.partial(step, 1), 0)
        lax.fori_loop(info[1 + nb + i], i, functools.partial(step, 0), 0)
        qm[0, qr] = (dqs[...] * (HD**-0.5)).T.astype(bf)
        return 0

    lax.fori_loop(0, nb, qblock, 0)
    for dst, base in ((dkeep, c * half), (dsend, (1 - c) * half)):
        rows = pl.ds(pl.multiple_of(base, half), half)
        dst[:, :128] = qm[0, rows]
        dst[:, 128:256] = dks[rows].astype(bf)
        dst[:, 256:] = dvs[rows].astype(bf)


def attn_bwd(pair, own, recv, do_own, do_recv, o_own, o_recv, starts, lse, info):
    half = own.shape[0]
    n = 2 * half
    wide = pl.BlockSpec((half, 384), lambda k, s: (0, pair))
    slim = pl.BlockSpec((half, 128), lambda k, s: (0, pair))
    whole = lambda a: pl.BlockSpec(a.shape, lambda k, s: (0, 0))
    return pl.pallas_call(
        functools.partial(bwd_kernel, 2 * pair),
        grid_spec=pltpu.PrefetchScalarGridSpec(
            num_scalar_prefetch=1,
            grid=(1,),
            in_specs=[wide, wide, slim, slim, slim, slim, whole(starts), whole(lse)],
            out_specs=[pl.BlockSpec((half, 384), lambda k, s: (0, 0))] * 2,
            scratch_shapes=[
                pltpu.VMEM((2, n, 128), bf), pltpu.VMEM((n, 128), bf), pltpu.VMEM((n, 128), bf), pltpu.VMEM((128, n), bf),
                pltpu.VMEM((2, n, 128), bf), pltpu.VMEM((2, n), f32), pltpu.VMEM((128, QB), f32), pltpu.VMEM((n, 128), f32),
                pltpu.VMEM((n, 128), f32)],
        ),
        out_shape=[jax.ShapeDtypeStruct((half, 384), bf)] * 2,
        cost_estimate=pl.CostEstimate(flops=n * n, bytes_accessed=n * 128, transcendentals=0),
        compiler_params=pltpu.CompilerParams(vmem_limit_bytes=40 << 20),
    )(info, own, recv, do_own, do_recv, o_own, o_recv, starts, lse)


def dot(left, right, dims=(((1,), (0,)), ((), ()))):
    return lax.dot_general(left, right, dims, preferred_element_type=f32)


def exchange(value, bit, dp_size):
    if bit:
        return lax.ppermute(value, "dp", [(i, i ^ bit) for i in range(dp_size)])
    return lax.ppermute(value, "tensor", [(0, 1), (1, 0)])


def flip(index, bits):
    for bit in bits:
        index = index + bit * (1 - 2 * ((index // bit) % 2))
    return index

def far_groups(dp_size):
    far = [1 << k for k in range(dp_size.bit_length() - 2, 1, -1)]
    return [tuple(far[k : k + 2]) for k in range(0, len(far), 2)]

def group_moves(group):
    if len(group) == 1:
        return [(1, group)]
    return [(1, group[:1]), (2, group[1:]), (3, group)]

def chunks_of(cols, which, count, until=None):
    tiles = cols // 128
    cuts = [128 * ((tiles * k) // count) for k in range(count + 1)]
    arrays = range(which, until + 1) if until else (which,)
    return tuple(
        (array, low, high - low, 128 * max(1, (high - low) * 2 // 3 // 128))
        for low, high in zip(cuts, cuts[1:]) for array in arrays)


def head_kernel(groups, chunks, tokens, *refs):
    shards, x_out, outs, (send_sem, recv_sem, local_sem) = refs[:4], refs[4], refs[5:9], refs[9:]
    dp, t = lax.axis_index("dp"), lax.axis_index("tensor")
    core = dp % 2
    away = core + t - 2 * core * t
    near = {1: (flip(dp, (1,)), t), 2: (flip(dp, (2,)), t), 0: (dp, 1 - t)}
    distant = [bits for group in groups for _, bits in group_moves(group)]
    swap = (dp - core + t, core)
    barrier = pltpu.get_barrier_semaphore()
    for device in list(near.values()) + [(flip(dp, bits), t) for bits in distant]:
        pl.semaphore_signal(barrier, inc=1, device_id=device, device_id_type=MESH_ID)

    @pl.when(away == 1)
    def _():
        pl.semaphore_signal(barrier, inc=1, device_id=swap, device_id_type=MESH_ID)

    local = [
        pltpu.make_async_copy(shards[k], outs[k].at[away, 0] if k < 2 else outs[k].at[0], local_sem.at[k]) for k in range(4)]
    for copy in local:
        copy.start()
    pl.semaphore_wait(barrier, len(near) + len(distant) + away)
    count = [0]

    def remote(src, dst, device):
        slot = count[0]
        count[0] += 1
        return pltpu.make_async_remote_copy(
            src_ref=src, dst_ref=dst, send_sem=send_sem.at[slot], recv_sem=recv_sem.at[slot],
            device_id=device, device_id_type=MESH_ID)

    def blocks(ref, index, first, held, low, size):
        return ref.at[index, pl.ds(first, held), :, pl.ds(low, size)]

    plans = []
    for which, low, size, part in chunks:
        shard, out = shards[which], outs[which]
        steps, held = [], 1
        for group in groups:
            moves = []
            for place, bits in group_moves(group):
                src = shard.at[:, pl.ds(low, size)] if held == 1 else blocks(out, away, 0, held, low, size)
                dst = out.at[away, place, :, pl.ds(low, size)] if held == 1 else blocks(out, away, place * held, held, low, size)
                moves.append(remote(src, dst, (flip(dp, bits), t)))
            held *= len(group_moves(group)) + 1
            steps.append(moves)
        a, b = (low, part), (low + part, size - part)
        steps.append([
            remote(blocks(out, away, 0, held, *a), blocks(out, away, 0, held, *a), near[0]),
            remote(blocks(out, away, 0, held, *b), blocks(out, away, held, held, *b), near[2]),
        ])
        steps.append(
            [remote(blocks(out, k, 0, held, *a), blocks(out, k, held, held, *a), near[2]) for k in range(2)]
            + [remote(blocks(out, away, 0, 2 * held, *b), blocks(out, away, 0, 2 * held, *b), near[0])])
        steps.append([
            remote(blocks(out, k, 0, 2 * held, low, size),
                   blocks(out, 1 - k, 2 * held, 2 * held, low, size), near[1]) for k in range(2)])
        plans.append(steps)
    later = []
    held = 1
    for group in groups:
        moves = []
        for place, bits in group_moves(group):
            for shard, out in zip(shards[2:], outs[2:]):
                src = shard if held == 1 else out.at[pl.ds(0, held)]
                dst = out.at[place] if held == 1 else out.at[pl.ds(place * held, held)]
                moves.append(remote(src, dst, (flip(dp, bits), t)))
        held *= len(group_moves(group)) + 1
        later.append(moves)
    depth = len(plans[0])
    swap_copy = remote(tokens, x_out, swap)
    stay_copy = pltpu.make_async_copy(tokens, x_out, local_sem.at[4])
    waited = set()

    def advance(number, phase):
        if number >= len(plans):
            return
        if phase > 0:
            for move in plans[number][phase - 1]:
                move.wait_recv()
        if phase == 1 and chunks[number][0] not in waited:
            waited.add(chunks[number][0])
            local[chunks[number][0]].wait()
        if phase < depth:
            for move in plans[number][phase]:
                move.start()

    advance(0, 0)

    @pl.when(away == 1)
    def _():
        swap_copy.start()

    @pl.when(away == 0)
    def _():
        stay_copy.start()

    far = len(groups)
    for number in range(len(plans)):
        if number == 0:
            for phase in range(1, far + 1):
                advance(0, phase)
            advance(1, 0)
        advance(number, far + 1)
        for phase in range(1, far + 1):
            advance(number + 1, phase)
        advance(number + 2, 0)
        if number == len(plans) - 2:
            for move in later[0]:
                move.start()
        advance(number, far + 2)
    for number in range(len(plans)):
        advance(number, depth)

    @pl.when(away == 1)
    def _():
        swap_copy.wait()

    @pl.when(away == 0)
    def _():
        stay_copy.wait()

    for which in sorted(set(range(4)) - waited):
        local[which].wait()
    for k, moves in enumerate(later):
        if k > 0:
            for move in moves:
                move.start()
        for move in moves:
            move.wait()
    for steps in plans:
        for moves in steps:
            for move in moves:
                move.wait_send()


def head(dp_size, tokens, shards, chunks):
    groups = far_groups(dp_size)
    partners = sum(len(group_moves(g)) for g in groups)
    slots = len(chunks) * (partners + 7) + 2 * partners + 1
    shapes = [(2, dp_size)] * 2 + [(dp_size // 4,)] * 2
    return pl.pallas_call(
        functools.partial(head_kernel, groups, chunks),
        in_specs=[VM] * 5,
        out_specs=[ANY] * 5,
        out_shape=[jax.ShapeDtypeStruct(tokens.shape, tokens.dtype)]
        + [jax.ShapeDtypeStruct(lead + s.shape, s.dtype) for lead, s in zip(shapes, shards)],
        scratch_shapes=[pltpu.SemaphoreType.DMA((slots,)), pltpu.SemaphoreType.DMA((slots,)), pltpu.SemaphoreType.DMA((5,))],
        compiler_params=pltpu.CompilerParams(collective_id=0, has_side_effects=True),
    )(tokens, *shards)


def tail_kernel(groups, tokens, own_lo, own_hi, rest_lo, rest_hi, small_lo, small_hi, x_out, total, vecs,
                part, got_core, got_near, got_last, got_far, vec, vec_core, vec_two, vec_one, vec_far, send_sem, recv_sem, local_sem):
    dp, t = lax.axis_index("dp"), lax.axis_index("tensor")
    core = dp % 2
    away = core + t - 2 * core * t
    near = {1: (flip(dp, (1,)), t), 2: (flip(dp, (2,)), t), 0: (dp, 1 - t)}
    distant = [bits for group in groups for _, bits in group_moves(group)]
    swap = (dp - core + t, core)
    barrier = pltpu.get_barrier_semaphore()
    for device in list(near.values()) + [(flip(dp, bits), t) for bits in distant]:
        pl.semaphore_signal(barrier, inc=1, device_id=device, device_id_type=MESH_ID)

    @pl.when(away == 1)
    def _():
        pl.semaphore_signal(barrier, inc=1, device_id=swap, device_id_type=MESH_ID)

    pl.semaphore_wait(barrier, len(near) + len(distant) + away)
    count = [0]

    def remote(src, dst, device):
        slot = count[0]
        count[0] += 1
        return pltpu.make_async_remote_copy(
            src_ref=src, dst_ref=dst, send_sem=send_sem.at[slot], recv_sem=recv_sem.at[slot],
            device_id=device, device_id_type=MESH_ID)

    swap_copy = remote(tokens, x_out, swap)
    stay_copy = pltpu.make_async_copy(tokens, x_out, local_sem.at[0])
    half, rows, cols = own_lo.shape
    cut = cols * 2 // 3 // 128 * 128
    a, b = pl.ds(0, cut), pl.ds(cut, cols - cut)
    quarter = half // 2
    to_core = [
        remote(rest_hi, got_core.at[0], near[1]), remote(own_hi, got_core.at[1], near[1]),
        remote(small_hi, vec_core, near[1])]
    for move in to_core:
        move.start()

    @pl.when(away == 1)
    def _():
        swap_copy.start()

    @pl.when(away == 0)
    def _():
        stay_copy.start()

    def add(*terms):
        out = terms[0].astype(f32)
        for term in terms[1:]:
            out = out + term.astype(f32)
        return out.astype(bf)

    for move in to_core:
        move.wait_recv()

    def sum_core(k, _):
        part[0, k] = add(own_lo[k], got_core[0, k])
        part[1, k] = add(rest_lo[k], got_core[1, k])
        vec[k] = add(small_lo[k], vec_core[k])
        return 0

    lax.fori_loop(0, half, sum_core, 0)
    upper, lower = pl.ds(quarter, quarter), pl.ds(0, quarter)
    mine, other = away, 1 - away
    to_near = [
        remote(part.at[0, upper, :, a], got_near.at[0, lower, :, a], near[2]),
        remote(part.at[1, upper, :, a], got_near.at[1, lower, :, a], near[2]),
        remote(part.at[other, :, :, b], got_near.at[0, :, :, b], near[0]),
        remote(vec.at[upper], vec_two, near[2])]
    for move in to_near:
        move.start()
    for move in to_near:
        move.wait_recv()

    def sum_near(k, _):
        for g in range(2):
            part[g, k, :, a] = add(part[g, k, :, a], got_near[g, k, :, a])
        for q in (k, k + quarter):
            part[mine, q, :, b] = add(part[mine, q, :, b], got_near[0, q, :, b])
        vec[k] = add(vec[k], vec_two[k])
        return 0

    lax.fori_loop(0, quarter, sum_near, 0)
    to_last = [
        remote(part.at[other, lower, :, a], got_last.at[:, :, a], near[0]),
        remote(part.at[mine, upper, :, b], got_last.at[:, :, b], near[2]),
        remote(vec.at[lower], vec_one, near[0])]
    for move in to_last:
        move.start()
    for move in to_last:
        move.wait_recv()

    def sum_last(k, _):
        part[mine, k] = add(part[mine, k], got_last[k])
        vec_one[k] = add(vec[k], vec_one[k])
        return 0

    lax.fori_loop(0, quarter, sum_last, 0)
    to_far = []
    held, used = quarter, 0
    for group in reversed(groups):
        moves = group_moves(group)
        held //= len(moves) + 1
        step = []
        for place, bits in moves:
            device = (flip(dp, bits), t)
            step.append(remote(part.at[mine, pl.ds(place * held, held)], got_far.at[pl.ds(used, held)], device))
            step.append(remote(vec_one.at[pl.ds(place * held, held)], vec_far.at[pl.ds(used, held)], device))
            used += held
        for move in step:
            move.start()
        for move in step:
            move.wait_recv()
        base = used - held * len(moves)

        def sum_far(k, _, base=base, held=held, count=len(moves)):
            part[mine, k] = add(part[mine, k], *[got_far[base + m * held + k] for m in range(count)])
            vec_one[k] = add(vec_one[k], *[vec_far[base + m * held + k] for m in range(count)])
            return 0

        lax.fori_loop(0, held, sum_far, 0)
        to_far += step
    total[...] = part[mine, 0].astype(f32)
    vecs[...] = vec_one[0].astype(f32)

    @pl.when(away == 1)
    def _():
        swap_copy.wait()

    @pl.when(away == 0)
    def _():
        stay_copy.wait()

    for move in to_core + to_near + to_last + to_far:
        move.wait_send()


def tail(dp_size, tokens, own, rest, small):
    groups = far_groups(dp_size)
    half, rows, cols = own[0].shape
    quarter = half // 2
    wide = small[0].shape[2]
    partners = sum(len(group_moves(g)) for g in groups)
    slots = 11 + 2 * partners
    return pl.pallas_call(
        functools.partial(tail_kernel, groups),
        in_specs=[VM] * 7,
        out_specs=[ANY, VM, VM],
        out_shape=[
            jax.ShapeDtypeStruct(tokens.shape, bf), jax.ShapeDtypeStruct((rows, cols), f32),
            jax.ShapeDtypeStruct((rows, wide), f32)],
        scratch_shapes=[
            pltpu.VMEM((2, half, rows, cols), bf), pltpu.VMEM((2, half, rows, cols), bf), pltpu.VMEM((2, half, rows, cols), bf),
            pltpu.VMEM((quarter, rows, cols), bf), pltpu.VMEM((quarter, rows, cols), bf),
            pltpu.VMEM((half, rows, wide), bf), pltpu.VMEM((half, rows, wide), bf), pltpu.VMEM((quarter, rows, wide), bf),
            pltpu.VMEM((quarter, rows, wide), bf), pltpu.VMEM((quarter, rows, wide), bf),
            pltpu.SemaphoreType.DMA((slots,)), pltpu.SemaphoreType.DMA((slots,)), pltpu.SemaphoreType.DMA((1,))],
        compiler_params=pltpu.CompilerParams(collective_id=1, has_side_effects=True, vmem_limit_bytes=48 << 20),
    )(tokens, *own, *rest, *small)


def far_exchange(value, dp_size):
    out, held = [], value.shape[0]
    (group,) = far_groups(dp_size)[-1:]
    held //= len(group_moves(group)) + 1
    for place, bits in group_moves(group):
        mask = sum(bits)
        piece = value[place * held : (place + 1) * held]
        out.append(lax.ppermute(piece, "dp", [(i, i ^ mask) for i in range(dp_size)]))
    return out


def far_sum(value, got, dp_size):
    held = got[0].shape[0]
    total = value[:held].astype(f32)
    for piece in got:
        total = total + piece.astype(f32)
    for group in far_groups(dp_size)[-2::-1]:
        total = total.astype(bf)
        held //= len(group_moves(group)) + 1
        moves = [
            lax.ppermute(total[place * held : (place + 1) * held], "dp", [(i, i ^ sum(bits)) for i in range(dp_size)])
            for place, bits in group_moves(group)]
        total = total[:held].astype(f32)
        for piece in moves:
            total = total + piece.astype(f32)
    return total


def add_low(left, right):
    return (left.astype(f32) + right.astype(f32)).astype(bf)


def order_matrix(owner, rows, width):
    natural = lax.broadcasted_iota(jnp.int32, (width, width), 0)
    place = lax.broadcasted_iota(jnp.int32, (width, width), 1)
    block = place // rows
    count = width // rows
    source = jnp.zeros_like(block)
    for k, bit in enumerate([1 << b for b in range(count.bit_length() - 2, 1, -1)] + [2, 1]):
        source = source + ((block // (1 << k)) % 2) * bit
    return ((source ^ owner) * rows + place % rows == natural).astype(bf)


def norm_parts(values):
    centered = values - jnp.mean(values, axis=-1, keepdims=True)
    inverse = lax.rsqrt(jnp.mean(centered * centered, axis=-1, keepdims=True) + EPSILON)
    return centered * inverse, inverse


def norm_back(hat, inverse, gain, grad):
    scaled = grad * gain
    return inverse * (
        scaled - jnp.mean(scaled, axis=-1, keepdims=True) - hat * jnp.mean(scaled * hat, axis=-1, keepdims=True))


def over_rows(total, body):
    def step(k, _):
        body(pl.ds(pl.multiple_of(k * ROWS, ROWS), ROWS))
        return 0

    lax.fori_loop(0, total // ROWS, step, 0)


def column_sum(ref, row, values):
    ref[row : row + 1] += jnp.sum(values, axis=0, keepdims=True)


def bias_row(vec_nat, group, cols):
    lanes = pl.ds(pl.multiple_of(group * cols, 128), cols)
    q, v = vec_nat[2:3, lanes], vec_nat[3:4, lanes]
    parts = []
    for g in range(cols // 128):
        part = slice(g * 128, (g + 1) * 128)
        parts += [q[:, part], jnp.zeros((1, 128), f32), v[:, part]]
    return jnp.concatenate(parts, axis=1)


def first_kernel(rows, info, tokens, pack, weight, x_out, n1_out, send, vec_rel, vec_nat, order):
    width, cols = tokens.shape[1], weight.shape[2] // 3
    order[...] = order_matrix(info[1], rows, width)
    small = pack[0, :, cols:].astype(f32).T[:VECS]
    vec_rel[...] = small
    vec_nat[...] = lax.dot_general(small.astype(bf), order[...], NT, preferred_element_type=f32)
    bias = bias_row(vec_nat, 1 - info[0], cols)

    def body(at):
        x = jnp.dot(tokens[at], order[...], preferred_element_type=f32)
        hat, _ = norm_parts(x)
        n1 = (hat * vec_rel[0:1] + vec_rel[1:2]).astype(bf)
        x_out[at] = x.astype(bf)
        n1_out[at] = n1
        send[at] = (jnp.dot(n1, weight[0], preferred_element_type=f32) + bias).astype(bf)

    over_rows(tokens.shape[0], body)


def own_kernel(info, n1, weight, vec_nat, out):
    bias = bias_row(vec_nat, info[0], weight.shape[2] // 3)

    def body(at):
        out[at] = (jnp.dot(n1[at], weight[0], preferred_element_type=f32) + bias).astype(bf)

    over_rows(n1.shape[0], body)


def picked(array, index):
    return pl.BlockSpec((1,) + array.shape[1:], lambda k, s: (index, 0, 0))


def whole(array):
    return pl.BlockSpec(array.shape, lambda k, s: (0,) * len(array.shape))


def one_call(kernel, info, inputs, specs, outs, scratch=(), limit=56):
    return pl.pallas_call(
        kernel,
        grid_spec=pltpu.PrefetchScalarGridSpec(
            num_scalar_prefetch=1, grid=(1,), in_specs=[s if s is not None else whole(a) for a, s in zip(inputs, specs)],
            out_specs=[whole(o) for o in outs], scratch_shapes=list(scratch)),
        out_shape=outs,
        cost_estimate=pl.CostEstimate(flops=1 << 22, bytes_accessed=1 << 18, transcendentals=0),
        compiler_params=pltpu.CompilerParams(vmem_limit_bytes=limit << 20),
    )(info, *inputs)


def like(shape, dtype):
    return jax.ShapeDtypeStruct(shape, dtype)


def project_first(info, rows, tokens, packs, weights):
    n, width = tokens.shape
    return one_call(
        functools.partial(first_kernel, rows), info, (tokens, packs, weights), (None, picked(packs, 0), picked(weights, 1)),
        [like((n, width), bf), like((n, width), bf), like((n, weights.shape[2]), bf), like((VECS, width), f32), like((VECS, width), f32)],
        [pltpu.VMEM((width, width), bf)])


def project_own(info, n1, weights, vec_nat):
    (out,) = one_call(
        own_kernel, info, (n1, weights, vec_nat), (None, picked(weights, 0), None), [like((n1.shape[0], weights.shape[2]), bf)])
    return out


def middle_kernel(rows, info, o_own, o_recv, packs, x, vec_rel, cot, cot_recv, middle, n2_out, cot_rel, d_mlp, order):
    width, cols = x.shape[1], o_own.shape[1]
    order[...] = order_matrix(info[1], rows, width)
    stay = info[2] == 1

    def body(at):
        branch = lax.dot_general(o_own[at], packs[0, :, :cols], NT, preferred_element_type=f32)
        branch = branch + lax.dot_general(o_recv[at], packs[1, :, :cols], NT, preferred_element_type=f32)
        mid = x[at].astype(f32) + BRANCH_SCALE * (branch + vec_rel[4:5])
        middle[at] = mid
        hat, _ = norm_parts(mid)
        n2_out[at] = (hat * vec_rel[5:6] + vec_rel[6:7]).astype(bf)
        grad = jnp.dot(jnp.where(stay, cot[at], cot_recv[at]), order[...], preferred_element_type=f32)
        cot_rel[at] = grad.astype(bf)
        d_mlp[at] = (BRANCH_SCALE * grad).astype(bf)

    over_rows(x.shape[0], body)


def middle_part(info, rows, o_own, o_recv, packs, x, vec_rel, cot, cot_recv):
    shape = x.shape
    return one_call(
        functools.partial(middle_kernel, rows), info, (o_own, o_recv, packs, x, vec_rel, cot, cot_recv), (None,) * 7,
        [like(shape, f32), like(shape, bf), like(shape, bf), like(shape, bf)], [pltpu.VMEM((shape[1], shape[1]), bf)])


def mlp_kernel(n2, d_mlp, bias, fc0, fc1, fc2, fc3, pr0, pr1, mlp, d_n2, fc_lo, fc_hi, pr_lo, pr_hi, d_bias,
               n2_t, d_t, w_fc, w_pr, act, d_pre, acc, back):
    step = pl.program_id(0)
    total, half = n2.shape[0], n2.shape[1] // 2

    @pl.when(step == 0)
    def _():
        n2_t[...] = n2[...].T
        d_t[...] = d_mlp[...].T
        acc[...] = jnp.zeros_like(acc)
        back[...] = jnp.zeros_like(back)

    at = 0
    for piece in (fc0, fc1, fc2, fc3):
        w_fc[at : at + piece.shape[0]] = piece[...]
        at += piece.shape[0]
    at = 0
    for piece in (pr0, pr1):
        w_pr[at : at + piece.shape[0]] = piece[...]
        at += piece.shape[0]
    root = 0.7978845608
    count = total // ROWS
    raw = {}
    sums = jnp.zeros((1, w_fc.shape[1]), f32)

    def products(k):
        rows = slice(k * ROWS, (k + 1) * ROWS)
        return (
            jnp.dot(n2[rows], w_fc[...], preferred_element_type=f32) + bias[...],
            jnp.dot(d_mlp[rows], w_pr[...], preferred_element_type=f32))

    raw[0] = products(0)
    for k in range(count):
        rows = slice(k * ROWS, (k + 1) * ROWS)
        if k + 1 < count:
            raw[k + 1] = products(k + 1)
        pre, d_act = raw.pop(k)
        square = pre * pre
        inner = jnp.tanh(pre * (root + root * 0.044715 * square))
        gate = 0.5 + 0.5 * inner
        act[rows] = (pre * gate).astype(bf)
        slope = gate + pre * (0.5 - 0.5 * inner * inner) * (root + root * 3 * 0.044715 * square)
        grad = d_act * slope
        sums = sums + jnp.sum(grad, axis=0, keepdims=True)
        d_pre[rows] = grad.astype(bf)
        acc[rows] += lax.dot_general(act[rows], w_pr[...], NT, preferred_element_type=f32)
        back[rows] += lax.dot_general(d_pre[rows], w_fc[...], NT, preferred_element_type=f32)
    d_bias[...] = sums
    for out, left, right, low in (
        (fc_hi, n2_t, d_pre, half), (pr_hi, d_t, act, half), (fc_lo, n2_t, d_pre, 0), (pr_lo, d_t, act, 0)):
        out[...] = jnp.dot(left[low : low + half], right[...], preferred_element_type=f32).astype(bf)

    @pl.when(step == pl.num_programs(0) - 1)
    def _():
        mlp[...] = acc[...]
        d_n2[...] = back[...]


def mlp_part(n2, d_mlp, bias, fc_parts, proj_parts, start=None):
    (total, width), hidden, half = n2.shape, bias.shape[1], n2.shape[1] // 2
    full = lambda a: pl.BlockSpec(a.shape, lambda k: (0, 0))
    col = lambda a: pl.BlockSpec((a.shape[0], HIDDEN), lambda k: (0, k))
    inputs = (n2, d_mlp, bias, *fc_parts, *proj_parts)
    grad = like((half, hidden), bf)
    outs = [like((total, width), f32)] * 2 + [grad] * 4 + [like((1, hidden), f32)]
    return pl.pallas_call(
        mlp_kernel,
        grid=(hidden // HIDDEN,),
        in_specs=[full(n2), full(d_mlp)] + [col(a) for a in inputs[2:]],
        out_specs=[full(outs[0])] * 2 + [col(o) for o in outs[2:]],
        out_shape=outs,
        scratch_shapes=[
            pltpu.VMEM((width, total), bf), pltpu.VMEM((width, total), bf), pltpu.VMEM((width, HIDDEN), bf),
            pltpu.VMEM((width, HIDDEN), bf), pltpu.VMEM((total, HIDDEN), bf), pltpu.VMEM((total, HIDDEN), bf),
            pltpu.VMEM((total, width), f32), pltpu.VMEM((total, width), f32)],
        cost_estimate=pl.CostEstimate(flops=1 << 22, bytes_accessed=1 << 18, transcendentals=0),
        compiler_params=pltpu.CompilerParams(vmem_limit_bytes=60 << 20),
    )(*inputs)


def after_kernel(rows, info, middle, mlp0, mlp1, back0, back1, cot, packs, vec_rel, block_out, d_middle, d_attn, do_own, do_send, sums, order):
    width, cols = middle.shape[1], do_own.shape[1]
    order[...] = order_matrix(info[1], rows, width)
    sums[...] = jnp.zeros_like(sums)

    def body(at):
        mid = middle[at]
        out = (mid + BRANCH_SCALE * (mlp0[at] + mlp1[at] + vec_rel[7:8])).astype(bf)
        block_out[at] = lax.dot_general(out, order[...], NT, preferred_element_type=f32).astype(bf)
        hat, inverse = norm_parts(mid)
        grad = back0[at] + back1[at]
        out_grad = cot[at].astype(f32)
        total = out_grad + norm_back(hat, inverse, vec_rel[5:6], grad)
        d_middle[at] = total
        low = (BRANCH_SCALE * total).astype(bf)
        d_attn[at] = low
        do_own[at] = jnp.dot(low, packs[0, :, :cols], preferred_element_type=f32).astype(bf)
        do_send[at] = jnp.dot(low, packs[1, :, :cols], preferred_element_type=f32).astype(bf)
        column_sum(sums, 0, BRANCH_SCALE * total)
        column_sum(sums, 1, grad * hat)
        column_sum(sums, 2, grad)
        column_sum(sums, 3, BRANCH_SCALE * out_grad)

    over_rows(middle.shape[0], body)


def after_part(info, rows, middle, mlps, backs, cot, packs, vec_rel, cols):
    shape = middle.shape
    slim = like((shape[0], cols), bf)
    return one_call(
        functools.partial(after_kernel, rows), info, (middle, *mlps, *backs, cot, packs, vec_rel), (None,) * 8,
        [like(shape, bf), like(shape, f32), like(shape, bf), slim, slim, like((8, shape[1]), f32)],
        [pltpu.VMEM((shape[1], shape[1]), bf)])


def grads_into(lo, hi, left_t, extra_t, d_qkv, o):
    half = left_t.shape[0] // 2
    wide = d_qkv.shape[1]
    for out, low in ((hi, half), (lo, 0)):
        out[:, :wide] = jnp.dot(left_t[low : low + half], d_qkv[...], preferred_element_type=f32).astype(bf)
        out[:, wide:] = jnp.dot(extra_t[low : low + half], o[...], preferred_element_type=f32).astype(bf)


def last_own_kernel(info, dq0, dq1, dq2, n1, d_attn, o_own, weight, lo, hi, part, sums, d_qkv, left_t, extra_t):
    left_t[...] = n1[...].T
    extra_t[...] = d_attn[...].T
    sums[...] = jnp.zeros_like(sums)
    for g, d in enumerate((dq0, dq1, dq2)):
        d_qkv[:, g * 384 : (g + 1) * 384] = d[...]
    grads_into(lo, hi, left_t, extra_t, d_qkv, o_own)

    def body(at):
        part[at] = lax.dot_general(d_qkv[at], weight[0], NT, preferred_element_type=f32)
        column_sum(sums, 0, d_qkv[at].astype(f32))

    over_rows(n1.shape[0], body)


def last_own(info, dq, n1, d_attn, o_own, weights):
    n, width = n1.shape
    wide, slim = weights.shape[2], o_own.shape[1]
    grad = like((width // 2, wide + slim), bf)
    return one_call(
        last_own_kernel, info, (*dq, n1, d_attn, o_own, weights), (None,) * 6 + (picked(weights, 0),),
        [grad, grad, like((n, width), f32), like((8, wide), f32)],
        [pltpu.VMEM((n, wide), bf), pltpu.VMEM((width, n), bf), pltpu.VMEM((width, n), bf)])


def last_kernel(rows, info, dq0, dq1, dq2, n1, d_attn, o_recv, weight, part, x, d_middle, vec_rel, own_sums, mid_sums, fc_rows,
                lo, hi, grad_out, small, d_qkv, left_t, extra_t, sums, vecs, nat, order):
    width, cols = x.shape[1], o_recv.shape[1]
    order[...] = order_matrix(info[1], rows, width)
    left_t[...] = n1[...].T
    extra_t[...] = d_attn[...].T
    sums[...] = jnp.zeros_like(sums)
    vecs[...] = jnp.zeros_like(vecs)
    for g, d in enumerate((dq0, dq1, dq2)):
        d_qkv[:, g * 384 : (g + 1) * 384] = d[...]
    grads_into(lo, hi, left_t, extra_t, d_qkv, o_recv)

    def body(at):
        grad = part[at] + lax.dot_general(d_qkv[at], weight[0], NT, preferred_element_type=f32)
        hat, inverse = norm_parts(x[at].astype(f32))
        grad_out[at] = (d_middle[at] + norm_back(hat, inverse, vec_rel[0:1], grad)).astype(bf)
        column_sum(sums, 0, d_qkv[at].astype(f32))
        column_sum(vecs, 0, grad * hat)
        column_sum(vecs, 1, grad)

    over_rows(x.shape[0], body)
    nat[...] = jnp.zeros_like(nat)
    for group, ref in ((info[0], own_sums), (1 - info[0], sums)):
        for row, part_index in ((0, 0), (1, 2)):
            picks = [ref[0:1, (3 * g + part_index) * 128 : (3 * g + part_index + 1) * 128] for g in range(cols // 128)]
            nat[row : row + 1, pl.ds(pl.multiple_of(group * cols, 128), cols)] = jnp.concatenate(picks, axis=1)
    fan = fc_rows.shape[0]
    nat[2 : 2 + fan] = fc_rows[...]
    moved = jnp.dot(nat[...].astype(bf), order[...], preferred_element_type=f32)
    vecs[2:4] = moved[0:2]
    vecs[4:8] = mid_sums[0:4]
    vecs[8 : 8 + fan] = moved[2 : 2 + fan]
    small[...] = vecs[...].T.astype(bf)


def last_part(info, rows, dq, n1, d_attn, o_recv, weights, part, x, d_middle, vec_rel, own_sums, mid_sums, fc_rows):
    n, width = n1.shape
    wide, slim = weights.shape[2], o_recv.shape[1]
    grad = like((width // 2, wide + slim), bf)
    inputs = (*dq, n1, d_attn, o_recv, weights, part, x, d_middle, vec_rel, own_sums, mid_sums, fc_rows)
    return one_call(
        functools.partial(last_kernel, rows), info, inputs, (None,) * 6 + (picked(weights, 1),) + (None,) * 7,
        [grad, grad, like((n, width), bf), like((width, SMALL), bf)],
        [pltpu.VMEM((n, wide), bf), pltpu.VMEM((width, n), bf), pltpu.VMEM((width, n), bf), pltpu.VMEM((8, wide), f32),
         pltpu.VMEM((SMALL, width), f32), pltpu.VMEM((8, width), f32), pltpu.VMEM((width, width), bf)])


def on_device(
    tokens, segment_ids, ln1_gain, ln1_bias, w_qkv, b_qv, w_attn_out, b_attn_out,
    ln2_gain, ln2_bias, w_fc, b_fc, w_proj, b_proj, cotangent,
):
    dp_size = lax.axis_size("dp")
    dp_pos, t_pos = lax.axis_index("dp"), lax.axis_index("tensor")
    core = dp_pos % 2
    rows = ln1_gain.shape[0]
    width = tokens.shape[1]
    cols = w_qkv.shape[2]
    hidden = w_fc.shape[1]
    fan = b_fc.shape[0] // rows
    far = [1 << k for k in range(dp_size.bit_length() - 2, 1, -1)]
    swap = []
    for d in range(dp_size):
        for t in range(2):
            if d % 2 != t:
                swap.append((2 * d + t, 2 * (d - d % 2 + t) + d % 2))
    mine = core == t_pos

    pairs = cols // 128

    def by_pair(parts):
        parts = parts.reshape(-1, 3, pairs, 128)
        return jnp.swapaxes(parts, 1, 2).reshape(-1, 3 * cols)

    def by_part(columns):
        return jnp.swapaxes(columns.reshape(-1, pairs, 3, 128), 1, 2).reshape(-1, 3, cols)

    seg_other = exchange(segment_ids, 1, dp_size)
    seg = jnp.where(mine, segment_ids, seg_other)[0]
    small = jnp.concatenate(
        [ln1_gain[:, None], ln1_bias[:, None], b_qv.T, b_attn_out[:, None], ln2_gain[:, None],
         ln2_bias[:, None], b_proj[:, None], b_fc.reshape(rows, fan)], axis=1)
    small = jnp.pad(small, ((0, 0), (0, SMALL - small.shape[1])))
    out_pack = jnp.concatenate([w_attn_out.T, small], axis=1)
    tokens, all_qkv, all_out, fc_far, proj_far = head(
        dp_size, tokens, (by_pair(w_qkv), out_pack, w_fc, w_proj.T), chunks_of(3 * cols, 0, 2) + chunks_of(cols + SMALL, 1, 1))
    all_qkv, all_out = (a.reshape(2, width, -1) for a in (all_qkv, all_out))
    fc_far, proj_far = fc_far.reshape(-1, hidden), proj_far.reshape(-1, hidden)
    fc_parts = [[fc_far], [exchange(fc_far, 0, dp_size)]]
    proj_half = exchange(proj_far, 2, dp_size)

    part = jnp.stack([core, dp_pos, jnp.where(mine, 1, 0)]).astype(jnp.int32)
    x, n1, qkv_send, vec_rel, vec_nat = project_first(part, rows, tokens, all_out, all_qkv)
    qkv_recv = exchange(qkv_send, 1, dp_size)
    fc_parts, proj_half, n1 = lax.optimization_barrier((fc_parts, proj_half, n1))
    fc_parts = [p + [exchange(p[0], 2, dp_size)] for p in fc_parts]
    proj_half = jnp.concatenate([proj_far, proj_half], axis=0)
    proj_parts = [[proj_half], [exchange(proj_half, 0, dp_size)]]
    qkv_own = project_own(part, n1, all_qkv, vec_nat)
    starts, info = attn_info(seg, core)
    o_own, o_send, lse = attn_fwd(qkv_own, qkv_recv, starts, info)
    o_recv = exchange(o_send, 1, dp_size)
    fc_parts, proj_parts = (
        [p + [exchange(e, 1, dp_size) for e in p] for p in parts] for parts in (fc_parts, proj_parts))
    cot_recv = lax.ppermute(cotangent, BOTH, swap)
    middle, n2, cot, d_mlp = middle_part(part, rows, o_own, o_recv, all_out, x, vec_rel, cotangent, cot_recv)
    fc_bias = vec_nat[8 : 8 + fan].T.reshape(2, 1, hidden)
    half = width // 2
    mlps, backs, d_b_fc, sum_fc, sum_proj = [], [], [], [], []
    for k in range(2):
        bias = lax.dynamic_index_in_dim(fc_bias, t_pos ^ k, 0, keepdims=False)
        out, back, fc_lo, fc_hi, pr_lo, pr_hi, d_bias = mlp_part(n2, d_mlp, bias, fc_parts[k], proj_parts[k])
        mlps.append(out)
        backs.append(back)
        d_b_fc.append(d_bias[0])
        sum_fc.append(add_low(fc_lo, exchange(fc_hi, 1, dp_size)))
        sum_proj.append(add_low(pr_lo, exchange(pr_hi, 1, dp_size)))
    block_out, d_middle, d_attn, do_own, do_send, mid_sums = after_part(
        part, rows, middle, mlps, backs, cot, all_out, vec_rel, cols)
    block_out = jnp.where(mine, block_out, lax.ppermute(block_out, BOTH, swap))
    do_recv = exchange(do_send, 1, dp_size)
    pick = lambda cond, a, b: jnp.where(cond, jnp.concatenate([a, b]), jnp.concatenate([b, a]))
    fc_rows = pick(t_pos == 0, *d_b_fc).reshape(width, fan).T

    near_size = half // 2
    dq_own, dq_recv = [], []
    last = (qkv_own, qkv_recv, do_own, do_recv, o_own, o_send)
    last, sum_fc, sum_proj = lax.optimization_barrier((last, sum_fc, sum_proj))
    fc_sent = exchange(sum_fc[1], 0, dp_size)
    proj_sent = [exchange(p[near_size:], 2, dp_size) for p in sum_proj]
    for g in range(pairs):
        if g == pairs - 1:
            sum_fc = add_low(sum_fc[0], fc_sent)
            sum_proj = [add_low(p[:near_size], r) for p, r in zip(sum_proj, proj_sent)]
            last, dq_own, sum_fc, sum_proj = lax.optimization_barrier((last, dq_own, sum_fc, sum_proj))
            fc_sent = exchange(sum_fc[near_size:], 2, dp_size)
            proj_sent = exchange(sum_proj[1], 0, dp_size)
        own_g, send_g = attn_bwd(g, *last, starts, lse, info)
        dq_own = dq_own + [own_g]
        dq_recv = dq_recv + [exchange(send_g, 1, dp_size)]
    sum_fc = add_low(sum_fc[:near_size], fc_sent)
    sum_proj = add_low(sum_proj[0], proj_sent)
    dq_own, sum_fc, sum_proj = lax.optimization_barrier((dq_own, sum_fc, sum_proj))
    fc_sent = far_exchange(sum_fc, dp_size)
    proj_sent = far_exchange(sum_proj, dp_size)
    own_lo, own_hi, d_n1, own_sums = last_own(part, dq_own, n1, d_attn, o_own, all_qkv)
    rest_lo, rest_hi, grad_tokens, d_small = last_part(
        part, rows, dq_recv, n1, d_attn, o_recv, all_qkv, d_n1, x, d_middle, vec_rel, own_sums, mid_sums, fc_rows)
    blocks = lambda arr: arr.reshape(dp_size // 2, rows, -1)
    grad_tokens, sum_a, vecs = tail(
        dp_size, grad_tokens, (blocks(own_lo), blocks(own_hi)), (blocks(rest_lo), blocks(rest_hi)),
        (blocks(d_small[:half]), blocks(d_small[half:])))
    owner = dp_pos - core + t_pos
    grad_tokens = dot(grad_tokens, order_matrix(owner, rows, width), NT).astype(bf)
    sum_fc, sum_proj = far_sum(sum_fc, fc_sent, dp_size), far_sum(sum_proj, proj_sent, dp_size)
    return (
        block_out,
        grad_tokens,
        vecs[:, 0],
        vecs[:, 1],
        by_part(sum_a[:, : 3 * cols]),
        vecs[:, 2:4].T,
        sum_a[:, 3 * cols :].T,
        vecs[:, 4],
        vecs[:, 5],
        vecs[:, 6],
        sum_fc.astype(f32),
        vecs[:, 8 : 8 + fan].reshape(rows * fan),
        sum_proj.astype(f32).T,
        vecs[:, 7],
    )


def solution(mesh):
    vec, tok = P("dp"), P(BOTH, None)
    in_specs = (
        tok, P("dp", None), vec, vec, P("dp", None, "tensor"), P(None, "dp"), P("tensor", "dp"),
        vec, vec, vec, P("dp", "tensor"), vec, P("tensor", "dp"), vec, tok,
    )
    out_specs = (
        tok, tok, vec, vec, P("dp", None, "tensor"), P(None, "dp"), P("tensor", "dp"),
        vec, vec, vec, P("dp", "tensor"), vec, P("tensor", "dp"), vec,
    )
    return jax.shard_map(on_device, mesh=mesh, in_specs=in_specs, out_specs=out_specs, check_vma=False)
```

```python
import functools

import jax
import jax.numpy as jnp
from jax import lax
from jax.experimental import pallas as pl
from jax.experimental.pallas import tpu as pltpu
from jax.sharding import PartitionSpec as P

HD = 64
QB = 256
NEG = -1e30
EPSILON = 1e-05
BRANCH_SCALE = 48.0 ** (-0.5)
SMALL = 128
VECS = 16
ROWS = 256
HIDDEN = 512
bf = jnp.bfloat16
f32 = jnp.float32
NT = (((1,), (1,)), ((), ()))
TN = (((0,), (0,)), ((), ()))
BOTH = ("dp", "tensor")
MESH_ID = pl.DeviceIdType.MESH
ANY = pl.BlockSpec(memory_space=pl.ANY)
VM = pl.BlockSpec(memory_space=pltpu.VMEM)
SM = pl.BlockSpec(memory_space=pltpu.SMEM)


def attn_info(seg, core):
    n=seg.shape[0]; nb=n//QB
    docs=jnp.arange(16,dtype=jnp.int32)
    first=jnp.sum((seg[None,:]<docs[:,None]).astype(jnp.int32),axis=1)
    starts=jnp.sum(jnp.where(seg[None,:]==docs[:,None],first[:,None],0),axis=0)
    blocks=starts.reshape(nb,QB)
    idx=jnp.arange(nb,dtype=jnp.int32)
    low=blocks[:,0]//QB
    mid=jnp.clip((blocks[:,QB-1]+QB-1)//QB,low,idx)
    return starts.reshape(1,n), jnp.concatenate([jnp.reshape(core,(1,)),low,mid]).astype(jnp.int32)

def attn_masks(kat, srow, diagonal):
    keys = lax.broadcasted_iota(jnp.int32, (QB, QB), 0)
    mask = keys >= (srow - kat)
    if diagonal:
        mask = mask & (keys <= lax.broadcasted_iota(jnp.int32, (QB, QB), 1))
    return mask


def head_lanes(values):
    low = (lax.broadcasted_iota(jnp.int32, (1, values.shape[1]), 1) % 128) < HD
    zero = jnp.zeros((), bf)
    return jnp.where(low, values, zero), jnp.where(low, zero, values)


def fwd_kernel(info, own, recv, st_ref, okeep, osend, lse_ref, qm, ks, vt, osc, acc):
    half, cols = own.shape[0], own.shape[1] // 3
    n, nb, heads, pairs = 2 * half, 2 * half // QB, cols // HD, cols // 128
    c = info[0]
    for base, src in ((c * half, own), ((1 - c) * half, recv)):
        rows = pl.ds(pl.multiple_of(base, half), half)
        for g in range(pairs):
            lanes = slice(g * 128, (g + 1) * 128)
            part = lambda k: src[:, (3 * g + k) * 128 : (3 * g + k + 1) * 128]
            qm[0, rows, lanes], qm[1, rows, lanes] = head_lanes(part(0) * bf(HD**-0.5))
            ks[rows, lanes] = part(1)
            vt[lanes, rows] = part(2).T

    def qblock(i, _):
        at = pl.multiple_of(i * QB, QB)
        qr = pl.ds(at, QB)
        srow = st_ref[:, qr]
        acc[...] = jnp.zeros_like(acc)

        def step(mode, j, carry):
            kat = pl.multiple_of(j * QB, QB)
            kr = pl.ds(kat, QB)
            if mode:
                mask = attn_masks(kat, srow, mode == 2)
            scores, mixed = [], []
            for h in range(heads):
                lanes = slice(h // 2 * 128, h // 2 * 128 + 128)
                one = lax.dot_general(ks[kr, lanes], qm[h % 2, qr, lanes], NT, preferred_element_type=f32)
                scores.append(jnp.where(mask, one, NEG) if mode else one)
            for h in range(heads):
                top, total = carry[h]
                new = jnp.maximum(top, jnp.max(scores[h], axis=0, keepdims=True))
                weights = jnp.exp(scores[h] - new)
                fade = jnp.exp(top - new)
                total = fade * total + jnp.sum(weights, axis=0, keepdims=True)
                mixed.append((new, total, fade, weights.astype(bf)))
            for h in range(heads):
                sub = slice(h * HD, (h + 1) * HD)
                acc[sub] = mixed[h][2] * acc[sub] + jnp.dot(vt[sub, kr], mixed[h][3], preferred_element_type=f32)
            return tuple(m[:2] for m in mixed)

        carry = step(2, i, ((jnp.full((1, QB), NEG, f32), jnp.zeros((1, QB), f32)),) * heads)
        carry = lax.fori_loop(info[1 + i], info[1 + nb + i], functools.partial(step, 1), carry)
        carry = lax.fori_loop(info[1 + nb + i], i, functools.partial(step, 0), carry)
        for h, (top, total) in enumerate(carry):
            sub = slice(h * HD, (h + 1) * HD)
            acc[sub] = acc[sub] / total
            lse_ref[h : h + 1, qr] = top + jnp.log(total)
        osc[qr] = acc[...].T.astype(bf)
        return 0

    lax.fori_loop(0, nb, qblock, 0)
    okeep[...] = osc[pl.ds(pl.multiple_of(c * half, half), half)]
    osend[...] = osc[pl.ds(pl.multiple_of((1 - c) * half, half), half)]


def attn_fwd(own, recv, starts, info):
    half, cols = own.shape[0], own.shape[1] // 3
    n = 2 * half
    return pl.pallas_call(
        fwd_kernel,
        in_specs=[SM, VM, VM, VM],
        out_specs=[VM] * 3,
        scratch_shapes=[
            pltpu.VMEM((2, n, cols), bf), pltpu.VMEM((n, cols), bf), pltpu.VMEM((cols, n), bf),
            pltpu.VMEM((n, cols), bf), pltpu.VMEM((cols, QB), f32)],
        out_shape=[jax.ShapeDtypeStruct((half, cols), bf)] * 2 + [jax.ShapeDtypeStruct((cols // HD, n), f32)],
        cost_estimate=pl.CostEstimate(flops=n * n, bytes_accessed=n * 128, transcendentals=0),
        compiler_params=pltpu.CompilerParams(vmem_limit_bytes=48 << 20),
    )(info, own, recv, starts)


def bwd_kernel(info, own, recv, doo, dor, oo, orr, st_ref, lse_ref, dkeep, dsend, qm, ks, vs, kt, dom, dlt, dqs, dks, dvs):
    half, cols = own.shape[0], own.shape[1] // 3
    n, nb, heads, pairs = 2 * half, 2 * half // QB, cols // HD, cols // 128
    c = info[0]
    lanes_of = lambda g: slice(g * 128, (g + 1) * 128)
    for base, src, do, o in ((c * half, own, doo, oo), ((1 - c) * half, recv, dor, orr)):
        rows = pl.ds(pl.multiple_of(base, half), half)
        for g in range(pairs):
            lanes = lanes_of(g)
            part = lambda k: src[:, (3 * g + k) * 128 : (3 * g + k + 1) * 128]
            qm[0, rows, lanes], qm[1, rows, lanes] = head_lanes(part(0) * bf(HD**-0.5))
            ks[rows, lanes] = part(1)
            vs[rows, lanes] = part(2)
            kt[lanes, rows] = part(1).T
            grad = do[:, lanes]
            dom[0, rows, lanes], dom[1, rows, lanes] = head_lanes(grad)
            prod = (grad.astype(f32) * o[:, lanes].astype(f32)).T
            for e in range(2):
                dlt[2 * g + e : 2 * g + e + 1, rows] = jnp.sum(prod[e * HD : (e + 1) * HD], axis=0, keepdims=True)
    dks[...] = jnp.zeros_like(dks)
    dvs[...] = jnp.zeros_like(dvs)

    def qblock(i, _):
        at = pl.multiple_of(i * QB, QB)
        qr = pl.ds(at, QB)
        srow = st_ref[:, qr]
        dqs[...] = jnp.zeros_like(dqs)

        def step(mode, j, carry):
            kat = pl.multiple_of(j * QB, QB)
            kr = pl.ds(kat, QB)
            if mode:
                mask = attn_masks(kat, srow, mode == 2)
            scores, softs, grads = [], [], []
            for h in range(heads):
                lanes = lanes_of(h // 2)
                one = lax.dot_general(ks[kr, lanes], qm[h % 2, qr, lanes], NT, preferred_element_type=f32)
                back = lax.dot_general(vs[kr, lanes], dom[h % 2, qr, lanes], NT, preferred_element_type=f32)
                scores.append((jnp.where(mask, one, NEG) if mode else one, back))
            for h in range(heads):
                soft = jnp.exp(scores[h][0] - lse_ref[h : h + 1, qr])
                grads.append((soft * (scores[h][1] - dlt[h : h + 1, qr])).astype(bf))
                softs.append(soft.astype(bf))
            for g in range(pairs):
                lanes = lanes_of(g)
                both = lambda ref: jnp.concatenate([ref[0, qr, lanes], ref[1, qr, lanes]], axis=0)
                two = slice(2 * g, 2 * g + 2)
                dvs[kr, lanes] += jnp.dot(jnp.concatenate(softs[two], axis=1), both(dom), preferred_element_type=f32)
                dks[kr, lanes] += jnp.dot(jnp.concatenate(grads[two], axis=1), both(qm), preferred_element_type=f32)
                for h in (2 * g, 2 * g + 1):
                    sub = slice(h * HD, (h + 1) * HD)
                    dqs[sub] += jnp.dot(kt[sub, kr], grads[h], preferred_element_type=f32)
            return carry

        step(2, i, 0)
        lax.fori_loop(info[1 + i], info[1 + nb + i], functools.partial(step, 1), 0)
        lax.fori_loop(info[1 + nb + i], i, functools.partial(step, 0), 0)
        qm[0, qr] = (dqs[...] * (HD**-0.5)).T.astype(bf)
        return 0

    lax.fori_loop(0, nb, qblock, 0)
    for dst, base in ((dkeep, c * half), (dsend, (1 - c) * half)):
        rows = pl.ds(pl.multiple_of(base, half), half)
        for g in range(pairs):
            for k, value in enumerate((qm[0, rows, lanes_of(g)], dks[rows, lanes_of(g)], dvs[rows, lanes_of(g)])):
                dst[:, (3 * g + k) * 128 : (3 * g + k + 1) * 128] = value.astype(bf)


def attn_bwd(own, recv, do_own, do_recv, o_own, o_recv, starts, lse, info):
    half, cols = own.shape[0], own.shape[1] // 3
    n = 2 * half
    return pl.pallas_call(
        bwd_kernel,
        in_specs=[SM] + [VM] * 8,
        out_specs=[VM] * 2,
        scratch_shapes=[
            pltpu.VMEM((2, n, cols), bf), pltpu.VMEM((n, cols), bf), pltpu.VMEM((n, cols), bf), pltpu.VMEM((cols, n), bf),
            pltpu.VMEM((2, n, cols), bf), pltpu.VMEM((cols // HD, n), f32), pltpu.VMEM((cols, QB), f32),
            pltpu.VMEM((n, cols), f32), pltpu.VMEM((n, cols), f32)],
        out_shape=[like((half, 3 * cols), bf)] * 2,
        cost_estimate=pl.CostEstimate(flops=n * n, bytes_accessed=n * 128, transcendentals=0),
        compiler_params=pltpu.CompilerParams(vmem_limit_bytes=56 << 20),
    )(info, own, recv, do_own, do_recv, o_own, o_recv, starts, lse)


def dot(left, right, dims=(((1,), (0,)), ((), ()))):
    return lax.dot_general(left, right, dims, preferred_element_type=f32)


def exchange(value, bit, dp_size):
    if bit:
        return lax.ppermute(value, "dp", [(i, i ^ bit) for i in range(dp_size)])
    return lax.ppermute(value, "tensor", [(0, 1), (1, 0)])


def flip(index, bits):
    for bit in bits:
        index = index + bit * (1 - 2 * ((index // bit) % 2))
    return index

def far_groups(dp_size):
    far = [1 << k for k in range(dp_size.bit_length() - 2, 1, -1)]
    return [tuple(far[k : k + 2]) for k in range(0, len(far), 2)]

def group_moves(group):
    if len(group) == 1:
        return [(1, group)]
    return [(1, group[:1]), (2, group[1:]), (3, group)]

def chunks_of(cols, which, count, until=None):
    tiles = cols // 128
    cuts = [128 * ((tiles * k) // count) for k in range(count + 1)]
    arrays = range(which, until + 1) if until else (which,)
    return tuple(
        (array, low, high - low, 128 * max(1, (high - low) * 2 // 3 // 128))
        for low, high in zip(cuts, cuts[1:]) for array in arrays)


def head_kernel(groups, chunks, tokens, *refs):
    shards, x_out, outs, (send_sem, recv_sem, local_sem) = refs[:4], refs[4], refs[5:9], refs[9:]
    dp, t = lax.axis_index("dp"), lax.axis_index("tensor")
    core = dp % 2
    away = core + t - 2 * core * t
    near = {1: (flip(dp, (1,)), t), 2: (flip(dp, (2,)), t), 0: (dp, 1 - t)}
    distant = [bits for group in groups for _, bits in group_moves(group)]
    swap = (dp - core + t, core)
    barrier = pltpu.get_barrier_semaphore()
    for device in list(near.values()) + [(flip(dp, bits), t) for bits in distant]:
        pl.semaphore_signal(barrier, inc=1, device_id=device, device_id_type=MESH_ID)

    @pl.when(away == 1)
    def _():
        pl.semaphore_signal(barrier, inc=1, device_id=swap, device_id_type=MESH_ID)

    local = [
        pltpu.make_async_copy(shards[k], outs[k].at[away, 0] if k < 2 else outs[k].at[0], local_sem.at[k]) for k in range(4)]
    for copy in local:
        copy.start()
    pl.semaphore_wait(barrier, len(near) + len(distant) + away)
    count = [0]

    def remote(src, dst, device):
        slot = count[0]
        count[0] += 1
        return pltpu.make_async_remote_copy(
            src_ref=src, dst_ref=dst, send_sem=send_sem.at[slot], recv_sem=recv_sem.at[slot],
            device_id=device, device_id_type=MESH_ID)

    def blocks(ref, index, first, held, low, size):
        return ref.at[index, pl.ds(first, held), :, pl.ds(low, size)]

    plans = []
    for which, low, size, part in chunks:
        shard, out = shards[which], outs[which]
        steps, held = [], 1
        for group in groups:
            moves = []
            for place, bits in group_moves(group):
                src = shard.at[:, pl.ds(low, size)] if held == 1 else blocks(out, away, 0, held, low, size)
                dst = out.at[away, place, :, pl.ds(low, size)] if held == 1 else blocks(out, away, place * held, held, low, size)
                moves.append(remote(src, dst, (flip(dp, bits), t)))
            held *= len(group_moves(group)) + 1
            steps.append(moves)
        a, b = (low, part), (low + part, size - part)
        steps.append([
            remote(blocks(out, away, 0, held, *a), blocks(out, away, 0, held, *a), near[0]),
            remote(blocks(out, away, 0, held, *b), blocks(out, away, held, held, *b), near[2]),
        ])
        steps.append(
            [remote(blocks(out, k, 0, held, *a), blocks(out, k, held, held, *a), near[2]) for k in range(2)]
            + [remote(blocks(out, away, 0, 2 * held, *b), blocks(out, away, 0, 2 * held, *b), near[0])])
        steps.append([
            remote(blocks(out, k, 0, 2 * held, low, size),
                   blocks(out, 1 - k, 2 * held, 2 * held, low, size), near[1]) for k in range(2)])
        plans.append(steps)
    later = []
    held = 1
    for group in groups:
        moves = []
        for place, bits in group_moves(group):
            for shard, out in zip(shards[2:], outs[2:]):
                src = shard if held == 1 else out.at[pl.ds(0, held)]
                dst = out.at[place] if held == 1 else out.at[pl.ds(place * held, held)]
                moves.append(remote(src, dst, (flip(dp, bits), t)))
        held *= len(group_moves(group)) + 1
        later.append(moves)
    depth = len(plans[0])
    swap_copy = remote(tokens, x_out, swap)
    stay_copy = pltpu.make_async_copy(tokens, x_out, local_sem.at[4])
    waited = set()

    def advance(number, phase):
        if number >= len(plans):
            return
        if phase > 0:
            for move in plans[number][phase - 1]:
                move.wait_recv()
        if phase == 1 and chunks[number][0] not in waited:
            waited.add(chunks[number][0])
            local[chunks[number][0]].wait()
        if phase < depth:
            for move in plans[number][phase]:
                move.start()

    advance(0, 0)

    @pl.when(away == 1)
    def _():
        swap_copy.start()

    @pl.when(away == 0)
    def _():
        stay_copy.start()

    far = len(groups)
    for number in range(len(plans)):
        if number == 0:
            for phase in range(1, far + 1):
                advance(0, phase)
            advance(1, 0)
        advance(number, far + 1)
        for phase in range(1, far + 1):
            advance(number + 1, phase)
        advance(number + 2, 0)
        if number == len(plans) - 2:
            for move in later[0]:
                move.start()
        advance(number, far + 2)
    for number in range(len(plans)):
        advance(number, depth)

    @pl.when(away == 1)
    def _():
        swap_copy.wait()

    @pl.when(away == 0)
    def _():
        stay_copy.wait()

    for which in sorted(set(range(4)) - waited):
        local[which].wait()
    for k, moves in enumerate(later):
        if k > 0:
            for move in moves:
                move.start()
        for move in moves:
            move.wait()
    for steps in plans:
        for moves in steps:
            for move in moves:
                move.wait_send()


def head(dp_size, tokens, shards, chunks):
    groups = far_groups(dp_size)
    partners = sum(len(group_moves(g)) for g in groups)
    slots = len(chunks) * (partners + 7) + 2 * partners + 1
    shapes = [(2, dp_size)] * 2 + [(dp_size // 4,)] * 2
    return pl.pallas_call(
        functools.partial(head_kernel, groups, chunks),
        in_specs=[VM] * 5,
        out_specs=[ANY] * 5,
        out_shape=[jax.ShapeDtypeStruct(tokens.shape, tokens.dtype)]
        + [jax.ShapeDtypeStruct(lead + s.shape, s.dtype) for lead, s in zip(shapes, shards)],
        scratch_shapes=[pltpu.SemaphoreType.DMA((slots,)), pltpu.SemaphoreType.DMA((slots,)), pltpu.SemaphoreType.DMA((5,))],
        compiler_params=pltpu.CompilerParams(collective_id=0, has_side_effects=True),
    )(tokens, *shards)


def tail_kernel(groups, tokens, own_lo, own_hi, rest_lo, rest_hi, small_lo, small_hi, x_out, total, vecs,
                part, got_core, got_near, got_last, got_far, vec, vec_core, vec_two, vec_one, vec_far, send_sem, recv_sem, local_sem):
    dp, t = lax.axis_index("dp"), lax.axis_index("tensor")
    core = dp % 2
    away = core + t - 2 * core * t
    near = {1: (flip(dp, (1,)), t), 2: (flip(dp, (2,)), t), 0: (dp, 1 - t)}
    distant = [bits for group in groups for _, bits in group_moves(group)]
    swap = (dp - core + t, core)
    barrier = pltpu.get_barrier_semaphore()
    for device in list(near.values()) + [(flip(dp, bits), t) for bits in distant]:
        pl.semaphore_signal(barrier, inc=1, device_id=device, device_id_type=MESH_ID)

    @pl.when(away == 1)
    def _():
        pl.semaphore_signal(barrier, inc=1, device_id=swap, device_id_type=MESH_ID)

    pl.semaphore_wait(barrier, len(near) + len(distant) + away)
    count = [0]

    def remote(src, dst, device):
        slot = count[0]
        count[0] += 1
        return pltpu.make_async_remote_copy(
            src_ref=src, dst_ref=dst, send_sem=send_sem.at[slot], recv_sem=recv_sem.at[slot],
            device_id=device, device_id_type=MESH_ID)

    swap_copy = remote(tokens, x_out, swap)
    stay_copy = pltpu.make_async_copy(tokens, x_out, local_sem.at[0])
    half, rows, cols = own_lo.shape
    cut = cols * 2 // 3 // 128 * 128
    a, b = pl.ds(0, cut), pl.ds(cut, cols - cut)
    quarter = half // 2
    to_core = [
        remote(rest_hi, got_core.at[0], near[1]), remote(own_hi, got_core.at[1], near[1]),
        remote(small_hi, vec_core, near[1])]
    for move in to_core:
        move.start()

    @pl.when(away == 1)
    def _():
        swap_copy.start()

    @pl.when(away == 0)
    def _():
        stay_copy.start()

    def add(*terms):
        out = terms[0].astype(f32)
        for term in terms[1:]:
            out = out + term.astype(f32)
        return out.astype(bf)

    for move in to_core:
        move.wait_recv()

    def sum_core(k, _):
        part[0, k] = add(own_lo[k], got_core[0, k])
        part[1, k] = add(rest_lo[k], got_core[1, k])
        vec[k] = add(small_lo[k], vec_core[k])
        return 0

    lax.fori_loop(0, half, sum_core, 0)
    upper, lower = pl.ds(quarter, quarter), pl.ds(0, quarter)
    mine, other = away, 1 - away
    to_near = [
        remote(part.at[0, upper, :, a], got_near.at[0, lower, :, a], near[2]),
        remote(part.at[1, upper, :, a], got_near.at[1, lower, :, a], near[2]),
        remote(part.at[other, :, :, b], got_near.at[0, :, :, b], near[0]),
        remote(vec.at[upper], vec_two, near[2])]
    for move in to_near:
        move.start()
    for move in to_near:
        move.wait_recv()

    def sum_near(k, _):
        for g in range(2):
            part[g, k, :, a] = add(part[g, k, :, a], got_near[g, k, :, a])
        for q in (k, k + quarter):
            part[mine, q, :, b] = add(part[mine, q, :, b], got_near[0, q, :, b])
        vec[k] = add(vec[k], vec_two[k])
        return 0

    lax.fori_loop(0, quarter, sum_near, 0)
    to_last = [
        remote(part.at[other, lower, :, a], got_last.at[:, :, a], near[0]),
        remote(part.at[mine, upper, :, b], got_last.at[:, :, b], near[2]),
        remote(vec.at[lower], vec_one, near[0])]
    for move in to_last:
        move.start()
    for move in to_last:
        move.wait_recv()

    def sum_last(k, _):
        part[mine, k] = add(part[mine, k], got_last[k])
        vec_one[k] = add(vec[k], vec_one[k])
        return 0

    lax.fori_loop(0, quarter, sum_last, 0)
    to_far = []
    held, used = quarter, 0
    for group in reversed(groups):
        moves = group_moves(group)
        held //= len(moves) + 1
        step = []
        for place, bits in moves:
            device = (flip(dp, bits), t)
            step.append(remote(part.at[mine, pl.ds(place * held, held)], got_far.at[pl.ds(used, held)], device))
            step.append(remote(vec_one.at[pl.ds(place * held, held)], vec_far.at[pl.ds(used, held)], device))
            used += held
        for move in step:
            move.start()
        for move in step:
            move.wait_recv()
        base = used - held * len(moves)

        def sum_far(k, _, base=base, held=held, count=len(moves)):
            part[mine, k] = add(part[mine, k], *[got_far[base + m * held + k] for m in range(count)])
            vec_one[k] = add(vec_one[k], *[vec_far[base + m * held + k] for m in range(count)])
            return 0

        lax.fori_loop(0, held, sum_far, 0)
        to_far += step
    total[...] = part[mine, 0].astype(f32)
    vecs[...] = vec_one[0].astype(f32)

    @pl.when(away == 1)
    def _():
        swap_copy.wait()

    @pl.when(away == 0)
    def _():
        stay_copy.wait()

    for move in to_core + to_near + to_last + to_far:
        move.wait_send()


def tail(dp_size, tokens, own, rest, small):
    groups = far_groups(dp_size)
    half, rows, cols = own[0].shape
    quarter = half // 2
    wide = small[0].shape[2]
    partners = sum(len(group_moves(g)) for g in groups)
    slots = 11 + 2 * partners
    return pl.pallas_call(
        functools.partial(tail_kernel, groups),
        in_specs=[VM] * 7,
        out_specs=[ANY, VM, VM],
        out_shape=[
            jax.ShapeDtypeStruct(tokens.shape, bf), jax.ShapeDtypeStruct((rows, cols), f32),
            jax.ShapeDtypeStruct((rows, wide), f32)],
        scratch_shapes=[
            pltpu.VMEM((2, half, rows, cols), bf), pltpu.VMEM((2, half, rows, cols), bf), pltpu.VMEM((2, half, rows, cols), bf),
            pltpu.VMEM((quarter, rows, cols), bf), pltpu.VMEM((quarter, rows, cols), bf),
            pltpu.VMEM((half, rows, wide), bf), pltpu.VMEM((half, rows, wide), bf), pltpu.VMEM((quarter, rows, wide), bf),
            pltpu.VMEM((quarter, rows, wide), bf), pltpu.VMEM((quarter, rows, wide), bf),
            pltpu.SemaphoreType.DMA((slots,)), pltpu.SemaphoreType.DMA((slots,)), pltpu.SemaphoreType.DMA((1,))],
        compiler_params=pltpu.CompilerParams(collective_id=1, has_side_effects=True, vmem_limit_bytes=48 << 20),
    )(tokens, *own, *rest, *small)


def far_exchange(value, dp_size):
    out, held = [], value.shape[0]
    (group,) = far_groups(dp_size)[-1:]
    held //= len(group_moves(group)) + 1
    for place, bits in group_moves(group):
        mask = sum(bits)
        piece = value[place * held : (place + 1) * held]
        out.append(lax.ppermute(piece, "dp", [(i, i ^ mask) for i in range(dp_size)]))
    return out


def far_sum(value, got, dp_size):
    held = got[0].shape[0]
    total = value[:held].astype(f32)
    for piece in got:
        total = total + piece.astype(f32)
    for group in far_groups(dp_size)[-2::-1]:
        total = total.astype(bf)
        held //= len(group_moves(group)) + 1
        moves = [
            lax.ppermute(total[place * held : (place + 1) * held], "dp", [(i, i ^ sum(bits)) for i in range(dp_size)])
            for place, bits in group_moves(group)]
        total = total[:held].astype(f32)
        for piece in moves:
            total = total + piece.astype(f32)
    return total


def add_low(*terms):
    out = terms[0].astype(f32)
    for term in terms[1:]:
        out = out + term.astype(f32)
    return out.astype(bf)


def order_matrix(owner, rows, width):
    place = lax.broadcasted_iota(jnp.int32, (1, width), 1)
    block = place // rows
    count = width // rows
    source = jnp.zeros_like(block)
    for k, bit in enumerate([1 << b for b in range(count.bit_length() - 2, 1, -1)] + [2, 1]):
        source = source + ((block // (1 << k)) % 2) * bit
    natural = (source ^ owner) * rows + place % rows
    return (lax.broadcasted_iota(jnp.int32, (width, width), 0) == natural).astype(f32).astype(bf)


def norm_parts(values):
    centered = values - jnp.mean(values, axis=-1, keepdims=True)
    inverse = lax.rsqrt(jnp.mean(centered * centered, axis=-1, keepdims=True) + EPSILON)
    return centered * inverse, inverse


def norm_back(hat, inverse, gain, grad):
    scaled = grad * gain
    return inverse * (
        scaled - jnp.mean(scaled, axis=-1, keepdims=True) - hat * jnp.mean(scaled * hat, axis=-1, keepdims=True))


def over_rows(total, body):
    def step(k, _):
        body(pl.ds(pl.multiple_of(k * ROWS, ROWS), ROWS))
        return 0

    lax.fori_loop(0, total // ROWS, step, 0)


def column_sum(ref, row, values):
    ref[row : row + 1] += jnp.sum(values, axis=0, keepdims=True)


def bias_row(vec_nat, group, cols):
    lanes = pl.ds(pl.multiple_of(group * cols, 128), cols)
    q, v = vec_nat[2:3, lanes], vec_nat[3:4, lanes]
    parts = []
    for g in range(cols // 128):
        part = slice(g * 128, (g + 1) * 128)
        parts += [q[:, part], jnp.zeros((1, 128), f32), v[:, part]]
    return jnp.concatenate(parts, axis=1)


def first_kernel(rows, info, tokens, pack, weight, x_out, n1_out, send, vec_rel, vec_nat, order):
    width, cols = tokens.shape[1], weight.shape[2] // 3
    order[...] = order_matrix(info[1], rows, width)
    small = pack[0, :, cols:].astype(f32).T[:VECS]
    vec_rel[...] = small
    vec_nat[...] = lax.dot_general(small.astype(bf), order[...], NT, preferred_element_type=f32)
    bias = bias_row(vec_nat, 1 - info[0], cols)

    def body(at):
        x = jnp.dot(tokens[at], order[...], preferred_element_type=f32)
        hat, _ = norm_parts(x)
        n1 = (hat * vec_rel[0:1] + vec_rel[1:2]).astype(bf)
        x_out[at] = x.astype(bf)
        n1_out[at] = n1
        send[at] = (jnp.dot(n1, weight[0], preferred_element_type=f32) + bias).astype(bf)

    over_rows(tokens.shape[0], body)


def own_kernel(info, n1, weight, vec_nat, out):
    bias = bias_row(vec_nat, info[0], weight.shape[2] // 3)

    def body(at):
        out[at] = (jnp.dot(n1[at], weight[0], preferred_element_type=f32) + bias).astype(bf)

    over_rows(n1.shape[0], body)


def picked(array, index):
    return pl.BlockSpec((1,) + array.shape[1:], lambda k, s: (index, 0, 0))


def whole(array):
    return pl.BlockSpec(array.shape, lambda k, s: (0,) * len(array.shape))


def one_call(kernel, info, inputs, specs, outs, scratch=(), limit=56):
    return pl.pallas_call(
        kernel,
        grid_spec=pltpu.PrefetchScalarGridSpec(
            num_scalar_prefetch=1, grid=(1,), in_specs=[s if s is not None else whole(a) for a, s in zip(inputs, specs)],
            out_specs=[whole(o) for o in outs], scratch_shapes=list(scratch)),
        out_shape=outs,
        cost_estimate=pl.CostEstimate(flops=1 << 22, bytes_accessed=1 << 18, transcendentals=0),
        compiler_params=pltpu.CompilerParams(vmem_limit_bytes=limit << 20),
    )(info, *inputs)


def like(shape, dtype):
    return jax.ShapeDtypeStruct(shape, dtype)


def project_first(info, rows, tokens, packs, weights):
    n, width = tokens.shape
    return one_call(
        functools.partial(first_kernel, rows), info, (tokens, packs, weights), (None, picked(packs, 0), picked(weights, 1)),
        [like((n, width), bf), like((n, width), bf), like((n, weights.shape[2]), bf), like((VECS, width), f32), like((VECS, width), f32)],
        [pltpu.VMEM((width, width), bf)])


def project_own(info, n1, weights, vec_nat):
    (out,) = one_call(
        own_kernel, info, (n1, weights, vec_nat), (None, picked(weights, 0), None), [like((n1.shape[0], weights.shape[2]), bf)])
    return out


def feed_kernel(rows, info, o_own, o_recv, packs, x, vec_rel, cot, cot_recv, bias, fc00, fc01, fc02, fc03, fc10, fc11, fc12, fc13,
                pr00, pr01, pr10, pr11, block_out, d_middle, d_attn, do_own, do_send, sums, fc_lo, fc_hi, pr_lo, pr_hi, d_bias,
                order, n2, d_mlp, n2_t, d_t, w_fc, w_pr, act, d_pre, acc, back):
    step = pl.program_id(0)
    width, cols = x.shape[1], o_own.shape[1]
    total, half = x.shape[0], width // 2

    @pl.when(step == 0)
    def _():
        order[...] = order_matrix(info[1], rows, width)
        stay = info[2] == 1
        acc[...] = jnp.zeros_like(acc)
        back[...] = jnp.zeros_like(back)

        def body(at):
            branch = lax.dot_general(o_own[at], packs[0, :, :cols], NT, preferred_element_type=f32)
            branch = branch + lax.dot_general(o_recv[at], packs[1, :, :cols], NT, preferred_element_type=f32)
            mid = x[at].astype(f32) + BRANCH_SCALE * (branch + vec_rel[4:5])
            d_middle[at] = mid
            hat, _ = norm_parts(mid)
            n2[at] = (hat * vec_rel[5:6] + vec_rel[6:7]).astype(bf)
            grad = jnp.dot(jnp.where(stay, cot[at], cot_recv[at]), order[...], preferred_element_type=f32)
            d_attn[at] = grad.astype(bf)
            d_mlp[at] = (BRANCH_SCALE * grad).astype(bf)

        over_rows(total, body)
        n2_t[...] = n2[...].T
        d_t[...] = d_mlp[...].T

    def load(target, pieces):
        at = 0
        for piece in pieces:
            target[at : at + piece.shape[0]] = piece[...]
            at += piece.shape[0]

    @pl.when(step < pl.num_programs(0) // 2)
    def _():
        load(w_fc, (fc00, fc01, fc02, fc03))
        load(w_pr, (pr00, pr01))

    @pl.when(step >= pl.num_programs(0) // 2)
    def _():
        load(w_fc, (fc10, fc11, fc12, fc13))
        load(w_pr, (pr10, pr11))

    root = 0.7978845608
    count = total // ROWS
    raw = {}
    grad_sum = jnp.zeros((1, w_fc.shape[1]), f32)

    def products(k):
        at = slice(k * ROWS, (k + 1) * ROWS)
        return (
            jnp.dot(n2[at], w_fc[...], preferred_element_type=f32) + bias[0],
            jnp.dot(d_mlp[at], w_pr[...], preferred_element_type=f32))

    raw[0] = products(0)
    for k in range(count):
        at = slice(k * ROWS, (k + 1) * ROWS)
        if k + 1 < count:
            raw[k + 1] = products(k + 1)
        pre, d_act = raw.pop(k)
        square = pre * pre
        inner = jnp.tanh(pre * (root + root * 0.044715 * square))
        gate = 0.5 + 0.5 * inner
        act[at] = (pre * gate).astype(bf)
        slope = gate + pre * (0.5 - 0.5 * inner * inner) * (root + root * 3 * 0.044715 * square)
        grad = d_act * slope
        grad_sum = grad_sum + jnp.sum(grad, axis=0, keepdims=True)
        d_pre[at] = grad.astype(bf)
        if k > 0:
            add_back(k - 1, acc, back, act, d_pre, w_pr, w_fc)
    add_back(count - 1, acc, back, act, d_pre, w_pr, w_fc)
    d_bias[0] = grad_sum
    for out, left, right, low in (
        (fc_hi, n2_t, d_pre, half), (pr_hi, d_t, act, half), (fc_lo, n2_t, d_pre, 0), (pr_lo, d_t, act, 0)):
        out[0] = jnp.dot(left[low : low + half], right[...], preferred_element_type=f32).astype(bf)

    @pl.when(step == pl.num_programs(0) - 1)
    def _():
        sums[...] = jnp.zeros_like(sums)

        def body(at):
            mid = d_middle[at]
            out = (mid + BRANCH_SCALE * (acc[at] + vec_rel[7:8])).astype(bf)
            block_out[at] = lax.dot_general(out, order[...], NT, preferred_element_type=f32).astype(bf)
            hat, inverse = norm_parts(mid)
            grad = back[at]
            out_grad = d_attn[at].astype(f32)
            entire = out_grad + norm_back(hat, inverse, vec_rel[5:6], grad)
            d_middle[at] = entire
            low = (BRANCH_SCALE * entire).astype(bf)
            d_attn[at] = low
            do_own[at] = jnp.dot(low, packs[0, :, :cols], preferred_element_type=f32).astype(bf)
            do_send[at] = jnp.dot(low, packs[1, :, :cols], preferred_element_type=f32).astype(bf)
            column_sum(sums, 0, BRANCH_SCALE * entire)
            column_sum(sums, 1, grad * hat)
            column_sum(sums, 2, grad)
            column_sum(sums, 3, BRANCH_SCALE * out_grad)

        over_rows(total, body)


def add_back(k, acc, back, act, d_pre, w_pr, w_fc):
    at = slice(k * ROWS, (k + 1) * ROWS)
    acc[at] += lax.dot_general(act[at], w_pr[...], NT, preferred_element_type=f32)
    back[at] += lax.dot_general(d_pre[at], w_fc[...], NT, preferred_element_type=f32)


def feed_part(info, rows, o_own, o_recv, packs, x, vec_rel, cot, cot_recv, bias, fc_parts, proj_parts):
    (total, width), cols = x.shape, o_own.shape[1]
    hidden, half = bias.shape[2], width // 2
    steps = hidden // HIDDEN
    fixed = lambda a: pl.BlockSpec(a.shape, lambda k, s: (0,) * len(a.shape), pipeline_mode=pl.Buffered(1))
    early = lambda a: pl.BlockSpec((a.shape[0], HIDDEN), lambda k, s: (0, jnp.minimum(k, steps - 1)))
    late = lambda a: pl.BlockSpec((a.shape[0], HIDDEN), lambda k, s: (0, jnp.maximum(k - steps, 0)))
    two = lambda a: pl.BlockSpec((1, a.shape[1], HIDDEN), lambda k, s: (k // steps, 0, k % steps))
    firsts = (o_own, o_recv, packs, x, vec_rel, cot, cot_recv)
    grad = like((2, half, hidden), bf)
    slim = like((total, cols), bf)
    plain = [like((total, width), bf), like((total, width), f32), like((total, width), bf), slim, slim, like((8, width), f32)]
    outs = plain + [grad] * 4 + [like((2, 1, hidden), f32)]
    return pl.pallas_call(
        functools.partial(feed_kernel, rows),
        grid_spec=pltpu.PrefetchScalarGridSpec(
            num_scalar_prefetch=1,
            grid=(2 * steps,),
            in_specs=[fixed(a) for a in firsts] + [two(bias)]
            + [early(a) for a in fc_parts[0]] + [late(a) for a in fc_parts[1]]
            + [early(a) for a in proj_parts[0]] + [late(a) for a in proj_parts[1]],
            out_specs=[fixed(o) for o in plain] + [two(o) for o in outs[len(plain) :]],
            scratch_shapes=[
                pltpu.VMEM((width, width), bf), pltpu.VMEM((total, width), bf), pltpu.VMEM((total, width), bf),
                pltpu.VMEM((width, total), bf), pltpu.VMEM((width, total), bf), pltpu.VMEM((width, HIDDEN), bf),
                pltpu.VMEM((width, HIDDEN), bf), pltpu.VMEM((total, HIDDEN), bf), pltpu.VMEM((total, HIDDEN), bf),
                pltpu.VMEM((total, width), f32), pltpu.VMEM((total, width), f32)],
        ),
        out_shape=outs,
        cost_estimate=pl.CostEstimate(flops=1 << 22, bytes_accessed=1 << 18, transcendentals=0),
        compiler_params=pltpu.CompilerParams(vmem_limit_bytes=60 << 20),
    )(info, *firsts, bias, *fc_parts[0], *fc_parts[1], *proj_parts[0], *proj_parts[1])


def grads_into(lo, hi, left_t, extra_t, d_qkv, o):
    half = left_t.shape[0] // 2
    wide = d_qkv.shape[1]
    for out, low in ((hi, half), (lo, 0)):
        out[:, :wide] = jnp.dot(left_t[low : low + half], d_qkv[...], preferred_element_type=f32).astype(bf)
        out[:, wide:] = jnp.dot(extra_t[low : low + half], o[...], preferred_element_type=f32).astype(bf)


def last_own_kernel(info, d_qkv, n1, d_attn, o_own, weight, lo, hi, part, sums, left_t, extra_t):
    left_t[...] = n1[...].T
    extra_t[...] = d_attn[...].T
    sums[...] = jnp.zeros_like(sums)
    grads_into(lo, hi, left_t, extra_t, d_qkv, o_own)

    def body(at):
        part[at] = lax.dot_general(d_qkv[at], weight[0], NT, preferred_element_type=f32)
        column_sum(sums, 0, d_qkv[at].astype(f32))

    over_rows(n1.shape[0], body)


def last_own(info, dq, n1, d_attn, o_own, weights):
    n, width = n1.shape
    wide, slim = weights.shape[2], o_own.shape[1]
    grad = like((width // 2, wide + slim), bf)
    return one_call(
        last_own_kernel, info, (dq, n1, d_attn, o_own, weights), (None,) * 4 + (picked(weights, 0),),
        [grad, grad, like((n, width), f32), like((8, wide), f32)],
        [pltpu.VMEM((width, n), bf), pltpu.VMEM((width, n), bf)])


def last_kernel(rows, info, d_qkv, n1, d_attn, o_recv, weight, part, x, d_middle, vec_rel, own_sums, mid_sums, fc_rows,
                lo, hi, grad_out, small, left_t, extra_t, sums, vecs, nat, order):
    width, cols = x.shape[1], o_recv.shape[1]
    order[...] = order_matrix(info[1], rows, width)
    left_t[...] = n1[...].T
    extra_t[...] = d_attn[...].T
    sums[...] = jnp.zeros_like(sums)
    vecs[...] = jnp.zeros_like(vecs)
    grads_into(lo, hi, left_t, extra_t, d_qkv, o_recv)

    def body(at):
        grad = part[at] + lax.dot_general(d_qkv[at], weight[0], NT, preferred_element_type=f32)
        hat, inverse = norm_parts(x[at].astype(f32))
        grad_out[at] = (d_middle[at] + norm_back(hat, inverse, vec_rel[0:1], grad)).astype(bf)
        column_sum(sums, 0, d_qkv[at].astype(f32))
        column_sum(vecs, 0, grad * hat)
        column_sum(vecs, 1, grad)

    over_rows(x.shape[0], body)
    nat[...] = jnp.zeros_like(nat)
    for group, ref in ((info[0], own_sums), (1 - info[0], sums)):
        for row, part_index in ((0, 0), (1, 2)):
            picks = [ref[0:1, (3 * g + part_index) * 128 : (3 * g + part_index + 1) * 128] for g in range(cols // 128)]
            nat[row : row + 1, pl.ds(pl.multiple_of(group * cols, 128), cols)] = jnp.concatenate(picks, axis=1)
    fan = fc_rows.shape[0]
    nat[2 : 2 + fan] = fc_rows[...]
    moved = jnp.dot(nat[...].astype(bf), order[...], preferred_element_type=f32)
    vecs[2:4] = moved[0:2]
    vecs[4:8] = mid_sums[0:4]
    vecs[8 : 8 + fan] = moved[2 : 2 + fan]
    small[...] = vecs[...].T.astype(bf)


def last_part(info, rows, dq, n1, d_attn, o_recv, weights, part, x, d_middle, vec_rel, own_sums, mid_sums, fc_rows):
    n, width = n1.shape
    wide, slim = weights.shape[2], o_recv.shape[1]
    grad = like((width // 2, wide + slim), bf)
    inputs = (dq, n1, d_attn, o_recv, weights, part, x, d_middle, vec_rel, own_sums, mid_sums, fc_rows)
    return one_call(
        functools.partial(last_kernel, rows), info, inputs, (None,) * 4 + (picked(weights, 1),) + (None,) * 7,
        [grad, grad, like((n, width), bf), like((width, SMALL), bf)],
        [pltpu.VMEM((width, n), bf), pltpu.VMEM((width, n), bf), pltpu.VMEM((8, wide), f32),
         pltpu.VMEM((SMALL, width), f32), pltpu.VMEM((8, width), f32), pltpu.VMEM((width, width), bf)])


def on_device(
    tokens, segment_ids, ln1_gain, ln1_bias, w_qkv, b_qv, w_attn_out, b_attn_out,
    ln2_gain, ln2_bias, w_fc, b_fc, w_proj, b_proj, cotangent,
):
    dp_size = lax.axis_size("dp")
    dp_pos, t_pos = lax.axis_index("dp"), lax.axis_index("tensor")
    core = dp_pos % 2
    rows = ln1_gain.shape[0]
    width = tokens.shape[1]
    cols = w_qkv.shape[2]
    hidden = w_fc.shape[1]
    fan = b_fc.shape[0] // rows
    far = [1 << k for k in range(dp_size.bit_length() - 2, 1, -1)]
    swap = []
    for d in range(dp_size):
        for t in range(2):
            if d % 2 != t:
                swap.append((2 * d + t, 2 * (d - d % 2 + t) + d % 2))
    mine = core == t_pos

    pairs = cols // 128

    def by_pair(parts):
        parts = parts.reshape(-1, 3, pairs, 128)
        return jnp.swapaxes(parts, 1, 2).reshape(-1, 3 * cols)

    def by_part(columns):
        return jnp.swapaxes(columns.reshape(-1, pairs, 3, 128), 1, 2).reshape(-1, 3, cols)

    seg_other = exchange(segment_ids, 1, dp_size)
    seg = jnp.where(mine, segment_ids, seg_other)[0]
    small = jnp.concatenate(
        [ln1_gain[:, None], ln1_bias[:, None], b_qv.T, b_attn_out[:, None], ln2_gain[:, None],
         ln2_bias[:, None], b_proj[:, None], b_fc.reshape(rows, fan)], axis=1)
    small = jnp.pad(small, ((0, 0), (0, SMALL - small.shape[1])))
    out_pack = jnp.concatenate([w_attn_out.T, small], axis=1)
    tokens, all_qkv, all_out, fc_far, proj_far = head(
        dp_size, tokens, (by_pair(w_qkv), out_pack, w_fc, w_proj.T), chunks_of(3 * cols, 0, 2) + chunks_of(cols + SMALL, 1, 1))
    all_qkv, all_out = (a.reshape(2, width, -1) for a in (all_qkv, all_out))
    fc_far, proj_far = fc_far.reshape(-1, hidden), proj_far.reshape(-1, hidden)
    fc_parts = [[fc_far], [exchange(fc_far, 0, dp_size)]]
    proj_half = exchange(proj_far, 2, dp_size)

    part = jnp.stack([core, dp_pos, jnp.where(mine, 1, 0)]).astype(jnp.int32)
    x, n1, qkv_send, vec_rel, vec_nat = project_first(part, rows, tokens, all_out, all_qkv)
    qkv_recv = exchange(qkv_send, 1, dp_size)
    fc_parts, proj_half, n1 = lax.optimization_barrier((fc_parts, proj_half, n1))
    fc_parts = [p + [exchange(p[0], 2, dp_size)] for p in fc_parts]
    proj_half = jnp.concatenate([proj_far, proj_half], axis=0)
    proj_parts = [[proj_half], [exchange(proj_half, 0, dp_size)]]
    qkv_own = project_own(part, n1, all_qkv, vec_nat)
    starts, info = attn_info(seg, core)
    o_own, o_send, lse = attn_fwd(qkv_own, qkv_recv, starts, info)
    fc_parts, proj_parts, o_own, o_send = lax.optimization_barrier((fc_parts, proj_parts, o_own, o_send))
    o_recv = exchange(o_send, 1, dp_size)
    fc_parts, proj_parts = (
        [p + [exchange(e, 1, dp_size) for e in p] for p in parts] for parts in (fc_parts, proj_parts))
    cot_recv = lax.ppermute(cotangent, BOTH, swap)
    fc_bias = vec_nat[8 : 8 + fan].T.reshape(2, 1, hidden)
    fc_bias = jnp.where(t_pos == 0, fc_bias, fc_bias[::-1])
    half = width // 2
    (block_out, d_middle, d_attn, do_own, do_send, mid_sums, fc_lo, fc_hi, pr_lo, pr_hi, d_b_fc) = feed_part(
        part, rows, o_own, o_recv, all_out, x, vec_rel, cotangent, cot_recv, fc_bias, fc_parts, proj_parts)
    do_recv = exchange(do_send, 1, dp_size)
    fc_got, pr_got = exchange(fc_hi, 1, dp_size), exchange(pr_hi, 1, dp_size)
    fc_rows = jnp.where(t_pos == 0, d_b_fc, d_b_fc[::-1]).reshape(width, fan).T

    near_size = half // 2
    fc_rest = add_low(fc_lo[1], fc_got[1])
    pr_rest = add_low(pr_lo[:, near_size:], pr_got[:, near_size:])
    last = (qkv_own, qkv_recv, do_own, do_recv, o_own, o_send)
    last, fc_rest, pr_rest = lax.optimization_barrier((last, fc_rest, pr_rest))
    fc_sent = exchange(fc_rest, 0, dp_size)
    pr_sent = exchange(pr_rest, 2, dp_size)
    dq_own, dq_send = attn_bwd(*last, starts, lse, info)
    dq_recv = exchange(dq_send, 1, dp_size)
    dq_own, fc_sent, pr_sent, block_out = lax.optimization_barrier((dq_own, fc_sent, pr_sent, block_out))
    fc_rest = add_low(fc_lo[0, near_size:], fc_got[0, near_size:], fc_sent[near_size:])
    pr_rest = add_low(pr_lo[1, :near_size], pr_got[1, :near_size], pr_sent[1])
    dq_own, fc_rest, pr_rest = lax.optimization_barrier((dq_own, fc_rest, pr_rest))
    fc_near = exchange(fc_rest, 2, dp_size)
    pr_near = exchange(pr_rest, 0, dp_size)
    own_lo, own_hi, d_n1, own_sums = last_own(part, dq_own, n1, d_attn, o_own, all_qkv)
    d_n1, fc_near, pr_near = lax.optimization_barrier((d_n1, fc_near, pr_near))
    sum_fc = add_low(fc_lo[0, :near_size], fc_got[0, :near_size], fc_sent[:near_size], fc_near)
    sum_proj = add_low(pr_lo[0, :near_size], pr_got[0, :near_size], pr_sent[0], pr_near)
    d_n1, sum_fc, sum_proj, block_out = lax.optimization_barrier((d_n1, sum_fc, sum_proj, block_out))
    block_recv = lax.ppermute(block_out, BOTH, swap)
    fc_sent = far_exchange(sum_fc, dp_size)
    proj_sent = far_exchange(sum_proj, dp_size)
    own_lo, own_hi, d_n1, own_sums = last_own(part, dq_own, n1, d_attn, o_own, all_qkv)
    rest_lo, rest_hi, grad_tokens, d_small = last_part(
        part, rows, dq_recv, n1, d_attn, o_recv, all_qkv, d_n1, x, d_middle, vec_rel, own_sums, mid_sums, fc_rows)
    blocks = lambda arr: arr.reshape(dp_size // 2, rows, -1)
    grad_tokens, sum_a, vecs = tail(
        dp_size, grad_tokens, (blocks(own_lo), blocks(own_hi)), (blocks(rest_lo), blocks(rest_hi)),
        (blocks(d_small[:half]), blocks(d_small[half:])))
    vecs, fc_sent, proj_sent, block_recv = lax.optimization_barrier((vecs, fc_sent, proj_sent, block_recv))
    block_out = jnp.where(mine, block_out, block_recv)
    owner = dp_pos - core + t_pos
    grad_tokens = dot(grad_tokens, order_matrix(owner, rows, width), NT).astype(bf)
    sum_fc, sum_proj = far_sum(sum_fc, fc_sent, dp_size), far_sum(sum_proj, proj_sent, dp_size)
    return (
        block_out,
        grad_tokens,
        vecs[:, 0],
        vecs[:, 1],
        by_part(sum_a[:, : 3 * cols]),
        vecs[:, 2:4].T,
        sum_a[:, 3 * cols :].T,
        vecs[:, 4],
        vecs[:, 5],
        vecs[:, 6],
        sum_fc.astype(f32),
        vecs[:, 8 : 8 + fan].reshape(rows * fan),
        sum_proj.astype(f32).T,
        vecs[:, 7],
    )


def solution(mesh):
    vec, tok = P("dp"), P(BOTH, None)
    in_specs = (
        tok, P("dp", None), vec, vec, P("dp", None, "tensor"), P(None, "dp"), P("tensor", "dp"),
        vec, vec, vec, P("dp", "tensor"), vec, P("tensor", "dp"), vec, tok,
    )
    out_specs = (
        tok, tok, vec, vec, P("dp", None, "tensor"), P(None, "dp"), P("tensor", "dp"),
        vec, vec, vec, P("dp", "tensor"), vec, P("tensor", "dp"), vec,
    )
    return jax.shard_map(on_device, mesh=mesh, in_specs=in_specs, out_specs=out_specs, check_vma=False)
```

```python
import functools

import jax
import jax.numpy as jnp
from jax import lax
from jax.experimental import pallas as pl
from jax.experimental.pallas import tpu as pltpu
from jax.sharding import PartitionSpec as P

HD = 64
QB = 256
NEG = -1e30
EPSILON = 1e-05
BRANCH_SCALE = 48.0 ** (-0.5)
SMALL = 128
VECS = 16
ROWS = 256
HIDDEN = 512
bf = jnp.bfloat16
f32 = jnp.float32
NT = (((1,), (1,)), ((), ()))
TN = (((0,), (0,)), ((), ()))
BOTH = ("dp", "tensor")
MESH_ID = pl.DeviceIdType.MESH
ANY = pl.BlockSpec(memory_space=pl.ANY)
VM = pl.BlockSpec(memory_space=pltpu.VMEM)
SM = pl.BlockSpec(memory_space=pltpu.SMEM)


def attn_info(seg, core):
    n=seg.shape[0]; nb=n//QB
    docs=jnp.arange(16,dtype=jnp.int32)
    first=jnp.sum((seg[None,:]<docs[:,None]).astype(jnp.int32),axis=1)
    starts=jnp.sum(jnp.where(seg[None,:]==docs[:,None],first[:,None],0),axis=0)
    blocks=starts.reshape(nb,QB)
    idx=jnp.arange(nb,dtype=jnp.int32)
    low=blocks[:,0]//QB
    mid=jnp.clip((blocks[:,QB-1]+QB-1)//QB,low,idx)
    return starts.reshape(1,n), jnp.concatenate([jnp.reshape(core,(1,)),low,mid]).astype(jnp.int32)

def attn_mask(kat, at, srow):
    keys = lax.broadcasted_iota(jnp.int32, (QB, QB), 0)
    rows = lax.broadcasted_iota(jnp.int32, (1, QB), 1) + (at - kat)
    return (keys >= srow - kat) & (keys <= rows)


def over_blocks(info, i, nb, step, carry):
    low, mid = info[1 + i], info[1 + nb + i]
    carry = lax.fori_loop(0, mid - low + 1, lambda k, c: step(True, jnp.where(k == 0, i, low + k - 1), c), carry)
    return lax.fori_loop(mid, i, functools.partial(step, False), carry)


def head_lanes(values):
    low = (lax.broadcasted_iota(jnp.int32, (1, values.shape[1]), 1) % 128) < HD
    zero = jnp.zeros((), bf)
    return jnp.where(low, values, zero), jnp.where(low, zero, values)


def fwd_kernel(info, own, recv, st_ref, okeep, osend, lse_ref, qm, ks, vt, osc, acc):
    half, cols = own.shape[0], own.shape[1] // 3
    n, nb, heads, pairs = 2 * half, 2 * half // QB, cols // HD, cols // 128
    c = info[0]
    for base, src in ((c * half, own), ((1 - c) * half, recv)):
        rows = pl.ds(pl.multiple_of(base, half), half)
        for g in range(pairs):
            lanes = slice(g * 128, (g + 1) * 128)
            part = lambda k: src[:, (3 * g + k) * 128 : (3 * g + k + 1) * 128]
            qm[0, rows, lanes], qm[1, rows, lanes] = head_lanes(part(0) * bf(HD**-0.5))
            ks[rows, lanes] = part(1)
            vt[lanes, rows] = part(2).T

    def qblock(i, _):
        at = pl.multiple_of(i * QB, QB)
        qr = pl.ds(at, QB)
        srow = st_ref[:, qr]
        acc[...] = jnp.zeros_like(acc)

        def step(masked, j, carry):
            kat = pl.multiple_of(j * QB, QB)
            kr = pl.ds(kat, QB)
            if masked:
                mask = attn_mask(kat, at, srow)
            scores, mixed = [], []
            for h in range(heads):
                lanes = slice(h // 2 * 128, h // 2 * 128 + 128)
                one = lax.dot_general(ks[kr, lanes], qm[h % 2, qr, lanes], NT, preferred_element_type=f32)
                scores.append(jnp.where(mask, one, NEG) if masked else one)
            for h in range(heads):
                top, total = carry[h]
                new = jnp.maximum(top, jnp.max(scores[h], axis=0, keepdims=True))
                weights = jnp.exp(scores[h] - new)
                fade = jnp.exp(top - new)
                total = fade * total + jnp.sum(weights, axis=0, keepdims=True)
                mixed.append((new, total, fade, weights.astype(bf)))
            for h in range(heads):
                sub = slice(h * HD, (h + 1) * HD)
                acc[sub] = mixed[h][2] * acc[sub] + jnp.dot(vt[sub, kr], mixed[h][3], preferred_element_type=f32)
            return tuple(m[:2] for m in mixed)

        carry = over_blocks(info, i, nb, step, ((jnp.full((1, QB), NEG, f32), jnp.zeros((1, QB), f32)),) * heads)
        for h, (top, total) in enumerate(carry):
            sub = slice(h * HD, (h + 1) * HD)
            acc[sub] = acc[sub] / total
            lse_ref[h : h + 1, qr] = top + jnp.log(total)
        osc[qr] = acc[...].T.astype(bf)
        return 0

    lax.fori_loop(0, nb, qblock, 0)
    okeep[...] = osc[pl.ds(pl.multiple_of(c * half, half), half)]
    osend[...] = osc[pl.ds(pl.multiple_of((1 - c) * half, half), half)]


def attn_fwd(own, recv, starts, info):
    half, cols = own.shape[0], own.shape[1] // 3
    n = 2 * half
    return pl.pallas_call(
        fwd_kernel,
        in_specs=[SM, VM, VM, VM],
        out_specs=[VM] * 3,
        scratch_shapes=[
            pltpu.VMEM((2, n, cols), bf), pltpu.VMEM((n, cols), bf), pltpu.VMEM((cols, n), bf),
            pltpu.VMEM((n, cols), bf), pltpu.VMEM((cols, QB), f32)],
        out_shape=[jax.ShapeDtypeStruct((half, cols), bf)] * 2 + [jax.ShapeDtypeStruct((cols // HD, n), f32)],
        cost_estimate=pl.CostEstimate(flops=n * n, bytes_accessed=n * 128, transcendentals=0),
        compiler_params=pltpu.CompilerParams(vmem_limit_bytes=48 << 20),
    )(info, own, recv, starts)


def bwd_kernel(info, own, recv, doo, dor, oo, orr, st_ref, lse_ref, dkeep, dsend, qm, ks, vs, kt, dom, dlt, dqs, dks, dvs):
    half, cols = own.shape[0], own.shape[1] // 3
    n, nb, heads, pairs = 2 * half, 2 * half // QB, cols // HD, cols // 128
    c = info[0]
    lanes_of = lambda g: slice(g * 128, (g + 1) * 128)
    for base, src, do, o in ((c * half, own, doo, oo), ((1 - c) * half, recv, dor, orr)):
        rows = pl.ds(pl.multiple_of(base, half), half)
        for g in range(pairs):
            lanes = lanes_of(g)
            part = lambda k: src[:, (3 * g + k) * 128 : (3 * g + k + 1) * 128]
            qm[0, rows, lanes], qm[1, rows, lanes] = head_lanes(part(0) * bf(HD**-0.5))
            ks[rows, lanes] = part(1)
            vs[rows, lanes] = part(2)
            kt[lanes, rows] = part(1).T
            grad = do[:, lanes]
            dom[0, rows, lanes], dom[1, rows, lanes] = head_lanes(grad)
            prod = (grad.astype(f32) * o[:, lanes].astype(f32)).T
            for e in range(2):
                dlt[2 * g + e : 2 * g + e + 1, rows] = jnp.sum(prod[e * HD : (e + 1) * HD], axis=0, keepdims=True)
    dks[...] = jnp.zeros_like(dks)
    dvs[...] = jnp.zeros_like(dvs)

    def qblock(i, _):
        at = pl.multiple_of(i * QB, QB)
        qr = pl.ds(at, QB)
        srow = st_ref[:, qr]
        dqs[...] = jnp.zeros_like(dqs)

        def step(masked, j, carry):
            kat = pl.multiple_of(j * QB, QB)
            kr = pl.ds(kat, QB)
            if masked:
                mask = attn_mask(kat, at, srow)
            scores, softs, grads = [], [], []
            for h in range(heads):
                lanes = lanes_of(h // 2)
                one = lax.dot_general(ks[kr, lanes], qm[h % 2, qr, lanes], NT, preferred_element_type=f32)
                back = lax.dot_general(vs[kr, lanes], dom[h % 2, qr, lanes], NT, preferred_element_type=f32)
                scores.append((jnp.where(mask, one, NEG) if masked else one, back))
            for h in range(heads):
                soft = jnp.exp(scores[h][0] - lse_ref[h : h + 1, qr])
                grads.append((soft * (scores[h][1] - dlt[h : h + 1, qr])).astype(bf))
                softs.append(soft.astype(bf))
            for g in range(pairs):
                lanes = lanes_of(g)
                both = lambda ref: jnp.concatenate([ref[0, qr, lanes], ref[1, qr, lanes]], axis=0)
                two = slice(2 * g, 2 * g + 2)
                dvs[kr, lanes] += jnp.dot(jnp.concatenate(softs[two], axis=1), both(dom), preferred_element_type=f32)
                dks[kr, lanes] += jnp.dot(jnp.concatenate(grads[two], axis=1), both(qm), preferred_element_type=f32)
                for h in (2 * g, 2 * g + 1):
                    sub = slice(h * HD, (h + 1) * HD)
                    dqs[sub] += jnp.dot(kt[sub, kr], grads[h], preferred_element_type=f32)
            return carry

        over_blocks(info, i, nb, step, 0)
        qm[0, qr] = (dqs[...] * (HD**-0.5)).T.astype(bf)
        return 0

    lax.fori_loop(0, nb, qblock, 0)
    for dst, base in ((dkeep, c * half), (dsend, (1 - c) * half)):
        rows = pl.ds(pl.multiple_of(base, half), half)
        for g in range(pairs):
            for k, value in enumerate((qm[0, rows, lanes_of(g)], dks[rows, lanes_of(g)], dvs[rows, lanes_of(g)])):
                dst[:, (3 * g + k) * 128 : (3 * g + k + 1) * 128] = value.astype(bf)


def attn_bwd(own, recv, do_own, do_recv, o_own, o_recv, starts, lse, info):
    half, cols = own.shape[0], own.shape[1] // 3
    n = 2 * half
    return pl.pallas_call(
        bwd_kernel,
        in_specs=[SM] + [VM] * 8,
        out_specs=[VM] * 2,
        scratch_shapes=[
            pltpu.VMEM((2, n, cols), bf), pltpu.VMEM((n, cols), bf), pltpu.VMEM((n, cols), bf), pltpu.VMEM((cols, n), bf),
            pltpu.VMEM((2, n, cols), bf), pltpu.VMEM((cols // HD, n), f32), pltpu.VMEM((cols, QB), f32),
            pltpu.VMEM((n, cols), f32), pltpu.VMEM((n, cols), f32)],
        out_shape=[like((half, 3 * cols), bf)] * 2,
        cost_estimate=pl.CostEstimate(flops=n * n, bytes_accessed=n * 128, transcendentals=0),
        compiler_params=pltpu.CompilerParams(vmem_limit_bytes=56 << 20),
    )(info, own, recv, do_own, do_recv, o_own, o_recv, starts, lse)


def dot(left, right, dims=(((1,), (0,)), ((), ()))):
    return lax.dot_general(left, right, dims, preferred_element_type=f32)


def exchange(value, bit, dp_size):
    if bit:
        return lax.ppermute(value, "dp", [(i, i ^ bit) for i in range(dp_size)])
    return lax.ppermute(value, "tensor", [(0, 1), (1, 0)])


def flip(index, bits):
    for bit in bits:
        index = index + bit * (1 - 2 * ((index // bit) % 2))
    return index

def far_groups(dp_size):
    far = [1 << k for k in range(dp_size.bit_length() - 2, 1, -1)]
    return [tuple(far[k : k + 2]) for k in range(0, len(far), 2)]

def group_moves(group):
    if len(group) == 1:
        return [(1, group)]
    return [(1, group[:1]), (2, group[1:]), (3, group)]

def chunks_of(cols, which, count, until=None):
    tiles = cols // 128
    cuts = [128 * ((tiles * k) // count) for k in range(count + 1)]
    arrays = range(which, until + 1) if until else (which,)
    return tuple(
        (array, low, high - low, high - low - 128)
        for low, high in zip(cuts, cuts[1:]) for array in arrays)


def head_kernel(groups, chunks, tokens, *refs):
    shards, x_out, outs, (send_sem, recv_sem, local_sem) = refs[:4], refs[4], refs[5:9], refs[9:]
    dp, t = lax.axis_index("dp"), lax.axis_index("tensor")
    core = dp % 2
    away = core + t - 2 * core * t
    near = {1: (flip(dp, (1,)), t), 2: (flip(dp, (2,)), t), 0: (dp, 1 - t)}
    distant = [bits for group in groups for _, bits in group_moves(group)]
    swap = (dp - core + t, core)
    barrier = pltpu.get_barrier_semaphore()
    for device in list(near.values()) + [(flip(dp, bits), t) for bits in distant]:
        pl.semaphore_signal(barrier, inc=1, device_id=device, device_id_type=MESH_ID)

    @pl.when(away == 1)
    def _():
        pl.semaphore_signal(barrier, inc=1, device_id=swap, device_id_type=MESH_ID)

    local = [
        pltpu.make_async_copy(shards[k], outs[k].at[away, 0] if k < 2 else outs[k].at[0], local_sem.at[k]) for k in range(4)]
    for copy in local:
        copy.start()
    pl.semaphore_wait(barrier, len(near) + len(distant) + away)
    count = [0]

    def remote(src, dst, device):
        slot = count[0]
        count[0] += 1
        return pltpu.make_async_remote_copy(
            src_ref=src, dst_ref=dst, send_sem=send_sem.at[slot], recv_sem=recv_sem.at[slot],
            device_id=device, device_id_type=MESH_ID)

    def blocks(ref, index, first, held, low, size):
        return ref.at[index, pl.ds(first, held), :, pl.ds(low, size)]

    plans = []
    for which, low, size, part in chunks:
        shard, out = shards[which], outs[which]
        steps, held = [], 1
        for group in groups:
            moves = []
            for place, bits in group_moves(group):
                src = shard.at[:, pl.ds(low, size)] if held == 1 else blocks(out, away, 0, held, low, size)
                dst = out.at[away, place, :, pl.ds(low, size)] if held == 1 else blocks(out, away, place * held, held, low, size)
                moves.append(remote(src, dst, (flip(dp, bits), t)))
            held *= len(group_moves(group)) + 1
            steps.append(moves)
        a, b = (low, part), (low + part, size - part)
        steps.append([
            remote(blocks(out, away, 0, held, *a), blocks(out, away, 0, held, *a), near[0]),
            remote(blocks(out, away, 0, held, *b), blocks(out, away, held, held, *b), near[2]),
        ])
        steps.append(
            [remote(blocks(out, k, 0, held, *a), blocks(out, k, held, held, *a), near[2]) for k in range(2)]
            + [remote(blocks(out, away, 0, 2 * held, *b), blocks(out, away, 0, 2 * held, *b), near[0])])
        steps.append([
            remote(blocks(out, k, 0, 2 * held, low, size),
                   blocks(out, 1 - k, 2 * held, 2 * held, low, size), near[1]) for k in range(2)])
        plans.append(steps)
    later = []
    held = 1
    for group in groups:
        moves = []
        for place, bits in group_moves(group):
            for shard, out in zip(shards[2:], outs[2:]):
                src = shard if held == 1 else out.at[pl.ds(0, held)]
                dst = out.at[place] if held == 1 else out.at[pl.ds(place * held, held)]
                moves.append(remote(src, dst, (flip(dp, bits), t)))
        held *= len(group_moves(group)) + 1
        later.append(moves)
    depth = len(plans[0])
    swap_copy = remote(tokens, x_out, swap)
    stay_copy = pltpu.make_async_copy(tokens, x_out, local_sem.at[4])
    waited = set()

    def advance(number, phase):
        if number >= len(plans):
            return
        if phase > 0:
            for move in plans[number][phase - 1]:
                move.wait_recv()
        if phase == 1 and chunks[number][0] not in waited:
            waited.add(chunks[number][0])
            local[chunks[number][0]].wait()
        if phase < depth:
            for move in plans[number][phase]:
                move.start()

    advance(0, 0)

    @pl.when(away == 1)
    def _():
        swap_copy.start()

    @pl.when(away == 0)
    def _():
        stay_copy.start()

    far = len(groups)
    for number in range(len(plans)):
        if number == 0:
            for phase in range(1, far + 1):
                advance(0, phase)
            advance(1, 0)
        advance(number, far + 1)
        for phase in range(1, far + 1):
            advance(number + 1, phase)
        advance(number + 2, 0)
        if number == len(plans) - 2:
            for move in later[0]:
                move.start()
        advance(number, far + 2)
    for number in range(len(plans)):
        advance(number, depth)

    @pl.when(away == 1)
    def _():
        swap_copy.wait()

    @pl.when(away == 0)
    def _():
        stay_copy.wait()

    for which in sorted(set(range(4)) - waited):
        local[which].wait()
    for k, moves in enumerate(later):
        if k > 0:
            for move in moves:
                move.start()
        for move in moves:
            move.wait()
    for steps in plans:
        for moves in steps:
            for move in moves:
                move.wait_send()


def head(dp_size, tokens, shards, chunks):
    groups = far_groups(dp_size)
    partners = sum(len(group_moves(g)) for g in groups)
    slots = len(chunks) * (partners + 7) + 2 * partners + 1
    shapes = [(2, dp_size)] * 2 + [(dp_size // 4,)] * 2
    return pl.pallas_call(
        functools.partial(head_kernel, groups, chunks),
        in_specs=[VM] * 5,
        out_specs=[ANY] * 5,
        out_shape=[jax.ShapeDtypeStruct(tokens.shape, tokens.dtype)]
        + [jax.ShapeDtypeStruct(lead + s.shape, s.dtype) for lead, s in zip(shapes, shards)],
        scratch_shapes=[pltpu.SemaphoreType.DMA((slots,)), pltpu.SemaphoreType.DMA((slots,)), pltpu.SemaphoreType.DMA((5,))],
        compiler_params=pltpu.CompilerParams(collective_id=0, has_side_effects=True),
    )(tokens, *shards)


def tail_kernel(groups, tokens, own_lo, own_hi, rest_lo, rest_hi, small_lo, small_hi, feed, x_out, total, vecs, feed_total,
                feed_part, feed_got, part, got_core, got_near, got_last, got_far, vec, vec_core, vec_two, vec_one, vec_far, send_sem, recv_sem, local_sem):
    dp, t = lax.axis_index("dp"), lax.axis_index("tensor")
    core = dp % 2
    away = core + t - 2 * core * t
    near = {1: (flip(dp, (1,)), t), 2: (flip(dp, (2,)), t), 0: (dp, 1 - t)}
    distant = [bits for group in groups for _, bits in group_moves(group)]
    swap = (dp - core + t, core)
    barrier = pltpu.get_barrier_semaphore()
    for device in list(near.values()) + [(flip(dp, bits), t) for bits in distant]:
        pl.semaphore_signal(barrier, inc=1, device_id=device, device_id_type=MESH_ID)

    @pl.when(away == 1)
    def _():
        pl.semaphore_signal(barrier, inc=1, device_id=swap, device_id_type=MESH_ID)

    pl.semaphore_wait(barrier, len(near) + len(distant) + away)
    count = [0]

    def remote(src, dst, device):
        slot = count[0]
        count[0] += 1
        return pltpu.make_async_remote_copy(
            src_ref=src, dst_ref=dst, send_sem=send_sem.at[slot], recv_sem=recv_sem.at[slot],
            device_id=device, device_id_type=MESH_ID)

    swap_copy = remote(tokens, x_out, swap)
    stay_copy = pltpu.make_async_copy(tokens, x_out, local_sem.at[0])
    half, rows, cols = own_lo.shape
    cut = cols * 2 // 3 // 128 * 128
    a, b = pl.ds(0, cut), pl.ds(cut, cols - cut)
    quarter = half // 2
    to_core = [
        remote(rest_hi, got_core.at[0], near[1]), remote(own_hi, got_core.at[1], near[1]),
        remote(small_hi, vec_core, near[1])]
    for move in to_core:
        move.start()

    @pl.when(away == 1)
    def _():
        swap_copy.start()

    @pl.when(away == 0)
    def _():
        stay_copy.start()

    feed_steps = []
    held, used = feed.shape[0], 0
    for number, group in enumerate(reversed(groups)):
        moves = group_moves(group)
        held //= len(moves) + 1
        source, step = feed if number == 0 else feed_part, []
        for place, bits in moves:
            step.append(remote(source.at[pl.ds(place * held, held)], feed_got.at[pl.ds(used, held)], (flip(dp, bits), t)))
            used += held
        feed_steps.append((step, source, held, used - held * len(moves), len(moves)))
    for move in feed_steps[0][0]:
        move.start()

    def add(*terms):
        out = terms[0].astype(f32)
        for term in terms[1:]:
            out = out + term.astype(f32)
        return out.astype(bf)

    for move in to_core:
        move.wait_recv()

    def sum_core(k, _):
        part[0, k] = add(own_lo[k], got_core[0, k])
        part[1, k] = add(rest_lo[k], got_core[1, k])
        vec[k] = add(small_lo[k], vec_core[k])
        return 0

    lax.fori_loop(0, half, sum_core, 0)
    upper, lower = pl.ds(quarter, quarter), pl.ds(0, quarter)
    mine, other = away, 1 - away
    to_near = [
        remote(part.at[0, upper, :, a], got_near.at[0, lower, :, a], near[2]),
        remote(part.at[1, upper, :, a], got_near.at[1, lower, :, a], near[2]),
        remote(part.at[other, :, :, b], got_near.at[0, :, :, b], near[0]),
        remote(vec.at[upper], vec_two, near[2])]
    for move in to_near:
        move.start()
    for move in to_near:
        move.wait_recv()

    def sum_near(k, _):
        for g in range(2):
            part[g, k, :, a] = add(part[g, k, :, a], got_near[g, k, :, a])
        for q in (k, k + quarter):
            part[mine, q, :, b] = add(part[mine, q, :, b], got_near[0, q, :, b])
        vec[k] = add(vec[k], vec_two[k])
        return 0

    lax.fori_loop(0, quarter, sum_near, 0)
    to_last = [
        remote(part.at[other, lower, :, a], got_last.at[:, :, a], near[0]),
        remote(part.at[mine, upper, :, b], got_last.at[:, :, b], near[2]),
        remote(vec.at[lower], vec_one, near[0])]
    for move in to_last:
        move.start()
    for move in to_last:
        move.wait_recv()

    def sum_last(k, _):
        part[mine, k] = add(part[mine, k], got_last[k])
        vec_one[k] = add(vec[k], vec_one[k])
        return 0

    lax.fori_loop(0, quarter, sum_last, 0)
    to_far = []
    held, used = quarter, 0
    for group in reversed(groups):
        moves = group_moves(group)
        held //= len(moves) + 1
        step = []
        for place, bits in moves:
            device = (flip(dp, bits), t)
            step.append(remote(part.at[mine, pl.ds(place * held, held)], got_far.at[pl.ds(used, held)], device))
            step.append(remote(vec_one.at[pl.ds(place * held, held)], vec_far.at[pl.ds(used, held)], device))
            used += held
        for move in step:
            move.start()
        for move in step:
            move.wait_recv()
        base = used - held * len(moves)

        def sum_far(k, _, base=base, held=held, count=len(moves)):
            part[mine, k] = add(part[mine, k], *[got_far[base + m * held + k] for m in range(count)])
            vec_one[k] = add(vec_one[k], *[vec_far[base + m * held + k] for m in range(count)])
            return 0

        lax.fori_loop(0, held, sum_far, 0)
        to_far += step
    for number, (step, source, held, base, moves) in enumerate(feed_steps):
        if number > 0:
            for move in step:
                move.start()
        for move in step:
            move.wait_recv()

        def sum_feed(k, _, source=source, held=held, base=base, moves=moves):
            feed_part[k] = add(source[k], *[feed_got[base + m * held + k] for m in range(moves)])
            return 0

        if number + 1 < len(feed_steps):
            lax.fori_loop(0, held, sum_feed, 0)
        else:
            out = source[0].astype(f32)
            for m in range(moves):
                out = out + feed_got[base + m * held].astype(f32)
            feed_total[...] = out
        to_far += step
    total[...] = part[mine, 0].astype(f32)
    vecs[...] = vec_one[0].astype(f32)

    @pl.when(away == 1)
    def _():
        swap_copy.wait()

    @pl.when(away == 0)
    def _():
        stay_copy.wait()

    for move in to_core + to_near + to_last + to_far:
        move.wait_send()


def tail(dp_size, tokens, own, rest, small, feed):
    groups = far_groups(dp_size)
    half, rows, cols = own[0].shape
    quarter = half // 2
    wide = small[0].shape[2]
    partners = sum(len(group_moves(g)) for g in groups)
    slots = 11 + 3 * partners
    return pl.pallas_call(
        functools.partial(tail_kernel, groups),
        in_specs=[VM] * 8,
        out_specs=[ANY, VM, VM, VM],
        out_shape=[
            jax.ShapeDtypeStruct(tokens.shape, bf), jax.ShapeDtypeStruct((rows, cols), f32),
            jax.ShapeDtypeStruct((rows, wide), f32), jax.ShapeDtypeStruct(feed.shape[1:], f32)],
        scratch_shapes=[
            pltpu.VMEM(feed.shape, bf), pltpu.VMEM(feed.shape, bf),
            pltpu.VMEM((2, half, rows, cols), bf), pltpu.VMEM((2, half, rows, cols), bf), pltpu.VMEM((2, half, rows, cols), bf),
            pltpu.VMEM((quarter, rows, cols), bf), pltpu.VMEM((quarter, rows, cols), bf),
            pltpu.VMEM((half, rows, wide), bf), pltpu.VMEM((half, rows, wide), bf), pltpu.VMEM((quarter, rows, wide), bf),
            pltpu.VMEM((quarter, rows, wide), bf), pltpu.VMEM((quarter, rows, wide), bf),
            pltpu.SemaphoreType.DMA((slots,)), pltpu.SemaphoreType.DMA((slots,)), pltpu.SemaphoreType.DMA((1,))],
        compiler_params=pltpu.CompilerParams(collective_id=1, has_side_effects=True, vmem_limit_bytes=48 << 20),
    )(tokens, *own, *rest, *small, feed)


def add_low(*terms):
    out = terms[0].astype(f32)
    for term in terms[1:]:
        out = out + term.astype(f32)
    return out.astype(bf)


def order_matrix(owner, rows, width):
    place = lax.broadcasted_iota(jnp.int32, (1, width), 1)
    block = place // rows
    count = width // rows
    source = jnp.zeros_like(block)
    for k, bit in enumerate([1 << b for b in range(count.bit_length() - 2, 1, -1)] + [2, 1]):
        source = source + ((block // (1 << k)) % 2) * bit
    natural = (source ^ owner) * rows + place % rows
    return (lax.broadcasted_iota(jnp.int32, (width, width), 0) == natural).astype(f32).astype(bf)


def norm_parts(values):
    centered = values - jnp.mean(values, axis=-1, keepdims=True)
    inverse = lax.rsqrt(jnp.mean(centered * centered, axis=-1, keepdims=True) + EPSILON)
    return centered * inverse, inverse


def norm_back(hat, inverse, gain, grad):
    scaled = grad * gain
    return inverse * (
        scaled - jnp.mean(scaled, axis=-1, keepdims=True) - hat * jnp.mean(scaled * hat, axis=-1, keepdims=True))


def over_rows(total, body):
    def step(k, _):
        body(pl.ds(pl.multiple_of(k * ROWS, ROWS), ROWS))
        return 0

    lax.fori_loop(0, total // ROWS, step, 0)


def column_sum(ref, row, values):
    ref[row : row + 1] += jnp.sum(values, axis=0, keepdims=True)


def bias_row(vec_nat, group, cols):
    lanes = pl.ds(pl.multiple_of(group * cols, 128), cols)
    q, v = vec_nat[2:3, lanes], vec_nat[3:4, lanes]
    parts = []
    for g in range(cols // 128):
        part = slice(g * 128, (g + 1) * 128)
        parts += [q[:, part], jnp.zeros((1, 128), f32), v[:, part]]
    return jnp.concatenate(parts, axis=1)


def first_kernel(rows, info, tokens, pack, weight, x_out, n1_out, send, vec_rel, vec_nat, order):
    width, cols = tokens.shape[1], weight.shape[2] // 3

    @pl.when(pl.program_id(0) == 0)
    def _():
        order[...] = order_matrix(info[1], rows, width)
        small = pack[0, :, cols:].astype(f32).T[:VECS]
        vec_rel[...] = small
        vec_nat[...] = lax.dot_general(small.astype(bf), order[...], NT, preferred_element_type=f32)

    x = jnp.dot(tokens[...], order[...], preferred_element_type=f32)
    hat, _ = norm_parts(x)
    n1 = (hat * vec_rel[0:1] + vec_rel[1:2]).astype(bf)
    x_out[...] = x.astype(bf)
    n1_out[...] = n1
    send[...] = (jnp.dot(n1, weight[0], preferred_element_type=f32) + bias_row(vec_nat, 1 - info[0], cols)).astype(bf)


def own_kernel(info, n1, weight, vec_nat, out):
    bias = bias_row(vec_nat, info[0], weight.shape[2] // 3)
    out[...] = (jnp.dot(n1[...], weight[0], preferred_element_type=f32) + bias).astype(bf)


def picked(array, index):
    return pl.BlockSpec((1,) + array.shape[1:], lambda k, s: (index, 0, 0))


def whole(array):
    return pl.BlockSpec(array.shape, lambda k, s: (0,) * len(array.shape))


def one_call(kernel, info, inputs, specs, outs, scratch=(), limit=56):
    return pl.pallas_call(
        kernel,
        grid_spec=pltpu.PrefetchScalarGridSpec(
            num_scalar_prefetch=1, grid=(1,), in_specs=[s if s is not None else whole(a) for a, s in zip(inputs, specs)],
            out_specs=[whole(o) for o in outs], scratch_shapes=list(scratch)),
        out_shape=outs,
        cost_estimate=pl.CostEstimate(flops=1 << 22, bytes_accessed=1 << 18, transcendentals=0),
        compiler_params=pltpu.CompilerParams(vmem_limit_bytes=limit << 20),
    )(info, *inputs)


def like(shape, dtype):
    return jax.ShapeDtypeStruct(shape, dtype)


def by_rows(kernel, info, inputs, specs, outs, scratch=(), flops=1 << 22):
    total = inputs[0].shape[0]

    def spec(array, given=None):
        if given is not None:
            return given
        if array.shape[0] == total:
            return pl.BlockSpec((ROWS,) + array.shape[1:], lambda k, s: (k, 0))
        return whole(array)

    return pl.pallas_call(
        kernel,
        grid_spec=pltpu.PrefetchScalarGridSpec(
            num_scalar_prefetch=1, grid=(total // ROWS,), in_specs=[spec(a, g) for a, g in zip(inputs, specs)],
            out_specs=[spec(o) for o in outs], scratch_shapes=list(scratch)),
        out_shape=outs,
        cost_estimate=pl.CostEstimate(flops=flops, bytes_accessed=1 << 18, transcendentals=0),
        compiler_params=pltpu.CompilerParams(vmem_limit_bytes=24 << 20),
    )(info, *inputs)


def project_first(info, rows, tokens, packs, weights):
    n, width = tokens.shape
    return by_rows(
        functools.partial(first_kernel, rows), info, (tokens, packs, weights), (None, picked(packs, 0), picked(weights, 1)),
        [like((n, width), bf), like((n, width), bf), like((n, weights.shape[2]), bf), like((VECS, width), f32), like((VECS, width), f32)],
        [pltpu.VMEM((width, width), bf)], 1 << 36)


def project_own(info, n1, weights, vec_nat):
    (out,) = by_rows(
        own_kernel, info, (n1, weights, vec_nat), (None, picked(weights, 0), None), [like((n1.shape[0], weights.shape[2]), bf)])
    return out


def feed_kernel(rows, info, o_own, o_recv, packs, x, vec_rel, cot, cot_recv, bias, fc00, fc01, fc02, fc03, fc10, fc11, fc12, fc13,
                pr00, pr01, pr10, pr11, block_out, d_middle, d_attn, do_own, do_send, sums, fc_lo, fc_hi, pr_lo, pr_hi, d_bias,
                order, n2, d_mlp, n2_t, d_t, w_fc, w_pr, act, d_pre, acc, back):
    step = pl.program_id(0)
    width, cols = x.shape[1], o_own.shape[1]
    total, half = x.shape[0], width // 2

    @pl.when(step == 0)
    def _():
        order[...] = order_matrix(info[1], rows, width)
        stay = info[2] == 1
        acc[...] = jnp.zeros_like(acc)
        back[...] = jnp.zeros_like(back)

        def body(at):
            branch = lax.dot_general(o_own[at], packs[0, :, :cols], NT, preferred_element_type=f32)
            branch = branch + lax.dot_general(o_recv[at], packs[1, :, :cols], NT, preferred_element_type=f32)
            mid = x[at].astype(f32) + BRANCH_SCALE * (branch + vec_rel[4:5])
            d_middle[at] = mid
            hat, _ = norm_parts(mid)
            n2[at] = (hat * vec_rel[5:6] + vec_rel[6:7]).astype(bf)
            grad = jnp.dot(jnp.where(stay, cot[at], cot_recv[at]), order[...], preferred_element_type=f32)
            d_attn[at] = grad.astype(bf)
            d_mlp[at] = (BRANCH_SCALE * grad).astype(bf)

        over_rows(total, body)
        n2_t[...] = n2[...].T
        d_t[...] = d_mlp[...].T

    def load(target, pieces):
        at = 0
        for piece in pieces:
            target[at : at + piece.shape[0]] = piece[...]
            at += piece.shape[0]

    @pl.when(step < pl.num_programs(0) // 2)
    def _():
        load(w_fc, (fc00, fc01, fc02, fc03))
        load(w_pr, (pr00, pr01))

    @pl.when(step >= pl.num_programs(0) // 2)
    def _():
        load(w_fc, (fc10, fc11, fc12, fc13))
        load(w_pr, (pr10, pr11))

    root = 0.7978845608
    count = total // ROWS
    raw = {}
    grad_sum = jnp.zeros((1, w_fc.shape[1]), f32)

    def products(k):
        at = slice(k * ROWS, (k + 1) * ROWS)
        return (
            jnp.dot(n2[at], w_fc[...], preferred_element_type=f32) + bias[0],
            jnp.dot(d_mlp[at], w_pr[...], preferred_element_type=f32))

    raw[0] = products(0)
    for k in range(count):
        at = slice(k * ROWS, (k + 1) * ROWS)
        if k + 1 < count:
            raw[k + 1] = products(k + 1)
        pre, d_act = raw.pop(k)
        square = pre * pre
        inner = jnp.tanh(pre * (root + root * 0.044715 * square))
        gate = 0.5 + 0.5 * inner
        act[at] = (pre * gate).astype(bf)
        slope = gate + pre * (0.5 - 0.5 * inner * inner) * (root + root * 3 * 0.044715 * square)
        grad = d_act * slope
        grad_sum = grad_sum + jnp.sum(grad, axis=0, keepdims=True)
        d_pre[at] = grad.astype(bf)
        if k > 0:
            add_back(k - 1, acc, back, act, d_pre, w_pr, w_fc)
    add_back(count - 1, acc, back, act, d_pre, w_pr, w_fc)
    d_bias[0] = grad_sum
    for out, left, right, low in (
        (fc_hi, n2_t, d_pre, half), (pr_hi, d_t, act, half), (fc_lo, n2_t, d_pre, 0), (pr_lo, d_t, act, 0)):
        out[0] = jnp.dot(left[low : low + half], right[...], preferred_element_type=f32).astype(bf)

    @pl.when(step == pl.num_programs(0) - 1)
    def _():
        sums[...] = jnp.zeros_like(sums)

        def body(at):
            mid = d_middle[at]
            out = (mid + BRANCH_SCALE * (acc[at] + vec_rel[7:8])).astype(bf)
            block_out[at] = lax.dot_general(out, order[...], NT, preferred_element_type=f32).astype(bf)
            hat, inverse = norm_parts(mid)
            grad = back[at]
            out_grad = d_attn[at].astype(f32)
            entire = out_grad + norm_back(hat, inverse, vec_rel[5:6], grad)
            d_middle[at] = entire
            low = (BRANCH_SCALE * entire).astype(bf)
            d_attn[at] = low
            do_own[at] = jnp.dot(low, packs[0, :, :cols], preferred_element_type=f32).astype(bf)
            do_send[at] = jnp.dot(low, packs[1, :, :cols], preferred_element_type=f32).astype(bf)
            column_sum(sums, 0, BRANCH_SCALE * entire)
            column_sum(sums, 1, grad * hat)
            column_sum(sums, 2, grad)
            column_sum(sums, 3, BRANCH_SCALE * out_grad)

        over_rows(total, body)


def add_back(k, acc, back, act, d_pre, w_pr, w_fc):
    at = slice(k * ROWS, (k + 1) * ROWS)
    acc[at] += lax.dot_general(act[at], w_pr[...], NT, preferred_element_type=f32)
    back[at] += lax.dot_general(d_pre[at], w_fc[...], NT, preferred_element_type=f32)


def feed_part(info, rows, o_own, o_recv, packs, x, vec_rel, cot, cot_recv, bias, fc_parts, proj_parts):
    (total, width), cols = x.shape, o_own.shape[1]
    hidden, half = bias.shape[2], width // 2
    steps = hidden // HIDDEN
    fixed = lambda a: pl.BlockSpec(a.shape, lambda k, s: (0,) * len(a.shape), pipeline_mode=pl.Buffered(1))
    early = lambda a: pl.BlockSpec((a.shape[0], HIDDEN), lambda k, s: (0, jnp.minimum(k, steps - 1)))
    late = lambda a: pl.BlockSpec((a.shape[0], HIDDEN), lambda k, s: (0, jnp.maximum(k - steps, 0)))
    two = lambda a: pl.BlockSpec((1, a.shape[1], HIDDEN), lambda k, s: (k // steps, 0, k % steps))
    firsts = (o_own, o_recv, packs, x, vec_rel, cot, cot_recv)
    grad = like((2, half, hidden), bf)
    slim = like((total, cols), bf)
    plain = [like((total, width), bf), like((total, width), f32), like((total, width), bf), slim, slim, like((8, width), f32)]
    outs = plain + [grad] * 4 + [like((2, 1, hidden), f32)]
    return pl.pallas_call(
        functools.partial(feed_kernel, rows),
        grid_spec=pltpu.PrefetchScalarGridSpec(
            num_scalar_prefetch=1,
            grid=(2 * steps,),
            in_specs=[fixed(a) for a in firsts] + [two(bias)]
            + [early(a) for a in fc_parts[0]] + [late(a) for a in fc_parts[1]]
            + [early(a) for a in proj_parts[0]] + [late(a) for a in proj_parts[1]],
            out_specs=[fixed(o) for o in plain] + [two(o) for o in outs[len(plain) :]],
            scratch_shapes=[
                pltpu.VMEM((width, width), bf), pltpu.VMEM((total, width), bf), pltpu.VMEM((total, width), bf),
                pltpu.VMEM((width, total), bf), pltpu.VMEM((width, total), bf), pltpu.VMEM((width, HIDDEN), bf),
                pltpu.VMEM((width, HIDDEN), bf), pltpu.VMEM((total, HIDDEN), bf), pltpu.VMEM((total, HIDDEN), bf),
                pltpu.VMEM((total, width), f32), pltpu.VMEM((total, width), f32)],
        ),
        out_shape=outs,
        cost_estimate=pl.CostEstimate(flops=1 << 22, bytes_accessed=1 << 18, transcendentals=0),
        compiler_params=pltpu.CompilerParams(vmem_limit_bytes=60 << 20),
    )(info, *firsts, bias, *fc_parts[0], *fc_parts[1], *proj_parts[0], *proj_parts[1])


def grads_into(lo, hi, left_t, extra_t, d_qkv, o):
    half = left_t.shape[0] // 2
    wide = d_qkv.shape[1]
    for out, low in ((hi, half), (lo, 0)):
        out[:, :wide] = jnp.dot(left_t[low : low + half], d_qkv[...], preferred_element_type=f32).astype(bf)
        out[:, wide:] = jnp.dot(extra_t[low : low + half], o[...], preferred_element_type=f32).astype(bf)


def last_own_kernel(info, d_qkv, n1, d_attn, o_own, weight, lo, hi, part, sums, left_t, extra_t):
    left_t[...] = n1[...].T
    extra_t[...] = d_attn[...].T
    sums[...] = jnp.zeros_like(sums)
    grads_into(lo, hi, left_t, extra_t, d_qkv, o_own)

    def body(at):
        part[at] = lax.dot_general(d_qkv[at], weight[0], NT, preferred_element_type=f32)
        column_sum(sums, 0, d_qkv[at].astype(f32))

    over_rows(n1.shape[0], body)


def last_own(info, dq, n1, d_attn, o_own, weights):
    n, width = n1.shape
    wide, slim = weights.shape[2], o_own.shape[1]
    grad = like((width // 2, wide + slim), bf)
    return one_call(
        last_own_kernel, info, (dq, n1, d_attn, o_own, weights), (None,) * 4 + (picked(weights, 0),),
        [grad, grad, like((n, width), f32), like((8, wide), f32)],
        [pltpu.VMEM((width, n), bf), pltpu.VMEM((width, n), bf)])


def last_kernel(rows, info, d_qkv, n1, d_attn, o_recv, weight, part, x, d_middle, vec_rel, own_sums, mid_sums, fc_rows,
                lo, hi, grad_out, small, left_t, extra_t, sums, vecs, nat, order):
    width, cols = x.shape[1], o_recv.shape[1]
    order[...] = order_matrix(info[1], rows, width)
    left_t[...] = n1[...].T
    extra_t[...] = d_attn[...].T
    sums[...] = jnp.zeros_like(sums)
    vecs[...] = jnp.zeros_like(vecs)
    grads_into(lo, hi, left_t, extra_t, d_qkv, o_recv)

    def body(at):
        grad = part[at] + lax.dot_general(d_qkv[at], weight[0], NT, preferred_element_type=f32)
        hat, inverse = norm_parts(x[at].astype(f32))
        grad_out[at] = (d_middle[at] + norm_back(hat, inverse, vec_rel[0:1], grad)).astype(bf)
        column_sum(sums, 0, d_qkv[at].astype(f32))
        column_sum(vecs, 0, grad * hat)
        column_sum(vecs, 1, grad)

    over_rows(x.shape[0], body)
    nat[...] = jnp.zeros_like(nat)
    for group, ref in ((info[0], own_sums), (1 - info[0], sums)):
        for row, part_index in ((0, 0), (1, 2)):
            picks = [ref[0:1, (3 * g + part_index) * 128 : (3 * g + part_index + 1) * 128] for g in range(cols // 128)]
            nat[row : row + 1, pl.ds(pl.multiple_of(group * cols, 128), cols)] = jnp.concatenate(picks, axis=1)
    fan = fc_rows.shape[0]
    nat[2 : 2 + fan] = fc_rows[...]
    moved = jnp.dot(nat[...].astype(bf), order[...], preferred_element_type=f32)
    vecs[2:4] = moved[0:2]
    vecs[4:8] = mid_sums[0:4]
    vecs[8 : 8 + fan] = moved[2 : 2 + fan]
    small[...] = vecs[...].T.astype(bf)


def last_part(info, rows, dq, n1, d_attn, o_recv, weights, part, x, d_middle, vec_rel, own_sums, mid_sums, fc_rows):
    n, width = n1.shape
    wide, slim = weights.shape[2], o_recv.shape[1]
    grad = like((width // 2, wide + slim), bf)
    inputs = (dq, n1, d_attn, o_recv, weights, part, x, d_middle, vec_rel, own_sums, mid_sums, fc_rows)
    return one_call(
        functools.partial(last_kernel, rows), info, inputs, (None,) * 4 + (picked(weights, 1),) + (None,) * 7,
        [grad, grad, like((n, width), bf), like((width, SMALL), bf)],
        [pltpu.VMEM((width, n), bf), pltpu.VMEM((width, n), bf), pltpu.VMEM((8, wide), f32),
         pltpu.VMEM((SMALL, width), f32), pltpu.VMEM((8, width), f32), pltpu.VMEM((width, width), bf)])


def on_device(
    tokens, segment_ids, ln1_gain, ln1_bias, w_qkv, b_qv, w_attn_out, b_attn_out,
    ln2_gain, ln2_bias, w_fc, b_fc, w_proj, b_proj, cotangent,
):
    dp_size = lax.axis_size("dp")
    dp_pos, t_pos = lax.axis_index("dp"), lax.axis_index("tensor")
    core = dp_pos % 2
    rows = ln1_gain.shape[0]
    width = tokens.shape[1]
    cols = w_qkv.shape[2]
    hidden = w_fc.shape[1]
    fan = b_fc.shape[0] // rows
    far = [1 << k for k in range(dp_size.bit_length() - 2, 1, -1)]
    swap = []
    for d in range(dp_size):
        for t in range(2):
            if d % 2 != t:
                swap.append((2 * d + t, 2 * (d - d % 2 + t) + d % 2))
    mine = core == t_pos

    pairs = cols // 128

    def by_pair(parts):
        parts = parts.reshape(-1, 3, pairs, 128)
        return jnp.swapaxes(parts, 1, 2).reshape(-1, 3 * cols)

    def by_part(columns):
        return jnp.swapaxes(columns.reshape(-1, pairs, 3, 128), 1, 2).reshape(-1, 3, cols)

    seg_other = exchange(segment_ids, 1, dp_size)
    seg = jnp.where(mine, segment_ids, seg_other)[0]
    small = jnp.concatenate(
        [ln1_gain[:, None], ln1_bias[:, None], b_qv.T, b_attn_out[:, None], ln2_gain[:, None],
         ln2_bias[:, None], b_proj[:, None], b_fc.reshape(rows, fan)], axis=1)
    small = jnp.pad(small, ((0, 0), (0, SMALL - small.shape[1])))
    out_pack = jnp.concatenate([w_attn_out.T, small], axis=1)
    tokens, all_qkv, all_out, fc_far, proj_far = head(
        dp_size, tokens, (by_pair(w_qkv), out_pack, w_fc, w_proj.T), chunks_of(3 * cols, 0, 2) + chunks_of(cols + SMALL, 1, 1))
    all_qkv, all_out = (a.reshape(2, width, -1) for a in (all_qkv, all_out))
    fc_far, proj_far = fc_far.reshape(-1, hidden), proj_far.reshape(-1, hidden)
    fc_parts = [[fc_far], [exchange(fc_far, 0, dp_size)]]
    proj_half = exchange(proj_far, 2, dp_size)

    part = jnp.stack([core, dp_pos, jnp.where(mine, 1, 0)]).astype(jnp.int32)
    x, n1, qkv_send, vec_rel, vec_nat = project_first(part, rows, tokens, all_out, all_qkv)
    qkv_recv = exchange(qkv_send, 1, dp_size)
    qkv_own = project_own(part, n1, all_qkv, vec_nat)
    fc_parts, proj_half, qkv_own = lax.optimization_barrier((fc_parts, proj_half, qkv_own))
    fc_parts = [p + [exchange(p[0], 2, dp_size)] for p in fc_parts]
    proj_half = jnp.concatenate([proj_far, proj_half], axis=0)
    proj_parts = [[proj_half], [exchange(proj_half, 0, dp_size)]]
    starts, info = attn_info(seg, core)
    o_own, o_send, lse = attn_fwd(qkv_own, qkv_recv, starts, info)
    fc_parts, proj_parts, o_own, o_send = lax.optimization_barrier((fc_parts, proj_parts, o_own, o_send))
    o_recv = exchange(o_send, 1, dp_size)
    fc_parts, proj_parts = (
        [p + [exchange(e, 1, dp_size) for e in p] for p in parts] for parts in (fc_parts, proj_parts))
    cot_recv = lax.ppermute(cotangent, BOTH, swap)
    fc_bias = vec_nat[8 : 8 + fan].T.reshape(2, 1, hidden)
    fc_bias = jnp.where(t_pos == 0, fc_bias, fc_bias[::-1])
    half = width // 2
    (block_out, d_middle, d_attn, do_own, do_send, mid_sums, fc_lo, fc_hi, pr_lo, pr_hi, d_b_fc) = feed_part(
        part, rows, o_own, o_recv, all_out, x, vec_rel, cotangent, cot_recv, fc_bias, fc_parts, proj_parts)
    do_recv = exchange(do_send, 1, dp_size)
    fc_got, pr_got = exchange(fc_hi, 1, dp_size), exchange(pr_hi, 1, dp_size)
    fc_rows = jnp.where(t_pos == 0, d_b_fc, d_b_fc[::-1]).reshape(width, fan).T

    near_size = half // 2
    fc_rest = add_low(fc_lo[1], fc_got[1])
    pr_rest = add_low(pr_lo[:, near_size:], pr_got[:, near_size:])
    last = (qkv_own, qkv_recv, do_own, do_recv, o_own, o_send)
    last, fc_rest, pr_rest = lax.optimization_barrier((last, fc_rest, pr_rest))
    fc_sent = exchange(fc_rest, 0, dp_size)
    pr_sent = exchange(pr_rest, 2, dp_size)
    block_recv = lax.ppermute(block_out, BOTH, swap)
    dq_own, dq_send = attn_bwd(*last, starts, lse, info)
    dq_recv = exchange(dq_send, 1, dp_size)
    dq_own, fc_sent, pr_sent = lax.optimization_barrier((dq_own, fc_sent, pr_sent))
    fc_rest = add_low(fc_lo[0, near_size:], fc_got[0, near_size:], fc_sent[near_size:])
    pr_rest = add_low(pr_lo[1, :near_size], pr_got[1, :near_size], pr_sent[1])
    dq_own, fc_rest, pr_rest = lax.optimization_barrier((dq_own, fc_rest, pr_rest))
    fc_near = exchange(fc_rest, 2, dp_size)
    pr_near = exchange(pr_rest, 0, dp_size)
    own_lo, own_hi, d_n1, own_sums = last_own(part, dq_own, n1, d_attn, o_own, all_qkv)
    d_n1, fc_near, pr_near = lax.optimization_barrier((d_n1, fc_near, pr_near))
    sum_fc = add_low(fc_lo[0, :near_size], fc_got[0, :near_size], fc_sent[:near_size], fc_near)
    sum_proj = add_low(pr_lo[0, :near_size], pr_got[0, :near_size], pr_sent[0], pr_near)
    feed = jnp.concatenate([sum_fc, sum_proj], axis=1).reshape(-1, rows, 2 * hidden)
    d_n1, feed = lax.optimization_barrier((d_n1, feed))
    rest_lo, rest_hi, grad_tokens, d_small = last_part(
        part, rows, dq_recv, n1, d_attn, o_recv, all_qkv, d_n1, x, d_middle, vec_rel, own_sums, mid_sums, fc_rows)
    blocks = lambda arr: arr.reshape(dp_size // 2, rows, -1)
    grad_tokens, sum_a, vecs, sum_feed = tail(
        dp_size, grad_tokens, (blocks(own_lo), blocks(own_hi)), (blocks(rest_lo), blocks(rest_hi)),
        (blocks(d_small[:half]), blocks(d_small[half:])), feed)
    vecs, block_recv = lax.optimization_barrier((vecs, block_recv))
    block_out = jnp.where(mine, block_out, block_recv)
    owner = dp_pos - core + t_pos
    grad_tokens = dot(grad_tokens, order_matrix(owner, rows, width), NT).astype(bf)
    return (
        block_out,
        grad_tokens,
        vecs[:, 0],
        vecs[:, 1],
        by_part(sum_a[:, : 3 * cols]),
        vecs[:, 2:4].T,
        sum_a[:, 3 * cols :].T,
        vecs[:, 4],
        vecs[:, 5],
        vecs[:, 6],
        sum_feed[:, :hidden],
        vecs[:, 8 : 8 + fan].reshape(rows * fan),
        sum_feed[:, hidden:].T,
        vecs[:, 7],
    )


def solution(mesh):
    vec, tok = P("dp"), P(BOTH, None)
    in_specs = (
        tok, P("dp", None), vec, vec, P("dp", None, "tensor"), P(None, "dp"), P("tensor", "dp"),
        vec, vec, vec, P("dp", "tensor"), vec, P("tensor", "dp"), vec, tok,
    )
    out_specs = (
        tok, tok, vec, vec, P("dp", None, "tensor"), P(None, "dp"), P("tensor", "dp"),
        vec, vec, vec, P("dp", "tensor"), vec, P("tensor", "dp"), vec,
    )
    return jax.shard_map(on_device, mesh=mesh, in_specs=in_specs, out_specs=out_specs, check_vma=False)
```

```python
import functools

import jax
import jax.numpy as jnp
from jax import lax
from jax.experimental import pallas as pl
from jax.experimental.pallas import tpu as pltpu
from jax.sharding import PartitionSpec as P

HD = 64
QB = 256
NEG = -1e30
EPSILON = 1e-05
BRANCH_SCALE = 48.0 ** (-0.5)
SMALL = 128
VECS = 16
ROWS = 256
HIDDEN = 512
bf = jnp.bfloat16
f32 = jnp.float32
NT = (((1,), (1,)), ((), ()))
TN = (((0,), (0,)), ((), ()))
BOTH = ("dp", "tensor")
MESH_ID = pl.DeviceIdType.MESH
ANY = pl.BlockSpec(memory_space=pl.ANY)
VM = pl.BlockSpec(memory_space=pltpu.VMEM)
SM = pl.BlockSpec(memory_space=pltpu.SMEM)


def attn_info(seg, core):
    n=seg.shape[0]; nb=n//QB
    docs=jnp.arange(16,dtype=jnp.int32)
    first=jnp.sum((seg[None,:]<docs[:,None]).astype(jnp.int32),axis=1)
    starts=jnp.sum(jnp.where(seg[None,:]==docs[:,None],first[:,None],0),axis=0)
    blocks=starts.reshape(nb,QB)
    idx=jnp.arange(nb,dtype=jnp.int32)
    low=blocks[:,0]//QB
    mid=jnp.clip((blocks[:,QB-1]+QB-1)//QB,low,idx)
    return starts.reshape(1,n), jnp.concatenate([jnp.reshape(core,(1,)),low,mid]).astype(jnp.int32)

def attn_mask(kat, at, srow):
    keys = lax.broadcasted_iota(jnp.int32, (QB, QB), 0)
    rows = lax.broadcasted_iota(jnp.int32, (1, QB), 1) + (at - kat)
    return (keys >= srow - kat) & (keys <= rows)


def over_blocks(info, i, nb, step, carry):
    low, mid = info[1 + i], info[1 + nb + i]
    carry = lax.fori_loop(0, mid - low + 1, lambda k, c: step(True, jnp.where(k == 0, i, low + k - 1), c), carry)
    return lax.fori_loop(mid, i, functools.partial(step, False), carry)


def head_lanes(values):
    low = (lax.broadcasted_iota(jnp.int32, (1, values.shape[1]), 1) % 128) < HD
    zero = jnp.zeros((), bf)
    return jnp.where(low, values, zero), jnp.where(low, zero, values)


def fwd_kernel(info, own, recv, st_ref, okeep, osend, lse_ref, qm, ks, vt, osc, acc):
    half, cols = own.shape[0], own.shape[1] // 3
    n, nb, heads, pairs = 2 * half, 2 * half // QB, cols // HD, cols // 128
    c = info[0]
    for base, src in ((c * half, own), ((1 - c) * half, recv)):
        rows = pl.ds(pl.multiple_of(base, half), half)
        for g in range(pairs):
            lanes = slice(g * 128, (g + 1) * 128)
            part = lambda k: src[:, (3 * g + k) * 128 : (3 * g + k + 1) * 128]
            qm[0, rows, lanes], qm[1, rows, lanes] = head_lanes(part(0) * bf(HD**-0.5))
            ks[rows, lanes] = part(1)
            vt[lanes, rows] = part(2).T

    def qblock(i, _):
        at = pl.multiple_of(i * QB, QB)
        qr = pl.ds(at, QB)
        srow = st_ref[:, qr]
        acc[...] = jnp.zeros_like(acc)

        def step(masked, j, carry):
            kat = pl.multiple_of(j * QB, QB)
            kr = pl.ds(kat, QB)
            if masked:
                mask = attn_mask(kat, at, srow)
            scores, mixed = [], []
            for h in range(heads):
                lanes = slice(h // 2 * 128, h // 2 * 128 + 128)
                one = lax.dot_general(ks[kr, lanes], qm[h % 2, qr, lanes], NT, preferred_element_type=f32)
                scores.append(jnp.where(mask, one, NEG) if masked else one)
            for h in range(heads):
                top, total = carry[h]
                new = jnp.maximum(top, jnp.max(scores[h], axis=0, keepdims=True))
                weights = jnp.exp(scores[h] - new)
                fade = jnp.exp(top - new)
                total = fade * total + jnp.sum(weights, axis=0, keepdims=True)
                mixed.append((new, total, fade, weights.astype(bf)))
            for h in range(heads):
                sub = slice(h * HD, (h + 1) * HD)
                acc[sub] = mixed[h][2] * acc[sub] + jnp.dot(vt[sub, kr], mixed[h][3], preferred_element_type=f32)
            return tuple(m[:2] for m in mixed)

        carry = over_blocks(info, i, nb, step, ((jnp.full((1, QB), NEG, f32), jnp.zeros((1, QB), f32)),) * heads)
        for h, (top, total) in enumerate(carry):
            sub = slice(h * HD, (h + 1) * HD)
            acc[sub] = acc[sub] / total
            lse_ref[h : h + 1, qr] = top + jnp.log(total)
        osc[qr] = acc[...].T.astype(bf)
        return 0

    lax.fori_loop(0, nb, qblock, 0)
    okeep[...] = osc[pl.ds(pl.multiple_of(c * half, half), half)]
    osend[...] = osc[pl.ds(pl.multiple_of((1 - c) * half, half), half)]


def attn_fwd(own, recv, starts, info):
    half, cols = own.shape[0], own.shape[1] // 3
    n = 2 * half
    return pl.pallas_call(
        fwd_kernel,
        in_specs=[SM, VM, VM, VM],
        out_specs=[VM] * 3,
        scratch_shapes=[
            pltpu.VMEM((2, n, cols), bf), pltpu.VMEM((n, cols), bf), pltpu.VMEM((cols, n), bf),
            pltpu.VMEM((n, cols), bf), pltpu.VMEM((cols, QB), f32)],
        out_shape=[jax.ShapeDtypeStruct((half, cols), bf)] * 2 + [jax.ShapeDtypeStruct((cols // HD, n), f32)],
        cost_estimate=pl.CostEstimate(flops=n * n, bytes_accessed=n * 128, transcendentals=0),
        compiler_params=pltpu.CompilerParams(vmem_limit_bytes=48 << 20),
    )(info, own, recv, starts)


def bwd_kernel(info, own, recv, doo, dor, oo, orr, st_ref, lse_ref, dkeep, dsend, qm, ks, vs, kt, dom, dlt, dqs, dks, dvs):
    half, cols = own.shape[0], own.shape[1] // 3
    n, nb, heads, pairs = 2 * half, 2 * half // QB, cols // HD, cols // 128
    c = info[0]
    lanes_of = lambda g: slice(g * 128, (g + 1) * 128)
    for base, src, do, o in ((c * half, own, doo, oo), ((1 - c) * half, recv, dor, orr)):
        rows = pl.ds(pl.multiple_of(base, half), half)
        for g in range(pairs):
            lanes = lanes_of(g)
            part = lambda k: src[:, (3 * g + k) * 128 : (3 * g + k + 1) * 128]
            qm[0, rows, lanes], qm[1, rows, lanes] = head_lanes(part(0) * bf(HD**-0.5))
            ks[rows, lanes] = part(1)
            vs[rows, lanes] = part(2)
            kt[lanes, rows] = part(1).T
            grad = do[:, lanes]
            dom[0, rows, lanes], dom[1, rows, lanes] = head_lanes(grad)
            prod = (grad.astype(f32) * o[:, lanes].astype(f32)).T
            for e in range(2):
                dlt[2 * g + e : 2 * g + e + 1, rows] = jnp.sum(prod[e * HD : (e + 1) * HD], axis=0, keepdims=True)
    dks[...] = jnp.zeros_like(dks)
    dvs[...] = jnp.zeros_like(dvs)

    def qblock(i, _):
        at = pl.multiple_of(i * QB, QB)
        qr = pl.ds(at, QB)
        srow = st_ref[:, qr]
        dqs[...] = jnp.zeros_like(dqs)

        def step(masked, j, carry):
            kat = pl.multiple_of(j * QB, QB)
            kr = pl.ds(kat, QB)
            if masked:
                mask = attn_mask(kat, at, srow)
            scores, softs, grads = [], [], []
            for h in range(heads):
                lanes = lanes_of(h // 2)
                one = lax.dot_general(ks[kr, lanes], qm[h % 2, qr, lanes], NT, preferred_element_type=f32)
                back = lax.dot_general(vs[kr, lanes], dom[h % 2, qr, lanes], NT, preferred_element_type=f32)
                scores.append((jnp.where(mask, one, NEG) if masked else one, back))
            for h in range(heads):
                soft = jnp.exp(scores[h][0] - lse_ref[h : h + 1, qr])
                grads.append((soft * (scores[h][1] - dlt[h : h + 1, qr])).astype(bf))
                softs.append(soft.astype(bf))
            for g in range(pairs):
                lanes = lanes_of(g)
                both = lambda ref: jnp.concatenate([ref[0, qr, lanes], ref[1, qr, lanes]], axis=0)
                two = slice(2 * g, 2 * g + 2)
                dvs[kr, lanes] += jnp.dot(jnp.concatenate(softs[two], axis=1), both(dom), preferred_element_type=f32)
                dks[kr, lanes] += jnp.dot(jnp.concatenate(grads[two], axis=1), both(qm), preferred_element_type=f32)
                for h in (2 * g, 2 * g + 1):
                    sub = slice(h * HD, (h + 1) * HD)
                    dqs[sub] += jnp.dot(kt[sub, kr], grads[h], preferred_element_type=f32)
            return carry

        over_blocks(info, i, nb, step, 0)
        qm[0, qr] = (dqs[...] * (HD**-0.5)).T.astype(bf)
        return 0

    lax.fori_loop(0, nb, qblock, 0)
    for dst, base in ((dkeep, c * half), (dsend, (1 - c) * half)):
        rows = pl.ds(pl.multiple_of(base, half), half)
        for g in range(pairs):
            for k, value in enumerate((qm[0, rows, lanes_of(g)], dks[rows, lanes_of(g)], dvs[rows, lanes_of(g)])):
                dst[:, (3 * g + k) * 128 : (3 * g + k + 1) * 128] = value.astype(bf)


def attn_bwd(own, recv, do_own, do_recv, o_own, o_recv, starts, lse, info):
    half, cols = own.shape[0], own.shape[1] // 3
    n = 2 * half
    return pl.pallas_call(
        bwd_kernel,
        in_specs=[SM] + [VM] * 8,
        out_specs=[VM] * 2,
        scratch_shapes=[
            pltpu.VMEM((2, n, cols), bf), pltpu.VMEM((n, cols), bf), pltpu.VMEM((n, cols), bf), pltpu.VMEM((cols, n), bf),
            pltpu.VMEM((2, n, cols), bf), pltpu.VMEM((cols // HD, n), f32), pltpu.VMEM((cols, QB), f32),
            pltpu.VMEM((n, cols), f32), pltpu.VMEM((n, cols), f32)],
        out_shape=[like((half, 3 * cols), bf)] * 2,
        cost_estimate=pl.CostEstimate(flops=n * n, bytes_accessed=n * 128, transcendentals=0),
        compiler_params=pltpu.CompilerParams(vmem_limit_bytes=56 << 20),
    )(info, own, recv, do_own, do_recv, o_own, o_recv, starts, lse)


def dot(left, right, dims=(((1,), (0,)), ((), ()))):
    return lax.dot_general(left, right, dims, preferred_element_type=f32)


def exchange(value, bit, dp_size):
    if bit:
        return lax.ppermute(value, "dp", [(i, i ^ bit) for i in range(dp_size)])
    return lax.ppermute(value, "tensor", [(0, 1), (1, 0)])


def flip(index, bits):
    for bit in bits:
        index = index + bit * (1 - 2 * ((index // bit) % 2))
    return index

def far_groups(dp_size):
    far = [1 << k for k in range(dp_size.bit_length() - 2, 1, -1)]
    return [tuple(far[k : k + 2]) for k in range(0, len(far), 2)]

def group_moves(group):
    if len(group) == 1:
        return [(1, group)]
    return [(1, group[:1]), (2, group[1:]), (3, group)]

def chunks_of(cols, which, count, until=None):
    tiles = cols // 128
    cuts = [128 * ((tiles * k) // count) for k in range(count + 1)]
    arrays = range(which, until + 1) if until else (which,)
    return tuple(
        (array, low, high - low, high - low - 128)
        for low, high in zip(cuts, cuts[1:]) for array in arrays)


def head_kernel(groups, chunks, tokens, *refs):
    shards, x_out, outs, (send_sem, recv_sem, local_sem) = refs[:4], refs[4], refs[5:9], refs[9:]
    dp, t = lax.axis_index("dp"), lax.axis_index("tensor")
    core = dp % 2
    away = core + t - 2 * core * t
    near = {1: (flip(dp, (1,)), t), 2: (flip(dp, (2,)), t), 0: (dp, 1 - t)}
    distant = [bits for group in groups for _, bits in group_moves(group)]
    swap = (dp - core + t, core)
    barrier = pltpu.get_barrier_semaphore()
    for device in list(near.values()) + [(flip(dp, bits), t) for bits in distant]:
        pl.semaphore_signal(barrier, inc=1, device_id=device, device_id_type=MESH_ID)

    @pl.when(away == 1)
    def _():
        pl.semaphore_signal(barrier, inc=1, device_id=swap, device_id_type=MESH_ID)

    local = [
        pltpu.make_async_copy(shards[k], outs[k].at[away, 0] if k < 2 else outs[k].at[0], local_sem.at[k]) for k in range(4)]
    for copy in local:
        copy.start()
    pl.semaphore_wait(barrier, len(near) + len(distant) + away)
    count = [0]

    def remote(src, dst, device):
        slot = count[0]
        count[0] += 1
        return pltpu.make_async_remote_copy(
            src_ref=src, dst_ref=dst, send_sem=send_sem.at[slot], recv_sem=recv_sem.at[slot],
            device_id=device, device_id_type=MESH_ID)

    def blocks(ref, index, first, held, low, size):
        return ref.at[index, pl.ds(first, held), :, pl.ds(low, size)]

    plans = []
    for which, low, size, part in chunks:
        shard, out = shards[which], outs[which]
        steps, held = [], 1
        for group in groups:
            moves = []
            for place, bits in group_moves(group):
                src = shard.at[:, pl.ds(low, size)] if held == 1 else blocks(out, away, 0, held, low, size)
                dst = out.at[away, place, :, pl.ds(low, size)] if held == 1 else blocks(out, away, place * held, held, low, size)
                moves.append(remote(src, dst, (flip(dp, bits), t)))
            held *= len(group_moves(group)) + 1
            steps.append(moves)
        a, b = (low, part), (low + part, size - part)
        steps.append([
            remote(blocks(out, away, 0, held, *a), blocks(out, away, 0, held, *a), near[0]),
            remote(blocks(out, away, 0, held, *b), blocks(out, away, held, held, *b), near[2]),
        ])
        steps.append(
            [remote(blocks(out, k, 0, held, *a), blocks(out, k, held, held, *a), near[2]) for k in range(2)]
            + [remote(blocks(out, away, 0, 2 * held, *b), blocks(out, away, 0, 2 * held, *b), near[0])])
        steps.append([
            remote(blocks(out, k, 0, 2 * held, low, size),
                   blocks(out, 1 - k, 2 * held, 2 * held, low, size), near[1]) for k in range(2)])
        plans.append(steps)
    later = []
    held = 1
    for group in groups:
        moves = []
        for place, bits in group_moves(group):
            for shard, out in zip(shards[2:], outs[2:]):
                src = shard if held == 1 else out.at[pl.ds(0, held)]
                dst = out.at[place] if held == 1 else out.at[pl.ds(place * held, held)]
                moves.append(remote(src, dst, (flip(dp, bits), t)))
        held *= len(group_moves(group)) + 1
        later.append(moves)
    depth = len(plans[0])
    swap_copy = remote(tokens, x_out, swap)
    stay_copy = pltpu.make_async_copy(tokens, x_out, local_sem.at[4])
    waited = set()

    def advance(number, phase):
        if number >= len(plans):
            return
        if phase > 0:
            for move in plans[number][phase - 1]:
                move.wait_recv()
        if phase == 1 and chunks[number][0] not in waited:
            waited.add(chunks[number][0])
            local[chunks[number][0]].wait()
        if phase < depth:
            for move in plans[number][phase]:
                move.start()

    advance(0, 0)

    @pl.when(away == 1)
    def _():
        swap_copy.start()

    @pl.when(away == 0)
    def _():
        stay_copy.start()

    far = len(groups)
    for number in range(len(plans)):
        if number == 0:
            for phase in range(1, far + 1):
                advance(0, phase)
            advance(1, 0)
        advance(number, far + 1)
        for phase in range(1, far + 1):
            advance(number + 1, phase)
        advance(number + 2, 0)
        if number == len(plans) - 2:
            for move in later[0]:
                move.start()
        advance(number, far + 2)
    for number in range(len(plans)):
        advance(number, depth)

    @pl.when(away == 1)
    def _():
        swap_copy.wait()

    @pl.when(away == 0)
    def _():
        stay_copy.wait()

    for which in sorted(set(range(4)) - waited):
        local[which].wait()
    for k, moves in enumerate(later):
        if k > 0:
            for move in moves:
                move.start()
        for move in moves:
            move.wait()
    for steps in plans:
        for moves in steps:
            for move in moves:
                move.wait_send()


def head(dp_size, tokens, shards, chunks):
    groups = far_groups(dp_size)
    partners = sum(len(group_moves(g)) for g in groups)
    slots = len(chunks) * (partners + 7) + 2 * partners + 1
    shapes = [(2, dp_size)] * 2 + [(dp_size // 4,)] * 2
    return pl.pallas_call(
        functools.partial(head_kernel, groups, chunks),
        in_specs=[VM] * 5,
        out_specs=[ANY] * 5,
        out_shape=[jax.ShapeDtypeStruct(tokens.shape, tokens.dtype)]
        + [jax.ShapeDtypeStruct(lead + s.shape, s.dtype) for lead, s in zip(shapes, shards)],
        scratch_shapes=[pltpu.SemaphoreType.DMA((slots,)), pltpu.SemaphoreType.DMA((slots,)), pltpu.SemaphoreType.DMA((5,))],
        compiler_params=pltpu.CompilerParams(collective_id=0, has_side_effects=True),
    )(tokens, *shards)


def tail_kernel(groups, tokens, own_lo, own_hi, rest_lo, rest_hi, small_lo, small_hi, feed, x_out, total, vecs, feed_total,
                feed_part, feed_got, part, got_core, got_near, got_last, got_far, vec, vec_core, vec_two, vec_one, vec_far, send_sem, recv_sem, local_sem):
    dp, t = lax.axis_index("dp"), lax.axis_index("tensor")
    core = dp % 2
    away = core + t - 2 * core * t
    near = {1: (flip(dp, (1,)), t), 2: (flip(dp, (2,)), t), 0: (dp, 1 - t)}
    distant = [bits for group in groups for _, bits in group_moves(group)]
    swap = (dp - core + t, core)
    barrier = pltpu.get_barrier_semaphore()
    for device in list(near.values()) + [(flip(dp, bits), t) for bits in distant]:
        pl.semaphore_signal(barrier, inc=1, device_id=device, device_id_type=MESH_ID)

    @pl.when(away == 1)
    def _():
        pl.semaphore_signal(barrier, inc=1, device_id=swap, device_id_type=MESH_ID)

    pl.semaphore_wait(barrier, len(near) + len(distant) + away)
    count = [0]

    def remote(src, dst, device):
        slot = count[0]
        count[0] += 1
        return pltpu.make_async_remote_copy(
            src_ref=src, dst_ref=dst, send_sem=send_sem.at[slot], recv_sem=recv_sem.at[slot],
            device_id=device, device_id_type=MESH_ID)

    swap_copy = remote(tokens, x_out, swap)
    stay_copy = pltpu.make_async_copy(tokens, x_out, local_sem.at[0])
    half, rows, cols = own_lo.shape
    quarter = half // 2
    chunks = [pl.ds(low, min(512, cols - low)) for low in range(0, cols, 512)]
    to_core = [[
        remote(rest_hi.at[:, :, c], got_core.at[0, :, :, c], near[1]),
        remote(own_hi.at[:, :, c], got_core.at[1, :, :, c], near[1])] for c in chunks]
    to_core[0].append(remote(small_hi, vec_core, near[1]))
    for moves in to_core:
        for move in moves:
            move.start()

    @pl.when(away == 1)
    def _():
        swap_copy.start()

    @pl.when(away == 0)
    def _():
        stay_copy.start()

    feed_steps = []
    held, used = feed.shape[0], 0
    for number, group in enumerate(reversed(groups)):
        moves = group_moves(group)
        held //= len(moves) + 1
        source, step = feed if number == 0 else feed_part, []
        for place, bits in moves:
            step.append(remote(source.at[pl.ds(place * held, held)], feed_got.at[pl.ds(used, held)], (flip(dp, bits), t)))
            used += held
        feed_steps.append((step, source, held, used - held * len(moves), len(moves)))
    for move in feed_steps[0][0]:
        move.start()

    def add(*terms):
        out = terms[0].astype(f32)
        for term in terms[1:]:
            out = out + term.astype(f32)
        return out.astype(bf)

    upper, lower = pl.ds(quarter, quarter), pl.ds(0, quarter)
    mine, other = away, 1 - away
    last = len(chunks) - 1
    steps, sent = {}, []

    def start(key, moves):
        steps[key] = moves
        sent.extend(moves)
        for move in moves:
            move.start()

    def arrive(key):
        for move in steps[key]:
            move.wait_recv()

    def core_stage(k):
        for move in to_core[k]:
            move.wait_recv()
        c = chunks[k]

        def body(q, _):
            part[0, q, :, c] = add(own_lo[q, :, c], got_core[0, q, :, c])
            part[1, q, :, c] = add(rest_lo[q, :, c], got_core[1, q, :, c])
            if k == 0:
                vec[q] = add(small_lo[q], vec_core[q])
            return 0

        lax.fori_loop(0, half, body, 0)
        start(("x", k), [
            remote(part.at[g, upper, :, c], got_near.at[g, lower, :, c], near[2]) for g in range(2)]
            + ([remote(vec.at[upper], vec_two, near[2])] if k == 0 else []))

    def x_stage(k):
        arrive(("x", k))
        c = chunks[k]

        def body(q, _):
            for g in range(2):
                part[g, q, :, c] = add(part[g, q, :, c], got_near[g, q, :, c])
            if k == 0:
                vec[q] = add(vec[q], vec_two[q])
            return 0

        lax.fori_loop(0, quarter, body, 0)
        start(("y", k), [remote(part.at[other, lower, :, c], got_last.at[:, :, c], near[0])]
              + ([remote(vec.at[lower], vec_one, near[0])] if k == 0 else []))

    def far_moves(number, k):
        held, used = quarter, 0
        for index, group in enumerate(reversed(groups)):
            moves = group_moves(group)
            held //= len(moves) + 1
            if index == number:
                out = []
                for m, (place, bits) in enumerate(moves):
                    device, c = (flip(dp, bits), t), chunks[k]
                    out.append(remote(part.at[mine, pl.ds(place * held, held), :, c], got_far.at[pl.ds(used + m * held, held), :, c], device))
                    if k == 0:
                        out.append(remote(vec_one.at[pl.ds(place * held, held)], vec_far.at[pl.ds(used + m * held, held)], device))
                return out, held, used, len(moves)
            used += held * len(moves)

    def y_stage(k):
        arrive(("y", k))
        c = chunks[k]

        def body(q, _):
            part[mine, q, :, c] = add(part[mine, q, :, c], got_last[q, :, c])
            if k == 0:
                vec_one[q] = add(vec[q], vec_one[q])
            return 0

        lax.fori_loop(0, quarter, body, 0)
        start(("z", 0, k), far_moves(0, k)[0])

    far_shape = []
    held, used = quarter, 0
    for group in reversed(groups):
        moves = len(group_moves(group))
        held //= moves + 1
        far_shape.append((held, used, moves))
        used += held * moves

    def z_stage(number, k):
        arrive(("z", number, k))
        c = chunks[k]
        held, base, moves = far_shape[number]

        def body(q, _):
            part[mine, q, :, c] = add(part[mine, q, :, c], *[got_far[base + m * held + q, :, c] for m in range(moves)])
            if k == 0:
                vec_one[q] = add(vec_one[q], *[vec_far[base + m * held + q] for m in range(moves)])
            return 0

        lax.fori_loop(0, held, body, 0)
        if number + 1 < len(groups):
            start(("z", number + 1, k), far_moves(number + 1, k)[0])

    for k in range(last + 1):
        core_stage(k)
    for k in range(last + 1):
        x_stage(k)
        if k > 0:
            y_stage(k - 1)
    y_stage(last)
    for number in range(len(groups)):
        for k in range(last + 1):
            z_stage(number, k)
    to_far = []
    for number, (step, source, held, base, moves) in enumerate(feed_steps):
        if number > 0:
            for move in step:
                move.start()
        for move in step:
            move.wait_recv()

        def sum_feed(k, _, source=source, held=held, base=base, moves=moves):
            feed_part[k] = add(source[k], *[feed_got[base + m * held + k] for m in range(moves)])
            return 0

        if number + 1 < len(feed_steps):
            lax.fori_loop(0, held, sum_feed, 0)
        else:
            out = source[0].astype(f32)
            for m in range(moves):
                out = out + feed_got[base + m * held].astype(f32)
            feed_total[...] = out
        to_far += step
    total[...] = part[mine, 0].astype(f32)
    vecs[...] = vec_one[0].astype(f32)

    @pl.when(away == 1)
    def _():
        swap_copy.wait()

    @pl.when(away == 0)
    def _():
        stay_copy.wait()

    for move in sum(to_core, []) + sent + to_far:
        move.wait_send()


def tail(dp_size, tokens, own, rest, small, feed):
    groups = far_groups(dp_size)
    half, rows, cols = own[0].shape
    quarter = half // 2
    wide = small[0].shape[2]
    partners = sum(len(group_moves(g)) for g in groups)
    slots = (-(-cols // 512)) * (5 + partners) + 4 + 2 * partners + 1
    return pl.pallas_call(
        functools.partial(tail_kernel, groups),
        in_specs=[VM] * 8,
        out_specs=[ANY, VM, VM, VM],
        out_shape=[
            jax.ShapeDtypeStruct(tokens.shape, bf), jax.ShapeDtypeStruct((rows, cols), f32),
            jax.ShapeDtypeStruct((rows, wide), f32), jax.ShapeDtypeStruct(feed.shape[1:], f32)],
        scratch_shapes=[
            pltpu.VMEM(feed.shape, bf), pltpu.VMEM(feed.shape, bf),
            pltpu.VMEM((2, half, rows, cols), bf), pltpu.VMEM((2, half, rows, cols), bf), pltpu.VMEM((2, half, rows, cols), bf),
            pltpu.VMEM((quarter, rows, cols), bf), pltpu.VMEM((quarter, rows, cols), bf),
            pltpu.VMEM((half, rows, wide), bf), pltpu.VMEM((half, rows, wide), bf), pltpu.VMEM((quarter, rows, wide), bf),
            pltpu.VMEM((quarter, rows, wide), bf), pltpu.VMEM((quarter, rows, wide), bf),
            pltpu.SemaphoreType.DMA((slots,)), pltpu.SemaphoreType.DMA((slots,)), pltpu.SemaphoreType.DMA((1,))],
        compiler_params=pltpu.CompilerParams(collective_id=1, has_side_effects=True, vmem_limit_bytes=48 << 20),
    )(tokens, *own, *rest, *small, feed)


def add_low(*terms):
    out = terms[0].astype(f32)
    for term in terms[1:]:
        out = out + term.astype(f32)
    return out.astype(bf)


def order_matrix(owner, rows, width):
    place = lax.broadcasted_iota(jnp.int32, (1, width), 1)
    block = place // rows
    count = width // rows
    natural = place % rows
    for k, bit in enumerate([1 << b for b in range(count.bit_length() - 2, 1, -1)] + [2, 1]):
        on, base = (block // (1 << k)) % 2, (owner // bit) % 2
        natural = natural + (on + base - 2 * on * base) * (bit * rows)
    return (lax.broadcasted_iota(jnp.int32, (width, width), 0) == natural).astype(f32).astype(bf)


def norm_parts(values):
    centered = values - jnp.mean(values, axis=-1, keepdims=True)
    inverse = lax.rsqrt(jnp.mean(centered * centered, axis=-1, keepdims=True) + EPSILON)
    return centered * inverse, inverse


def norm_back(hat, inverse, gain, grad):
    scaled = grad * gain
    return inverse * (
        scaled - jnp.mean(scaled, axis=-1, keepdims=True) - hat * jnp.mean(scaled * hat, axis=-1, keepdims=True))


def over_rows(total, body):
    def step(k, _):
        body(pl.ds(pl.multiple_of(k * ROWS, ROWS), ROWS))
        return 0

    lax.fori_loop(0, total // ROWS, step, 0)


def column_sum(ref, row, values):
    ref[row : row + 1] += jnp.sum(values, axis=0, keepdims=True)


def bias_row(vec_nat, group, cols):
    lanes = pl.ds(pl.multiple_of(group * cols, 128), cols)
    q, v = vec_nat[2:3, lanes], vec_nat[3:4, lanes]
    parts = []
    for g in range(cols // 128):
        part = slice(g * 128, (g + 1) * 128)
        parts += [q[:, part], jnp.zeros((1, 128), f32), v[:, part]]
    return jnp.concatenate(parts, axis=1)


def first_kernel(rows, info, tokens, pack, weight, x_out, n1_out, send, vec_rel, vec_nat, order):
    width, cols = tokens.shape[1], weight.shape[2] // 3

    @pl.when(pl.program_id(0) == 0)
    def _():
        order[...] = order_matrix(info[1], rows, width)
        small = pack[0, :, cols:].astype(f32).T[:VECS]
        vec_rel[...] = small
        vec_nat[...] = lax.dot_general(small.astype(bf), order[...], NT, preferred_element_type=f32)

    x = jnp.dot(tokens[...], order[...], preferred_element_type=f32)
    hat, _ = norm_parts(x)
    n1 = (hat * vec_rel[0:1] + vec_rel[1:2]).astype(bf)
    x_out[...] = x.astype(bf)
    n1_out[...] = n1
    send[...] = (jnp.dot(n1, weight[0], preferred_element_type=f32) + bias_row(vec_nat, 1 - info[0], cols)).astype(bf)


def own_kernel(info, n1, weight, vec_nat, out):
    bias = bias_row(vec_nat, info[0], weight.shape[2] // 3)
    out[...] = (jnp.dot(n1[...], weight[0], preferred_element_type=f32) + bias).astype(bf)


def picked(array, index):
    return pl.BlockSpec((1,) + array.shape[1:], lambda k, s: (index, 0, 0))


def whole(array):
    return pl.BlockSpec(array.shape, lambda k, s: (0,) * len(array.shape))


def one_call(kernel, info, inputs, specs, outs, scratch=(), limit=56):
    return pl.pallas_call(
        kernel,
        grid_spec=pltpu.PrefetchScalarGridSpec(
            num_scalar_prefetch=1, grid=(1,), in_specs=[s if s is not None else whole(a) for a, s in zip(inputs, specs)],
            out_specs=[whole(o) for o in outs], scratch_shapes=list(scratch)),
        out_shape=outs,
        cost_estimate=pl.CostEstimate(flops=1 << 22, bytes_accessed=1 << 18, transcendentals=0),
        compiler_params=pltpu.CompilerParams(vmem_limit_bytes=limit << 20),
    )(info, *inputs)


def like(shape, dtype):
    return jax.ShapeDtypeStruct(shape, dtype)


def by_rows(kernel, info, inputs, specs, outs, scratch=(), flops=1 << 22):
    total = inputs[0].shape[0]

    def spec(array, given=None):
        if given is not None:
            return given
        if array.shape[0] == total:
            return pl.BlockSpec((ROWS,) + array.shape[1:], lambda k, s: (k, 0))
        return whole(array)

    return pl.pallas_call(
        kernel,
        grid_spec=pltpu.PrefetchScalarGridSpec(
            num_scalar_prefetch=1, grid=(total // ROWS,), in_specs=[spec(a, g) for a, g in zip(inputs, specs)],
            out_specs=[spec(o) for o in outs], scratch_shapes=list(scratch)),
        out_shape=outs,
        cost_estimate=pl.CostEstimate(flops=flops, bytes_accessed=1 << 18, transcendentals=0),
        compiler_params=pltpu.CompilerParams(vmem_limit_bytes=24 << 20),
    )(info, *inputs)


def project_first(info, rows, tokens, packs, weights):
    n, width = tokens.shape
    return by_rows(
        functools.partial(first_kernel, rows), info, (tokens, packs, weights), (None, picked(packs, 0), picked(weights, 1)),
        [like((n, width), bf), like((n, width), bf), like((n, weights.shape[2]), bf), like((VECS, width), f32), like((VECS, width), f32)],
        [pltpu.VMEM((width, width), bf)], 1 << 36)


def project_own(info, n1, weights, vec_nat):
    (out,) = by_rows(
        own_kernel, info, (n1, weights, vec_nat), (None, picked(weights, 0), None), [like((n1.shape[0], weights.shape[2]), bf)])
    return out


def middle_kernel(rows, x, o_own, o_send, cot, cot_recv, packs, vec_rel, fc00, fc01, fc10, fc11, pr0, pr1,
                  middle, n2, cot_rel, d_mlp, o_recv, fc_got, pr_got, order, send_sem, recv_sem):
    dp, t = lax.axis_index("dp"), lax.axis_index("tensor")
    core = dp % 2
    away = core + t - 2 * core * t
    partner = (flip(dp, (1,)), t)
    barrier = pltpu.get_barrier_semaphore()
    pl.semaphore_signal(barrier, inc=1, device_id=partner, device_id_type=MESH_ID)
    pl.semaphore_wait(barrier, 1)
    size = fc00.shape[0]
    copies = [
        pltpu.make_async_remote_copy(
            src_ref=src, dst_ref=dst, send_sem=send_sem.at[k], recv_sem=recv_sem.at[k], device_id=partner, device_id_type=MESH_ID)
        for k, (src, dst) in enumerate((
            (o_send, o_recv), (fc00, fc_got.at[0, pl.ds(0, size)]), (fc01, fc_got.at[0, pl.ds(size, size)]), (pr0, pr_got.at[0]),
            (fc10, fc_got.at[1, pl.ds(0, size)]), (fc11, fc_got.at[1, pl.ds(size, size)]), (pr1, pr_got.at[1])))]
    for copy in copies:
        copy.start()
    order[...] = order_matrix(dp, rows, x.shape[1])
    cols = o_own.shape[1]

    def cot_rows(at):
        grad = jnp.dot(jnp.where(away == 0, cot[at], cot_recv[at]), order[...], preferred_element_type=f32)
        cot_rel[at] = grad.astype(bf)
        d_mlp[at] = (BRANCH_SCALE * grad).astype(bf)

    over_rows(x.shape[0], cot_rows)
    copies[0].wait_recv()

    def body(at):
        branch = lax.dot_general(o_own[at], packs[0, :, :cols], NT, preferred_element_type=f32)
        branch = branch + lax.dot_general(o_recv[at], packs[1, :, :cols], NT, preferred_element_type=f32)
        mid = x[at].astype(f32) + BRANCH_SCALE * (branch + vec_rel[4:5])
        middle[at] = mid
        hat, _ = norm_parts(mid)
        n2[at] = (hat * vec_rel[5:6] + vec_rel[6:7]).astype(bf)

    over_rows(x.shape[0], body)
    for copy in copies[1:]:
        copy.wait_recv()
    for copy in copies:
        copy.wait_send()


def middle_part(rows, x, o_own, o_send, cot, cot_recv, packs, vec_rel, fc_parts, proj_parts):
    shape, half = x.shape, x.shape[1] // 2
    hidden = proj_parts[0].shape[1]
    got = like((2, half, hidden), bf)
    return pl.pallas_call(
        functools.partial(middle_kernel, rows),
        in_specs=[VM] * 7 + [ANY] * 6,
        out_specs=[VM] * 5 + [ANY] * 2,
        out_shape=[like(shape, f32), like(shape, bf), like(shape, bf), like(shape, bf), like(o_send.shape, bf), got, got],
        scratch_shapes=[
            pltpu.VMEM((shape[1], shape[1]), bf), pltpu.SemaphoreType.DMA((7,)), pltpu.SemaphoreType.DMA((7,))],
        compiler_params=pltpu.CompilerParams(collective_id=2, has_side_effects=True, vmem_limit_bytes=36 << 20),
    )(x, o_own, o_send, cot, cot_recv, packs, vec_rel, *fc_parts[0], *fc_parts[1], *proj_parts)


def after_kernel(rows, info, middle, mlp, back, cot, packs, vec_rel, block_out, d_middle, d_attn, do_own, do_send, sums, order):
    @pl.when(pl.program_id(0) == 0)
    def _():
        order[...] = order_matrix(info[1], rows, middle.shape[1])
        sums[...] = jnp.zeros_like(sums)

    cols = do_own.shape[1]
    mid = middle[...]
    out = (mid + BRANCH_SCALE * (mlp[...] + vec_rel[7:8])).astype(bf)
    block_out[...] = lax.dot_general(out, order[...], NT, preferred_element_type=f32).astype(bf)
    hat, inverse = norm_parts(mid)
    grad = back[...]
    out_grad = cot[...].astype(f32)
    entire = out_grad + norm_back(hat, inverse, vec_rel[5:6], grad)
    d_middle[...] = entire
    low = (BRANCH_SCALE * entire).astype(bf)
    d_attn[...] = low
    do_own[...] = jnp.dot(low, packs[0, :, :cols], preferred_element_type=f32).astype(bf)
    do_send[...] = jnp.dot(low, packs[1, :, :cols], preferred_element_type=f32).astype(bf)
    column_sum(sums, 0, BRANCH_SCALE * entire)
    column_sum(sums, 1, grad * hat)
    column_sum(sums, 2, grad)
    column_sum(sums, 3, BRANCH_SCALE * out_grad)


def after_part(info, rows, middle, mlp, back, cot, packs, vec_rel, cols):
    shape = middle.shape
    slim = like((shape[0], cols), bf)
    return by_rows(
        functools.partial(after_kernel, rows), info, (middle, mlp, back, cot, packs, vec_rel), (None,) * 6,
        [like(shape, bf), like(shape, f32), like(shape, bf), slim, slim, like((8, shape[1]), f32)],
        [pltpu.VMEM((shape[1], shape[1]), bf)])


def feed_kernel(n2, d_mlp, bias, fc_got, pr_got, fc00, fc01, fc10, fc11, pr0, pr1,
                acc, back, fc_lo, fc_hi, pr_lo, pr_hi, d_bias, n2_t, d_t, w_fc, w_pr, act, d_pre):
    step = pl.program_id(0)
    total, half = n2.shape[0], n2.shape[1] // 2

    @pl.when(step == 0)
    def _():
        acc[...] = jnp.zeros_like(acc)
        back[...] = jnp.zeros_like(back)
        n2_t[...] = n2[...].T
        d_t[...] = d_mlp[...].T

    @pl.when(step < pl.num_programs(0) // 2)
    def _():
        w_fc[: half // 2], w_fc[half // 2 : half], w_pr[:half] = fc00[...], fc01[...], pr0[...]

    @pl.when(step >= pl.num_programs(0) // 2)
    def _():
        w_fc[: half // 2], w_fc[half // 2 : half], w_pr[:half] = fc10[...], fc11[...], pr1[...]

    w_fc[half:], w_pr[half:] = fc_got[0], pr_got[0]
    root = 0.7978845608
    count = total // ROWS
    raw = {}
    grad_sum = jnp.zeros((1, w_fc.shape[1]), f32)

    def products(k):
        at = slice(k * ROWS, (k + 1) * ROWS)
        return (
            jnp.dot(n2[at], w_fc[...], preferred_element_type=f32) + bias[0],
            jnp.dot(d_mlp[at], w_pr[...], preferred_element_type=f32))

    def add_back(k):
        at = slice(k * ROWS, (k + 1) * ROWS)
        acc[at] += lax.dot_general(act[at], w_pr[...], NT, preferred_element_type=f32)
        back[at] += lax.dot_general(d_pre[at], w_fc[...], NT, preferred_element_type=f32)

    raw[0] = products(0)
    for k in range(count):
        at = slice(k * ROWS, (k + 1) * ROWS)
        if k + 1 < count:
            raw[k + 1] = products(k + 1)
        pre, d_act = raw.pop(k)
        square = pre * pre
        inner = jnp.tanh(pre * (root + root * 0.044715 * square))
        gate = 0.5 + 0.5 * inner
        act[at] = (pre * gate).astype(bf)
        slope = gate + pre * (0.5 - 0.5 * inner * inner) * (root + root * 3 * 0.044715 * square)
        grad = d_act * slope
        grad_sum = grad_sum + jnp.sum(grad, axis=0, keepdims=True)
        d_pre[at] = grad.astype(bf)
        if k > 0:
            add_back(k - 1)
    add_back(count - 1)
    d_bias[0] = grad_sum
    for out, left, right, low in (
        (fc_hi, n2_t, d_pre, half), (pr_hi, d_t, act, half), (fc_lo, n2_t, d_pre, 0), (pr_lo, d_t, act, 0)):
        out[0] = jnp.dot(left[low : low + half], right[...], preferred_element_type=f32).astype(bf)


def feed_part(n2, d_mlp, bias, fc_got, pr_got, fc_parts, proj_parts):
    (total, width), hidden, half = n2.shape, bias.shape[2], n2.shape[1] // 2
    steps = hidden // HIDDEN
    fixed = lambda a: pl.BlockSpec(a.shape, lambda k: (0,) * len(a.shape), pipeline_mode=pl.Buffered(1))
    early = lambda a: pl.BlockSpec((a.shape[0], HIDDEN), lambda k: (0, jnp.minimum(k, steps - 1)))
    late = lambda a: pl.BlockSpec((a.shape[0], HIDDEN), lambda k: (0, jnp.maximum(k - steps, 0)))
    two = lambda a: pl.BlockSpec((1, a.shape[1], HIDDEN), lambda k: (k // steps, 0, k % steps))
    grad = like((2, half, hidden), bf)
    sums = [like((total, width), f32)] * 2
    outs = sums + [grad] * 4 + [like((2, 1, hidden), f32)]
    return pl.pallas_call(
        feed_kernel,
        grid=(2 * steps,),
        in_specs=[fixed(n2), fixed(d_mlp), two(bias), two(fc_got), two(pr_got)]
        + [early(a) for a in fc_parts[0]] + [late(a) for a in fc_parts[1]] + [early(proj_parts[0]), late(proj_parts[1])],
        out_specs=[fixed(o) for o in sums] + [two(o) for o in outs[2:]],
        out_shape=outs,
        scratch_shapes=[
            pltpu.VMEM((width, total), bf), pltpu.VMEM((width, total), bf), pltpu.VMEM((width, HIDDEN), bf),
            pltpu.VMEM((width, HIDDEN), bf), pltpu.VMEM((total, HIDDEN), bf), pltpu.VMEM((total, HIDDEN), bf)],
        cost_estimate=pl.CostEstimate(flops=1 << 22, bytes_accessed=1 << 18, transcendentals=0),
        compiler_params=pltpu.CompilerParams(vmem_limit_bytes=48 << 20),
    )(n2, d_mlp, bias, fc_got, pr_got, *fc_parts[0], *fc_parts[1], *proj_parts)


def grads_into(lo, hi, left_t, extra_t, d_qkv, o):
    half = left_t.shape[0] // 2
    wide = d_qkv.shape[1]
    for out, low in ((hi, half), (lo, 0)):
        out[:, :wide] = jnp.dot(left_t[low : low + half], d_qkv[...], preferred_element_type=f32).astype(bf)
        out[:, wide:] = jnp.dot(extra_t[low : low + half], o[...], preferred_element_type=f32).astype(bf)


def last_own_kernel(info, d_qkv, n1, d_attn, o_own, weight, lo, hi, part, sums, left_t, extra_t):
    left_t[...] = n1[...].T
    extra_t[...] = d_attn[...].T
    sums[...] = jnp.zeros_like(sums)
    grads_into(lo, hi, left_t, extra_t, d_qkv, o_own)

    def body(at):
        part[at] = lax.dot_general(d_qkv[at], weight[0], NT, preferred_element_type=f32)
        column_sum(sums, 0, d_qkv[at].astype(f32))

    over_rows(n1.shape[0], body)


def last_own(info, dq, n1, d_attn, o_own, weights):
    n, width = n1.shape
    wide, slim = weights.shape[2], o_own.shape[1]
    grad = like((width // 2, wide + slim), bf)
    return one_call(
        last_own_kernel, info, (dq, n1, d_attn, o_own, weights), (None,) * 4 + (picked(weights, 0),),
        [grad, grad, like((n, width), f32), like((8, wide), f32)],
        [pltpu.VMEM((width, n), bf), pltpu.VMEM((width, n), bf)])


def last_kernel(rows, info, d_qkv, n1, d_attn, o_recv, weight, part, x, d_middle, vec_rel, own_sums, mid_sums, fc_rows,
                lo, hi, grad_out, small, left_t, extra_t, sums, vecs, nat, order):
    width, cols = x.shape[1], o_recv.shape[1]
    order[...] = order_matrix(info[1], rows, width)
    left_t[...] = n1[...].T
    extra_t[...] = d_attn[...].T
    sums[...] = jnp.zeros_like(sums)
    vecs[...] = jnp.zeros_like(vecs)
    grads_into(lo, hi, left_t, extra_t, d_qkv, o_recv)

    def body(at):
        grad = part[at] + lax.dot_general(d_qkv[at], weight[0], NT, preferred_element_type=f32)
        hat, inverse = norm_parts(x[at].astype(f32))
        grad_out[at] = (d_middle[at] + norm_back(hat, inverse, vec_rel[0:1], grad)).astype(bf)
        column_sum(sums, 0, d_qkv[at].astype(f32))
        column_sum(vecs, 0, grad * hat)
        column_sum(vecs, 1, grad)

    over_rows(x.shape[0], body)
    nat[...] = jnp.zeros_like(nat)
    for group, ref in ((info[0], own_sums), (1 - info[0], sums)):
        for row, part_index in ((0, 0), (1, 2)):
            picks = [ref[0:1, (3 * g + part_index) * 128 : (3 * g + part_index + 1) * 128] for g in range(cols // 128)]
            nat[row : row + 1, pl.ds(pl.multiple_of(group * cols, 128), cols)] = jnp.concatenate(picks, axis=1)
    fan = fc_rows.shape[0]
    nat[2 : 2 + fan] = fc_rows[...]
    moved = jnp.dot(nat[...].astype(bf), order[...], preferred_element_type=f32)
    vecs[2:4] = moved[0:2]
    vecs[4:8] = mid_sums[0:4]
    vecs[8 : 8 + fan] = moved[2 : 2 + fan]
    small[...] = vecs[...].T.astype(bf)


def last_part(info, rows, dq, n1, d_attn, o_recv, weights, part, x, d_middle, vec_rel, own_sums, mid_sums, fc_rows):
    n, width = n1.shape
    wide, slim = weights.shape[2], o_recv.shape[1]
    grad = like((width // 2, wide + slim), bf)
    inputs = (dq, n1, d_attn, o_recv, weights, part, x, d_middle, vec_rel, own_sums, mid_sums, fc_rows)
    return one_call(
        functools.partial(last_kernel, rows), info, inputs, (None,) * 4 + (picked(weights, 1),) + (None,) * 7,
        [grad, grad, like((n, width), bf), like((width, SMALL), bf)],
        [pltpu.VMEM((width, n), bf), pltpu.VMEM((width, n), bf), pltpu.VMEM((8, wide), f32),
         pltpu.VMEM((SMALL, width), f32), pltpu.VMEM((8, width), f32), pltpu.VMEM((width, width), bf)])


def on_device(
    tokens, segment_ids, ln1_gain, ln1_bias, w_qkv, b_qv, w_attn_out, b_attn_out,
    ln2_gain, ln2_bias, w_fc, b_fc, w_proj, b_proj, cotangent,
):
    dp_size = lax.axis_size("dp")
    dp_pos, t_pos = lax.axis_index("dp"), lax.axis_index("tensor")
    core = dp_pos % 2
    rows = ln1_gain.shape[0]
    width = tokens.shape[1]
    cols = w_qkv.shape[2]
    hidden = w_fc.shape[1]
    fan = b_fc.shape[0] // rows
    far = [1 << k for k in range(dp_size.bit_length() - 2, 1, -1)]
    swap = []
    for d in range(dp_size):
        for t in range(2):
            if d % 2 != t:
                swap.append((2 * d + t, 2 * (d - d % 2 + t) + d % 2))
    mine = core == t_pos

    pairs = cols // 128

    def by_pair(parts):
        parts = parts.reshape(-1, 3, pairs, 128)
        return jnp.swapaxes(parts, 1, 2).reshape(-1, 3 * cols)

    def by_part(columns):
        return jnp.swapaxes(columns.reshape(-1, pairs, 3, 128), 1, 2).reshape(-1, 3, cols)

    seg_other = exchange(segment_ids, 1, dp_size)
    seg = jnp.where(mine, segment_ids, seg_other)[0]
    small = jnp.concatenate(
        [ln1_gain[:, None], ln1_bias[:, None], b_qv.T, b_attn_out[:, None], ln2_gain[:, None],
         ln2_bias[:, None], b_proj[:, None], b_fc.reshape(rows, fan)], axis=1)
    small = jnp.pad(small, ((0, 0), (0, SMALL - small.shape[1])))
    out_pack = jnp.concatenate([w_attn_out.T, small], axis=1)
    tokens, all_qkv, all_out, fc_far, proj_far = head(
        dp_size, tokens, (by_pair(w_qkv), out_pack, w_fc, w_proj.T), chunks_of(3 * cols, 0, 2) + chunks_of(cols + SMALL, 1, 1))
    all_qkv, all_out = (a.reshape(2, width, -1) for a in (all_qkv, all_out))
    fc_far, proj_far = fc_far.reshape(-1, hidden), proj_far.reshape(-1, hidden)
    fc_parts = [[fc_far], [exchange(fc_far, 0, dp_size)]]
    proj_half = exchange(proj_far, 2, dp_size)

    part = jnp.stack([core, dp_pos, jnp.where(mine, 1, 0)]).astype(jnp.int32)
    x, n1, qkv_send, vec_rel, vec_nat = project_first(part, rows, tokens, all_out, all_qkv)
    qkv_recv = exchange(qkv_send, 1, dp_size)
    qkv_own = project_own(part, n1, all_qkv, vec_nat)
    fc_parts, proj_half, qkv_own = lax.optimization_barrier((fc_parts, proj_half, qkv_own))
    fc_parts = [p + [exchange(p[0], 2, dp_size)] for p in fc_parts]
    proj_half = jnp.concatenate([proj_far, proj_half], axis=0)
    proj_parts = [proj_half, exchange(proj_half, 0, dp_size)]
    starts, info = attn_info(seg, core)
    o_own, o_send, lse = attn_fwd(qkv_own, qkv_recv, starts, info)
    cot_recv = lax.ppermute(cotangent, BOTH, swap)
    fc_bias = vec_nat[8 : 8 + fan].T.reshape(2, 1, hidden)
    fc_bias = jnp.where(t_pos == 0, fc_bias, fc_bias[::-1])
    half = width // 2
    middle, n2, cot, d_mlp, o_recv, fc_got, pr_got = middle_part(
        rows, x, o_own, o_send, cotangent, cot_recv, all_out, vec_rel, fc_parts, proj_parts)
    mlp, back, fc_lo, fc_hi, pr_lo, pr_hi, d_b_fc = feed_part(n2, d_mlp, fc_bias, fc_got, pr_got, fc_parts, proj_parts)
    fc_got, pr_got = exchange(fc_hi, 1, dp_size), exchange(pr_hi, 1, dp_size)
    block_out, d_middle, d_attn, do_own, do_send, mid_sums = after_part(
        part, rows, middle, mlp, back, cot, all_out, vec_rel, cols)
    do_recv = exchange(do_send, 1, dp_size)
    fc_rows = jnp.where(t_pos == 0, d_b_fc, d_b_fc[::-1]).reshape(width, fan).T

    near_size = half // 2
    fc_rest = add_low(fc_lo[1], fc_got[1])
    pr_rest = add_low(pr_lo[:, near_size:], pr_got[:, near_size:])
    last = (qkv_own, qkv_recv, do_own, do_recv, o_own, o_send)
    last, fc_rest, pr_rest = lax.optimization_barrier((last, fc_rest, pr_rest))
    fc_sent = exchange(fc_rest, 0, dp_size)
    pr_sent = exchange(pr_rest, 2, dp_size)
    block_recv = lax.ppermute(block_out, BOTH, swap)
    dq_own, dq_send = attn_bwd(*last, starts, lse, info)
    dq_recv = exchange(dq_send, 1, dp_size)
    dq_own, fc_sent, pr_sent = lax.optimization_barrier((dq_own, fc_sent, pr_sent))
    fc_rest = add_low(fc_lo[0, near_size:], fc_got[0, near_size:], fc_sent[near_size:])
    pr_rest = add_low(pr_lo[1, :near_size], pr_got[1, :near_size], pr_sent[1])
    dq_own, fc_rest, pr_rest = lax.optimization_barrier((dq_own, fc_rest, pr_rest))
    fc_near = exchange(fc_rest, 2, dp_size)
    pr_near = exchange(pr_rest, 0, dp_size)
    own_lo, own_hi, d_n1, own_sums = last_own(part, dq_own, n1, d_attn, o_own, all_qkv)
    d_n1, fc_near, pr_near = lax.optimization_barrier((d_n1, fc_near, pr_near))
    sum_fc = add_low(fc_lo[0, :near_size], fc_got[0, :near_size], fc_sent[:near_size], fc_near)
    sum_proj = add_low(pr_lo[0, :near_size], pr_got[0, :near_size], pr_sent[0], pr_near)
    feed = jnp.concatenate([sum_fc, sum_proj], axis=1).reshape(-1, rows, 2 * hidden)
    d_n1, feed = lax.optimization_barrier((d_n1, feed))
    rest_lo, rest_hi, grad_tokens, d_small = last_part(
        part, rows, dq_recv, n1, d_attn, o_recv, all_qkv, d_n1, x, d_middle, vec_rel, own_sums, mid_sums, fc_rows)
    blocks = lambda arr: arr.reshape(dp_size // 2, rows, -1)
    grad_tokens, sum_a, vecs, sum_feed = tail(
        dp_size, grad_tokens, (blocks(own_lo), blocks(own_hi)), (blocks(rest_lo), blocks(rest_hi)),
        (blocks(d_small[:half]), blocks(d_small[half:])), feed)
    vecs, block_recv = lax.optimization_barrier((vecs, block_recv))
    block_out = jnp.where(mine, block_out, block_recv)
    owner = dp_pos - core + t_pos
    grad_tokens = dot(grad_tokens, order_matrix(owner, rows, width), NT).astype(bf)
    return (
        block_out,
        grad_tokens,
        vecs[:, 0],
        vecs[:, 1],
        by_part(sum_a[:, : 3 * cols]),
        vecs[:, 2:4].T,
        sum_a[:, 3 * cols :].T,
        vecs[:, 4],
        vecs[:, 5],
        vecs[:, 6],
        sum_feed[:, :hidden],
        vecs[:, 8 : 8 + fan].reshape(rows * fan),
        sum_feed[:, hidden:].T,
        vecs[:, 7],
    )


def solution(mesh):
    vec, tok = P("dp"), P(BOTH, None)
    in_specs = (
        tok, P("dp", None), vec, vec, P("dp", None, "tensor"), P(None, "dp"), P("tensor", "dp"),
        vec, vec, vec, P("dp", "tensor"), vec, P("tensor", "dp"), vec, tok,
    )
    out_specs = (
        tok, tok, vec, vec, P("dp", None, "tensor"), P(None, "dp"), P("tensor", "dp"),
        vec, vec, vec, P("dp", "tensor"), vec, P("tensor", "dp"), vec,
    )
    return jax.shard_map(on_device, mesh=mesh, in_specs=in_specs, out_specs=out_specs, check_vma=False)
```

```python
import functools

import jax
import jax.numpy as jnp
from jax import lax
from jax.experimental import pallas as pl
from jax.experimental.pallas import tpu as pltpu
from jax.sharding import PartitionSpec as P

HD = 64
QB = 256
NEG = -1e30
EPSILON = 1e-05
BRANCH_SCALE = 48.0 ** (-0.5)
SMALL = 128
VECS = 16
ROWS = 256
HIDDEN = 768
bf = jnp.bfloat16
f32 = jnp.float32
NT = (((1,), (1,)), ((), ()))
TN = (((0,), (0,)), ((), ()))
BOTH = ("dp", "tensor")
MESH_ID = pl.DeviceIdType.MESH
ANY = pl.BlockSpec(memory_space=pl.ANY)
VM = pl.BlockSpec(memory_space=pltpu.VMEM)
SM = pl.BlockSpec(memory_space=pltpu.SMEM)


def attn_mask(kat, at, srow):
    keys = lax.broadcasted_iota(jnp.int32, (QB, QB), 0)
    rows = lax.broadcasted_iota(jnp.int32, (1, QB), 1) + (at - kat)
    return (keys >= srow - kat) & (keys <= rows)


def over_blocks(bounds, i, step, carry):
    low = bounds[0, i * QB] // QB
    mid = jnp.minimum((bounds[0, i * QB + QB - 1] + QB - 1) // QB, i)
    carry = lax.fori_loop(0, mid - low + 1, lambda k, c: step(True, jnp.where(k == 0, i, low + k - 1), c), carry)
    return lax.fori_loop(mid, i, functools.partial(step, False), carry)


def head_lanes(values):
    low = (lax.broadcasted_iota(jnp.int32, (1, values.shape[1]), 1) % 128) < HD
    zero = jnp.zeros((), bf)
    return jnp.where(low, values, zero), jnp.where(low, zero, values)


def fwd_kernel(info, bounds, own, recv, st_ref, okeep, osend, lse_ref, qm, ks, vt, osc, acc):
    half, cols = own.shape[0], own.shape[1] // 3
    n, nb, heads, pairs = 2 * half, 2 * half // QB, cols // HD, cols // 128
    c = info[0]
    for base, src in ((c * half, own), ((1 - c) * half, recv)):
        rows = pl.ds(pl.multiple_of(base, half), half)
        for g in range(pairs):
            lanes = slice(g * 128, (g + 1) * 128)
            part = lambda k: src[:, (3 * g + k) * 128 : (3 * g + k + 1) * 128]
            qm[0, rows, lanes], qm[1, rows, lanes] = head_lanes(part(0) * bf(HD**-0.5))
            ks[rows, lanes] = part(1)
            vt[lanes, rows] = part(2).T

    def qblock(i, _):
        at = pl.multiple_of(i * QB, QB)
        qr = pl.ds(at, QB)
        srow = st_ref[:, qr]
        acc[...] = jnp.zeros_like(acc)

        def step(masked, j, carry):
            kat = pl.multiple_of(j * QB, QB)
            kr = pl.ds(kat, QB)
            if masked:
                mask = attn_mask(kat, at, srow)
            scores, mixed = [], []
            for h in range(heads):
                lanes = slice(h // 2 * 128, h // 2 * 128 + 128)
                one = lax.dot_general(ks[kr, lanes], qm[h % 2, qr, lanes], NT, preferred_element_type=f32)
                scores.append(jnp.where(mask, one, NEG) if masked else one)
            for h in range(heads):
                top, total = carry[h]
                new = jnp.maximum(top, jnp.max(scores[h], axis=0, keepdims=True))
                weights = jnp.exp(scores[h] - new)
                fade = jnp.exp(top - new)
                total = fade * total + jnp.sum(weights, axis=0, keepdims=True)
                mixed.append((new, total, fade, weights.astype(bf)))
            for h in range(heads):
                sub = slice(h * HD, (h + 1) * HD)
                acc[sub] = mixed[h][2] * acc[sub] + jnp.dot(vt[sub, kr], mixed[h][3], preferred_element_type=f32)
            return tuple(m[:2] for m in mixed)

        carry = over_blocks(bounds, i, step, ((jnp.full((1, QB), NEG, f32), jnp.zeros((1, QB), f32)),) * heads)
        for h, (top, total) in enumerate(carry):
            sub = slice(h * HD, (h + 1) * HD)
            acc[sub] = acc[sub] / total
            lse_ref[h : h + 1, qr] = top + jnp.log(total)
        osc[qr] = acc[...].T.astype(bf)
        return 0

    lax.fori_loop(0, nb, qblock, 0)
    okeep[...] = osc[pl.ds(pl.multiple_of(c * half, half), half)]
    osend[...] = osc[pl.ds(pl.multiple_of((1 - c) * half, half), half)]


def attn_fwd(own, recv, starts, info):
    half, cols = own.shape[0], own.shape[1] // 3
    n = 2 * half
    return pl.pallas_call(
        fwd_kernel,
        in_specs=[SM, SM, VM, VM, VM],
        out_specs=[VM] * 3,
        scratch_shapes=[
            pltpu.VMEM((2, n, cols), bf), pltpu.VMEM((n, cols), bf), pltpu.VMEM((cols, n), bf),
            pltpu.VMEM((n, cols), bf), pltpu.VMEM((cols, QB), f32)],
        out_shape=[jax.ShapeDtypeStruct((half, cols), bf)] * 2 + [jax.ShapeDtypeStruct((cols // HD, n), f32)],
        cost_estimate=pl.CostEstimate(flops=n * n, bytes_accessed=n * 128, transcendentals=0),
        compiler_params=pltpu.CompilerParams(vmem_limit_bytes=30 << 20),
    )(info, starts, own, recv, starts)


def bwd_kernel(info, bounds, own, recv, doo, dor, oo, orr, st_ref, lse_ref, dkeep, dsend, qm, ks, vs, kt, dom, dlt, dqs, dks, dvs):
    half, cols = own.shape[0], own.shape[1] // 3
    n, nb, heads, pairs = 2 * half, 2 * half // QB, cols // HD, cols // 128
    c = info[0]
    lanes_of = lambda g: slice(g * 128, (g + 1) * 128)
    for base, src, do, o in ((c * half, own, doo, oo), ((1 - c) * half, recv, dor, orr)):
        rows = pl.ds(pl.multiple_of(base, half), half)
        for g in range(pairs):
            lanes = lanes_of(g)
            part = lambda k: src[:, (3 * g + k) * 128 : (3 * g + k + 1) * 128]
            qm[0, rows, lanes], qm[1, rows, lanes] = head_lanes(part(0) * bf(HD**-0.5))
            ks[rows, lanes] = part(1)
            vs[rows, lanes] = part(2)
            kt[lanes, rows] = part(1).T
            grad = do[:, lanes]
            dom[0, rows, lanes], dom[1, rows, lanes] = head_lanes(grad)
            prod = (grad.astype(f32) * o[:, lanes].astype(f32)).T
            for e in range(2):
                dlt[2 * g + e : 2 * g + e + 1, rows] = jnp.sum(prod[e * HD : (e + 1) * HD], axis=0, keepdims=True)
    dks[...] = jnp.zeros_like(dks)
    dvs[...] = jnp.zeros_like(dvs)

    def qblock(i, _):
        at = pl.multiple_of(i * QB, QB)
        qr = pl.ds(at, QB)
        srow = st_ref[:, qr]
        dqs[...] = jnp.zeros_like(dqs)

        def step(masked, j, carry):
            kat = pl.multiple_of(j * QB, QB)
            kr = pl.ds(kat, QB)
            if masked:
                mask = attn_mask(kat, at, srow)
            scores, softs, grads = [], [], []
            for h in range(heads):
                lanes = lanes_of(h // 2)
                one = lax.dot_general(ks[kr, lanes], qm[h % 2, qr, lanes], NT, preferred_element_type=f32)
                back = lax.dot_general(vs[kr, lanes], dom[h % 2, qr, lanes], NT, preferred_element_type=f32)
                scores.append((jnp.where(mask, one, NEG) if masked else one, back))
            for h in range(heads):
                soft = jnp.exp(scores[h][0] - lse_ref[h : h + 1, qr])
                grads.append((soft * (scores[h][1] - dlt[h : h + 1, qr])).astype(bf))
                softs.append(soft.astype(bf))
            for g in range(pairs):
                lanes = lanes_of(g)
                both = lambda ref: jnp.concatenate([ref[0, qr, lanes], ref[1, qr, lanes]], axis=0)
                two = slice(2 * g, 2 * g + 2)
                dvs[kr, lanes] += jnp.dot(jnp.concatenate(softs[two], axis=1), both(dom), preferred_element_type=f32)
                dks[kr, lanes] += jnp.dot(jnp.concatenate(grads[two], axis=1), both(qm), preferred_element_type=f32)
                for h in (2 * g, 2 * g + 1):
                    sub = slice(h * HD, (h + 1) * HD)
                    dqs[sub] += jnp.dot(kt[sub, kr], grads[h], preferred_element_type=f32)
            return carry

        over_blocks(bounds, i, step, 0)
        qm[0, qr] = (dqs[...] * (HD**-0.5)).T.astype(bf)
        return 0

    lax.fori_loop(0, nb, qblock, 0)
    for dst, base in ((dkeep, c * half), (dsend, (1 - c) * half)):
        rows = pl.ds(pl.multiple_of(base, half), half)
        for g in range(pairs):
            for k, value in enumerate((qm[0, rows, lanes_of(g)], dks[rows, lanes_of(g)], dvs[rows, lanes_of(g)])):
                dst[:, (3 * g + k) * 128 : (3 * g + k + 1) * 128] = value.astype(bf)


def attn_bwd(own, recv, do_own, do_recv, o_own, o_recv, starts, lse, info):
    half, cols = own.shape[0], own.shape[1] // 3
    n = 2 * half
    return pl.pallas_call(
        bwd_kernel,
        in_specs=[SM, SM] + [VM] * 8,
        out_specs=[VM] * 2,
        scratch_shapes=[
            pltpu.VMEM((2, n, cols), bf), pltpu.VMEM((n, cols), bf), pltpu.VMEM((n, cols), bf), pltpu.VMEM((cols, n), bf),
            pltpu.VMEM((2, n, cols), bf), pltpu.VMEM((cols // HD, n), f32), pltpu.VMEM((cols, QB), f32),
            pltpu.VMEM((n, cols), f32), pltpu.VMEM((n, cols), f32)],
        out_shape=[like((half, 3 * cols), bf)] * 2,
        cost_estimate=pl.CostEstimate(flops=n * n, bytes_accessed=n * 128, transcendentals=0),
        compiler_params=pltpu.CompilerParams(vmem_limit_bytes=56 << 20),
    )(info, starts, own, recv, do_own, do_recv, o_own, o_recv, starts, lse)


def dot(left, right, dims=(((1,), (0,)), ((), ()))):
    return lax.dot_general(left, right, dims, preferred_element_type=f32)


def exchange(value, bit, dp_size):
    if bit:
        return lax.ppermute(value, "dp", [(i, i ^ bit) for i in range(dp_size)])
    return lax.ppermute(value, "tensor", [(0, 1), (1, 0)])


def flip(index, bits):
    for bit in bits:
        index = index + bit * (1 - 2 * ((index // bit) % 2))
    return index

def far_groups(dp_size):
    far = [1 << k for k in range(dp_size.bit_length() - 2, 1, -1)]
    return [tuple(far[k : k + 2]) for k in range(0, len(far), 2)]

def group_moves(group):
    if len(group) == 1:
        return [(1, group)]
    return [(1, group[:1]), (2, group[1:]), (3, group)]

def chunks_of(cols, which, count, until=None):
    tiles = cols // 128
    cuts = [128 * ((tiles * k) // count) for k in range(count + 1)]
    arrays = range(which, until + 1) if until else (which,)
    return tuple(
        (array, low, high - low, high - low - 128)
        for low, high in zip(cuts, cuts[1:]) for array in arrays)


def head_kernel(groups, chunks, tokens, seg, *refs):
    shards, x_out, seg_out, outs, (send_sem, recv_sem, local_sem) = refs[:4], refs[4], refs[5], refs[6:10], refs[10:]
    dp, t = lax.axis_index("dp"), lax.axis_index("tensor")
    core = dp % 2
    away = core + t - 2 * core * t
    near = {1: (flip(dp, (1,)), t), 2: (flip(dp, (2,)), t), 0: (dp, 1 - t)}
    distant = [bits for group in groups for _, bits in group_moves(group)]
    swap = (dp - core + t, core)
    barrier = pltpu.get_barrier_semaphore()
    for device in list(near.values()) + [(flip(dp, bits), t) for bits in distant]:
        pl.semaphore_signal(barrier, inc=1, device_id=device, device_id_type=MESH_ID)

    @pl.when(away == 1)
    def _():
        pl.semaphore_signal(barrier, inc=1, device_id=swap, device_id_type=MESH_ID)

    local = [
        pltpu.make_async_copy(shards[k], outs[k].at[away, 0] if k < 2 else outs[k].at[0], local_sem.at[k]) for k in range(4)]
    for copy in local:
        copy.start()
    pl.semaphore_wait(barrier, len(near) + len(distant) + away)
    count = [0]

    def remote(src, dst, device):
        slot = count[0]
        count[0] += 1
        return pltpu.make_async_remote_copy(
            src_ref=src, dst_ref=dst, send_sem=send_sem.at[slot], recv_sem=recv_sem.at[slot],
            device_id=device, device_id_type=MESH_ID)

    def blocks(ref, index, first, held, low, size):
        return ref.at[index, pl.ds(first, held), :, pl.ds(low, size)]

    plans = []
    for which, low, size, part in chunks:
        shard, out = shards[which], outs[which]
        steps, held = [], 1
        for group in groups:
            moves = []
            for place, bits in group_moves(group):
                src = shard.at[:, pl.ds(low, size)] if held == 1 else blocks(out, away, 0, held, low, size)
                dst = out.at[away, place, :, pl.ds(low, size)] if held == 1 else blocks(out, away, place * held, held, low, size)
                moves.append(remote(src, dst, (flip(dp, bits), t)))
            held *= len(group_moves(group)) + 1
            steps.append(moves)
        a, b = (low, part), (low + part, size - part)
        steps.append([
            remote(blocks(out, away, 0, held, *a), blocks(out, away, 0, held, *a), near[0]),
            remote(blocks(out, away, 0, held, *b), blocks(out, away, held, held, *b), near[2]),
        ])
        steps.append(
            [remote(blocks(out, k, 0, held, *a), blocks(out, k, held, held, *a), near[2]) for k in range(2)]
            + [remote(blocks(out, away, 0, 2 * held, *b), blocks(out, away, 0, 2 * held, *b), near[0])])
        steps.append([
            remote(blocks(out, k, 0, 2 * held, low, size),
                   blocks(out, 1 - k, 2 * held, 2 * held, low, size), near[1]) for k in range(2)])
        plans.append(steps)
    later = []
    held = 1
    for group in groups:
        moves = []
        for place, bits in group_moves(group):
            for shard, out in zip(shards[2:], outs[2:]):
                src = shard if held == 1 else out.at[pl.ds(0, held)]
                dst = out.at[place] if held == 1 else out.at[pl.ds(place * held, held)]
                moves.append(remote(src, dst, (flip(dp, bits), t)))
        held *= len(group_moves(group)) + 1
        later.append(moves)
    depth = len(plans[0])
    swap_copy = remote(tokens, x_out, swap)
    seg_copy = remote(seg, seg_out, near[1])
    stay_copy = pltpu.make_async_copy(tokens, x_out, local_sem.at[4])
    waited = set()

    def advance(number, phase):
        if number >= len(plans):
            return
        if phase > 0:
            for move in plans[number][phase - 1]:
                move.wait_recv()
        if phase == 1 and chunks[number][0] not in waited:
            waited.add(chunks[number][0])
            local[chunks[number][0]].wait()
        if phase < depth:
            for move in plans[number][phase]:
                move.start()

    advance(0, 0)
    seg_copy.start()

    @pl.when(away == 1)
    def _():
        swap_copy.start()

    @pl.when(away == 0)
    def _():
        stay_copy.start()

    far = len(groups)
    for number in range(len(plans)):
        if number == 0:
            for phase in range(1, far + 1):
                advance(0, phase)
            for k in range(1, len(plans)):
                advance(k, 0)
            for move in later[0]:
                move.start()
        advance(number, far + 1)
        for phase in range(1, far + 1):
            advance(number + 1, phase)
        advance(number, far + 2)
    for number in range(len(plans)):
        advance(number, depth)

    @pl.when(away == 1)
    def _():
        swap_copy.wait()

    @pl.when(away == 0)
    def _():
        stay_copy.wait()

    seg_copy.wait()
    for which in sorted(set(range(4)) - waited):
        local[which].wait()
    for k, moves in enumerate(later):
        if k > 0:
            for move in moves:
                move.start()
        for move in moves:
            move.wait()
    for steps in plans:
        for moves in steps:
            for move in moves:
                move.wait_send()


def head(dp_size, tokens, seg, shards, chunks):
    groups = far_groups(dp_size)
    partners = sum(len(group_moves(g)) for g in groups)
    slots = len(chunks) * (partners + 7) + 2 * partners + 2
    shapes = [(2, dp_size)] * 2 + [(dp_size // 4,)] * 2
    return pl.pallas_call(
        functools.partial(head_kernel, groups, chunks),
        in_specs=[VM] * 6,
        out_specs=[ANY] * 6,
        out_shape=[jax.ShapeDtypeStruct(a.shape, a.dtype) for a in (tokens, seg)]
        + [jax.ShapeDtypeStruct(lead + s.shape, s.dtype) for lead, s in zip(shapes, shards)],
        scratch_shapes=[pltpu.SemaphoreType.DMA((slots,)), pltpu.SemaphoreType.DMA((slots,)), pltpu.SemaphoreType.DMA((5,))],
        compiler_params=pltpu.CompilerParams(collective_id=0, has_side_effects=True),
    )(tokens, seg, *shards)


def tail_kernel(groups, tokens, own_lo, own_hi, rest_lo, rest_hi, small_lo, small_hi, feed, x_out, total, vecs, feed_total,
                feed_part, feed_got, part, got_core, got_near, got_last, got_far, vec, vec_core, vec_two, vec_one, vec_far, send_sem, recv_sem):
    dp, t = lax.axis_index("dp"), lax.axis_index("tensor")
    core = dp % 2
    away = core + t - 2 * core * t
    near = {1: (flip(dp, (1,)), t), 2: (flip(dp, (2,)), t), 0: (dp, 1 - t)}
    distant = [bits for group in groups for _, bits in group_moves(group)]
    swap = (dp - core + t, core)
    barrier = pltpu.get_barrier_semaphore()
    for device in list(near.values()) + [(flip(dp, bits), t) for bits in distant]:
        pl.semaphore_signal(barrier, inc=1, device_id=device, device_id_type=MESH_ID)

    @pl.when(away == 1)
    def _():
        pl.semaphore_signal(barrier, inc=1, device_id=swap, device_id_type=MESH_ID)

    pl.semaphore_wait(barrier, len(near) + len(distant) + away)
    count = [0]

    def remote(src, dst, device):
        slot = count[0]
        count[0] += 1
        return pltpu.make_async_remote_copy(
            src_ref=src, dst_ref=dst, send_sem=send_sem.at[slot], recv_sem=recv_sem.at[slot],
            device_id=device, device_id_type=MESH_ID)

    swap_copy = remote(tokens, x_out, swap)
    half, rows, cols = own_lo.shape
    quarter = half // 2
    chunks = [pl.ds(low, min(512, cols - low)) for low in range(0, cols, 512)]
    to_core = [[
        remote(rest_hi.at[:, :, c], got_core.at[0, :, :, c], near[1]),
        remote(own_hi.at[:, :, c], got_core.at[1, :, :, c], near[1])] for c in chunks]
    to_core[0].append(remote(small_hi, vec_core, near[1]))
    for moves in to_core:
        for move in moves:
            move.start()

    @pl.when(away == 1)
    def _():
        swap_copy.start()

    feed_steps = []
    held, used = feed.shape[0], 0
    for number, group in enumerate(reversed(groups)):
        moves = group_moves(group)
        held //= len(moves) + 1
        source, step = feed if number == 0 else feed_part, []
        for place, bits in moves:
            step.append(remote(source.at[pl.ds(place * held, held)], feed_got.at[pl.ds(used, held)], (flip(dp, bits), t)))
            used += held
        feed_steps.append((step, source, held, used - held * len(moves), len(moves)))
    for move in feed_steps[0][0]:
        move.start()

    def add(*terms):
        out = terms[0].astype(f32)
        for term in terms[1:]:
            out = out + term.astype(f32)
        return out.astype(bf)

    upper, lower = pl.ds(quarter, quarter), pl.ds(0, quarter)
    mine, other = away, 1 - away
    last = len(chunks) - 1
    steps, sent = {}, []

    def start(key, moves):
        steps[key] = moves
        sent.extend(moves)
        for move in moves:
            move.start()

    def arrive(key):
        for move in steps[key]:
            move.wait_recv()

    def core_stage(k):
        for move in to_core[k]:
            move.wait_recv()
        c = chunks[k]

        def body(q, _):
            part[0, q, :, c] = add(own_lo[q, :, c], got_core[0, q, :, c])
            part[1, q, :, c] = add(rest_lo[q, :, c], got_core[1, q, :, c])
            if k == 0:
                vec[q] = add(small_lo[q], vec_core[q])
            return 0

        lax.fori_loop(0, half, body, 0)
        start(("x", k), [
            remote(part.at[g, upper, :, c], got_near.at[g, lower, :, c], near[2]) for g in range(2)]
            + ([remote(vec.at[upper], vec_two, near[2])] if k == 0 else []))

    def x_stage(k):
        arrive(("x", k))
        c = chunks[k]

        def body(q, _):
            for g in range(2):
                part[g, q, :, c] = add(part[g, q, :, c], got_near[g, q, :, c])
            if k == 0:
                vec[q] = add(vec[q], vec_two[q])
            return 0

        lax.fori_loop(0, quarter, body, 0)
        start(("y", k), [remote(part.at[other, lower, :, c], got_last.at[:, :, c], near[0])]
              + ([remote(vec.at[lower], vec_one, near[0])] if k == 0 else []))

    def far_moves(number, k):
        held, used = quarter, 0
        for index, group in enumerate(reversed(groups)):
            moves = group_moves(group)
            held //= len(moves) + 1
            if index == number:
                out = []
                for m, (place, bits) in enumerate(moves):
                    device, c = (flip(dp, bits), t), chunks[k]
                    out.append(remote(part.at[mine, pl.ds(place * held, held), :, c], got_far.at[pl.ds(used + m * held, held), :, c], device))
                    if k == 0:
                        out.append(remote(vec_one.at[pl.ds(place * held, held)], vec_far.at[pl.ds(used + m * held, held)], device))
                return out, held, used, len(moves)
            used += held * len(moves)

    def y_stage(k):
        arrive(("y", k))
        c = chunks[k]

        def body(q, _):
            part[mine, q, :, c] = add(part[mine, q, :, c], got_last[q, :, c])
            if k == 0:
                vec_one[q] = add(vec[q], vec_one[q])
            return 0

        lax.fori_loop(0, quarter, body, 0)
        start(("z", 0, k), far_moves(0, k)[0])

    far_shape = []
    held, used = quarter, 0
    for group in reversed(groups):
        moves = len(group_moves(group))
        held //= moves + 1
        far_shape.append((held, used, moves))
        used += held * moves

    def z_stage(number, k):
        arrive(("z", number, k))
        c = chunks[k]
        held, base, moves = far_shape[number]

        def body(q, _):
            part[mine, q, :, c] = add(part[mine, q, :, c], *[got_far[base + m * held + q, :, c] for m in range(moves)])
            if k == 0:
                vec_one[q] = add(vec_one[q], *[vec_far[base + m * held + q] for m in range(moves)])
            return 0

        lax.fori_loop(0, held, body, 0)
        if number + 1 < len(groups):
            start(("z", number + 1, k), far_moves(number + 1, k)[0])

    for k in range(last + 1):
        core_stage(k)
    for k in range(last + 1):
        x_stage(k)
        if k > 0:
            y_stage(k - 1)
    y_stage(last)
    for number in range(len(groups)):
        for k in range(last + 1):
            z_stage(number, k)
    to_far = []
    for number, (step, source, held, base, moves) in enumerate(feed_steps):
        if number > 0:
            for move in step:
                move.start()
        for move in step:
            move.wait_recv()

        def sum_feed(k, _, source=source, held=held, base=base, moves=moves):
            feed_part[k] = add(source[k], *[feed_got[base + m * held + k] for m in range(moves)])
            return 0

        if number + 1 < len(feed_steps):
            lax.fori_loop(0, held, sum_feed, 0)
        else:
            out = source[0].astype(f32)
            for m in range(moves):
                out = out + feed_got[base + m * held].astype(f32)
            feed_total[...] = out
        to_far += step
    total[...] = part[mine, 0].astype(f32)
    vecs[...] = vec_one[0].astype(f32)

    @pl.when(away == 1)
    def _():
        swap_copy.wait()

    for move in sum(to_core, []) + sent + to_far:
        move.wait_send()


def tail(dp_size, tokens, own, rest, small, feed):
    groups = far_groups(dp_size)
    half, rows, cols = own[0].shape
    quarter = half // 2
    wide = small[0].shape[2]
    partners = sum(len(group_moves(g)) for g in groups)
    slots = (-(-cols // 512)) * (5 + partners) + 4 + 2 * partners + 1
    return pl.pallas_call(
        functools.partial(tail_kernel, groups),
        in_specs=[VM] * 8,
        out_specs=[ANY, VM, VM, VM],
        out_shape=[
            jax.ShapeDtypeStruct(tokens.shape, bf), jax.ShapeDtypeStruct((rows, cols), f32),
            jax.ShapeDtypeStruct((rows, wide), f32), jax.ShapeDtypeStruct(feed.shape[1:], f32)],
        scratch_shapes=[
            pltpu.VMEM(feed.shape, bf), pltpu.VMEM(feed.shape, bf),
            pltpu.VMEM((2, half, rows, cols), bf), pltpu.VMEM((2, half, rows, cols), bf), pltpu.VMEM((2, half, rows, cols), bf),
            pltpu.VMEM((quarter, rows, cols), bf), pltpu.VMEM((quarter, rows, cols), bf),
            pltpu.VMEM((half, rows, wide), bf), pltpu.VMEM((half, rows, wide), bf), pltpu.VMEM((quarter, rows, wide), bf),
            pltpu.VMEM((quarter, rows, wide), bf), pltpu.VMEM((quarter, rows, wide), bf),
            pltpu.SemaphoreType.DMA((slots,)), pltpu.SemaphoreType.DMA((slots,))],
        compiler_params=pltpu.CompilerParams(collective_id=1, has_side_effects=True, vmem_limit_bytes=48 << 20),
    )(tokens, *own, *rest, *small, feed)


def add_low(*terms):
    out = terms[0].astype(f32)
    for term in terms[1:]:
        out = out + term.astype(f32)
    return out.astype(bf)


def order_matrix(owner, rows, width):
    place = lax.broadcasted_iota(jnp.int32, (1, width), 1)
    block = place // rows
    count = width // rows
    natural = place % rows
    for k, bit in enumerate([1 << b for b in range(count.bit_length() - 2, 1, -1)] + [2, 1]):
        on, base = (block // (1 << k)) % 2, (owner // bit) % 2
        natural = natural + (on + base - 2 * on * base) * (bit * rows)
    return (lax.broadcasted_iota(jnp.int32, (width, width), 0) == natural).astype(f32).astype(bf)


def norm_parts(values):
    centered = values - jnp.mean(values, axis=-1, keepdims=True)
    inverse = lax.rsqrt(jnp.mean(centered * centered, axis=-1, keepdims=True) + EPSILON)
    return centered * inverse, inverse


def norm_back(hat, inverse, gain, grad):
    scaled = grad * gain
    return inverse * (
        scaled - jnp.mean(scaled, axis=-1, keepdims=True) - hat * jnp.mean(scaled * hat, axis=-1, keepdims=True))


def over_rows(total, body):
    def step(k, _):
        body(pl.ds(pl.multiple_of(k * ROWS, ROWS), ROWS))
        return 0

    lax.fori_loop(0, total // ROWS, step, 0)


def column_sum(ref, row, values):
    ref[row : row + 1] += jnp.sum(values, axis=0, keepdims=True)


def bias_row(vec_nat, group, cols):
    lanes = pl.ds(pl.multiple_of(group * cols, 128), cols)
    q, v = vec_nat[2:3, lanes], vec_nat[3:4, lanes]
    parts = []
    for g in range(cols // 128):
        part = slice(g * 128, (g + 1) * 128)
        parts += [q[:, part], jnp.zeros((1, 128), f32), v[:, part]]
    return jnp.concatenate(parts, axis=1)


def fan_matrix(fan):
    row = lax.broadcasted_iota(jnp.int32, (128 * fan, 1), 0)
    unit = lax.broadcasted_iota(jnp.int32, (128 * fan, 128 * fan), 1)
    return (unit == (row % 128) * fan + row // 128).astype(f32).astype(bf)


def first_kernel(rows, fan, info, tokens, pack, weight, seg, seg_other, x_out, n1_out, send, vec_rel, vec_nat, fc_bias, starts, order, fan_rows):
    width, cols = tokens.shape[1], weight.shape[2] // 3

    @pl.when(pl.program_id(0) == 0)
    def _():
        order[...] = order_matrix(info[1], rows, width)
        small = pack[0, :, cols:].astype(f32).T[:VECS]
        vec_rel[...] = small
        vec_nat[...] = lax.dot_general(small.astype(bf), order[...], NT, preferred_element_type=f32)
        count = width // 128
        fan_rows[...] = jnp.zeros_like(fan_rows)
        for k in range(count):
            for m in range(fan):
                fan_rows[k : k + 1, m * 128 : (m + 1) * 128] = vec_nat[8 + m : 9 + m, k * 128 : (k + 1) * 128]
        bias = jnp.dot(fan_rows[...].astype(bf), fan_matrix(fan), preferred_element_type=f32)
        for k in range(count):
            fc_bias[:, k * 128 * fan : (k + 1) * 128 * fan] = bias[k : k + 1]
        docs = jnp.where(info[2] == 1, seg[...], seg_other[...]).astype(f32)
        begin = jnp.zeros_like(docs)
        for d in range(1, 16):
            before = jnp.sum(jnp.where(docs < d, 1.0, 0.0), axis=1, keepdims=True)
            begin = jnp.where(docs == d, before, begin)
        starts[...] = begin.astype(jnp.int32)

    x = jnp.dot(tokens[...], order[...], preferred_element_type=f32)
    hat, _ = norm_parts(x)
    n1 = (hat * vec_rel[0:1] + vec_rel[1:2]).astype(bf)
    x_out[...] = x.astype(bf)
    n1_out[...] = n1
    send[...] = (jnp.dot(n1, weight[0], preferred_element_type=f32) + bias_row(vec_nat, 1 - info[0], cols)).astype(bf)


def own_kernel(n1, send, weights, vec_nat, out, recv, weight, send_sem, recv_sem, local_sem):
    dp, t = lax.axis_index("dp"), lax.axis_index("tensor")
    partner = (flip(dp, (1,)), t)
    barrier = pltpu.get_barrier_semaphore()
    pl.semaphore_signal(barrier, inc=1, device_id=partner, device_id_type=MESH_ID)
    load = pltpu.make_async_copy(weights.at[0], weight, local_sem.at[0])
    load.start()
    pl.semaphore_wait(barrier, 1)
    copy = pltpu.make_async_remote_copy(
        src_ref=send, dst_ref=recv, send_sem=send_sem.at[0], recv_sem=recv_sem.at[0], device_id=partner, device_id_type=MESH_ID)
    copy.start()
    load.wait()
    bias = bias_row(vec_nat, dp % 2, weight.shape[1] // 3)

    def body(at):
        out[at] = (jnp.dot(n1[at], weight[...], preferred_element_type=f32) + bias).astype(bf)

    over_rows(n1.shape[0], body)
    copy.wait()


def picked(array, index):
    return pl.BlockSpec((1,) + array.shape[1:], lambda k, s: (index, 0, 0))


def whole(array):
    return pl.BlockSpec(array.shape, lambda k, s: (0,) * len(array.shape))


def one_call(kernel, info, inputs, specs, outs, scratch=(), limit=56):
    return pl.pallas_call(
        kernel,
        grid_spec=pltpu.PrefetchScalarGridSpec(
            num_scalar_prefetch=1, grid=(1,), in_specs=[s if s is not None else whole(a) for a, s in zip(inputs, specs)],
            out_specs=[whole(o) for o in outs], scratch_shapes=list(scratch)),
        out_shape=outs,
        cost_estimate=pl.CostEstimate(flops=1 << 22, bytes_accessed=1 << 18, transcendentals=0),
        compiler_params=pltpu.CompilerParams(vmem_limit_bytes=limit << 20),
    )(info, *inputs)


def like(shape, dtype):
    return jax.ShapeDtypeStruct(shape, dtype)


def by_rows(kernel, info, inputs, specs, outs, scratch=(), flops=1 << 22):
    total = inputs[0].shape[0]

    def spec(array, given=None):
        if given is not None:
            return given
        if array.shape[0] == total:
            return pl.BlockSpec((ROWS,) + array.shape[1:], lambda k, s: (k, 0))
        return whole(array)

    return pl.pallas_call(
        kernel,
        grid_spec=pltpu.PrefetchScalarGridSpec(
            num_scalar_prefetch=1, grid=(total // ROWS,), in_specs=[spec(a, g) for a, g in zip(inputs, specs)],
            out_specs=[spec(o) for o in outs], scratch_shapes=list(scratch)),
        out_shape=outs,
        cost_estimate=pl.CostEstimate(flops=flops, bytes_accessed=1 << 18, transcendentals=0),
        compiler_params=pltpu.CompilerParams(vmem_limit_bytes=60 << 20),
    )(info, *inputs)


def project_first(info, rows, fan, tokens, packs, weights, seg, seg_other):
    n, width = tokens.shape
    vecs = like((VECS, width), f32)
    return by_rows(
        functools.partial(first_kernel, rows, fan), info, (tokens, packs, weights, seg, seg_other),
        (None, picked(packs, 0), picked(weights, 1), None, None),
        [like((n, width), bf), like((n, width), bf), like((n, weights.shape[2]), bf), vecs, vecs, like((1, width * fan), f32),
         like(seg.shape, jnp.int32)],
        [pltpu.VMEM((width, width), bf), pltpu.VMEM((8, 128 * fan), f32)])


def project_own(n1, send, weights, vec_nat):
    return pl.pallas_call(
        own_kernel,
        in_specs=[VM, ANY, ANY, VM],
        out_specs=[VM, ANY],
        out_shape=[like(send.shape, bf)] * 2,
        scratch_shapes=[
            pltpu.VMEM(weights.shape[1:], bf), pltpu.SemaphoreType.DMA((1,)), pltpu.SemaphoreType.DMA((1,)),
            pltpu.SemaphoreType.DMA((1,))],
        compiler_params=pltpu.CompilerParams(collective_id=3, has_side_effects=True, vmem_limit_bytes=24 << 20),
    )(n1, send, weights, vec_nat)


def middle_kernel(rows, x, o_own, o_send, cot, cot_recv, packs, vec_rel, fc00, fc01, fc10, fc11, pr0, pr1,
                  middle, n2, cot_rel, d_mlp, o_recv, fc_got, pr_got, order, send_sem, recv_sem):
    dp, t = lax.axis_index("dp"), lax.axis_index("tensor")
    core = dp % 2
    away = core + t - 2 * core * t
    partner = (flip(dp, (1,)), t)
    barrier = pltpu.get_barrier_semaphore()
    pl.semaphore_signal(barrier, inc=1, device_id=partner, device_id_type=MESH_ID)
    pl.semaphore_wait(barrier, 1)
    size = fc00.shape[0]
    copies = [
        pltpu.make_async_remote_copy(
            src_ref=src, dst_ref=dst, send_sem=send_sem.at[k], recv_sem=recv_sem.at[k], device_id=partner, device_id_type=MESH_ID)
        for k, (src, dst) in enumerate((
            (o_send, o_recv), (fc00, fc_got.at[0, pl.ds(0, size)]), (fc01, fc_got.at[0, pl.ds(size, size)]), (pr0, pr_got.at[0]),
            (fc10, fc_got.at[1, pl.ds(0, size)]), (fc11, fc_got.at[1, pl.ds(size, size)]), (pr1, pr_got.at[1])))]
    for copy in copies:
        copy.start()
    order[...] = order_matrix(dp, rows, x.shape[1])
    cols = o_own.shape[1]

    def cot_rows(at):
        grad = jnp.dot(jnp.where(away == 0, cot[at], cot_recv[at]), order[...], preferred_element_type=f32)
        cot_rel[at] = grad.astype(bf)
        d_mlp[at] = (BRANCH_SCALE * grad).astype(bf)

    over_rows(x.shape[0], cot_rows)
    copies[0].wait_recv()

    def body(at):
        branch = lax.dot_general(o_own[at], packs[0, :, :cols], NT, preferred_element_type=f32)
        branch = branch + lax.dot_general(o_recv[at], packs[1, :, :cols], NT, preferred_element_type=f32)
        mid = x[at].astype(f32) + BRANCH_SCALE * (branch + vec_rel[4:5])
        middle[at] = mid
        hat, _ = norm_parts(mid)
        n2[at] = (hat * vec_rel[5:6] + vec_rel[6:7]).astype(bf)

    over_rows(x.shape[0], body)
    for copy in copies[1:]:
        copy.wait_recv()
    for copy in copies:
        copy.wait_send()


def middle_part(rows, x, o_own, o_send, cot, cot_recv, packs, vec_rel, fc_parts, proj_parts):
    shape, half = x.shape, x.shape[1] // 2
    hidden = proj_parts[0].shape[1]
    got = like((2, half, hidden), bf)
    return pl.pallas_call(
        functools.partial(middle_kernel, rows),
        in_specs=[VM] * 7 + [ANY] * 6,
        out_specs=[VM] * 5 + [ANY] * 2,
        out_shape=[like(shape, f32), like(shape, bf), like(shape, bf), like(shape, bf), like(o_send.shape, bf), got, got],
        scratch_shapes=[
            pltpu.VMEM((shape[1], shape[1]), bf), pltpu.SemaphoreType.DMA((7,)), pltpu.SemaphoreType.DMA((7,))],
        compiler_params=pltpu.CompilerParams(collective_id=2, has_side_effects=True, vmem_limit_bytes=36 << 20),
    )(x, o_own, o_send, cot, cot_recv, packs, vec_rel, *fc_parts[0], *fc_parts[1], *proj_parts)


def after_kernel(rows, info, middle, mlp, back, cot, packs, vec_rel, block_out, d_middle, d_attn, do_own, do_send, sums, order):
    @pl.when(pl.program_id(0) == 0)
    def _():
        order[...] = order_matrix(info[1], rows, middle.shape[1])
        sums[...] = jnp.zeros_like(sums)

    cols = do_own.shape[1]
    mid = middle[...]
    out = (mid + BRANCH_SCALE * (mlp[...] + vec_rel[7:8])).astype(bf)
    block_out[...] = lax.dot_general(out, order[...], NT, preferred_element_type=f32).astype(bf)
    hat, inverse = norm_parts(mid)
    grad = back[...]
    out_grad = cot[...].astype(f32)
    entire = out_grad + norm_back(hat, inverse, vec_rel[5:6], grad)
    d_middle[...] = entire
    low = (BRANCH_SCALE * entire).astype(bf)
    d_attn[...] = low
    do_own[...] = jnp.dot(low, packs[0, :, :cols], preferred_element_type=f32).astype(bf)
    do_send[...] = jnp.dot(low, packs[1, :, :cols], preferred_element_type=f32).astype(bf)
    column_sum(sums, 0, BRANCH_SCALE * entire)
    column_sum(sums, 1, grad * hat)
    column_sum(sums, 2, grad)
    column_sum(sums, 3, BRANCH_SCALE * out_grad)


def after_part(info, rows, middle, mlp, back, cot, packs, vec_rel, cols):
    shape = middle.shape
    slim = like((shape[0], cols), bf)
    return by_rows(
        functools.partial(after_kernel, rows), info, (middle, mlp, back, cot, packs, vec_rel), (None,) * 6,
        [like(shape, bf), like(shape, f32), like(shape, bf), slim, slim, like((8, shape[1]), f32)],
        [pltpu.VMEM((shape[1], shape[1]), bf)])


def feed_kernel(info, n2, d_mlp, bias, fc_got, pr_got, fc00, fc01, fc10, fc11, pr0, pr1,
                acc, back, fc_lo, fc_hi, pr_lo, pr_hi, d_bias, n2_t, d_t, w_fc, w_pr, act, d_pre):
    step = pl.program_id(0)
    total, half = n2.shape[0], n2.shape[1] // 2

    @pl.when(step == 0)
    def _():
        acc[...] = jnp.zeros_like(acc)
        back[...] = jnp.zeros_like(back)
        n2_t[...] = n2[...].T
        d_t[...] = d_mlp[...].T

    @pl.when(step < pl.num_programs(0) // 2)
    def _():
        w_fc[: half // 2], w_fc[half // 2 : half], w_pr[:half] = fc00[...], fc01[...], pr0[...]

    @pl.when(step >= pl.num_programs(0) // 2)
    def _():
        w_fc[: half // 2], w_fc[half // 2 : half], w_pr[:half] = fc10[...], fc11[...], pr1[...]

    w_fc[half:], w_pr[half:] = fc_got[0], pr_got[0]
    root = 0.7978845608
    count = total // ROWS
    raw = {}
    grad_sum = jnp.zeros((1, w_fc.shape[1]), f32)

    def products(k):
        at = slice(k * ROWS, (k + 1) * ROWS)
        return (
            jnp.dot(n2[at], w_fc[...], preferred_element_type=f32) + bias[...],
            jnp.dot(d_mlp[at], w_pr[...], preferred_element_type=f32))

    def add_back(k):
        at = slice(k * ROWS, (k + 1) * ROWS)
        acc[at] += lax.dot_general(act[at], w_pr[...], NT, preferred_element_type=f32)
        back[at] += lax.dot_general(d_pre[at], w_fc[...], NT, preferred_element_type=f32)

    raw[0] = products(0)
    for k in range(count):
        at = slice(k * ROWS, (k + 1) * ROWS)
        if k + 1 < count:
            raw[k + 1] = products(k + 1)
        pre, d_act = raw.pop(k)
        square = pre * pre
        inner = jnp.tanh(pre * (root + root * 0.044715 * square))
        gate = 0.5 + 0.5 * inner
        act[at] = (pre * gate).astype(bf)
        slope = gate + pre * (0.5 - 0.5 * inner * inner) * (root + root * 3 * 0.044715 * square)
        grad = d_act * slope
        grad_sum = grad_sum + jnp.sum(grad, axis=0, keepdims=True)
        d_pre[at] = grad.astype(bf)
        if k > 0:
            add_back(k - 1)
    add_back(count - 1)
    d_bias[...] = grad_sum
    for out, left, right, low in (
        (fc_hi, n2_t, d_pre, half), (pr_hi, d_t, act, half), (fc_lo, n2_t, d_pre, 0), (pr_lo, d_t, act, 0)):
        out[0] = jnp.dot(left[low : low + half], right[...], preferred_element_type=f32).astype(bf)


def feed_part(info, n2, d_mlp, bias, fc_got, pr_got, fc_parts, proj_parts):
    (total, width), hidden, half = n2.shape, bias.shape[1] // 2, n2.shape[1] // 2
    steps = hidden // HIDDEN
    fixed = lambda a: pl.BlockSpec(a.shape, lambda k, s: (0,) * len(a.shape), pipeline_mode=pl.Buffered(1))
    early = lambda a: pl.BlockSpec((a.shape[0], HIDDEN), lambda k, s: (0, jnp.minimum(k, steps - 1)))
    late = lambda a: pl.BlockSpec((a.shape[0], HIDDEN), lambda k, s: (0, jnp.maximum(k - steps, 0)))
    two = lambda a: pl.BlockSpec((1, a.shape[1], HIDDEN), lambda k, s: (k // steps, 0, k % steps))
    unit = pl.BlockSpec((1, HIDDEN), lambda k, s: (0, (s[3] + (k // steps) * (1 - 2 * s[3])) * steps + k % steps))
    grad = like((2, half, hidden), bf)
    sums = [like((total, width), f32)] * 2
    return pl.pallas_call(
        feed_kernel,
        grid_spec=pltpu.PrefetchScalarGridSpec(
            num_scalar_prefetch=1,
            grid=(2 * steps,),
            in_specs=[fixed(n2), fixed(d_mlp), unit, two(fc_got), two(pr_got)]
            + [early(a) for a in fc_parts[0]] + [late(a) for a in fc_parts[1]] + [early(proj_parts[0]), late(proj_parts[1])],
            out_specs=[fixed(o) for o in sums] + [two(grad)] * 4 + [unit],
            scratch_shapes=[
                pltpu.VMEM((width, total), bf), pltpu.VMEM((width, total), bf), pltpu.VMEM((width, HIDDEN), bf),
                pltpu.VMEM((width, HIDDEN), bf), pltpu.VMEM((total, HIDDEN), bf), pltpu.VMEM((total, HIDDEN), bf)],
        ),
        out_shape=sums + [grad] * 4 + [like((1, 2 * hidden), f32)],
        cost_estimate=pl.CostEstimate(flops=1 << 22, bytes_accessed=1 << 18, transcendentals=0),
        compiler_params=pltpu.CompilerParams(vmem_limit_bytes=60 << 20),
    )(info, n2, d_mlp, bias, fc_got, pr_got, *fc_parts[0], *fc_parts[1], *proj_parts)


def grads_into(lo, hi, left_t, extra_t, d_qkv, o):
    half = left_t.shape[0] // 2
    wide = d_qkv.shape[1]
    for out, low in ((hi, half), (lo, 0)):
        out[:, :wide] = jnp.dot(left_t[low : low + half], d_qkv[...], preferred_element_type=f32).astype(bf)
        out[:, wide:] = jnp.dot(extra_t[low : low + half], o[...], preferred_element_type=f32).astype(bf)


def last_own_kernel(info, d_qkv, n1, d_attn, o_own, weight, lo, hi, part, sums, left_t, extra_t):
    left_t[...] = n1[...].T
    extra_t[...] = d_attn[...].T
    sums[...] = jnp.zeros_like(sums)
    grads_into(lo, hi, left_t, extra_t, d_qkv, o_own)

    def body(at):
        part[at] = lax.dot_general(d_qkv[at], weight[0], NT, preferred_element_type=f32)
        column_sum(sums, 0, d_qkv[at].astype(f32))

    over_rows(n1.shape[0], body)


def last_own(info, dq, n1, d_attn, o_own, weights):
    n, width = n1.shape
    wide, slim = weights.shape[2], o_own.shape[1]
    grad = like((width // 2, wide + slim), bf)
    return one_call(
        last_own_kernel, info, (dq, n1, d_attn, o_own, weights), (None,) * 4 + (picked(weights, 0),),
        [grad, grad, like((n, width), f32), like((8, wide), f32)],
        [pltpu.VMEM((width, n), bf), pltpu.VMEM((width, n), bf)])


def last_kernel(rows, fan, info, d_qkv, n1, d_attn, o_recv, weight, part, x, d_middle, vec_rel, own_sums, mid_sums, fc_grad,
                lo, hi, grad_out, small, left_t, extra_t, sums, vecs, nat, order, fan_rows):
    width, cols = x.shape[1], o_recv.shape[1]
    order[...] = order_matrix(info[1], rows, width)
    left_t[...] = n1[...].T
    extra_t[...] = d_attn[...].T
    sums[...] = jnp.zeros_like(sums)
    vecs[...] = jnp.zeros_like(vecs)
    grads_into(lo, hi, left_t, extra_t, d_qkv, o_recv)

    def body(at):
        grad = part[at] + lax.dot_general(d_qkv[at], weight[0], NT, preferred_element_type=f32)
        hat, inverse = norm_parts(x[at].astype(f32))
        grad_in = (d_middle[at] + norm_back(hat, inverse, vec_rel[0:1], grad)).astype(bf)
        grad_out[at] = lax.dot_general(grad_in, order[...], NT, preferred_element_type=f32).astype(bf)
        column_sum(sums, 0, d_qkv[at].astype(f32))
        column_sum(vecs, 0, grad * hat)
        column_sum(vecs, 1, grad)

    over_rows(x.shape[0], body)
    nat[...] = jnp.zeros_like(nat)
    for group, ref in ((info[0], own_sums), (1 - info[0], sums)):
        for row, part_index in ((0, 0), (1, 2)):
            picks = [ref[0:1, (3 * g + part_index) * 128 : (3 * g + part_index + 1) * 128] for g in range(cols // 128)]
            nat[row : row + 1, pl.ds(pl.multiple_of(group * cols, 128), cols)] = jnp.concatenate(picks, axis=1)
    count = width // 128
    fan_rows[...] = jnp.zeros_like(fan_rows)
    for k in range(count):
        fan_rows[k : k + 1] = fc_grad[:, k * 128 * fan : (k + 1) * 128 * fan]
    spread = lax.dot_general(fan_rows[...].astype(bf), fan_matrix(fan), NT, preferred_element_type=f32)
    for k in range(count):
        for m in range(fan):
            nat[2 + m : 3 + m, k * 128 : (k + 1) * 128] = spread[k : k + 1, m * 128 : (m + 1) * 128]
    moved = jnp.dot(nat[...].astype(bf), order[...], preferred_element_type=f32)
    vecs[2:4] = moved[0:2]
    vecs[4:8] = mid_sums[0:4]
    vecs[8 : 8 + fan] = moved[2 : 2 + fan]
    small[...] = vecs[...].T.astype(bf)


def last_part(info, rows, dq, n1, d_attn, o_recv, weights, part, x, d_middle, vec_rel, own_sums, mid_sums, fc_grad):
    n, width = n1.shape
    wide, slim = weights.shape[2], o_recv.shape[1]
    grad = like((width // 2, wide + slim), bf)
    inputs = (dq, n1, d_attn, o_recv, weights, part, x, d_middle, vec_rel, own_sums, mid_sums, fc_grad)
    fan = fc_grad.shape[1] // width
    return one_call(
        functools.partial(last_kernel, rows, fan), info, inputs, (None,) * 4 + (picked(weights, 1),) + (None,) * 7,
        [grad, grad, like((n, width), bf), like((width, SMALL), bf)],
        [pltpu.VMEM((width, n), bf), pltpu.VMEM((width, n), bf), pltpu.VMEM((8, wide), f32),
         pltpu.VMEM((SMALL, width), f32), pltpu.VMEM((8, width), f32), pltpu.VMEM((width, width), bf),
         pltpu.VMEM((8, 128 * fan), f32)])


def on_device(
    tokens, segment_ids, ln1_gain, ln1_bias, w_qkv, b_qv, w_attn_out, b_attn_out,
    ln2_gain, ln2_bias, w_fc, b_fc, w_proj, b_proj, cotangent,
):
    dp_size = lax.axis_size("dp")
    dp_pos, t_pos = lax.axis_index("dp"), lax.axis_index("tensor")
    core = dp_pos % 2
    rows = ln1_gain.shape[0]
    width = tokens.shape[1]
    cols = w_qkv.shape[2]
    hidden = w_fc.shape[1]
    fan = b_fc.shape[0] // rows
    far = [1 << k for k in range(dp_size.bit_length() - 2, 1, -1)]
    swap = []
    for d in range(dp_size):
        for t in range(2):
            if d % 2 != t:
                swap.append((2 * d + t, 2 * (d - d % 2 + t) + d % 2))
    mine = core == t_pos

    pairs = cols // 128

    def by_pair(parts):
        parts = parts.reshape(-1, 3, pairs, 128)
        return jnp.swapaxes(parts, 1, 2).reshape(-1, 3 * cols)

    def by_part(columns):
        return jnp.swapaxes(columns.reshape(-1, pairs, 3, 128), 1, 2).reshape(-1, 3, cols)

    flat = jnp.concatenate([ln1_gain, ln1_bias, b_qv.reshape(-1), b_attn_out, ln2_gain, ln2_bias, b_proj])
    small = jnp.concatenate([flat.reshape(8, rows).T, b_fc.reshape(rows, fan)], axis=1)
    small = jnp.pad(small, ((0, 0), (0, SMALL - small.shape[1])))
    out_pack = jnp.concatenate([w_attn_out.T, small], axis=1)
    tokens, seg_other, all_qkv, all_out, fc_far, proj_far = head(
        dp_size, tokens, segment_ids, (by_pair(w_qkv), out_pack, w_fc, w_proj.T), chunks_of(3 * cols, 0, 2) + chunks_of(cols + SMALL, 1, 1))
    all_qkv, all_out = (a.reshape(2, width, -1) for a in (all_qkv, all_out))
    fc_far, proj_far = fc_far.reshape(-1, hidden), proj_far.reshape(-1, hidden)
    fc_parts = [[fc_far], [exchange(fc_far, 0, dp_size)]]
    proj_half = exchange(proj_far, 2, dp_size)

    part = jnp.stack([core, dp_pos, jnp.where(mine, 1, 0), t_pos]).astype(jnp.int32)
    x, n1, qkv_send, vec_rel, vec_nat, fc_bias, starts = project_first(
        part, rows, fan, tokens, all_out, all_qkv, segment_ids, seg_other)
    qkv_own, qkv_recv = project_own(n1, qkv_send, all_qkv, vec_nat)
    fc_parts, proj_half, qkv_own = lax.optimization_barrier((fc_parts, proj_half, qkv_own))
    fc_parts = [p + [exchange(p[0], 2, dp_size)] for p in fc_parts]
    proj_half = jnp.concatenate([proj_far, proj_half], axis=0)
    proj_parts = [proj_half, exchange(proj_half, 0, dp_size)]
    o_own, o_send, lse = attn_fwd(qkv_own, qkv_recv, starts, part)
    cot_recv = lax.ppermute(cotangent, BOTH, swap)
    half = width // 2
    middle, n2, cot, d_mlp, o_recv, fc_got, pr_got = middle_part(
        rows, x, o_own, o_send, cotangent, cot_recv, all_out, vec_rel, fc_parts, proj_parts)
    mlp, back, fc_lo, fc_hi, pr_lo, pr_hi, fc_grad = feed_part(
        part, n2, d_mlp, fc_bias, fc_got, pr_got, fc_parts, proj_parts)
    fc_got, pr_got = exchange(fc_hi, 1, dp_size), exchange(pr_hi, 1, dp_size)
    block_out, d_middle, d_attn, do_own, do_send, mid_sums = after_part(
        part, rows, middle, mlp, back, cot, all_out, vec_rel, cols)
    do_recv = exchange(do_send, 1, dp_size)

    near_size = half // 2
    fc_rest = add_low(fc_lo[1], fc_got[1])
    pr_rest = add_low(pr_lo[:, near_size:], pr_got[:, near_size:])
    last = (qkv_own, qkv_recv, do_own, do_recv, o_own, o_send)
    last, fc_rest, pr_rest = lax.optimization_barrier((last, fc_rest, pr_rest))
    fc_sent = exchange(fc_rest, 0, dp_size)
    pr_sent = exchange(pr_rest, 2, dp_size)
    block_recv = lax.ppermute(block_out, BOTH, swap)
    dq_own, dq_send = attn_bwd(*last, starts, lse, part)
    dq_recv = exchange(dq_send, 1, dp_size)
    dq_own, fc_sent, pr_sent = lax.optimization_barrier((dq_own, fc_sent, pr_sent))
    fc_rest = add_low(fc_lo[0, near_size:], fc_got[0, near_size:], fc_sent[near_size:])
    pr_rest = add_low(pr_lo[1, :near_size], pr_got[1, :near_size], pr_sent[1])
    dq_own, fc_rest, pr_rest = lax.optimization_barrier((dq_own, fc_rest, pr_rest))
    fc_near = exchange(fc_rest, 2, dp_size)
    pr_near = exchange(pr_rest, 0, dp_size)
    own_lo, own_hi, d_n1, own_sums = last_own(part, dq_own, n1, d_attn, o_own, all_qkv)
    d_n1, fc_near, pr_near = lax.optimization_barrier((d_n1, fc_near, pr_near))
    sum_fc = add_low(fc_lo[0, :near_size], fc_got[0, :near_size], fc_sent[:near_size], fc_near)
    sum_proj = add_low(pr_lo[0, :near_size], pr_got[0, :near_size], pr_sent[0], pr_near)
    feed = jnp.concatenate([sum_fc, sum_proj], axis=1).reshape(-1, rows, 2 * hidden)
    d_n1, feed = lax.optimization_barrier((d_n1, feed))
    rest_lo, rest_hi, grad_tokens, d_small = last_part(
        part, rows, dq_recv, n1, d_attn, o_recv, all_qkv, d_n1, x, d_middle, vec_rel, own_sums, mid_sums, fc_grad)
    blocks = lambda arr: arr.reshape(dp_size // 2, rows, -1)
    grad_recv, sum_a, vecs, sum_feed = tail(
        dp_size, grad_tokens, (blocks(own_lo), blocks(own_hi)), (blocks(rest_lo), blocks(rest_hi)),
        (blocks(d_small[:half]), blocks(d_small[half:])), feed)
    vecs, block_recv = lax.optimization_barrier((vecs, block_recv))
    block_out = jnp.where(mine, block_out, block_recv)
    grad_tokens = jnp.where(mine, grad_tokens, grad_recv)
    return (
        block_out,
        grad_tokens,
        vecs[:, 0],
        vecs[:, 1],
        by_part(sum_a[:, : 3 * cols]),
        vecs[:, 2:4].T,
        sum_a[:, 3 * cols :].T,
        vecs[:, 4],
        vecs[:, 5],
        vecs[:, 6],
        sum_feed[:, :hidden],
        vecs[:, 8 : 8 + fan].reshape(rows * fan),
        sum_feed[:, hidden:].T,
        vecs[:, 7],
    )


def solution(mesh):
    vec, tok = P("dp"), P(BOTH, None)
    in_specs = (
        tok, P("dp", None), vec, vec, P("dp", None, "tensor"), P(None, "dp"), P("tensor", "dp"),
        vec, vec, vec, P("dp", "tensor"), vec, P("tensor", "dp"), vec, tok,
    )
    out_specs = (
        tok, tok, vec, vec, P("dp", None, "tensor"), P(None, "dp"), P("tensor", "dp"),
        vec, vec, vec, P("dp", "tensor"), vec, P("tensor", "dp"), vec,
    )
    return jax.shard_map(on_device, mesh=mesh, in_specs=in_specs, out_specs=out_specs, check_vma=False)
```

```python
import functools

import jax
import jax.numpy as jnp
from jax import lax
from jax.experimental import pallas as pl
from jax.experimental.pallas import tpu as pltpu
from jax.sharding import PartitionSpec as P

HD = 64
QB = 256
NEG = -1e30
EPSILON = 1e-05
BRANCH_SCALE = 48.0 ** (-0.5)
SMALL = 128
VECS = 16
ROWS = 256
HIDDEN = 768
bf = jnp.bfloat16
f32 = jnp.float32
NT = (((1,), (1,)), ((), ()))
TN = (((0,), (0,)), ((), ()))
BOTH = ("dp", "tensor")
MESH_ID = pl.DeviceIdType.MESH
ANY = pl.BlockSpec(memory_space=pl.ANY)
VM = pl.BlockSpec(memory_space=pltpu.VMEM)
SM = pl.BlockSpec(memory_space=pltpu.SMEM)


def attn_mask(kat, at, srow):
    keys = lax.broadcasted_iota(jnp.int32, (QB, QB), 0)
    rows = lax.broadcasted_iota(jnp.int32, (1, QB), 1) + (at - kat)
    return (keys >= srow - kat) & (keys <= rows)


def over_blocks(bounds, i, step, carry):
    low = bounds[0, i * QB] // QB
    mid = jnp.minimum((bounds[0, i * QB + QB - 1] + QB - 1) // QB, i)
    carry = lax.fori_loop(0, mid - low + 1, lambda k, c: step(True, jnp.where(k == 0, i, low + k - 1), c), carry)
    return lax.fori_loop(mid, i, functools.partial(step, False), carry)


def head_lanes(values):
    low = (lax.broadcasted_iota(jnp.int32, (1, values.shape[1]), 1) % 128) < HD
    zero = jnp.zeros((), bf)
    return jnp.where(low, values, zero), jnp.where(low, zero, values)


def fwd_kernel(info, bounds, own, recv, st_ref, okeep, osend, lse_ref, qm, ks, vt, osc, acc):
    half, cols = own.shape[0], own.shape[1] // 3
    n, nb, heads, pairs = 2 * half, 2 * half // QB, cols // HD, cols // 128
    c = info[0]
    for base, src in ((c * half, own), ((1 - c) * half, recv)):
        rows = pl.ds(pl.multiple_of(base, half), half)
        for g in range(pairs):
            lanes = slice(g * 128, (g + 1) * 128)
            part = lambda k: src[:, (3 * g + k) * 128 : (3 * g + k + 1) * 128]
            qm[0, rows, lanes], qm[1, rows, lanes] = head_lanes(part(0) * bf(HD**-0.5))
            ks[rows, lanes] = part(1)
            vt[lanes, rows] = part(2).T

    def qblock(i, _):
        at = pl.multiple_of(i * QB, QB)
        qr = pl.ds(at, QB)
        srow = st_ref[:, qr]
        acc[...] = jnp.zeros_like(acc)

        def step(masked, j, carry):
            kat = pl.multiple_of(j * QB, QB)
            kr = pl.ds(kat, QB)
            if masked:
                mask = attn_mask(kat, at, srow)
            scores, mixed = [], []
            for h in range(heads):
                lanes = slice(h // 2 * 128, h // 2 * 128 + 128)
                one = lax.dot_general(ks[kr, lanes], qm[h % 2, qr, lanes], NT, preferred_element_type=f32)
                scores.append(jnp.where(mask, one, NEG) if masked else one)
            for h in range(heads):
                top, total = carry[h]
                new = jnp.maximum(top, jnp.max(scores[h], axis=0, keepdims=True))
                weights = jnp.exp(scores[h] - new)
                fade = jnp.exp(top - new)
                total = fade * total + jnp.sum(weights, axis=0, keepdims=True)
                mixed.append((new, total, fade, weights.astype(bf)))
            for h in range(heads):
                sub = slice(h * HD, (h + 1) * HD)
                acc[sub] = mixed[h][2] * acc[sub] + jnp.dot(vt[sub, kr], mixed[h][3], preferred_element_type=f32)
            return tuple(m[:2] for m in mixed)

        carry = over_blocks(bounds, i, step, ((jnp.full((1, QB), NEG, f32), jnp.zeros((1, QB), f32)),) * heads)
        for h, (top, total) in enumerate(carry):
            sub = slice(h * HD, (h + 1) * HD)
            acc[sub] = acc[sub] / total
            lse_ref[h : h + 1, qr] = top + jnp.log(total)
        osc[qr] = acc[...].T.astype(bf)
        return 0

    lax.fori_loop(0, nb, qblock, 0)
    okeep[...] = osc[pl.ds(pl.multiple_of(c * half, half), half)]
    osend[...] = osc[pl.ds(pl.multiple_of((1 - c) * half, half), half)]


def attn_fwd(own, recv, starts, info):
    half, cols = own.shape[0], own.shape[1] // 3
    n = 2 * half
    return pl.pallas_call(
        fwd_kernel,
        in_specs=[SM, SM, VM, VM, VM],
        out_specs=[VM] * 3,
        scratch_shapes=[
            pltpu.VMEM((2, n, cols), bf), pltpu.VMEM((n, cols), bf), pltpu.VMEM((cols, n), bf),
            pltpu.VMEM((n, cols), bf), pltpu.VMEM((cols, QB), f32)],
        out_shape=[jax.ShapeDtypeStruct((half, cols), bf)] * 2 + [jax.ShapeDtypeStruct((cols // HD, n), f32)],
        cost_estimate=pl.CostEstimate(flops=n * n, bytes_accessed=n * 128, transcendentals=0),
        compiler_params=pltpu.CompilerParams(vmem_limit_bytes=30 << 20),
    )(info, starts, own, recv, starts)


def bwd_kernel(info, bounds, own, recv, doo, dor, oo, orr, st_ref, lse_ref, dkeep, dsend, qm, ks, vs, kt, dom, dlt, dqs, dks, dvs):
    half, cols = own.shape[0], own.shape[1] // 3
    n, nb, heads, pairs = 2 * half, 2 * half // QB, cols // HD, cols // 128
    c = info[0]
    lanes_of = lambda g: slice(g * 128, (g + 1) * 128)
    for base, src, do, o in ((c * half, own, doo, oo), ((1 - c) * half, recv, dor, orr)):
        rows = pl.ds(pl.multiple_of(base, half), half)
        for g in range(pairs):
            lanes = lanes_of(g)
            part = lambda k: src[:, (3 * g + k) * 128 : (3 * g + k + 1) * 128]
            qm[0, rows, lanes], qm[1, rows, lanes] = head_lanes(part(0) * bf(HD**-0.5))
            ks[rows, lanes] = part(1)
            vs[rows, lanes] = part(2)
            kt[lanes, rows] = part(1).T
            grad = do[:, lanes]
            dom[0, rows, lanes], dom[1, rows, lanes] = head_lanes(grad)
            prod = (grad.astype(f32) * o[:, lanes].astype(f32)).T
            for e in range(2):
                dlt[2 * g + e : 2 * g + e + 1, rows] = jnp.sum(prod[e * HD : (e + 1) * HD], axis=0, keepdims=True)
    dks[...] = jnp.zeros_like(dks)
    dvs[...] = jnp.zeros_like(dvs)

    def qblock(i, _):
        at = pl.multiple_of(i * QB, QB)
        qr = pl.ds(at, QB)
        srow = st_ref[:, qr]
        dqs[...] = jnp.zeros_like(dqs)

        def step(masked, j, carry):
            kat = pl.multiple_of(j * QB, QB)
            kr = pl.ds(kat, QB)
            if masked:
                mask = attn_mask(kat, at, srow)
            scores, softs, grads = [], [], []
            for h in range(heads):
                lanes = lanes_of(h // 2)
                one = lax.dot_general(ks[kr, lanes], qm[h % 2, qr, lanes], NT, preferred_element_type=f32)
                back = lax.dot_general(vs[kr, lanes], dom[h % 2, qr, lanes], NT, preferred_element_type=f32)
                scores.append((jnp.where(mask, one, NEG) if masked else one, back))
            for h in range(heads):
                soft = jnp.exp(scores[h][0] - lse_ref[h : h + 1, qr])
                grads.append((soft * (scores[h][1] - dlt[h : h + 1, qr])).astype(bf))
                softs.append(soft.astype(bf))
            for g in range(pairs):
                lanes = lanes_of(g)
                both = lambda ref: jnp.concatenate([ref[0, qr, lanes], ref[1, qr, lanes]], axis=0)
                two = slice(2 * g, 2 * g + 2)
                dvs[kr, lanes] += jnp.dot(jnp.concatenate(softs[two], axis=1), both(dom), preferred_element_type=f32)
                dks[kr, lanes] += jnp.dot(jnp.concatenate(grads[two], axis=1), both(qm), preferred_element_type=f32)
                for h in (2 * g, 2 * g + 1):
                    sub = slice(h * HD, (h + 1) * HD)
                    dqs[sub] += jnp.dot(kt[sub, kr], grads[h], preferred_element_type=f32)
            return carry

        over_blocks(bounds, i, step, 0)
        qm[0, qr] = (dqs[...] * (HD**-0.5)).T.astype(bf)
        return 0

    lax.fori_loop(0, nb, qblock, 0)
    for dst, base in ((dkeep, c * half), (dsend, (1 - c) * half)):
        rows = pl.ds(pl.multiple_of(base, half), half)
        for g in range(pairs):
            for k, value in enumerate((qm[0, rows, lanes_of(g)], dks[rows, lanes_of(g)], dvs[rows, lanes_of(g)])):
                dst[:, (3 * g + k) * 128 : (3 * g + k + 1) * 128] = value.astype(bf)


def attn_bwd(own, recv, do_own, do_recv, o_own, o_recv, starts, lse, info):
    half, cols = own.shape[0], own.shape[1] // 3
    n = 2 * half
    return pl.pallas_call(
        bwd_kernel,
        in_specs=[SM, SM] + [VM] * 8,
        out_specs=[VM] * 2,
        scratch_shapes=[
            pltpu.VMEM((2, n, cols), bf), pltpu.VMEM((n, cols), bf), pltpu.VMEM((n, cols), bf), pltpu.VMEM((cols, n), bf),
            pltpu.VMEM((2, n, cols), bf), pltpu.VMEM((cols // HD, n), f32), pltpu.VMEM((cols, QB), f32),
            pltpu.VMEM((n, cols), f32), pltpu.VMEM((n, cols), f32)],
        out_shape=[like((half, 3 * cols), bf)] * 2,
        cost_estimate=pl.CostEstimate(flops=n * n, bytes_accessed=n * 128, transcendentals=0),
        compiler_params=pltpu.CompilerParams(vmem_limit_bytes=56 << 20),
    )(info, starts, own, recv, do_own, do_recv, o_own, o_recv, starts, lse)


def dot(left, right, dims=(((1,), (0,)), ((), ()))):
    return lax.dot_general(left, right, dims, preferred_element_type=f32)


def exchange(value, bit, dp_size):
    if bit:
        return lax.ppermute(value, "dp", [(i, i ^ bit) for i in range(dp_size)])
    return lax.ppermute(value, "tensor", [(0, 1), (1, 0)])


def flip(index, bits):
    for bit in bits:
        index = index + bit * (1 - 2 * ((index // bit) % 2))
    return index

def far_groups(dp_size):
    far = [1 << k for k in range(dp_size.bit_length() - 2, 1, -1)]
    return [tuple(far[k : k + 2]) for k in range(0, len(far), 2)]

def group_moves(group):
    if len(group) == 1:
        return [(1, group)]
    return [(1, group[:1]), (2, group[1:]), (3, group)]

def chunks_of(cols, which, count, until=None):
    tiles = cols // 128
    cuts = [128 * ((tiles * k) // count) for k in range(count + 1)]
    arrays = range(which, until + 1) if until else (which,)
    return tuple(
        (array, low, high - low, 128 * ((high - low) // 256 + (high - low) // 128 % 2))
        for low, high in zip(cuts, cuts[1:]) for array in arrays)


def head_kernel(groups, chunks, tokens, seg, *refs):
    shards, x_out, seg_out, outs, (send_sem, recv_sem, local_sem) = refs[:4], refs[4], refs[5], refs[6:10], refs[10:]
    dp, t = lax.axis_index("dp"), lax.axis_index("tensor")
    core = dp % 2
    away = core + t - 2 * core * t
    near = {1: (flip(dp, (1,)), t), 2: (flip(dp, (2,)), t), 0: (dp, 1 - t)}
    distant = [bits for group in groups for _, bits in group_moves(group)]
    swap = (dp - core + t, core)
    barrier = pltpu.get_barrier_semaphore()
    for device in list(near.values()) + [(flip(dp, bits), t) for bits in distant]:
        pl.semaphore_signal(barrier, inc=1, device_id=device, device_id_type=MESH_ID)

    @pl.when(away == 1)
    def _():
        pl.semaphore_signal(barrier, inc=1, device_id=swap, device_id_type=MESH_ID)

    local = [
        pltpu.make_async_copy(shards[k], outs[k].at[away, 0] if k < 2 else outs[k].at[0], local_sem.at[k]) for k in range(4)]
    for copy in local:
        copy.start()
    pl.semaphore_wait(barrier, len(near) + len(distant) + away)
    count = [0]

    def remote(src, dst, device):
        slot = count[0]
        count[0] += 1
        return pltpu.make_async_remote_copy(
            src_ref=src, dst_ref=dst, send_sem=send_sem.at[slot], recv_sem=recv_sem.at[slot],
            device_id=device, device_id_type=MESH_ID)

    def blocks(ref, index, first, held, low, size):
        return ref.at[index, pl.ds(first, held), :, pl.ds(low, size)]

    plans = []
    for which, low, size, part in chunks:
        shard, out = shards[which], outs[which]
        steps, held = [], 1
        for group in groups:
            moves = []
            for place, bits in group_moves(group):
                src = shard.at[:, pl.ds(low, size)] if held == 1 else blocks(out, away, 0, held, low, size)
                dst = out.at[away, place, :, pl.ds(low, size)] if held == 1 else blocks(out, away, place * held, held, low, size)
                moves.append(remote(src, dst, (flip(dp, bits), t)))
            held *= len(group_moves(group)) + 1
            steps.append(moves)
        a, b = (low, part), (low + part, size - part)
        steps.append([
            remote(blocks(out, away, 0, held, *a), blocks(out, away, 0, held, *a), near[0]),
            remote(blocks(out, away, 0, held, *b), blocks(out, away, held, held, *b), near[2]),
        ])
        steps.append(
            [remote(blocks(out, k, 0, held, *a), blocks(out, k, held, held, *a), near[2]) for k in range(2)]
            + [remote(blocks(out, away, 0, 2 * held, *b), blocks(out, away, 0, 2 * held, *b), near[0])])
        steps.append([
            remote(blocks(out, k, 0, 2 * held, low, size),
                   blocks(out, 1 - k, 2 * held, 2 * held, low, size), near[1]) for k in range(2)])
        plans.append(steps)
    later = []
    held = 1
    for group in groups:
        moves = []
        for place, bits in group_moves(group):
            for shard, out in zip(shards[2:], outs[2:]):
                src = shard if held == 1 else out.at[pl.ds(0, held)]
                dst = out.at[place] if held == 1 else out.at[pl.ds(place * held, held)]
                moves.append(remote(src, dst, (flip(dp, bits), t)))
        held *= len(group_moves(group)) + 1
        later.append(moves)
    depth = len(plans[0])
    swap_copy = remote(tokens, x_out, swap)
    seg_copy = remote(seg, seg_out, near[1])
    stay_copy = pltpu.make_async_copy(tokens, x_out, local_sem.at[4])
    waited = set()

    def advance(number, phase):
        if number >= len(plans):
            return
        if phase > 0:
            for move in plans[number][phase - 1]:
                move.wait_recv()
        if phase == 1 and chunks[number][0] not in waited:
            waited.add(chunks[number][0])
            local[chunks[number][0]].wait()
        if phase < depth:
            for move in plans[number][phase]:
                move.start()

    advance(0, 0)
    seg_copy.start()

    @pl.when(away == 1)
    def _():
        swap_copy.start()

    @pl.when(away == 0)
    def _():
        stay_copy.start()

    far = len(groups)
    for number in range(len(plans)):
        if number == 0:
            for phase in range(1, far + 1):
                advance(0, phase)
            for k in range(1, len(plans)):
                advance(k, 0)
            for move in later[0]:
                move.start()
        advance(number, far + 1)
        for phase in range(1, far + 1):
            advance(number + 1, phase)
        advance(number, far + 2)
    for number in range(len(plans)):
        advance(number, depth)

    @pl.when(away == 1)
    def _():
        swap_copy.wait()

    @pl.when(away == 0)
    def _():
        stay_copy.wait()

    seg_copy.wait()
    for which in sorted(set(range(4)) - waited):
        local[which].wait()
    for k, moves in enumerate(later):
        if k > 0:
            for move in moves:
                move.start()
        for move in moves:
            move.wait()
    for steps in plans:
        for moves in steps:
            for move in moves:
                move.wait_send()


def head(dp_size, tokens, seg, shards, chunks):
    groups = far_groups(dp_size)
    partners = sum(len(group_moves(g)) for g in groups)
    slots = len(chunks) * (partners + 7) + 2 * partners + 2
    shapes = [(2, dp_size)] * 2 + [(dp_size // 4,)] * 2
    return pl.pallas_call(
        functools.partial(head_kernel, groups, chunks),
        in_specs=[VM] * 6,
        out_specs=[ANY] * 6,
        out_shape=[jax.ShapeDtypeStruct(a.shape, a.dtype) for a in (tokens, seg)]
        + [jax.ShapeDtypeStruct(lead + s.shape, s.dtype) for lead, s in zip(shapes, shards)],
        scratch_shapes=[pltpu.SemaphoreType.DMA((slots,)), pltpu.SemaphoreType.DMA((slots,)), pltpu.SemaphoreType.DMA((5,))],
        compiler_params=pltpu.CompilerParams(collective_id=0, has_side_effects=True),
    )(tokens, seg, *shards)


def tail_kernel(groups, own_lo, own_hi, rest_lo, rest_hi, small_lo, small_hi, feed, total, vecs, feed_total,
                feed_part, feed_got, part, got_core, got_near, got_last, got_far, vec, vec_core, vec_two, vec_one, vec_far, send_sem, recv_sem):
    dp, t = lax.axis_index("dp"), lax.axis_index("tensor")
    core = dp % 2
    away = core + t - 2 * core * t
    near = {1: (flip(dp, (1,)), t), 2: (flip(dp, (2,)), t), 0: (dp, 1 - t)}
    distant = [bits for group in groups for _, bits in group_moves(group)]
    barrier = pltpu.get_barrier_semaphore()
    for device in list(near.values()) + [(flip(dp, bits), t) for bits in distant]:
        pl.semaphore_signal(barrier, inc=1, device_id=device, device_id_type=MESH_ID)

    pl.semaphore_wait(barrier, len(near) + len(distant))
    count = [0]

    def remote(src, dst, device):
        slot = count[0]
        count[0] += 1
        return pltpu.make_async_remote_copy(
            src_ref=src, dst_ref=dst, send_sem=send_sem.at[slot], recv_sem=recv_sem.at[slot],
            device_id=device, device_id_type=MESH_ID)

    half, rows, cols = own_lo.shape
    quarter = half // 2
    chunks = [pl.ds(low, min(512, cols - low)) for low in range(0, cols, 512)]
    to_core = [[
        remote(rest_hi.at[:, :, c], got_core.at[0, :, :, c], near[1]),
        remote(own_hi.at[:, :, c], got_core.at[1, :, :, c], near[1])] for c in chunks]
    to_core[0].append(remote(small_hi, vec_core, near[1]))
    for moves in to_core:
        for move in moves:
            move.start()

    feed_steps = []
    held, used = feed.shape[0], 0
    for number, group in enumerate(reversed(groups)):
        moves = group_moves(group)
        held //= len(moves) + 1
        source, step = feed if number == 0 else feed_part, []
        for place, bits in moves:
            step.append(remote(source.at[pl.ds(place * held, held)], feed_got.at[pl.ds(used, held)], (flip(dp, bits), t)))
            used += held
        feed_steps.append((step, source, held, used - held * len(moves), len(moves)))
    for move in feed_steps[0][0]:
        move.start()

    def add(*terms):
        out = terms[0].astype(f32)
        for term in terms[1:]:
            out = out + term.astype(f32)
        return out.astype(bf)

    upper, lower = pl.ds(quarter, quarter), pl.ds(0, quarter)
    mine, other = away, 1 - away
    last = len(chunks) - 1
    steps, sent = {}, []

    def start(key, moves):
        steps[key] = moves
        sent.extend(moves)
        for move in moves:
            move.start()

    def arrive(key):
        for move in steps[key]:
            move.wait_recv()

    def core_stage(k):
        for move in to_core[k]:
            move.wait_recv()
        c = chunks[k]

        def body(q, _):
            part[0, q, :, c] = add(own_lo[q, :, c], got_core[0, q, :, c])
            part[1, q, :, c] = add(rest_lo[q, :, c], got_core[1, q, :, c])
            if k == 0:
                vec[q] = add(small_lo[q], vec_core[q])
            return 0

        lax.fori_loop(0, half, body, 0)
        if k == 1:
            start(("x", k), [remote(part.at[other, :, :, c], got_near.at[0, :, :, c], near[0])])
        else:
            start(("x", k), [
                remote(part.at[g, upper, :, c], got_near.at[g, lower, :, c], near[2]) for g in range(2)]
                + ([remote(vec.at[upper], vec_two, near[2])] if k == 0 else []))

    def x_stage(k):
        arrive(("x", k))
        c = chunks[k]

        def body(q, _):
            if k == 1:
                part[mine, q, :, c] = add(part[mine, q, :, c], got_near[0, q, :, c])
                return 0
            for g in range(2):
                part[g, q, :, c] = add(part[g, q, :, c], got_near[g, q, :, c])
            if k == 0:
                vec[q] = add(vec[q], vec_two[q])
            return 0

        lax.fori_loop(0, half if k == 1 else quarter, body, 0)
        if k == 1:
            start(("y", k), [remote(part.at[mine, upper, :, c], got_last.at[:, :, c], near[2])])
        else:
            start(("y", k), [remote(part.at[other, lower, :, c], got_last.at[:, :, c], near[0])]
                  + ([remote(vec.at[lower], vec_one, near[0])] if k == 0 else []))

    def far_moves(number, k):
        held, used = quarter, 0
        for index, group in enumerate(reversed(groups)):
            moves = group_moves(group)
            held //= len(moves) + 1
            if index == number:
                out = []
                for m, (place, bits) in enumerate(moves):
                    device, c = (flip(dp, bits), t), chunks[k]
                    out.append(remote(part.at[mine, pl.ds(place * held, held), :, c], got_far.at[pl.ds(used + m * held, held), :, c], device))
                    if k == 0:
                        out.append(remote(vec_one.at[pl.ds(place * held, held)], vec_far.at[pl.ds(used + m * held, held)], device))
                return out, held, used, len(moves)
            used += held * len(moves)

    def y_stage(k):
        arrive(("y", k))
        c = chunks[k]

        def body(q, _):
            part[mine, q, :, c] = add(part[mine, q, :, c], got_last[q, :, c])
            if k == 0:
                vec_one[q] = add(vec[q], vec_one[q])
            return 0

        lax.fori_loop(0, quarter, body, 0)
        start(("z", 0, k), far_moves(0, k)[0])

    far_shape = []
    held, used = quarter, 0
    for group in reversed(groups):
        moves = len(group_moves(group))
        held //= moves + 1
        far_shape.append((held, used, moves))
        used += held * moves

    def z_stage(number, k):
        arrive(("z", number, k))
        c = chunks[k]
        held, base, moves = far_shape[number]

        def body(q, _):
            part[mine, q, :, c] = add(part[mine, q, :, c], *[got_far[base + m * held + q, :, c] for m in range(moves)])
            if k == 0:
                vec_one[q] = add(vec_one[q], *[vec_far[base + m * held + q] for m in range(moves)])
            return 0

        lax.fori_loop(0, held, body, 0)
        if number + 1 < len(groups):
            start(("z", number + 1, k), far_moves(number + 1, k)[0])

    for k in range(last + 1):
        core_stage(k)
    for k in range(last + 1):
        x_stage(k)
        if k > 0:
            y_stage(k - 1)
    y_stage(last)
    for number in range(len(groups)):
        for k in range(last + 1):
            z_stage(number, k)
    to_far = []
    for number, (step, source, held, base, moves) in enumerate(feed_steps):
        if number > 0:
            for move in step:
                move.start()
        for move in step:
            move.wait_recv()

        def sum_feed(k, _, source=source, held=held, base=base, moves=moves):
            feed_part[k] = add(source[k], *[feed_got[base + m * held + k] for m in range(moves)])
            return 0

        if number + 1 < len(feed_steps):
            lax.fori_loop(0, held, sum_feed, 0)
        else:
            out = source[0].astype(f32)
            for m in range(moves):
                out = out + feed_got[base + m * held].astype(f32)
            feed_total[...] = out
        to_far += step
    total[...] = part[mine, 0].astype(f32)
    vecs[...] = vec_one[0].astype(f32)

    for move in sum(to_core, []) + sent + to_far:
        move.wait_send()


def tail(dp_size, own, rest, small, feed):
    groups = far_groups(dp_size)
    half, rows, cols = own[0].shape
    quarter = half // 2
    wide = small[0].shape[2]
    partners = sum(len(group_moves(g)) for g in groups)
    slots = (-(-cols // 512)) * (5 + partners) + 3 + 2 * partners
    return pl.pallas_call(
        functools.partial(tail_kernel, groups),
        in_specs=[VM] * 7,
        out_specs=[VM, VM, VM],
        out_shape=[
            jax.ShapeDtypeStruct((rows, cols), f32),
            jax.ShapeDtypeStruct((rows, wide), f32), jax.ShapeDtypeStruct(feed.shape[1:], f32)],
        scratch_shapes=[
            pltpu.VMEM(feed.shape, bf), pltpu.VMEM(feed.shape, bf),
            pltpu.VMEM((2, half, rows, cols), bf), pltpu.VMEM((2, half, rows, cols), bf), pltpu.VMEM((2, half, rows, cols), bf),
            pltpu.VMEM((quarter, rows, cols), bf), pltpu.VMEM((quarter, rows, cols), bf),
            pltpu.VMEM((half, rows, wide), bf), pltpu.VMEM((half, rows, wide), bf), pltpu.VMEM((quarter, rows, wide), bf),
            pltpu.VMEM((quarter, rows, wide), bf), pltpu.VMEM((quarter, rows, wide), bf),
            pltpu.SemaphoreType.DMA((slots,)), pltpu.SemaphoreType.DMA((slots,))],
        compiler_params=pltpu.CompilerParams(collective_id=1, has_side_effects=True, vmem_limit_bytes=48 << 20),
    )(*own, *rest, *small, feed)


def add_low(*terms):
    out = terms[0].astype(f32)
    for term in terms[1:]:
        out = out + term.astype(f32)
    return out.astype(bf)


def order_matrix(owner, rows, width):
    place = lax.broadcasted_iota(jnp.int32, (1, width), 1)
    block = place // rows
    count = width // rows
    natural = place % rows
    for k, bit in enumerate([1 << b for b in range(count.bit_length() - 2, 1, -1)] + [2, 1]):
        on, base = (block // (1 << k)) % 2, (owner // bit) % 2
        natural = natural + (on + base - 2 * on * base) * (bit * rows)
    return (lax.broadcasted_iota(jnp.int32, (width, width), 0) == natural).astype(f32).astype(bf)


def norm_parts(values):
    centered = values - jnp.mean(values, axis=-1, keepdims=True)
    inverse = lax.rsqrt(jnp.mean(centered * centered, axis=-1, keepdims=True) + EPSILON)
    return centered * inverse, inverse


def norm_back(hat, inverse, gain, grad):
    scaled = grad * gain
    return inverse * (
        scaled - jnp.mean(scaled, axis=-1, keepdims=True) - hat * jnp.mean(scaled * hat, axis=-1, keepdims=True))


def over_rows(total, body):
    def step(k, _):
        body(pl.ds(pl.multiple_of(k * ROWS, ROWS), ROWS))
        return 0

    lax.fori_loop(0, total // ROWS, step, 0)


def column_sum(ref, row, values):
    ref[row : row + 1] += jnp.sum(values, axis=0, keepdims=True)


def bias_row(vec_nat, group, cols):
    lanes = pl.ds(pl.multiple_of(group * cols, 128), cols)
    q, v = vec_nat[2:3, lanes], vec_nat[3:4, lanes]
    parts = []
    for g in range(cols // 128):
        part = slice(g * 128, (g + 1) * 128)
        parts += [q[:, part], jnp.zeros((1, 128), f32), v[:, part]]
    return jnp.concatenate(parts, axis=1)


def fan_matrix(fan):
    row = lax.broadcasted_iota(jnp.int32, (128 * fan, 1), 0)
    unit = lax.broadcasted_iota(jnp.int32, (128 * fan, 128 * fan), 1)
    return (unit == (row % 128) * fan + row // 128).astype(f32).astype(bf)


def first_kernel(rows, fan, info, tokens, pack, weight, seg, seg_other, x_out, n1_out, send, vec_rel, vec_nat, fc_bias, starts, order, fan_rows):
    width, cols = tokens.shape[1], weight.shape[2] // 3

    @pl.when(pl.program_id(0) == 0)
    def _():
        order[...] = order_matrix(info[1], rows, width)
        small = pack[0, :, cols:].astype(f32).T[:VECS]
        vec_rel[...] = small
        vec_nat[...] = lax.dot_general(small.astype(bf), order[...], NT, preferred_element_type=f32)
        count = width // 128
        fan_rows[...] = jnp.zeros_like(fan_rows)
        for k in range(count):
            for m in range(fan):
                fan_rows[k : k + 1, m * 128 : (m + 1) * 128] = vec_nat[8 + m : 9 + m, k * 128 : (k + 1) * 128]
        bias = jnp.dot(fan_rows[...].astype(bf), fan_matrix(fan), preferred_element_type=f32)
        for k in range(count):
            fc_bias[:, k * 128 * fan : (k + 1) * 128 * fan] = bias[k : k + 1]
        docs = jnp.where(info[2] == 1, seg[...], seg_other[...]).astype(f32)
        begin = jnp.zeros_like(docs)
        for d in range(1, 16):
            before = jnp.sum(jnp.where(docs < d, 1.0, 0.0), axis=1, keepdims=True)
            begin = jnp.where(docs == d, before, begin)
        starts[...] = begin.astype(jnp.int32)

    x = jnp.dot(tokens[...], order[...], preferred_element_type=f32)
    hat, _ = norm_parts(x)
    n1 = (hat * vec_rel[0:1] + vec_rel[1:2]).astype(bf)
    x_out[...] = x.astype(bf)
    n1_out[...] = n1
    send[...] = (jnp.dot(n1, weight[0], preferred_element_type=f32) + bias_row(vec_nat, 1 - info[0], cols)).astype(bf)


def own_kernel(n1, send, weights, vec_nat, out, recv, weight, send_sem, recv_sem, local_sem):
    dp, t = lax.axis_index("dp"), lax.axis_index("tensor")
    partner = (flip(dp, (1,)), t)
    barrier = pltpu.get_barrier_semaphore()
    pl.semaphore_signal(barrier, inc=1, device_id=partner, device_id_type=MESH_ID)
    load = pltpu.make_async_copy(weights.at[0], weight, local_sem.at[0])
    load.start()
    pl.semaphore_wait(barrier, 1)
    copy = pltpu.make_async_remote_copy(
        src_ref=send, dst_ref=recv, send_sem=send_sem.at[0], recv_sem=recv_sem.at[0], device_id=partner, device_id_type=MESH_ID)
    copy.start()
    load.wait()
    bias = bias_row(vec_nat, dp % 2, weight.shape[1] // 3)

    def body(at):
        out[at] = (jnp.dot(n1[at], weight[...], preferred_element_type=f32) + bias).astype(bf)

    over_rows(n1.shape[0], body)
    copy.wait()


def picked(array, index):
    return pl.BlockSpec((1,) + array.shape[1:], lambda k, s: (index, 0, 0))


def whole(array):
    return pl.BlockSpec(array.shape, lambda k, s: (0,) * len(array.shape))


def like(shape, dtype):
    return jax.ShapeDtypeStruct(shape, dtype)


def by_rows(kernel, info, inputs, specs, outs, scratch=(), flops=1 << 22):
    total = inputs[0].shape[0]

    def spec(array, given=None):
        if given is not None:
            return given
        if array.shape[0] == total:
            return pl.BlockSpec((ROWS,) + array.shape[1:], lambda k, s: (k, 0))
        return whole(array)

    return pl.pallas_call(
        kernel,
        grid_spec=pltpu.PrefetchScalarGridSpec(
            num_scalar_prefetch=1, grid=(total // ROWS,), in_specs=[spec(a, g) for a, g in zip(inputs, specs)],
            out_specs=[spec(o) for o in outs], scratch_shapes=list(scratch)),
        out_shape=outs,
        cost_estimate=pl.CostEstimate(flops=flops, bytes_accessed=1 << 18, transcendentals=0),
        compiler_params=pltpu.CompilerParams(vmem_limit_bytes=60 << 20),
    )(info, *inputs)


def project_first(info, rows, fan, tokens, packs, weights, seg, seg_other):
    n, width = tokens.shape
    vecs = like((VECS, width), f32)
    return by_rows(
        functools.partial(first_kernel, rows, fan), info, (tokens, packs, weights, seg, seg_other),
        (None, picked(packs, 0), picked(weights, 1), None, None),
        [like((n, width), bf), like((n, width), bf), like((n, weights.shape[2]), bf), vecs, vecs, like((1, width * fan), f32),
         like(seg.shape, jnp.int32)],
        [pltpu.VMEM((width, width), bf), pltpu.VMEM((8, 128 * fan), f32)])


def project_own(n1, send, weights, vec_nat):
    return pl.pallas_call(
        own_kernel,
        in_specs=[VM, ANY, ANY, VM],
        out_specs=[VM, ANY],
        out_shape=[like(send.shape, bf)] * 2,
        scratch_shapes=[
            pltpu.VMEM(weights.shape[1:], bf), pltpu.SemaphoreType.DMA((1,)), pltpu.SemaphoreType.DMA((1,)),
            pltpu.SemaphoreType.DMA((1,))],
        compiler_params=pltpu.CompilerParams(collective_id=3, has_side_effects=True, vmem_limit_bytes=24 << 20),
    )(n1, send, weights, vec_nat)


def middle_kernel(rows, x, o_own, o_send, cot, cot_recv, packs, vec_rel, fc00, fc01, fc10, fc11, pr0, pr1,
                  middle, n2, cot_rel, d_mlp, o_recv, fc_got, pr_got, order, send_sem, recv_sem):
    dp, t = lax.axis_index("dp"), lax.axis_index("tensor")
    core = dp % 2
    away = core + t - 2 * core * t
    partner = (flip(dp, (1,)), t)
    barrier = pltpu.get_barrier_semaphore()
    pl.semaphore_signal(barrier, inc=1, device_id=partner, device_id_type=MESH_ID)
    pl.semaphore_wait(barrier, 1)
    size = fc00.shape[0]
    copies = [
        pltpu.make_async_remote_copy(
            src_ref=src, dst_ref=dst, send_sem=send_sem.at[k], recv_sem=recv_sem.at[k], device_id=partner, device_id_type=MESH_ID)
        for k, (src, dst) in enumerate((
            (o_send, o_recv), (fc00, fc_got.at[0, pl.ds(0, size)]), (fc01, fc_got.at[0, pl.ds(size, size)]), (pr0, pr_got.at[0]),
            (fc10, fc_got.at[1, pl.ds(0, size)]), (fc11, fc_got.at[1, pl.ds(size, size)]), (pr1, pr_got.at[1])))]
    for copy in copies:
        copy.start()
    order[...] = order_matrix(dp, rows, x.shape[1])
    cols = o_own.shape[1]

    def cot_rows(at):
        grad = jnp.dot(jnp.where(away == 0, cot[at], cot_recv[at]), order[...], preferred_element_type=f32)
        cot_rel[at] = grad.astype(bf)
        d_mlp[at] = (BRANCH_SCALE * grad).astype(bf)

    over_rows(x.shape[0], cot_rows)
    copies[0].wait_recv()

    def body(at):
        branch = lax.dot_general(o_own[at], packs[0, :, :cols], NT, preferred_element_type=f32)
        branch = branch + lax.dot_general(o_recv[at], packs[1, :, :cols], NT, preferred_element_type=f32)
        mid = x[at].astype(f32) + BRANCH_SCALE * (branch + vec_rel[4:5])
        middle[at] = mid
        hat, _ = norm_parts(mid)
        n2[at] = (hat * vec_rel[5:6] + vec_rel[6:7]).astype(bf)

    over_rows(x.shape[0], body)
    for copy in copies[1:]:
        copy.wait_recv()
    for copy in copies:
        copy.wait_send()


def middle_part(rows, x, o_own, o_send, cot, cot_recv, packs, vec_rel, fc_parts, proj_parts):
    shape, half = x.shape, x.shape[1] // 2
    hidden = proj_parts[0].shape[1]
    got = like((2, half, hidden), bf)
    return pl.pallas_call(
        functools.partial(middle_kernel, rows),
        in_specs=[VM] * 7 + [ANY] * 6,
        out_specs=[VM] * 5 + [ANY] * 2,
        out_shape=[like(shape, f32), like(shape, bf), like(shape, bf), like(shape, bf), like(o_send.shape, bf), got, got],
        scratch_shapes=[
            pltpu.VMEM((shape[1], shape[1]), bf), pltpu.SemaphoreType.DMA((7,)), pltpu.SemaphoreType.DMA((7,))],
        compiler_params=pltpu.CompilerParams(collective_id=2, has_side_effects=True, vmem_limit_bytes=36 << 20),
    )(x, o_own, o_send, cot, cot_recv, packs, vec_rel, *fc_parts[0], *fc_parts[1], *proj_parts)


def after_kernel(rows, info, middle, mlp, back, cot, packs, vec_rel, block_out, d_middle, d_attn, do_own, do_send, sums, order):
    @pl.when(pl.program_id(0) == 0)
    def _():
        order[...] = order_matrix(info[1], rows, middle.shape[1])
        sums[...] = jnp.zeros_like(sums)

    cols = do_own.shape[1]
    mid = middle[...]
    out = (mid + BRANCH_SCALE * (mlp[...] + vec_rel[7:8])).astype(bf)
    block_out[...] = lax.dot_general(out, order[...], NT, preferred_element_type=f32).astype(bf)
    hat, inverse = norm_parts(mid)
    grad = back[...]
    out_grad = cot[...].astype(f32)
    entire = out_grad + norm_back(hat, inverse, vec_rel[5:6], grad)
    d_middle[...] = entire
    low = (BRANCH_SCALE * entire).astype(bf)
    d_attn[...] = low
    do_own[...] = jnp.dot(low, packs[0, :, :cols], preferred_element_type=f32).astype(bf)
    do_send[...] = jnp.dot(low, packs[1, :, :cols], preferred_element_type=f32).astype(bf)
    column_sum(sums, 0, BRANCH_SCALE * entire)
    column_sum(sums, 1, grad * hat)
    column_sum(sums, 2, grad)
    column_sum(sums, 3, BRANCH_SCALE * out_grad)


def after_part(info, rows, middle, mlp, back, cot, packs, vec_rel, cols):
    shape = middle.shape
    slim = like((shape[0], cols), bf)
    return by_rows(
        functools.partial(after_kernel, rows), info, (middle, mlp, back, cot, packs, vec_rel), (None,) * 6,
        [like(shape, bf), like(shape, f32), like(shape, bf), slim, slim, like((8, shape[1]), f32)],
        [pltpu.VMEM((shape[1], shape[1]), bf)])


def feed_kernel(info, n2, d_mlp, bias, fc_got, pr_got, fc00, fc01, fc10, fc11, pr0, pr1,
                acc, back, fc_lo, fc_hi, pr_lo, pr_hi, d_bias, n2_t, d_t, w_fc, w_pr, act, d_pre):
    step = pl.program_id(0)
    total, half = n2.shape[0], n2.shape[1] // 2

    @pl.when(step == 0)
    def _():
        acc[...] = jnp.zeros_like(acc)
        back[...] = jnp.zeros_like(back)
        n2_t[...] = n2[...].T
        d_t[...] = d_mlp[...].T

    @pl.when(step < pl.num_programs(0) // 2)
    def _():
        w_fc[: half // 2], w_fc[half // 2 : half], w_pr[:half] = fc00[...], fc01[...], pr0[...]

    @pl.when(step >= pl.num_programs(0) // 2)
    def _():
        w_fc[: half // 2], w_fc[half // 2 : half], w_pr[:half] = fc10[...], fc11[...], pr1[...]

    w_fc[half:], w_pr[half:] = fc_got[0], pr_got[0]
    root = 0.7978845608
    count = total // ROWS
    raw = {}
    grad_sum = jnp.zeros((1, w_fc.shape[1]), f32)

    def products(k):
        at = slice(k * ROWS, (k + 1) * ROWS)
        return (
            jnp.dot(n2[at], w_fc[...], preferred_element_type=f32) + bias[...],
            jnp.dot(d_mlp[at], w_pr[...], preferred_element_type=f32))

    def add_back(k):
        at = slice(k * ROWS, (k + 1) * ROWS)
        acc[at] += lax.dot_general(act[at], w_pr[...], NT, preferred_element_type=f32)
        back[at] += lax.dot_general(d_pre[at], w_fc[...], NT, preferred_element_type=f32)

    raw[0] = products(0)
    for k in range(count):
        at = slice(k * ROWS, (k + 1) * ROWS)
        if k + 1 < count:
            raw[k + 1] = products(k + 1)
        pre, d_act = raw.pop(k)
        square = pre * pre
        inner = jnp.tanh(pre * (root + root * 0.044715 * square))
        gate = 0.5 + 0.5 * inner
        act[at] = (pre * gate).astype(bf)
        slope = gate + pre * (0.5 - 0.5 * inner * inner) * (root + root * 3 * 0.044715 * square)
        grad = d_act * slope
        grad_sum = grad_sum + jnp.sum(grad, axis=0, keepdims=True)
        d_pre[at] = grad.astype(bf)
        if k > 0:
            add_back(k - 1)
    add_back(count - 1)
    d_bias[...] = grad_sum
    for out, left, right, low in (
        (fc_hi, n2_t, d_pre, half), (pr_hi, d_t, act, half), (fc_lo, n2_t, d_pre, 0), (pr_lo, d_t, act, 0)):
        out[0] = jnp.dot(left[low : low + half], right[...], preferred_element_type=f32).astype(bf)


def feed_part(info, n2, d_mlp, bias, fc_got, pr_got, fc_parts, proj_parts):
    (total, width), hidden, half = n2.shape, bias.shape[1] // 2, n2.shape[1] // 2
    steps = hidden // HIDDEN
    fixed = lambda a: pl.BlockSpec(a.shape, lambda k, s: (0,) * len(a.shape), pipeline_mode=pl.Buffered(1))
    early = lambda a: pl.BlockSpec((a.shape[0], HIDDEN), lambda k, s: (0, jnp.minimum(k, steps - 1)))
    late = lambda a: pl.BlockSpec((a.shape[0], HIDDEN), lambda k, s: (0, jnp.maximum(k - steps, 0)))
    two = lambda a: pl.BlockSpec((1, a.shape[1], HIDDEN), lambda k, s: (k // steps, 0, k % steps))
    unit = pl.BlockSpec((1, HIDDEN), lambda k, s: (0, (s[3] + (k // steps) * (1 - 2 * s[3])) * steps + k % steps))
    grad = like((2, half, hidden), bf)
    sums = [like((total, width), f32)] * 2
    return pl.pallas_call(
        feed_kernel,
        grid_spec=pltpu.PrefetchScalarGridSpec(
            num_scalar_prefetch=1,
            grid=(2 * steps,),
            in_specs=[fixed(n2), fixed(d_mlp), unit, two(fc_got), two(pr_got)]
            + [early(a) for a in fc_parts[0]] + [late(a) for a in fc_parts[1]] + [early(proj_parts[0]), late(proj_parts[1])],
            out_specs=[fixed(o) for o in sums] + [two(grad)] * 4 + [unit],
            scratch_shapes=[
                pltpu.VMEM((width, total), bf), pltpu.VMEM((width, total), bf), pltpu.VMEM((width, HIDDEN), bf),
                pltpu.VMEM((width, HIDDEN), bf), pltpu.VMEM((total, HIDDEN), bf), pltpu.VMEM((total, HIDDEN), bf)],
        ),
        out_shape=sums + [grad] * 4 + [like((1, 2 * hidden), f32)],
        cost_estimate=pl.CostEstimate(flops=1 << 22, bytes_accessed=1 << 18, transcendentals=0),
        compiler_params=pltpu.CompilerParams(vmem_limit_bytes=60 << 20),
    )(info, n2, d_mlp, bias, fc_got, pr_got, *fc_parts[0], *fc_parts[1], *proj_parts)


def weight_kernel(n1, d_attn, d_qkv, o, lo, hi, left_t):
    step, half = pl.program_id(0), left_t.shape[0] // 2

    @pl.when(step == 0)
    def _():
        left_t[...] = n1[...].T

    def products(right):
        for out, low in ((hi, half), (lo, 0)):
            out[...] = jnp.dot(left_t[low : low + half], right[...], preferred_element_type=f32).astype(bf)

    @pl.when(step < pl.num_programs(0) - 1)
    def _():
        products(d_qkv)

    @pl.when(step == pl.num_programs(0) - 1)
    def _():
        left_t[...] = d_attn[...].T
        products(o)


def weight_part(n1, d_attn, d_qkv, o):
    (n, width), cols = n1.shape, o.shape[1]
    steps = d_qkv.shape[1] // cols
    fixed = lambda a: pl.BlockSpec(a.shape, lambda k: (0, 0), pipeline_mode=pl.Buffered(1))
    out = pl.BlockSpec((width // 2, cols), lambda k: (0, k))
    grad = like((width // 2, d_qkv.shape[1] + cols), bf)
    return pl.pallas_call(
        weight_kernel,
        grid=(steps + 1,),
        in_specs=[fixed(n1), fixed(d_attn), pl.BlockSpec((n, cols), lambda k: (0, jnp.minimum(k, steps - 1))), fixed(o)],
        out_specs=[out, out],
        out_shape=[grad, grad],
        scratch_shapes=[pltpu.VMEM((width, n), bf)],
        cost_estimate=pl.CostEstimate(flops=1 << 22, bytes_accessed=1 << 18, transcendentals=0),
        compiler_params=pltpu.CompilerParams(vmem_limit_bytes=32 << 20),
    )(n1, d_attn, d_qkv, o)


def token_kernel(rows, fan, info, own, rest, x, d_middle, weights, vec_rel, mid_sums, fc_grad, grad_out, small, own_sums, rest_sums, vecs, nat, order, fan_rows):
    width, cols = x.shape[1], own.shape[1] // 3
    step = pl.program_id(0)

    @pl.when(step == 0)
    def _():
        order[...] = order_matrix(info[1], rows, width)
        for ref in (own_sums, rest_sums, vecs, nat, fan_rows):
            ref[...] = jnp.zeros_like(ref)

    grad = lax.dot_general(own[...], weights[0], NT, preferred_element_type=f32)
    grad = grad + lax.dot_general(rest[...], weights[1], NT, preferred_element_type=f32)
    hat, inverse = norm_parts(x[...].astype(f32))
    low = (d_middle[...] + norm_back(hat, inverse, vec_rel[0:1], grad)).astype(bf)
    grad_out[...] = lax.dot_general(low, order[...], NT, preferred_element_type=f32).astype(bf)
    column_sum(own_sums, 0, own[...].astype(f32))
    column_sum(rest_sums, 0, rest[...].astype(f32))
    column_sum(vecs, 0, grad * hat)
    column_sum(vecs, 1, grad)

    @pl.when(step == pl.num_programs(0) - 1)
    def _():
        for group, ref in ((info[0], own_sums), (1 - info[0], rest_sums)):
            for row, part_index in ((0, 0), (1, 2)):
                picks = [ref[0:1, (3 * g + part_index) * 128 : (3 * g + part_index + 1) * 128] for g in range(cols // 128)]
                nat[row : row + 1, pl.ds(pl.multiple_of(group * cols, 128), cols)] = jnp.concatenate(picks, axis=1)
        count = width // 128
        for k in range(count):
            fan_rows[k : k + 1] = fc_grad[:, k * 128 * fan : (k + 1) * 128 * fan]
        spread = lax.dot_general(fan_rows[...].astype(bf), fan_matrix(fan), NT, preferred_element_type=f32)
        for k in range(count):
            for m in range(fan):
                nat[2 + m : 3 + m, k * 128 : (k + 1) * 128] = spread[k : k + 1, m * 128 : (m + 1) * 128]
        moved = jnp.dot(nat[...].astype(bf), order[...], preferred_element_type=f32)
        vecs[2:4] = moved[0:2]
        vecs[4:8] = mid_sums[0:4]
        vecs[8 : 8 + fan] = moved[2 : 2 + fan]
        small[...] = vecs[...].T.astype(bf)


def token_part(info, rows, own, rest, x, d_middle, weights, vec_rel, mid_sums, fc_grad):
    n, width = x.shape
    wide, fan = own.shape[1], fc_grad.shape[1] // width
    return by_rows(
        functools.partial(token_kernel, rows, fan), info, (own, rest, x, d_middle, weights, vec_rel, mid_sums, fc_grad), (None,) * 8,
        [like((n, width), bf), like((width, SMALL), bf)],
        [pltpu.VMEM((8, wide), f32), pltpu.VMEM((8, wide), f32), pltpu.VMEM((SMALL, width), f32), pltpu.VMEM((8, width), f32),
         pltpu.VMEM((width, width), bf), pltpu.VMEM((8, 128 * fan), f32)])


def on_device(
    tokens, segment_ids, ln1_gain, ln1_bias, w_qkv, b_qv, w_attn_out, b_attn_out,
    ln2_gain, ln2_bias, w_fc, b_fc, w_proj, b_proj, cotangent,
):
    dp_size = lax.axis_size("dp")
    dp_pos, t_pos = lax.axis_index("dp"), lax.axis_index("tensor")
    core = dp_pos % 2
    rows = ln1_gain.shape[0]
    width = tokens.shape[1]
    cols = w_qkv.shape[2]
    hidden = w_fc.shape[1]
    fan = b_fc.shape[0] // rows
    far = [1 << k for k in range(dp_size.bit_length() - 2, 1, -1)]
    swap = []
    for d in range(dp_size):
        for t in range(2):
            if d % 2 != t:
                swap.append((2 * d + t, 2 * (d - d % 2 + t) + d % 2))
    mine = core == t_pos

    pairs = cols // 128

    def by_pair(parts):
        parts = parts.reshape(-1, 3, pairs, 128)
        return jnp.swapaxes(parts, 1, 2).reshape(-1, 3 * cols)

    def by_part(columns):
        return jnp.swapaxes(columns.reshape(-1, pairs, 3, 128), 1, 2).reshape(-1, 3, cols)

    flat = jnp.concatenate([ln1_gain, ln1_bias, b_qv.reshape(-1), b_attn_out, ln2_gain, ln2_bias, b_proj])
    small = jnp.concatenate([flat.reshape(8, rows).T, b_fc.reshape(rows, fan)], axis=1)
    small = jnp.pad(small, ((0, 0), (0, SMALL - small.shape[1])))
    out_pack = jnp.concatenate([w_attn_out.T, small], axis=1)
    tokens, seg_other, all_qkv, all_out, fc_far, proj_far = head(
        dp_size, tokens, segment_ids, (by_pair(w_qkv), out_pack, w_fc, w_proj.T), chunks_of(3 * cols, 0, 2) + chunks_of(cols + SMALL, 1, 1))
    all_qkv, all_out = (a.reshape(2, width, -1) for a in (all_qkv, all_out))
    fc_far, proj_far = fc_far.reshape(-1, hidden), proj_far.reshape(-1, hidden)
    fc_parts = [[fc_far], [exchange(fc_far, 0, dp_size)]]
    proj_half = exchange(proj_far, 2, dp_size)

    part = jnp.stack([core, dp_pos, jnp.where(mine, 1, 0), t_pos]).astype(jnp.int32)
    x, n1, qkv_send, vec_rel, vec_nat, fc_bias, starts = project_first(
        part, rows, fan, tokens, all_out, all_qkv, segment_ids, seg_other)
    qkv_own, qkv_recv = project_own(n1, qkv_send, all_qkv, vec_nat)
    fc_parts, proj_half, qkv_own = lax.optimization_barrier((fc_parts, proj_half, qkv_own))
    fc_parts = [p + [exchange(p[0], 2, dp_size)] for p in fc_parts]
    proj_half = jnp.concatenate([proj_far, proj_half], axis=0)
    proj_parts = [proj_half, exchange(proj_half, 0, dp_size)]
    o_own, o_send, lse = attn_fwd(qkv_own, qkv_recv, starts, part)
    cot_recv = lax.ppermute(cotangent, BOTH, swap)
    half = width // 2
    middle, n2, cot, d_mlp, o_recv, fc_got, pr_got = middle_part(
        rows, x, o_own, o_send, cotangent, cot_recv, all_out, vec_rel, fc_parts, proj_parts)
    mlp, back, fc_lo, fc_hi, pr_lo, pr_hi, fc_grad = feed_part(
        part, n2, d_mlp, fc_bias, fc_got, pr_got, fc_parts, proj_parts)
    fc_got, pr_got = exchange(fc_hi, 1, dp_size), exchange(pr_hi, 1, dp_size)
    block_out, d_middle, d_attn, do_own, do_send, mid_sums = after_part(
        part, rows, middle, mlp, back, cot, all_out, vec_rel, cols)
    do_recv = exchange(do_send, 1, dp_size)

    near_size = half // 2
    fc_rest = add_low(fc_lo[1], fc_got[1])
    pr_rest = add_low(pr_lo[:, near_size:], pr_got[:, near_size:])
    last = (qkv_own, qkv_recv, do_own, do_recv, o_own, o_send)
    last, fc_rest, pr_rest = lax.optimization_barrier((last, fc_rest, pr_rest))
    fc_sent = exchange(fc_rest, 0, dp_size)
    pr_sent = exchange(pr_rest, 2, dp_size)
    block_recv = lax.ppermute(block_out, BOTH, swap)
    dq_own, dq_send = attn_bwd(*last, starts, lse, part)
    dq_recv = exchange(dq_send, 1, dp_size)
    dq_own, fc_sent, pr_sent = lax.optimization_barrier((dq_own, fc_sent, pr_sent))
    fc_rest = add_low(fc_lo[0, near_size:], fc_got[0, near_size:], fc_sent[near_size:])
    pr_rest = add_low(pr_lo[1, :near_size], pr_got[1, :near_size], pr_sent[1])
    dq_own, fc_rest, pr_rest = lax.optimization_barrier((dq_own, fc_rest, pr_rest))
    fc_near = exchange(fc_rest, 2, dp_size)
    pr_near = exchange(pr_rest, 0, dp_size)
    own_lo, own_hi = weight_part(n1, d_attn, dq_own, o_own)
    own_lo, fc_near, pr_near = lax.optimization_barrier((own_lo, fc_near, pr_near))
    sum_fc = add_low(fc_lo[0, :near_size], fc_got[0, :near_size], fc_sent[:near_size], fc_near)
    sum_proj = add_low(pr_lo[0, :near_size], pr_got[0, :near_size], pr_sent[0], pr_near)
    feed = jnp.concatenate([sum_fc, sum_proj], axis=1).reshape(-1, rows, 2 * hidden)
    dq_recv, feed = lax.optimization_barrier((dq_recv, feed))
    grad_tokens, d_small = token_part(part, rows, dq_own, dq_recv, x, d_middle, all_qkv, vec_rel, mid_sums, fc_grad)
    grad_recv = lax.ppermute(grad_tokens, BOTH, swap)
    dq_recv, d_small = lax.optimization_barrier((dq_recv, d_small))
    rest_lo, rest_hi = weight_part(n1, d_attn, dq_recv, o_recv)
    blocks = lambda arr: arr.reshape(dp_size // 2, rows, -1)
    sum_a, vecs, sum_feed = tail(
        dp_size, (blocks(own_lo), blocks(own_hi)), (blocks(rest_lo), blocks(rest_hi)),
        (blocks(d_small[:half]), blocks(d_small[half:])), feed)
    vecs, block_recv, grad_recv = lax.optimization_barrier((vecs, block_recv, grad_recv))
    block_out = jnp.where(mine, block_out, block_recv)
    grad_tokens = jnp.where(mine, grad_tokens, grad_recv)
    return (
        block_out,
        grad_tokens,
        vecs[:, 0],
        vecs[:, 1],
        by_part(sum_a[:, : 3 * cols]),
        vecs[:, 2:4].T,
        sum_a[:, 3 * cols :].T,
        vecs[:, 4],
        vecs[:, 5],
        vecs[:, 6],
        sum_feed[:, :hidden],
        vecs[:, 8 : 8 + fan].reshape(rows * fan),
        sum_feed[:, hidden:].T,
        vecs[:, 7],
    )


def solution(mesh):
    vec, tok = P("dp"), P(BOTH, None)
    in_specs = (
        tok, P("dp", None), vec, vec, P("dp", None, "tensor"), P(None, "dp"), P("tensor", "dp"),
        vec, vec, vec, P("dp", "tensor"), vec, P("tensor", "dp"), vec, tok,
    )
    out_specs = (
        tok, tok, vec, vec, P("dp", None, "tensor"), P(None, "dp"), P("tensor", "dp"),
        vec, vec, vec, P("dp", "tensor"), vec, P("tensor", "dp"), vec,
    )
    return jax.shard_map(on_device, mesh=mesh, in_specs=in_specs, out_specs=out_specs, check_vma=False)
```

```python
import functools

import jax
import jax.numpy as jnp
from jax import lax
from jax.experimental import pallas as pl
from jax.experimental.pallas import tpu as pltpu
from jax.sharding import PartitionSpec as P

HD = 64
QB = 256
NEG = -1e30
EPSILON = 1e-05
BRANCH_SCALE = 48.0 ** (-0.5)
SMALL = 128
VECS = 16
ROWS = 256
HIDDEN = 768
bf = jnp.bfloat16
f32 = jnp.float32
NT = (((1,), (1,)), ((), ()))
TN = (((0,), (0,)), ((), ()))
BOTH = ("dp", "tensor")
MESH_ID = pl.DeviceIdType.MESH
ANY = pl.BlockSpec(memory_space=pl.ANY)
VM = pl.BlockSpec(memory_space=pltpu.VMEM)
HBM = pl.BlockSpec(memory_space=pltpu.HBM)
SM = pl.BlockSpec(memory_space=pltpu.SMEM)


def attn_mask(kat, at, srow):
    keys = lax.broadcasted_iota(jnp.int32, (QB, QB), 0)
    rows = lax.broadcasted_iota(jnp.int32, (1, QB), 1) + (at - kat)
    return (keys >= srow - kat) & (keys <= rows)


def over_blocks(bounds, i, step, carry):
    low = bounds[0, i * QB] // QB
    mid = jnp.minimum((bounds[0, i * QB + QB - 1] + QB - 1) // QB, i)
    carry = lax.fori_loop(0, mid - low + 1, lambda k, c: step(True, jnp.where(k == 0, i, low + k - 1), c), carry)
    return lax.fori_loop(mid, i, functools.partial(step, False), carry)


def head_lanes(values):
    low = (lax.broadcasted_iota(jnp.int32, (1, values.shape[1]), 1) % 128) < HD
    zero = jnp.zeros((), bf)
    return jnp.where(low, values, zero), jnp.where(low, zero, values)


def fwd_kernel(info, bounds, own, recv, st_ref, okeep, osend, lse_ref, qm, ks, vt, osc, acc):
    half, cols = own.shape[0], own.shape[1] // 3
    n, nb, heads, pairs = 2 * half, 2 * half // QB, cols // HD, cols // 128
    c = info[0]
    for base, src in ((c * half, own), ((1 - c) * half, recv)):
        rows = pl.ds(pl.multiple_of(base, half), half)
        for g in range(pairs):
            lanes = slice(g * 128, (g + 1) * 128)
            part = lambda k: src[:, (3 * g + k) * 128 : (3 * g + k + 1) * 128]
            qm[0, rows, lanes], qm[1, rows, lanes] = head_lanes(part(0) * bf(HD**-0.5))
            ks[rows, lanes] = part(1)
            vt[lanes, rows] = part(2).T

    def qblock(i, _):
        at = pl.multiple_of(i * QB, QB)
        qr = pl.ds(at, QB)
        srow = st_ref[:, qr]
        acc[...] = jnp.zeros_like(acc)

        def step(masked, j, carry):
            kat = pl.multiple_of(j * QB, QB)
            kr = pl.ds(kat, QB)
            if masked:
                mask = attn_mask(kat, at, srow)
            scores, mixed = [], []
            for h in range(heads):
                lanes = slice(h // 2 * 128, h // 2 * 128 + 128)
                one = lax.dot_general(ks[kr, lanes], qm[h % 2, qr, lanes], NT, preferred_element_type=f32)
                scores.append(jnp.where(mask, one, NEG) if masked else one)
            for h in range(heads):
                top, total = carry[h]
                new = jnp.maximum(top, jnp.max(scores[h], axis=0, keepdims=True))
                weights = jnp.exp(scores[h] - new)
                fade = jnp.exp(top - new)
                total = fade * total + jnp.sum(weights, axis=0, keepdims=True)
                mixed.append((new, total, fade, weights.astype(bf)))
            for h in range(heads):
                sub = slice(h * HD, (h + 1) * HD)
                acc[sub] = mixed[h][2] * acc[sub] + jnp.dot(vt[sub, kr], mixed[h][3], preferred_element_type=f32)
            return tuple(m[:2] for m in mixed)

        carry = over_blocks(bounds, i, step, ((jnp.full((1, QB), NEG, f32), jnp.zeros((1, QB), f32)),) * heads)
        for h, (top, total) in enumerate(carry):
            sub = slice(h * HD, (h + 1) * HD)
            acc[sub] = acc[sub] / total
            lse_ref[h : h + 1, qr] = top + jnp.log(total)
        osc[qr] = acc[...].T.astype(bf)
        return 0

    lax.fori_loop(0, nb, qblock, 0)
    okeep[...] = osc[pl.ds(pl.multiple_of(c * half, half), half)]
    osend[...] = osc[pl.ds(pl.multiple_of((1 - c) * half, half), half)]


def attn_fwd(own, recv, starts, info):
    half, cols = own.shape[0], own.shape[1] // 3
    n = 2 * half
    return pl.pallas_call(
        fwd_kernel,
        in_specs=[SM, SM, VM, VM, VM],
        out_specs=[VM] * 3,
        scratch_shapes=[
            pltpu.VMEM((2, n, cols), bf), pltpu.VMEM((n, cols), bf), pltpu.VMEM((cols, n), bf),
            pltpu.VMEM((n, cols), bf), pltpu.VMEM((cols, QB), f32)],
        out_shape=[jax.ShapeDtypeStruct((half, cols), bf)] * 2 + [jax.ShapeDtypeStruct((cols // HD, n), f32)],
        cost_estimate=pl.CostEstimate(flops=n * n, bytes_accessed=n * 128, transcendentals=0),
        compiler_params=pltpu.CompilerParams(vmem_limit_bytes=30 << 20),
    )(info, starts, own, recv, starts)


def bwd_kernel(info, bounds, own, recv, doo, dor, oo, orr, st_ref, lse_ref, dkeep, dsend, qm, ks, vs, kt, dom, dlt, dqs, dks, dvs):
    half, cols = own.shape[0], own.shape[1] // 3
    n, nb, heads, pairs = 2 * half, 2 * half // QB, cols // HD, cols // 128
    c = info[0]
    lanes_of = lambda g: slice(g * 128, (g + 1) * 128)
    for base, src, do, o in ((c * half, own, doo, oo), ((1 - c) * half, recv, dor, orr)):
        rows = pl.ds(pl.multiple_of(base, half), half)
        for g in range(pairs):
            lanes = lanes_of(g)
            part = lambda k: src[:, (3 * g + k) * 128 : (3 * g + k + 1) * 128]
            qm[0, rows, lanes], qm[1, rows, lanes] = head_lanes(part(0) * bf(HD**-0.5))
            ks[rows, lanes] = part(1)
            vs[rows, lanes] = part(2)
            kt[lanes, rows] = part(1).T
            grad = do[:, lanes]
            dom[0, rows, lanes], dom[1, rows, lanes] = head_lanes(grad)
            prod = (grad.astype(f32) * o[:, lanes].astype(f32)).T
            for e in range(2):
                dlt[2 * g + e : 2 * g + e + 1, rows] = jnp.sum(prod[e * HD : (e + 1) * HD], axis=0, keepdims=True)
    dks[...] = jnp.zeros_like(dks)
    dvs[...] = jnp.zeros_like(dvs)

    def qblock(i, _):
        at = pl.multiple_of(i * QB, QB)
        qr = pl.ds(at, QB)
        srow = st_ref[:, qr]
        dqs[...] = jnp.zeros_like(dqs)

        def step(masked, j, carry):
            kat = pl.multiple_of(j * QB, QB)
            kr = pl.ds(kat, QB)
            if masked:
                mask = attn_mask(kat, at, srow)
            scores, softs, grads = [], [], []
            for h in range(heads):
                lanes = lanes_of(h // 2)
                one = lax.dot_general(ks[kr, lanes], qm[h % 2, qr, lanes], NT, preferred_element_type=f32)
                back = lax.dot_general(vs[kr, lanes], dom[h % 2, qr, lanes], NT, preferred_element_type=f32)
                scores.append((jnp.where(mask, one, NEG) if masked else one, back))
            for h in range(heads):
                soft = jnp.exp(scores[h][0] - lse_ref[h : h + 1, qr])
                grads.append((soft * (scores[h][1] - dlt[h : h + 1, qr])).astype(bf))
                softs.append(soft.astype(bf))
            for g in range(pairs):
                lanes = lanes_of(g)
                both = lambda ref: jnp.concatenate([ref[0, qr, lanes], ref[1, qr, lanes]], axis=0)
                two = slice(2 * g, 2 * g + 2)
                dvs[kr, lanes] += jnp.dot(jnp.concatenate(softs[two], axis=1), both(dom), preferred_element_type=f32)
                dks[kr, lanes] += jnp.dot(jnp.concatenate(grads[two], axis=1), both(qm), preferred_element_type=f32)
                for h in (2 * g, 2 * g + 1):
                    sub = slice(h * HD, (h + 1) * HD)
                    dqs[sub] += jnp.dot(kt[sub, kr], grads[h], preferred_element_type=f32)
            return carry

        over_blocks(bounds, i, step, 0)
        qm[0, qr] = (dqs[...] * (HD**-0.5)).T.astype(bf)
        return 0

    lax.fori_loop(0, nb, qblock, 0)
    for dst, base in ((dkeep, c * half), (dsend, (1 - c) * half)):
        rows = pl.ds(pl.multiple_of(base, half), half)
        for g in range(pairs):
            for k, value in enumerate((qm[0, rows, lanes_of(g)], dks[rows, lanes_of(g)], dvs[rows, lanes_of(g)])):
                dst[:, (3 * g + k) * 128 : (3 * g + k + 1) * 128] = value.astype(bf)


def attn_bwd(own, recv, do_own, do_recv, o_own, o_recv, starts, lse, info):
    half, cols = own.shape[0], own.shape[1] // 3
    n = 2 * half
    return pl.pallas_call(
        bwd_kernel,
        in_specs=[SM, SM] + [VM] * 8,
        out_specs=[VM] * 2,
        scratch_shapes=[
            pltpu.VMEM((2, n, cols), bf), pltpu.VMEM((n, cols), bf), pltpu.VMEM((n, cols), bf), pltpu.VMEM((cols, n), bf),
            pltpu.VMEM((2, n, cols), bf), pltpu.VMEM((cols // HD, n), f32), pltpu.VMEM((cols, QB), f32),
            pltpu.VMEM((n, cols), f32), pltpu.VMEM((n, cols), f32)],
        out_shape=[like((half, 3 * cols), bf)] * 2,
        cost_estimate=pl.CostEstimate(flops=n * n, bytes_accessed=n * 128, transcendentals=0),
        compiler_params=pltpu.CompilerParams(vmem_limit_bytes=56 << 20),
    )(info, starts, own, recv, do_own, do_recv, o_own, o_recv, starts, lse)


def dot(left, right, dims=(((1,), (0,)), ((), ()))):
    return lax.dot_general(left, right, dims, preferred_element_type=f32)


def exchange(value, bit, dp_size):
    if bit:
        return lax.ppermute(value, "dp", [(i, i ^ bit) for i in range(dp_size)])
    return lax.ppermute(value, "tensor", [(0, 1), (1, 0)])


def flip(index, bits):
    for bit in bits:
        index = index + bit * (1 - 2 * ((index // bit) % 2))
    return index

def far_groups(dp_size):
    far = [1 << k for k in range(dp_size.bit_length() - 2, 1, -1)]
    return [tuple(far[k : k + 2]) for k in range(0, len(far), 2)]

def group_moves(group):
    if len(group) == 1:
        return [(1, group)]
    return [(1, group[:1]), (2, group[1:]), (3, group)]

def chunks_of(cols, which, count, until=None):
    tiles = cols // 128
    cuts = [128 * ((tiles * k) // count) for k in range(count + 1)]
    arrays = range(which, until + 1) if until else (which,)
    return tuple(
        (array, low, high - low, 128 * ((high - low) // 256 + (high - low) // 128 % 2))
        for low, high in zip(cuts, cuts[1:]) for array in arrays)


def head_kernel(groups, chunks, tokens, seg, *refs):
    shards, x_out, seg_out, outs, (send_sem, recv_sem, local_sem) = refs[:4], refs[4], refs[5], refs[6:10], refs[10:]
    dp, t = lax.axis_index("dp"), lax.axis_index("tensor")
    core = dp % 2
    away = core + t - 2 * core * t
    near = {1: (flip(dp, (1,)), t), 2: (flip(dp, (2,)), t), 0: (dp, 1 - t)}
    distant = [bits for group in groups for _, bits in group_moves(group)]
    swap = (dp - core + t, core)
    barrier = pltpu.get_barrier_semaphore()
    for device in list(near.values()) + [(flip(dp, bits), t) for bits in distant]:
        pl.semaphore_signal(barrier, inc=1, device_id=device, device_id_type=MESH_ID)

    @pl.when(away == 1)
    def _():
        pl.semaphore_signal(barrier, inc=1, device_id=swap, device_id_type=MESH_ID)

    local = [
        pltpu.make_async_copy(shards[k], outs[k].at[away, 0] if k < 2 else outs[k].at[0], local_sem.at[k]) for k in range(4)]
    for copy in local:
        copy.start()
    pl.semaphore_wait(barrier, len(near) + len(distant) + away)
    count = [0]

    def remote(src, dst, device):
        slot = count[0]
        count[0] += 1
        return pltpu.make_async_remote_copy(
            src_ref=src, dst_ref=dst, send_sem=send_sem.at[slot], recv_sem=recv_sem.at[slot],
            device_id=device, device_id_type=MESH_ID)

    def blocks(ref, index, first, held, low, size):
        return ref.at[index, pl.ds(first, held), :, pl.ds(low, size)]

    plans = []
    for which, low, size, part in chunks:
        shard, out = shards[which], outs[which]
        steps, held = [], 1
        for group in groups:
            moves = []
            for place, bits in group_moves(group):
                src = shard.at[:, pl.ds(low, size)] if held == 1 else blocks(out, away, 0, held, low, size)
                dst = out.at[away, place, :, pl.ds(low, size)] if held == 1 else blocks(out, away, place * held, held, low, size)
                moves.append(remote(src, dst, (flip(dp, bits), t)))
            held *= len(group_moves(group)) + 1
            steps.append(moves)
        a, b = (low, part), (low + part, size - part)
        steps.append([
            remote(blocks(out, away, 0, held, *a), blocks(out, away, 0, held, *a), near[0]),
            remote(blocks(out, away, 0, held, *b), blocks(out, away, held, held, *b), near[2]),
        ])
        steps.append(
            [remote(blocks(out, k, 0, held, *a), blocks(out, k, held, held, *a), near[2]) for k in range(2)]
            + [remote(blocks(out, away, 0, 2 * held, *b), blocks(out, away, 0, 2 * held, *b), near[0])])
        steps.append([
            remote(blocks(out, k, 0, 2 * held, low, size),
                   blocks(out, 1 - k, 2 * held, 2 * held, low, size), near[1]) for k in range(2)])
        plans.append(steps)
    later = []
    held = 1
    for group in groups:
        moves = []
        for place, bits in group_moves(group):
            for shard, out in zip(shards[2:], outs[2:]):
                src = shard if held == 1 else out.at[pl.ds(0, held)]
                dst = out.at[place] if held == 1 else out.at[pl.ds(place * held, held)]
                moves.append(remote(src, dst, (flip(dp, bits), t)))
        held *= len(group_moves(group)) + 1
        later.append(moves)
    depth = len(plans[0])
    swap_copy = remote(tokens, x_out, swap)
    seg_copy = remote(seg, seg_out, near[1])
    stay_copy = pltpu.make_async_copy(tokens, x_out, local_sem.at[4])
    waited = set()

    def advance(number, phase):
        if number >= len(plans):
            return
        if phase > 0:
            for move in plans[number][phase - 1]:
                move.wait_recv()
        if phase == 1 and chunks[number][0] not in waited:
            waited.add(chunks[number][0])
            local[chunks[number][0]].wait()
        if phase < depth:
            for move in plans[number][phase]:
                move.start()

    advance(0, 0)
    seg_copy.start()

    @pl.when(away == 1)
    def _():
        swap_copy.start()

    @pl.when(away == 0)
    def _():
        stay_copy.start()

    far = len(groups)
    for number in range(len(plans)):
        if number == 0:
            for phase in range(1, far + 1):
                advance(0, phase)
            for k in range(1, len(plans)):
                advance(k, 0)
            for move in later[0]:
                move.start()
        advance(number, far + 1)
        for phase in range(1, far + 1):
            advance(number + 1, phase)
        advance(number, far + 2)
    for number in range(len(plans)):
        advance(number, depth)

    @pl.when(away == 1)
    def _():
        swap_copy.wait()

    @pl.when(away == 0)
    def _():
        stay_copy.wait()

    seg_copy.wait()
    for which in sorted(set(range(4)) - waited):
        local[which].wait()
    for k, moves in enumerate(later):
        if k > 0:
            for move in moves:
                move.start()
        for move in moves:
            move.wait()
    for steps in plans:
        for moves in steps:
            for move in moves:
                move.wait_send()


def head(dp_size, tokens, seg, shards, chunks):
    groups = far_groups(dp_size)
    partners = sum(len(group_moves(g)) for g in groups)
    slots = len(chunks) * (partners + 7) + 2 * partners + 2
    shapes = [(2, dp_size)] * 2 + [(dp_size // 4,)] * 2
    return pl.pallas_call(
        functools.partial(head_kernel, groups, chunks),
        in_specs=[VM] * 6,
        out_specs=[ANY] * 6,
        out_shape=[jax.ShapeDtypeStruct(a.shape, a.dtype) for a in (tokens, seg)]
        + [jax.ShapeDtypeStruct(lead + s.shape, s.dtype) for lead, s in zip(shapes, shards)],
        scratch_shapes=[pltpu.SemaphoreType.DMA((slots,)), pltpu.SemaphoreType.DMA((slots,)), pltpu.SemaphoreType.DMA((5,))],
        compiler_params=pltpu.CompilerParams(collective_id=0, has_side_effects=True),
    )(tokens, seg, *shards)


def tail_kernel(groups, own_lo, own_hi, rest_lo, rest_hi, small_lo, small_hi, feed, total, vecs, feed_total,
                feed_part, feed_got, part, got_core, got_near, got_last, got_far, vec, vec_core, vec_two, vec_one, vec_far, send_sem, recv_sem):
    dp, t = lax.axis_index("dp"), lax.axis_index("tensor")
    core = dp % 2
    away = core + t - 2 * core * t
    near = {1: (flip(dp, (1,)), t), 2: (flip(dp, (2,)), t), 0: (dp, 1 - t)}
    distant = [bits for group in groups for _, bits in group_moves(group)]
    barrier = pltpu.get_barrier_semaphore()
    for device in list(near.values()) + [(flip(dp, bits), t) for bits in distant]:
        pl.semaphore_signal(barrier, inc=1, device_id=device, device_id_type=MESH_ID)

    pl.semaphore_wait(barrier, len(near) + len(distant))
    count = [0]

    def remote(src, dst, device):
        slot = count[0]
        count[0] += 1
        return pltpu.make_async_remote_copy(
            src_ref=src, dst_ref=dst, send_sem=send_sem.at[slot], recv_sem=recv_sem.at[slot],
            device_id=device, device_id_type=MESH_ID)

    half, rows, cols = own_lo.shape
    quarter = half // 2
    chunks = [pl.ds(low, min(384, cols - low)) for low in range(0, cols, 384)]
    to_core = [[
        remote(rest_hi.at[:, :, c], got_core.at[0, :, :, c], near[1]),
        remote(own_hi.at[:, :, c], got_core.at[1, :, :, c], near[1])] for c in chunks]
    to_core[0].append(remote(small_hi, vec_core, near[1]))
    for moves in to_core:
        for move in moves:
            move.start()

    feed_steps = []
    held, used = feed.shape[0], 0
    for number, group in enumerate(reversed(groups)):
        moves = group_moves(group)
        held //= len(moves) + 1
        source, step = feed if number == 0 else feed_part, []
        for place, bits in moves:
            step.append(remote(source.at[pl.ds(place * held, held)], feed_got.at[pl.ds(used, held)], (flip(dp, bits), t)))
            used += held
        feed_steps.append((step, source, held, used - held * len(moves), len(moves)))
    for move in feed_steps[0][0]:
        move.start()

    def add(*terms):
        out = terms[0].astype(f32)
        for term in terms[1:]:
            out = out + term.astype(f32)
        return out.astype(bf)

    upper, lower = pl.ds(quarter, quarter), pl.ds(0, quarter)
    mine, other = away, 1 - away
    last = len(chunks) - 1
    steps, sent = {}, []

    def start(key, moves):
        steps[key] = moves
        sent.extend(moves)
        for move in moves:
            move.start()

    def arrive(key):
        for move in steps[key]:
            move.wait_recv()

    def core_stage(k):
        for move in to_core[k]:
            move.wait_recv()
        c = chunks[k]

        def body(q, _):
            part[0, q, :, c] = add(own_lo[q, :, c], got_core[0, q, :, c])
            part[1, q, :, c] = add(rest_lo[q, :, c], got_core[1, q, :, c])
            if k == 0:
                vec[q] = add(small_lo[q], vec_core[q])
            return 0

        lax.fori_loop(0, half, body, 0)
        if k % 2 == 1:
            start(("x", k), [remote(part.at[other, :, :, c], got_near.at[0, :, :, c], near[0])])
        else:
            start(("x", k), [
                remote(part.at[g, upper, :, c], got_near.at[g, lower, :, c], near[2]) for g in range(2)]
                + ([remote(vec.at[upper], vec_two, near[2])] if k == 0 else []))

    def x_stage(k):
        arrive(("x", k))
        c = chunks[k]

        def body(q, _):
            if k % 2 == 1:
                part[mine, q, :, c] = add(part[mine, q, :, c], got_near[0, q, :, c])
                return 0
            for g in range(2):
                part[g, q, :, c] = add(part[g, q, :, c], got_near[g, q, :, c])
            if k == 0:
                vec[q] = add(vec[q], vec_two[q])
            return 0

        lax.fori_loop(0, half if k % 2 == 1 else quarter, body, 0)
        if k % 2 == 1:
            start(("y", k), [remote(part.at[mine, upper, :, c], got_last.at[:, :, c], near[2])])
        else:
            start(("y", k), [remote(part.at[other, lower, :, c], got_last.at[:, :, c], near[0])]
                  + ([remote(vec.at[lower], vec_one, near[0])] if k == 0 else []))

    def far_moves(number, k):
        held, used = quarter, 0
        for index, group in enumerate(reversed(groups)):
            moves = group_moves(group)
            held //= len(moves) + 1
            if index == number:
                out = []
                for m, (place, bits) in enumerate(moves):
                    device, c = (flip(dp, bits), t), chunks[k]
                    out.append(remote(part.at[mine, pl.ds(place * held, held), :, c], got_far.at[pl.ds(used + m * held, held), :, c], device))
                    if k == 0:
                        out.append(remote(vec_one.at[pl.ds(place * held, held)], vec_far.at[pl.ds(used + m * held, held)], device))
                return out, held, used, len(moves)
            used += held * len(moves)

    def y_stage(k):
        arrive(("y", k))
        c = chunks[k]

        def body(q, _):
            part[mine, q, :, c] = add(part[mine, q, :, c], got_last[q, :, c])
            if k == 0:
                vec_one[q] = add(vec[q], vec_one[q])
            return 0

        lax.fori_loop(0, quarter, body, 0)
        start(("z", 0, k), far_moves(0, k)[0])

    far_shape = []
    held, used = quarter, 0
    for group in reversed(groups):
        moves = len(group_moves(group))
        held //= moves + 1
        far_shape.append((held, used, moves))
        used += held * moves

    def z_stage(number, k):
        arrive(("z", number, k))
        c = chunks[k]
        held, base, moves = far_shape[number]

        def body(q, _):
            part[mine, q, :, c] = add(part[mine, q, :, c], *[got_far[base + m * held + q, :, c] for m in range(moves)])
            if k == 0:
                vec_one[q] = add(vec_one[q], *[vec_far[base + m * held + q] for m in range(moves)])
            return 0

        lax.fori_loop(0, held, body, 0)
        if number + 1 < len(groups):
            start(("z", number + 1, k), far_moves(number + 1, k)[0])

    for k in range(last + 1):
        core_stage(k)
    for k in range(last + 1):
        x_stage(k)
        if k > 0:
            y_stage(k - 1)
    y_stage(last)
    for number in range(len(groups)):
        for k in range(last + 1):
            z_stage(number, k)
    to_far = []
    for number, (step, source, held, base, moves) in enumerate(feed_steps):
        if number > 0:
            for move in step:
                move.start()
        for move in step:
            move.wait_recv()

        def sum_feed(k, _, source=source, held=held, base=base, moves=moves):
            feed_part[k] = add(source[k], *[feed_got[base + m * held + k] for m in range(moves)])
            return 0

        if number + 1 < len(feed_steps):
            lax.fori_loop(0, held, sum_feed, 0)
        else:
            out = source[0].astype(f32)
            for m in range(moves):
                out = out + feed_got[base + m * held].astype(f32)
            feed_total[...] = out
        to_far += step
    total[...] = part[mine, 0].astype(f32)
    vecs[...] = vec_one[0].astype(f32)

    for move in sum(to_core, []) + sent + to_far:
        move.wait_send()


def tail(dp_size, own, rest, small, feed):
    groups = far_groups(dp_size)
    half, rows, cols = own[0].shape
    quarter = half // 2
    wide = small[0].shape[2]
    partners = sum(len(group_moves(g)) for g in groups)
    slots = (-(-cols // 384)) * (5 + partners) + 3 + 2 * partners
    return pl.pallas_call(
        functools.partial(tail_kernel, groups),
        in_specs=[VM] * 7,
        out_specs=[VM, VM, VM],
        out_shape=[
            jax.ShapeDtypeStruct((rows, cols), f32),
            jax.ShapeDtypeStruct((rows, wide), f32), jax.ShapeDtypeStruct(feed.shape[1:], f32)],
        scratch_shapes=[
            pltpu.VMEM(feed.shape, bf), pltpu.VMEM(feed.shape, bf),
            pltpu.VMEM((2, half, rows, cols), bf), pltpu.VMEM((2, half, rows, cols), bf), pltpu.VMEM((2, half, rows, cols), bf),
            pltpu.VMEM((quarter, rows, cols), bf), pltpu.VMEM((quarter, rows, cols), bf),
            pltpu.VMEM((half, rows, wide), bf), pltpu.VMEM((half, rows, wide), bf), pltpu.VMEM((quarter, rows, wide), bf),
            pltpu.VMEM((quarter, rows, wide), bf), pltpu.VMEM((quarter, rows, wide), bf),
            pltpu.SemaphoreType.DMA((slots,)), pltpu.SemaphoreType.DMA((slots,))],
        compiler_params=pltpu.CompilerParams(collective_id=1, has_side_effects=True, vmem_limit_bytes=48 << 20),
    )(*own, *rest, *small, feed)


def add_low(*terms):
    out = terms[0].astype(f32)
    for term in terms[1:]:
        out = out + term.astype(f32)
    return out.astype(bf)


def order_matrix(owner, rows, width):
    place = lax.broadcasted_iota(jnp.int32, (1, width), 1)
    block = place // rows
    count = width // rows
    natural = place % rows
    for k, bit in enumerate([1 << b for b in range(count.bit_length() - 2, 1, -1)] + [2, 1]):
        on, base = (block // (1 << k)) % 2, (owner // bit) % 2
        natural = natural + (on + base - 2 * on * base) * (bit * rows)
    return (lax.broadcasted_iota(jnp.int32, (width, width), 0) == natural).astype(f32).astype(bf)


def norm_parts(values):
    centered = values - jnp.mean(values, axis=-1, keepdims=True)
    inverse = lax.rsqrt(jnp.mean(centered * centered, axis=-1, keepdims=True) + EPSILON)
    return centered * inverse, inverse


def norm_back(hat, inverse, gain, grad):
    scaled = grad * gain
    return inverse * (
        scaled - jnp.mean(scaled, axis=-1, keepdims=True) - hat * jnp.mean(scaled * hat, axis=-1, keepdims=True))


def over_rows(total, body):
    def step(k, _):
        body(pl.ds(pl.multiple_of(k * ROWS, ROWS), ROWS))
        return 0

    lax.fori_loop(0, total // ROWS, step, 0)


def column_sum(ref, row, values):
    ref[row : row + 1] += jnp.sum(values, axis=0, keepdims=True)


def bias_row(vec_nat, group, cols):
    lanes = pl.ds(pl.multiple_of(group * cols, 128), cols)
    q, v = vec_nat[6:7, lanes], vec_nat[7:8, lanes]
    parts = []
    for g in range(cols // 128):
        part = slice(g * 128, (g + 1) * 128)
        parts += [q[:, part], jnp.zeros((1, 128), f32), v[:, part]]
    return jnp.concatenate(parts, axis=1)


def fan_matrix(fan):
    row = lax.broadcasted_iota(jnp.int32, (128 * fan, 1), 0)
    unit = lax.broadcasted_iota(jnp.int32, (128 * fan, 128 * fan), 1)
    return (unit == (row % 128) * fan + row // 128).astype(f32).astype(bf)


def first_kernel(rows, fan, info, tokens, pack, weight, seg, seg_other, x_out, n1_out, send, vec_rel, vec_nat, fc_bias, starts, order, fan_rows):
    width, cols = tokens.shape[1], weight.shape[2] // 3

    @pl.when(pl.program_id(0) == 0)
    def _():
        order[...] = order_matrix(info[1], rows, width)
        small = pack[0, :, cols:].astype(f32).T[:VECS]
        vec_rel[...] = small
        vec_nat[...] = lax.dot_general(small.astype(bf), order[...], NT, preferred_element_type=f32)
        count = width // 128
        fan_rows[...] = jnp.zeros_like(fan_rows)
        for k in range(count):
            for m in range(fan):
                fan_rows[k : k + 1, m * 128 : (m + 1) * 128] = vec_nat[8 + m : 9 + m, k * 128 : (k + 1) * 128]
        bias = jnp.dot(fan_rows[...].astype(bf), fan_matrix(fan), preferred_element_type=f32)
        for k in range(count):
            fc_bias[:, k * 128 * fan : (k + 1) * 128 * fan] = bias[k : k + 1]
        docs = jnp.where(info[2] == 1, seg[...], seg_other[...]).astype(f32)
        begin = jnp.zeros_like(docs)
        for d in range(1, 16):
            before = jnp.sum(jnp.where(docs < d, 1.0, 0.0), axis=1, keepdims=True)
            begin = jnp.where(docs == d, before, begin)
        starts[...] = begin.astype(jnp.int32)

    x = jnp.dot(tokens[...], order[...], preferred_element_type=f32)
    hat, _ = norm_parts(x)
    n1 = (hat * vec_rel[0:1] + vec_rel[1:2]).astype(bf)
    x_out[...] = x.astype(bf)
    n1_out[...] = n1
    send[...] = (jnp.dot(n1, weight[0], preferred_element_type=f32) + bias_row(vec_nat, 1 - info[0], cols)).astype(bf)


def own_kernel(n1, send, weights, vec_nat, out, recv, weight, send_sem, recv_sem, local_sem):
    dp, t = lax.axis_index("dp"), lax.axis_index("tensor")
    partner = (flip(dp, (1,)), t)
    barrier = pltpu.get_barrier_semaphore()
    pl.semaphore_signal(barrier, inc=1, device_id=partner, device_id_type=MESH_ID)
    load = pltpu.make_async_copy(weights.at[0], weight, local_sem.at[0])
    load.start()
    pl.semaphore_wait(barrier, 1)
    copy = pltpu.make_async_remote_copy(
        src_ref=send, dst_ref=recv, send_sem=send_sem.at[0], recv_sem=recv_sem.at[0], device_id=partner, device_id_type=MESH_ID)
    copy.start()
    load.wait()
    bias = bias_row(vec_nat, dp % 2, weight.shape[1] // 3)

    def body(at):
        out[at] = (jnp.dot(n1[at], weight[...], preferred_element_type=f32) + bias).astype(bf)

    over_rows(n1.shape[0], body)
    copy.wait()


def picked(array, index):
    return pl.BlockSpec((1,) + array.shape[1:], lambda k, s: (index, 0, 0))


def whole(array):
    return pl.BlockSpec(array.shape, lambda k, s: (0,) * len(array.shape))


def like(shape, dtype):
    return jax.ShapeDtypeStruct(shape, dtype)


def by_rows(kernel, info, inputs, specs, outs, scratch=(), limit=60):
    total = inputs[0].shape[0]

    def spec(array, given=None):
        if given is not None:
            return given
        if array.shape[0] == total:
            return pl.BlockSpec((ROWS,) + array.shape[1:], lambda k, s: (k, 0))
        return whole(array)

    return pl.pallas_call(
        kernel,
        grid_spec=pltpu.PrefetchScalarGridSpec(
            num_scalar_prefetch=1, grid=(total // ROWS,), in_specs=[spec(a, g) for a, g in zip(inputs, specs)],
            out_specs=[spec(o) for o in outs], scratch_shapes=list(scratch)),
        out_shape=outs,
        cost_estimate=pl.CostEstimate(flops=1 << 22, bytes_accessed=1 << 18, transcendentals=0),
        compiler_params=pltpu.CompilerParams(vmem_limit_bytes=limit << 20),
    )(info, *inputs)


def project_first(info, rows, fan, tokens, packs, weights, seg, seg_other):
    n, width = tokens.shape
    vecs = like((VECS, width), f32)
    return by_rows(
        functools.partial(first_kernel, rows, fan), info, (tokens, packs, weights, seg, seg_other),
        (None, picked(packs, 0), picked(weights, 1), None, None),
        [like((n, width), bf), like((n, width), bf), like((n, weights.shape[2]), bf), vecs, vecs, like((1, width * fan), f32),
         like(seg.shape, jnp.int32)],
        [pltpu.VMEM((width, width), bf), pltpu.VMEM((8, 128 * fan), f32)])


def project_own(n1, send, weights, vec_nat):
    return pl.pallas_call(
        own_kernel,
        in_specs=[VM, HBM, HBM, VM],
        out_specs=[VM, ANY],
        out_shape=[like(send.shape, bf)] * 2,
        scratch_shapes=[
            pltpu.VMEM(weights.shape[1:], bf), pltpu.SemaphoreType.DMA((1,)), pltpu.SemaphoreType.DMA((1,)),
            pltpu.SemaphoreType.DMA((1,))],
        compiler_params=pltpu.CompilerParams(collective_id=3, has_side_effects=True, vmem_limit_bytes=24 << 20),
    )(n1, send, weights, vec_nat)


def middle_kernel(rows, x, o_own, o_send, cot, cot_recv, packs, vec_rel, fc00, fc01, fc10, fc11, pr0, pr1,
                  middle, n2, cot_rel, d_mlp, o_recv, fc_got, pr_got, order, send_sem, recv_sem):
    dp, t = lax.axis_index("dp"), lax.axis_index("tensor")
    core = dp % 2
    away = core + t - 2 * core * t
    partner = (flip(dp, (1,)), t)
    barrier = pltpu.get_barrier_semaphore()
    pl.semaphore_signal(barrier, inc=1, device_id=partner, device_id_type=MESH_ID)
    pl.semaphore_wait(barrier, 1)
    size = fc00.shape[0]
    copies = [
        pltpu.make_async_remote_copy(
            src_ref=src, dst_ref=dst, send_sem=send_sem.at[k], recv_sem=recv_sem.at[k], device_id=partner, device_id_type=MESH_ID)
        for k, (src, dst) in enumerate((
            (o_send, o_recv), (fc00, fc_got.at[0, pl.ds(0, size)]), (fc01, fc_got.at[0, pl.ds(size, size)]), (pr0, pr_got.at[0]),
            (fc10, fc_got.at[1, pl.ds(0, size)]), (fc11, fc_got.at[1, pl.ds(size, size)]), (pr1, pr_got.at[1])))]
    for copy in copies:
        copy.start()
    order[...] = order_matrix(dp, rows, x.shape[1])
    cols = o_own.shape[1]

    def cot_rows(at):
        grad = jnp.dot(jnp.where(away == 0, cot[at], cot_recv[at]), order[...], preferred_element_type=f32)
        cot_rel[at] = grad.astype(bf)
        d_mlp[at] = (BRANCH_SCALE * grad).astype(bf)

    over_rows(x.shape[0], cot_rows)
    copies[0].wait_recv()

    def body(at):
        branch = lax.dot_general(o_own[at], packs[0, :, :cols], NT, preferred_element_type=f32)
        branch = branch + lax.dot_general(o_recv[at], packs[1, :, :cols], NT, preferred_element_type=f32)
        mid = x[at].astype(f32) + BRANCH_SCALE * (branch + vec_rel[2:3])
        middle[at] = mid
        hat, _ = norm_parts(mid)
        n2[at] = (hat * vec_rel[3:4] + vec_rel[4:5]).astype(bf)

    over_rows(x.shape[0], body)
    for copy in copies[1:]:
        copy.wait_recv()
    for copy in copies:
        copy.wait_send()


def middle_part(rows, x, o_own, o_send, cot, cot_recv, packs, vec_rel, fc_parts, proj_parts):
    shape, half = x.shape, x.shape[1] // 2
    hidden = proj_parts[0].shape[1]
    got = like((2, half, hidden), bf)
    return pl.pallas_call(
        functools.partial(middle_kernel, rows),
        in_specs=[VM] * 7 + [HBM] * 6,
        out_specs=[VM] * 5 + [ANY] * 2,
        out_shape=[like(shape, f32), like(shape, bf), like(shape, bf), like(shape, bf), like(o_send.shape, bf), got, got],
        scratch_shapes=[
            pltpu.VMEM((shape[1], shape[1]), bf), pltpu.SemaphoreType.DMA((7,)), pltpu.SemaphoreType.DMA((7,))],
        compiler_params=pltpu.CompilerParams(collective_id=2, has_side_effects=True, vmem_limit_bytes=36 << 20),
    )(x, o_own, o_send, cot, cot_recv, packs, vec_rel, *fc_parts[0], *fc_parts[1], *proj_parts)


def after_kernel(rows, info, middle, mlp, back, cot, packs, vec_rel, block_out, d_middle, d_attn, do_own, do_send, sums, order):
    @pl.when(pl.program_id(0) == 0)
    def _():
        order[...] = order_matrix(info[1], rows, middle.shape[1])
        sums[...] = jnp.zeros_like(sums)

    cols = do_own.shape[1]
    mid = middle[...]
    out = (mid + BRANCH_SCALE * (mlp[...] + vec_rel[5:6])).astype(bf)
    block_out[...] = lax.dot_general(out, order[...], NT, preferred_element_type=f32).astype(bf)
    hat, inverse = norm_parts(mid)
    grad = back[...]
    out_grad = cot[...].astype(f32)
    entire = out_grad + norm_back(hat, inverse, vec_rel[3:4], grad)
    d_middle[...] = entire
    low = (BRANCH_SCALE * entire).astype(bf)
    d_attn[...] = low
    do_own[...] = jnp.dot(low, packs[0, :, :cols], preferred_element_type=f32).astype(bf)
    do_send[...] = jnp.dot(low, packs[1, :, :cols], preferred_element_type=f32).astype(bf)
    column_sum(sums, 0, BRANCH_SCALE * entire)
    column_sum(sums, 1, grad * hat)
    column_sum(sums, 2, grad)
    column_sum(sums, 3, BRANCH_SCALE * out_grad)


def after_part(info, rows, middle, mlp, back, cot, packs, vec_rel, cols):
    shape = middle.shape
    slim = like((shape[0], cols), bf)
    return by_rows(
        functools.partial(after_kernel, rows), info, (middle, mlp, back, cot, packs, vec_rel), (None,) * 6,
        [like(shape, bf), like(shape, f32), like(shape, bf), slim, slim, like((8, shape[1]), f32)],
        [pltpu.VMEM((shape[1], shape[1]), bf)])


def feed_kernel(info, n2, d_mlp, bias, fc_got, pr_got, fc00, fc01, fc10, fc11, pr0, pr1,
                acc, back, fc_lo, fc_hi, pr_lo, pr_hi, d_bias, n2_t, d_t, w_fc, w_pr, act, d_pre):
    step = pl.program_id(0)
    total, half = n2.shape[0], n2.shape[1] // 2

    @pl.when(step == 0)
    def _():
        acc[...] = jnp.zeros_like(acc)
        back[...] = jnp.zeros_like(back)
        n2_t[...] = n2[...].T
        d_t[...] = d_mlp[...].T

    @pl.when(step < pl.num_programs(0) // 2)
    def _():
        w_fc[: half // 2], w_fc[half // 2 : half], w_pr[:half] = fc00[...], fc01[...], pr0[...]

    @pl.when(step >= pl.num_programs(0) // 2)
    def _():
        w_fc[: half // 2], w_fc[half // 2 : half], w_pr[:half] = fc10[...], fc11[...], pr1[...]

    w_fc[half:], w_pr[half:] = fc_got[0], pr_got[0]
    root = 0.7978845608
    count = total // ROWS
    raw = {}
    grad_sum = jnp.zeros((1, w_fc.shape[1]), f32)

    def products(k):
        at = slice(k * ROWS, (k + 1) * ROWS)
        return (
            jnp.dot(n2[at], w_fc[...], preferred_element_type=f32) + bias[...],
            jnp.dot(d_mlp[at], w_pr[...], preferred_element_type=f32))

    def add_back(k):
        at = slice(k * ROWS, (k + 1) * ROWS)
        acc[at] += lax.dot_general(act[at], w_pr[...], NT, preferred_element_type=f32)
        back[at] += lax.dot_general(d_pre[at], w_fc[...], NT, preferred_element_type=f32)

    raw[0] = products(0)
    for k in range(count):
        at = slice(k * ROWS, (k + 1) * ROWS)
        if k + 1 < count:
            raw[k + 1] = products(k + 1)
        pre, d_act = raw.pop(k)
        square = pre * pre
        inner = jnp.tanh(pre * (root + root * 0.044715 * square))
        gate = 0.5 + 0.5 * inner
        act[at] = (pre * gate).astype(bf)
        slope = gate + pre * (0.5 - 0.5 * inner * inner) * (root + root * 3 * 0.044715 * square)
        grad = d_act * slope
        grad_sum = grad_sum + jnp.sum(grad, axis=0, keepdims=True)
        d_pre[at] = grad.astype(bf)
        if k > 0:
            add_back(k - 1)
    add_back(count - 1)
    d_bias[...] = grad_sum
    for out, left, right, low in (
        (fc_hi, n2_t, d_pre, half), (pr_hi, d_t, act, half), (fc_lo, n2_t, d_pre, 0), (pr_lo, d_t, act, 0)):
        out[0] = jnp.dot(left[low : low + half], right[...], preferred_element_type=f32).astype(bf)


def feed_part(info, n2, d_mlp, bias, fc_got, pr_got, fc_parts, proj_parts):
    (total, width), hidden, half = n2.shape, bias.shape[1] // 2, n2.shape[1] // 2
    steps = hidden // HIDDEN
    fixed = lambda a: pl.BlockSpec(a.shape, lambda k, s: (0,) * len(a.shape), pipeline_mode=pl.Buffered(1))
    early = lambda a: pl.BlockSpec((a.shape[0], HIDDEN), lambda k, s: (0, jnp.minimum(k, steps - 1)))
    late = lambda a: pl.BlockSpec((a.shape[0], HIDDEN), lambda k, s: (0, jnp.maximum(k - steps, 0)))
    two = lambda a: pl.BlockSpec((1, a.shape[1], HIDDEN), lambda k, s: (k // steps, 0, k % steps))
    unit = pl.BlockSpec((1, HIDDEN), lambda k, s: (0, (s[3] + (k // steps) * (1 - 2 * s[3])) * steps + k % steps))
    grad = like((2, half, hidden), bf)
    sums = [like((total, width), f32)] * 2
    return pl.pallas_call(
        feed_kernel,
        grid_spec=pltpu.PrefetchScalarGridSpec(
            num_scalar_prefetch=1,
            grid=(2 * steps,),
            in_specs=[fixed(n2), fixed(d_mlp), unit, two(fc_got), two(pr_got)]
            + [early(a) for a in fc_parts[0]] + [late(a) for a in fc_parts[1]] + [early(proj_parts[0]), late(proj_parts[1])],
            out_specs=[fixed(o) for o in sums] + [two(grad)] * 4 + [unit],
            scratch_shapes=[
                pltpu.VMEM((width, total), bf), pltpu.VMEM((width, total), bf), pltpu.VMEM((width, HIDDEN), bf),
                pltpu.VMEM((width, HIDDEN), bf), pltpu.VMEM((total, HIDDEN), bf), pltpu.VMEM((total, HIDDEN), bf)],
        ),
        out_shape=sums + [grad] * 4 + [like((1, 2 * hidden), f32)],
        cost_estimate=pl.CostEstimate(flops=1 << 22, bytes_accessed=1 << 18, transcendentals=0),
        compiler_params=pltpu.CompilerParams(vmem_limit_bytes=46 << 20),
    )(info, n2, d_mlp, bias, fc_got, pr_got, *fc_parts[0], *fc_parts[1], *proj_parts)


def weight_kernel(n1, d_attn, d_qkv, o, lo, hi, left_t):
    step, half = pl.program_id(0), left_t.shape[0] // 2

    @pl.when(step == 0)
    def _():
        left_t[...] = n1[...].T

    def products(right):
        for out, low in ((hi, half), (lo, 0)):
            out[...] = jnp.dot(left_t[low : low + half], right[...], preferred_element_type=f32).astype(bf)

    @pl.when(step < pl.num_programs(0) - 1)
    def _():
        products(d_qkv)

    @pl.when(step == pl.num_programs(0) - 1)
    def _():
        left_t[...] = d_attn[...].T
        products(o)


def weight_part(n1, d_attn, d_qkv, o):
    (n, width), cols = n1.shape, o.shape[1]
    steps = d_qkv.shape[1] // cols
    fixed = lambda a: pl.BlockSpec(a.shape, lambda k: (0, 0), pipeline_mode=pl.Buffered(1))
    out = pl.BlockSpec((width // 2, cols), lambda k: (0, k))
    grad = like((width // 2, d_qkv.shape[1] + cols), bf)
    return pl.pallas_call(
        weight_kernel,
        grid=(steps + 1,),
        in_specs=[fixed(n1), fixed(d_attn), pl.BlockSpec((n, cols), lambda k: (0, jnp.minimum(k, steps - 1))), fixed(o)],
        out_specs=[out, out],
        out_shape=[grad, grad],
        scratch_shapes=[pltpu.VMEM((width, n), bf)],
        cost_estimate=pl.CostEstimate(flops=1 << 22, bytes_accessed=1 << 18, transcendentals=0),
        compiler_params=pltpu.CompilerParams(vmem_limit_bytes=32 << 20),
    )(n1, d_attn, d_qkv, o)


def token_kernel(rows, fan, info, own, rest, x, d_middle, weights, vec_rel, mid_sums, fc_grad, grad_out, small, own_sums, rest_sums, vecs, nat, order, fan_rows):
    width, cols = x.shape[1], own.shape[1] // 3
    step = pl.program_id(0)

    @pl.when(step == 0)
    def _():
        order[...] = order_matrix(info[1], rows, width)
        for ref in (own_sums, rest_sums, vecs, nat, fan_rows):
            ref[...] = jnp.zeros_like(ref)

    grad = lax.dot_general(own[...], weights[0], NT, preferred_element_type=f32)
    grad = grad + lax.dot_general(rest[...], weights[1], NT, preferred_element_type=f32)
    hat, inverse = norm_parts(x[...].astype(f32))
    low = (d_middle[...] + norm_back(hat, inverse, vec_rel[0:1], grad)).astype(bf)
    grad_out[...] = lax.dot_general(low, order[...], NT, preferred_element_type=f32).astype(bf)
    column_sum(own_sums, 0, own[...].astype(f32))
    column_sum(rest_sums, 0, rest[...].astype(f32))
    column_sum(vecs, 0, grad * hat)
    column_sum(vecs, 1, grad)

    @pl.when(step == pl.num_programs(0) - 1)
    def _():
        for group, ref in ((info[0], own_sums), (1 - info[0], rest_sums)):
            for row, part_index in ((0, 0), (1, 2)):
                picks = [ref[0:1, (3 * g + part_index) * 128 : (3 * g + part_index + 1) * 128] for g in range(cols // 128)]
                nat[row : row + 1, pl.ds(pl.multiple_of(group * cols, 128), cols)] = jnp.concatenate(picks, axis=1)
        count = width // 128
        for k in range(count):
            fan_rows[k : k + 1] = fc_grad[:, k * 128 * fan : (k + 1) * 128 * fan]
        spread = lax.dot_general(fan_rows[...].astype(bf), fan_matrix(fan), NT, preferred_element_type=f32)
        for k in range(count):
            for m in range(fan):
                nat[2 + m : 3 + m, k * 128 : (k + 1) * 128] = spread[k : k + 1, m * 128 : (m + 1) * 128]
        moved = jnp.dot(nat[...].astype(bf), order[...], preferred_element_type=f32)
        vecs[2:4] = moved[0:2]
        vecs[4:8] = mid_sums[0:4]
        vecs[8 : 8 + fan] = moved[2 : 2 + fan]
        small[...] = vecs[...].T.astype(bf)


def token_part(info, rows, own, rest, x, d_middle, weights, vec_rel, mid_sums, fc_grad):
    n, width = x.shape
    wide, fan = own.shape[1], fc_grad.shape[1] // width
    return by_rows(
        functools.partial(token_kernel, rows, fan), info, (own, rest, x, d_middle, weights, vec_rel, mid_sums, fc_grad), (None,) * 8,
        [like((n, width), bf), like((width, SMALL), bf)],
        [pltpu.VMEM((8, wide), f32), pltpu.VMEM((8, wide), f32), pltpu.VMEM((SMALL, width), f32), pltpu.VMEM((8, width), f32),
         pltpu.VMEM((width, width), bf), pltpu.VMEM((8, 128 * fan), f32)], 32)


def on_device(
    tokens, segment_ids, ln1_gain, ln1_bias, w_qkv, b_qv, w_attn_out, b_attn_out,
    ln2_gain, ln2_bias, w_fc, b_fc, w_proj, b_proj, cotangent,
):
    dp_size = lax.axis_size("dp")
    dp_pos, t_pos = lax.axis_index("dp"), lax.axis_index("tensor")
    core = dp_pos % 2
    rows = ln1_gain.shape[0]
    width = tokens.shape[1]
    cols = w_qkv.shape[2]
    hidden = w_fc.shape[1]
    fan = b_fc.shape[0] // rows
    far = [1 << k for k in range(dp_size.bit_length() - 2, 1, -1)]
    swap = []
    for d in range(dp_size):
        for t in range(2):
            if d % 2 != t:
                swap.append((2 * d + t, 2 * (d - d % 2 + t) + d % 2))
    mine = core == t_pos

    pairs = cols // 128

    def by_pair(parts):
        parts = parts.reshape(-1, 3, pairs, 128)
        return jnp.swapaxes(parts, 1, 2).reshape(-1, 3 * cols)

    def by_part(columns):
        return jnp.swapaxes(columns.reshape(-1, pairs, 3, 128), 1, 2).reshape(-1, 3, cols)

    small = jnp.concatenate([jnp.stack([ln1_gain, ln1_bias, b_attn_out, ln2_gain, ln2_bias, b_proj]), b_qv], axis=0)
    small = jnp.concatenate([small.T, b_fc.reshape(rows, fan)], axis=1)
    small = jnp.pad(small, ((0, 0), (0, SMALL - small.shape[1])))
    out_pack = jnp.concatenate([w_attn_out.T, small], axis=1)
    tokens, seg_other, all_qkv, all_out, fc_far, proj_far = head(
        dp_size, tokens, segment_ids, (by_pair(w_qkv), out_pack, w_fc, w_proj.T), chunks_of(3 * cols, 0, 2) + chunks_of(cols + SMALL, 1, 1))
    all_qkv, all_out = (a.reshape(2, width, -1) for a in (all_qkv, all_out))
    fc_far, proj_far = fc_far.reshape(-1, hidden), proj_far.reshape(-1, hidden)
    fc_parts = [[fc_far], [exchange(fc_far, 0, dp_size)]]
    proj_half = exchange(proj_far, 2, dp_size)

    part = jnp.stack([core, dp_pos, jnp.where(mine, 1, 0), t_pos]).astype(jnp.int32)
    x, n1, qkv_send, vec_rel, vec_nat, fc_bias, starts = project_first(
        part, rows, fan, tokens, all_out, all_qkv, segment_ids, seg_other)
    qkv_own, qkv_recv = project_own(n1, qkv_send, all_qkv, vec_nat)
    fc_parts, proj_half, qkv_own = lax.optimization_barrier((fc_parts, proj_half, qkv_own))
    fc_parts = [p + [exchange(p[0], 2, dp_size)] for p in fc_parts]
    proj_half = jnp.concatenate([proj_far, proj_half], axis=0)
    proj_parts = [proj_half, exchange(proj_half, 0, dp_size)]
    o_own, o_send, lse = attn_fwd(qkv_own, qkv_recv, starts, part)
    cot_recv = lax.ppermute(cotangent, BOTH, swap)
    half = width // 2
    middle, n2, cot, d_mlp, o_recv, fc_got, pr_got = middle_part(
        rows, x, o_own, o_send, cotangent, cot_recv, all_out, vec_rel, fc_parts, proj_parts)
    mlp, back, fc_lo, fc_hi, pr_lo, pr_hi, fc_grad = feed_part(
        part, n2, d_mlp, fc_bias, fc_got, pr_got, fc_parts, proj_parts)
    fc_got, pr_got = exchange(fc_hi, 1, dp_size), exchange(pr_hi, 1, dp_size)
    block_out, d_middle, d_attn, do_own, do_send, mid_sums = after_part(
        part, rows, middle, mlp, back, cot, all_out, vec_rel, cols)
    do_recv = exchange(do_send, 1, dp_size)

    near_size = half // 2
    fc_rest = add_low(fc_lo[1], fc_got[1])
    pr_rest = add_low(pr_lo[:, near_size:], pr_got[:, near_size:])
    last = (qkv_own, qkv_recv, do_own, do_recv, o_own, o_send)
    last, fc_rest, pr_rest = lax.optimization_barrier((last, fc_rest, pr_rest))
    fc_sent = exchange(fc_rest, 0, dp_size)
    pr_sent = exchange(pr_rest, 2, dp_size)
    block_recv = lax.ppermute(block_out, BOTH, swap)
    dq_own, dq_send = attn_bwd(*last, starts, lse, part)
    dq_recv = exchange(dq_send, 1, dp_size)
    dq_own, fc_sent, pr_sent = lax.optimization_barrier((dq_own, fc_sent, pr_sent))
    fc_rest = add_low(fc_lo[0, near_size:], fc_got[0, near_size:], fc_sent[near_size:])
    pr_rest = add_low(pr_lo[1, :near_size], pr_got[1, :near_size], pr_sent[1])
    dq_own, fc_rest, pr_rest = lax.optimization_barrier((dq_own, fc_rest, pr_rest))
    fc_near = exchange(fc_rest, 2, dp_size)
    pr_near = exchange(pr_rest, 0, dp_size)
    own_lo, own_hi = weight_part(n1, d_attn, dq_own, o_own)
    own_lo, dq_recv = lax.optimization_barrier((own_lo, dq_recv))
    grad_tokens, d_small = token_part(part, rows, dq_own, dq_recv, x, d_middle, all_qkv, vec_rel, mid_sums, fc_grad)
    grad_recv = lax.ppermute(grad_tokens, BOTH, swap)
    d_small, fc_near, pr_near = lax.optimization_barrier((d_small, fc_near, pr_near))
    sum_fc = add_low(fc_lo[0, :near_size], fc_got[0, :near_size], fc_sent[:near_size], fc_near)
    sum_proj = add_low(pr_lo[0, :near_size], pr_got[0, :near_size], pr_sent[0], pr_near)
    feed = jnp.concatenate([sum_fc, sum_proj], axis=1).reshape(-1, rows, 2 * hidden)
    dq_recv, d_small, feed = lax.optimization_barrier((dq_recv, d_small, feed))
    rest_lo, rest_hi = weight_part(n1, d_attn, dq_recv, o_recv)
    blocks = lambda arr: arr.reshape(dp_size // 2, rows, -1)
    sum_a, vecs, sum_feed = tail(
        dp_size, (blocks(own_lo), blocks(own_hi)), (blocks(rest_lo), blocks(rest_hi)),
        (blocks(d_small[:half]), blocks(d_small[half:])), feed)
    vecs, block_recv, grad_recv = lax.optimization_barrier((vecs, block_recv, grad_recv))
    block_out = jnp.where(mine, block_out, block_recv)
    grad_tokens = jnp.where(mine, grad_tokens, grad_recv)
    return (
        block_out,
        grad_tokens,
        vecs[:, 0],
        vecs[:, 1],
        by_part(sum_a[:, : 3 * cols]),
        vecs[:, 2:4].T,
        sum_a[:, 3 * cols :].T,
        vecs[:, 4],
        vecs[:, 5],
        vecs[:, 6],
        sum_feed[:, :hidden],
        vecs[:, 8 : 8 + fan].reshape(rows * fan),
        sum_feed[:, hidden:].T,
        vecs[:, 7],
    )


def solution(mesh):
    vec, tok = P("dp"), P(BOTH, None)
    in_specs = (
        tok, P("dp", None), vec, vec, P("dp", None, "tensor"), P(None, "dp"), P("tensor", "dp"),
        vec, vec, vec, P("dp", "tensor"), vec, P("tensor", "dp"), vec, tok,
    )
    out_specs = (
        tok, tok, vec, vec, P("dp", None, "tensor"), P(None, "dp"), P("tensor", "dp"),
        vec, vec, vec, P("dp", "tensor"), vec, P("tensor", "dp"), vec,
    )
    return jax.shard_map(on_device, mesh=mesh, in_specs=in_specs, out_specs=out_specs, check_vma=False)
```

```python
import functools

import jax
import jax.numpy as jnp
from jax import lax
from jax.experimental import pallas as pl
from jax.experimental.pallas import tpu as pltpu
from jax.sharding import PartitionSpec as P

HD = 64
QB = 256
NEG = -1e30
EPSILON = 1e-05
BRANCH_SCALE = 48.0 ** (-0.5)
SMALL = 128
VECS = 16
ROWS = 256
HIDDEN = 768
bf = jnp.bfloat16
f32 = jnp.float32
NT = (((1,), (1,)), ((), ()))
TN = (((0,), (0,)), ((), ()))
BOTH = ("dp", "tensor")
MESH_ID = pl.DeviceIdType.MESH
ANY = pl.BlockSpec(memory_space=pl.ANY)
VM = pl.BlockSpec(memory_space=pltpu.VMEM)
HBM = pl.BlockSpec(memory_space=pltpu.HBM)
SM = pl.BlockSpec(memory_space=pltpu.SMEM)


def attn_mask(kat, at, srow):
    keys = lax.broadcasted_iota(jnp.int32, (QB, QB), 0)
    rows = lax.broadcasted_iota(jnp.int32, (1, QB), 1) + (at - kat)
    return (keys >= srow - kat) & (keys <= rows)


def over_blocks(bounds, i, step, carry):
    low = bounds[0, i * QB] // QB
    mid = jnp.minimum((bounds[0, i * QB + QB - 1] + QB - 1) // QB, i)
    carry = lax.fori_loop(0, mid - low + 1, lambda k, c: step(True, jnp.where(k == 0, i, low + k - 1), c), carry)
    return lax.fori_loop(mid, i, functools.partial(step, False), carry)


def head_lanes(values):
    low = (lax.broadcasted_iota(jnp.int32, (1, values.shape[1]), 1) % 128) < HD
    zero = jnp.zeros((), bf)
    return jnp.where(low, values, zero), jnp.where(low, zero, values)


def fwd_kernel(info, bounds, own, recv, st_ref, okeep, osend, lse_ref, qm, ks, vt, osc, acc):
    half, cols = own.shape[0], own.shape[1] // 3
    n, nb, heads, pairs = 2 * half, 2 * half // QB, cols // HD, cols // 128
    c = info[0]
    for base, src in ((c * half, own), ((1 - c) * half, recv)):
        rows = pl.ds(pl.multiple_of(base, half), half)
        for g in range(pairs):
            lanes = slice(g * 128, (g + 1) * 128)
            part = lambda k: src[:, (3 * g + k) * 128 : (3 * g + k + 1) * 128]
            qm[0, rows, lanes], qm[1, rows, lanes] = head_lanes(part(0) * bf(HD**-0.5))
            ks[rows, lanes] = part(1)
            vt[lanes, rows] = part(2).T

    def qblock(i, _):
        at = pl.multiple_of(i * QB, QB)
        qr = pl.ds(at, QB)
        srow = st_ref[:, qr]
        acc[...] = jnp.zeros_like(acc)

        def step(masked, j, carry):
            kat = pl.multiple_of(j * QB, QB)
            kr = pl.ds(kat, QB)
            if masked:
                mask = attn_mask(kat, at, srow)
            scores, mixed = [], []
            for h in range(heads):
                lanes = slice(h // 2 * 128, h // 2 * 128 + 128)
                one = lax.dot_general(ks[kr, lanes], qm[h % 2, qr, lanes], NT, preferred_element_type=f32)
                scores.append(jnp.where(mask, one, NEG) if masked else one)
            for h in range(heads):
                top, total = carry[h]
                new = jnp.maximum(top, jnp.max(scores[h], axis=0, keepdims=True))
                weights = jnp.exp(scores[h] - new)
                fade = jnp.exp(top - new)
                total = fade * total + jnp.sum(weights, axis=0, keepdims=True)
                mixed.append((new, total, fade, weights.astype(bf)))
            for h in range(heads):
                sub = slice(h * HD, (h + 1) * HD)
                acc[sub] = mixed[h][2] * acc[sub] + jnp.dot(vt[sub, kr], mixed[h][3], preferred_element_type=f32)
            return tuple(m[:2] for m in mixed)

        carry = over_blocks(bounds, i, step, ((jnp.full((1, QB), NEG, f32), jnp.zeros((1, QB), f32)),) * heads)
        for h, (top, total) in enumerate(carry):
            sub = slice(h * HD, (h + 1) * HD)
            acc[sub] = acc[sub] / total
            lse_ref[h : h + 1, qr] = top + jnp.log(total)
        osc[qr] = acc[...].T.astype(bf)
        return 0

    lax.fori_loop(0, nb, qblock, 0)
    okeep[...] = osc[pl.ds(pl.multiple_of(c * half, half), half)]
    osend[...] = osc[pl.ds(pl.multiple_of((1 - c) * half, half), half)]


def attn_fwd(own, recv, starts, info):
    half, cols = own.shape[0], own.shape[1] // 3
    n = 2 * half
    return pl.pallas_call(
        fwd_kernel,
        in_specs=[SM, SM, VM, VM, VM],
        out_specs=[VM] * 3,
        scratch_shapes=[
            pltpu.VMEM((2, n, cols), bf), pltpu.VMEM((n, cols), bf), pltpu.VMEM((cols, n), bf),
            pltpu.VMEM((n, cols), bf), pltpu.VMEM((cols, QB), f32)],
        out_shape=[jax.ShapeDtypeStruct((half, cols), bf)] * 2 + [jax.ShapeDtypeStruct((cols // HD, n), f32)],
        cost_estimate=pl.CostEstimate(flops=n * n, bytes_accessed=n * 128, transcendentals=0),
        compiler_params=pltpu.CompilerParams(vmem_limit_bytes=30 << 20),
    )(info, starts, own, recv, starts)


def bwd_kernel(info, bounds, own, recv, doo, dor, oo, orr, st_ref, lse_ref, dkeep, dsend, qm, ks, vs, kt, dom, dlt, dqs, dks, dvs):
    half, cols = own.shape[0], own.shape[1] // 3
    n, nb, heads, pairs = 2 * half, 2 * half // QB, cols // HD, cols // 128
    c = info[0]
    lanes_of = lambda g: slice(g * 128, (g + 1) * 128)
    for base, src, do, o in ((c * half, own, doo, oo), ((1 - c) * half, recv, dor, orr)):
        rows = pl.ds(pl.multiple_of(base, half), half)
        for g in range(pairs):
            lanes = lanes_of(g)
            part = lambda k: src[:, (3 * g + k) * 128 : (3 * g + k + 1) * 128]
            qm[0, rows, lanes], qm[1, rows, lanes] = head_lanes(part(0) * bf(HD**-0.5))
            ks[rows, lanes] = part(1)
            vs[rows, lanes] = part(2)
            kt[lanes, rows] = part(1).T
            grad = do[:, lanes]
            dom[0, rows, lanes], dom[1, rows, lanes] = head_lanes(grad)
            prod = (grad.astype(f32) * o[:, lanes].astype(f32)).T
            for e in range(2):
                dlt[2 * g + e : 2 * g + e + 1, rows] = jnp.sum(prod[e * HD : (e + 1) * HD], axis=0, keepdims=True)
    dks[...] = jnp.zeros_like(dks)
    dvs[...] = jnp.zeros_like(dvs)

    def qblock(i, _):
        at = pl.multiple_of(i * QB, QB)
        qr = pl.ds(at, QB)
        srow = st_ref[:, qr]
        dqs[...] = jnp.zeros_like(dqs)

        def step(masked, j, carry):
            kat = pl.multiple_of(j * QB, QB)
            kr = pl.ds(kat, QB)
            if masked:
                mask = attn_mask(kat, at, srow)
            scores, softs, grads = [], [], []
            for h in range(heads):
                lanes = lanes_of(h // 2)
                one = lax.dot_general(ks[kr, lanes], qm[h % 2, qr, lanes], NT, preferred_element_type=f32)
                back = lax.dot_general(vs[kr, lanes], dom[h % 2, qr, lanes], NT, preferred_element_type=f32)
                scores.append((jnp.where(mask, one, NEG) if masked else one, back))
            for h in range(heads):
                soft = jnp.exp(scores[h][0] - lse_ref[h : h + 1, qr])
                grads.append((soft * (scores[h][1] - dlt[h : h + 1, qr])).astype(bf))
                softs.append(soft.astype(bf))
            for g in range(pairs):
                lanes = lanes_of(g)
                both = lambda ref: jnp.concatenate([ref[0, qr, lanes], ref[1, qr, lanes]], axis=0)
                two = slice(2 * g, 2 * g + 2)
                dvs[kr, lanes] += jnp.dot(jnp.concatenate(softs[two], axis=1), both(dom), preferred_element_type=f32)
                dks[kr, lanes] += jnp.dot(jnp.concatenate(grads[two], axis=1), both(qm), preferred_element_type=f32)
                for h in (2 * g, 2 * g + 1):
                    sub = slice(h * HD, (h + 1) * HD)
                    dqs[sub] += jnp.dot(kt[sub, kr], grads[h], preferred_element_type=f32)
            return carry

        over_blocks(bounds, i, step, 0)
        qm[0, qr] = (dqs[...] * (HD**-0.5)).T.astype(bf)
        return 0

    lax.fori_loop(0, nb, qblock, 0)
    for dst, base in ((dkeep, c * half), (dsend, (1 - c) * half)):
        rows = pl.ds(pl.multiple_of(base, half), half)
        for g in range(pairs):
            for k, value in enumerate((qm[0, rows, lanes_of(g)], dks[rows, lanes_of(g)], dvs[rows, lanes_of(g)])):
                dst[:, (3 * g + k) * 128 : (3 * g + k + 1) * 128] = value.astype(bf)


def attn_bwd(own, recv, do_own, do_recv, o_own, o_recv, starts, lse, info):
    half, cols = own.shape[0], own.shape[1] // 3
    n = 2 * half
    return pl.pallas_call(
        bwd_kernel,
        in_specs=[SM, SM] + [VM] * 8,
        out_specs=[VM] * 2,
        scratch_shapes=[
            pltpu.VMEM((2, n, cols), bf), pltpu.VMEM((n, cols), bf), pltpu.VMEM((n, cols), bf), pltpu.VMEM((cols, n), bf),
            pltpu.VMEM((2, n, cols), bf), pltpu.VMEM((cols // HD, n), f32), pltpu.VMEM((cols, QB), f32),
            pltpu.VMEM((n, cols), f32), pltpu.VMEM((n, cols), f32)],
        out_shape=[like((half, 3 * cols), bf)] * 2,
        cost_estimate=pl.CostEstimate(flops=n * n, bytes_accessed=n * 128, transcendentals=0),
        compiler_params=pltpu.CompilerParams(vmem_limit_bytes=56 << 20),
    )(info, starts, own, recv, do_own, do_recv, o_own, o_recv, starts, lse)


def dot(left, right, dims=(((1,), (0,)), ((), ()))):
    return lax.dot_general(left, right, dims, preferred_element_type=f32)


def exchange(value, bit, dp_size):
    if bit:
        return lax.ppermute(value, "dp", [(i, i ^ bit) for i in range(dp_size)])
    return lax.ppermute(value, "tensor", [(0, 1), (1, 0)])


def flip(index, bits):
    for bit in bits:
        index = index + bit * (1 - 2 * ((index // bit) % 2))
    return index

def far_groups(dp_size):
    far = [1 << k for k in range(dp_size.bit_length() - 2, 1, -1)]
    return [tuple(far[k : k + 2]) for k in range(0, len(far), 2)]

def group_moves(group):
    if len(group) == 1:
        return [(1, group)]
    return [(1, group[:1]), (2, group[1:]), (3, group)]

def chunks_of(cols, which, count, until=None):
    tiles = cols // 128
    cuts = [128 * ((tiles * k) // count) for k in range(count + 1)]
    arrays = range(which, until + 1) if until else (which,)
    return tuple(
        (array, low, high - low, 128 * ((high - low) // 256 + (high - low) // 128 % 2))
        for low, high in zip(cuts, cuts[1:]) for array in arrays)


def head_kernel(groups, chunks, tokens, seg, *refs):
    shards, x_out, seg_out, outs, (send_sem, recv_sem, local_sem) = refs[:4], refs[4], refs[5], refs[6:10], refs[10:]
    dp, t = lax.axis_index("dp"), lax.axis_index("tensor")
    core = dp % 2
    away = core + t - 2 * core * t
    near = {1: (flip(dp, (1,)), t), 2: (flip(dp, (2,)), t), 0: (dp, 1 - t)}
    distant = [bits for group in groups for _, bits in group_moves(group)]
    swap = (dp - core + t, core)
    barrier = pltpu.get_barrier_semaphore()
    for device in list(near.values()) + [(flip(dp, bits), t) for bits in distant]:
        pl.semaphore_signal(barrier, inc=1, device_id=device, device_id_type=MESH_ID)

    @pl.when(away == 1)
    def _():
        pl.semaphore_signal(barrier, inc=1, device_id=swap, device_id_type=MESH_ID)

    local = [
        pltpu.make_async_copy(shards[k], outs[k].at[away, 0] if k < 2 else outs[k].at[0], local_sem.at[k]) for k in range(4)]
    for copy in local:
        copy.start()
    pl.semaphore_wait(barrier, len(near) + len(distant) + away)
    count = [0]

    def remote(src, dst, device):
        slot = count[0]
        count[0] += 1
        return pltpu.make_async_remote_copy(
            src_ref=src, dst_ref=dst, send_sem=send_sem.at[slot], recv_sem=recv_sem.at[slot],
            device_id=device, device_id_type=MESH_ID)

    def blocks(ref, index, first, held, low, size):
        return ref.at[index, pl.ds(first, held), :, pl.ds(low, size)]

    plans = []
    for which, low, size, part in chunks:
        shard, out = shards[which], outs[which]
        steps, held = [], 1
        for group in groups:
            moves = []
            for place, bits in group_moves(group):
                src = shard.at[:, pl.ds(low, size)] if held == 1 else blocks(out, away, 0, held, low, size)
                dst = out.at[away, place, :, pl.ds(low, size)] if held == 1 else blocks(out, away, place * held, held, low, size)
                moves.append(remote(src, dst, (flip(dp, bits), t)))
            held *= len(group_moves(group)) + 1
            steps.append(moves)
        a, b = (low, part), (low + part, size - part)
        steps.append([
            remote(blocks(out, away, 0, held, *a), blocks(out, away, 0, held, *a), near[0]),
            remote(blocks(out, away, 0, held, *b), blocks(out, away, held, held, *b), near[2]),
        ])
        steps.append(
            [remote(blocks(out, k, 0, held, *a), blocks(out, k, held, held, *a), near[2]) for k in range(2)]
            + [remote(blocks(out, away, 0, 2 * held, *b), blocks(out, away, 0, 2 * held, *b), near[0])])
        steps.append([
            remote(blocks(out, k, 0, 2 * held, low, size),
                   blocks(out, 1 - k, 2 * held, 2 * held, low, size), near[1]) for k in range(2)])
        plans.append(steps)
    later = []
    held = 1
    for group in groups:
        moves = []
        for place, bits in group_moves(group):
            for shard, out in zip(shards[2:], outs[2:]):
                src = shard if held == 1 else out.at[pl.ds(0, held)]
                dst = out.at[place] if held == 1 else out.at[pl.ds(place * held, held)]
                moves.append(remote(src, dst, (flip(dp, bits), t)))
        held *= len(group_moves(group)) + 1
        later.append(moves)
    depth = len(plans[0])
    swap_copy = remote(tokens, x_out, swap)
    seg_copy = remote(seg, seg_out, near[1])
    stay_copy = pltpu.make_async_copy(tokens, x_out, local_sem.at[4])
    waited = set()

    def advance(number, phase):
        if number >= len(plans):
            return
        if phase > 0:
            for move in plans[number][phase - 1]:
                move.wait_recv()
        if phase == 1 and chunks[number][0] not in waited:
            waited.add(chunks[number][0])
            local[chunks[number][0]].wait()
        if phase < depth:
            for move in plans[number][phase]:
                move.start()

    advance(0, 0)
    seg_copy.start()

    @pl.when(away == 1)
    def _():
        swap_copy.start()

    @pl.when(away == 0)
    def _():
        stay_copy.start()

    far = len(groups)
    for number in range(len(plans)):
        if number == 0:
            for phase in range(1, far + 1):
                advance(0, phase)
            for k in range(1, len(plans)):
                advance(k, 0)
            for move in later[0]:
                move.start()
        advance(number, far + 1)
        for phase in range(1, far + 1):
            advance(number + 1, phase)
        advance(number, far + 2)
    for number in range(len(plans)):
        advance(number, depth)

    @pl.when(away == 1)
    def _():
        swap_copy.wait()

    @pl.when(away == 0)
    def _():
        stay_copy.wait()

    seg_copy.wait()
    for which in sorted(set(range(4)) - waited):
        local[which].wait()
    for k, moves in enumerate(later):
        if k > 0:
            for move in moves:
                move.start()
        for move in moves:
            move.wait()
    for steps in plans:
        for moves in steps:
            for move in moves:
                move.wait_send()


def head(dp_size, tokens, seg, shards, chunks):
    groups = far_groups(dp_size)
    partners = sum(len(group_moves(g)) for g in groups)
    slots = len(chunks) * (partners + 7) + 2 * partners + 2
    shapes = [(2, dp_size)] * 2 + [(dp_size // 4,)] * 2
    return pl.pallas_call(
        functools.partial(head_kernel, groups, chunks),
        in_specs=[VM] * 6,
        out_specs=[ANY] * 6,
        out_shape=[jax.ShapeDtypeStruct(a.shape, a.dtype) for a in (tokens, seg)]
        + [jax.ShapeDtypeStruct(lead + s.shape, s.dtype) for lead, s in zip(shapes, shards)],
        scratch_shapes=[pltpu.SemaphoreType.DMA((slots,)), pltpu.SemaphoreType.DMA((slots,)), pltpu.SemaphoreType.DMA((5,))],
        compiler_params=pltpu.CompilerParams(collective_id=0, has_side_effects=True),
    )(tokens, seg, *shards)


def tail_kernel(groups, own_lo, own_hi, rest_lo, rest_hi, small_lo, small_hi, feed, total, vecs, feed_total,
                feed_part, feed_got, part, got_core, got_near, got_last, got_far, vec, vec_core, vec_two, vec_one, vec_far, send_sem, recv_sem):
    dp, t = lax.axis_index("dp"), lax.axis_index("tensor")
    core = dp % 2
    away = core + t - 2 * core * t
    near = {1: (flip(dp, (1,)), t), 2: (flip(dp, (2,)), t), 0: (dp, 1 - t)}
    distant = [bits for group in groups for _, bits in group_moves(group)]
    barrier = pltpu.get_barrier_semaphore()
    for device in list(near.values()) + [(flip(dp, bits), t) for bits in distant]:
        pl.semaphore_signal(barrier, inc=1, device_id=device, device_id_type=MESH_ID)

    pl.semaphore_wait(barrier, len(near) + len(distant))
    count = [0]

    def remote(src, dst, device):
        slot = count[0]
        count[0] += 1
        return pltpu.make_async_remote_copy(
            src_ref=src, dst_ref=dst, send_sem=send_sem.at[slot], recv_sem=recv_sem.at[slot],
            device_id=device, device_id_type=MESH_ID)

    half, rows, cols = own_lo.shape
    quarter = half // 2
    chunks = [pl.ds(low, min(384, cols - low)) for low in range(0, cols, 384)]
    to_core = [[
        remote(rest_hi.at[:, :, c], got_core.at[0, :, :, c], near[1]),
        remote(own_hi.at[:, :, c], got_core.at[1, :, :, c], near[1])] for c in chunks]
    to_core[0].append(remote(small_hi, vec_core, near[1]))
    for moves in to_core:
        for move in moves:
            move.start()

    feed_steps = []
    held, used = feed.shape[0], 0
    for number, group in enumerate(reversed(groups)):
        moves = group_moves(group)
        held //= len(moves) + 1
        source, step = feed if number == 0 else feed_part, []
        for place, bits in moves:
            step.append(remote(source.at[pl.ds(place * held, held)], feed_got.at[pl.ds(used, held)], (flip(dp, bits), t)))
            used += held
        feed_steps.append((step, source, held, used - held * len(moves), len(moves)))
    for move in feed_steps[0][0]:
        move.start()

    def add(*terms):
        out = terms[0].astype(f32)
        for term in terms[1:]:
            out = out + term.astype(f32)
        return out.astype(bf)

    upper, lower = pl.ds(quarter, quarter), pl.ds(0, quarter)
    mine, other = away, 1 - away
    last = len(chunks) - 1
    steps, sent = {}, []

    def start(key, moves):
        steps[key] = moves
        sent.extend(moves)
        for move in moves:
            move.start()

    def arrive(key):
        for move in steps[key]:
            move.wait_recv()

    def core_stage(k):
        for move in to_core[k]:
            move.wait_recv()
        c = chunks[k]

        def body(q, _):
            part[0, q, :, c] = add(own_lo[q, :, c], got_core[0, q, :, c])
            part[1, q, :, c] = add(rest_lo[q, :, c], got_core[1, q, :, c])
            if k == 0:
                vec[q] = add(small_lo[q], vec_core[q])
            return 0

        lax.fori_loop(0, half, body, 0)
        if k % 2 == 1:
            start(("x", k), [remote(part.at[other, :, :, c], got_near.at[0, :, :, c], near[0])])
        else:
            start(("x", k), [
                remote(part.at[g, upper, :, c], got_near.at[g, lower, :, c], near[2]) for g in range(2)]
                + ([remote(vec.at[upper], vec_two, near[2])] if k == 0 else []))

    def x_stage(k):
        arrive(("x", k))
        c = chunks[k]

        def body(q, _):
            if k % 2 == 1:
                part[mine, q, :, c] = add(part[mine, q, :, c], got_near[0, q, :, c])
                return 0
            for g in range(2):
                part[g, q, :, c] = add(part[g, q, :, c], got_near[g, q, :, c])
            if k == 0:
                vec[q] = add(vec[q], vec_two[q])
            return 0

        lax.fori_loop(0, half if k % 2 == 1 else quarter, body, 0)
        if k % 2 == 1:
            start(("y", k), [remote(part.at[mine, upper, :, c], got_last.at[:, :, c], near[2])])
        else:
            start(("y", k), [remote(part.at[other, lower, :, c], got_last.at[:, :, c], near[0])]
                  + ([remote(vec.at[lower], vec_one, near[0])] if k == 0 else []))

    def far_moves(number, k):
        held, used = quarter, 0
        for index, group in enumerate(reversed(groups)):
            moves = group_moves(group)
            held //= len(moves) + 1
            if index == number:
                out = []
                for m, (place, bits) in enumerate(moves):
                    device, c = (flip(dp, bits), t), chunks[k]
                    out.append(remote(part.at[mine, pl.ds(place * held, held), :, c], got_far.at[pl.ds(used + m * held, held), :, c], device))
                    if k == 0:
                        out.append(remote(vec_one.at[pl.ds(place * held, held)], vec_far.at[pl.ds(used + m * held, held)], device))
                return out, held, used, len(moves)
            used += held * len(moves)

    def y_stage(k):
        arrive(("y", k))
        c = chunks[k]

        def body(q, _):
            part[mine, q, :, c] = add(part[mine, q, :, c], got_last[q, :, c])
            if k == 0:
                vec_one[q] = add(vec[q], vec_one[q])
            return 0

        lax.fori_loop(0, quarter, body, 0)
        start(("z", 0, k), far_moves(0, k)[0])

    far_shape = []
    held, used = quarter, 0
    for group in reversed(groups):
        moves = len(group_moves(group))
        held //= moves + 1
        far_shape.append((held, used, moves))
        used += held * moves

    def z_stage(number, k):
        arrive(("z", number, k))
        c = chunks[k]
        held, base, moves = far_shape[number]

        def body(q, _):
            part[mine, q, :, c] = add(part[mine, q, :, c], *[got_far[base + m * held + q, :, c] for m in range(moves)])
            if k == 0:
                vec_one[q] = add(vec_one[q], *[vec_far[base + m * held + q] for m in range(moves)])
            return 0

        lax.fori_loop(0, held, body, 0)
        if number + 1 < len(groups):
            start(("z", number + 1, k), far_moves(number + 1, k)[0])

    for k in range(last + 1):
        core_stage(k)
    for k in range(last + 1):
        x_stage(k)
        if k > 0:
            y_stage(k - 1)
    y_stage(last)
    for number in range(len(groups)):
        for k in range(last + 1):
            z_stage(number, k)
    to_far = []
    for number, (step, source, held, base, moves) in enumerate(feed_steps):
        if number > 0:
            for move in step:
                move.start()
        for move in step:
            move.wait_recv()

        def sum_feed(k, _, source=source, held=held, base=base, moves=moves):
            feed_part[k] = add(source[k], *[feed_got[base + m * held + k] for m in range(moves)])
            return 0

        if number + 1 < len(feed_steps):
            lax.fori_loop(0, held, sum_feed, 0)
        else:
            out = source[0].astype(f32)
            for m in range(moves):
                out = out + feed_got[base + m * held].astype(f32)
            feed_total[...] = out
        to_far += step
    total[...] = part[mine, 0].astype(f32)
    vecs[...] = vec_one[0].astype(f32)

    for move in sum(to_core, []) + sent + to_far:
        move.wait_send()


def tail(dp_size, own, rest, small, feed):
    groups = far_groups(dp_size)
    half, rows, cols = own[0].shape
    quarter = half // 2
    wide = small[0].shape[2]
    partners = sum(len(group_moves(g)) for g in groups)
    slots = (-(-cols // 384)) * (5 + partners) + 3 + 2 * partners
    return pl.pallas_call(
        functools.partial(tail_kernel, groups),
        in_specs=[VM] * 7,
        out_specs=[VM, VM, VM],
        out_shape=[
            jax.ShapeDtypeStruct((rows, cols), f32),
            jax.ShapeDtypeStruct((rows, wide), f32), jax.ShapeDtypeStruct(feed.shape[1:], f32)],
        scratch_shapes=[
            pltpu.VMEM(feed.shape, bf), pltpu.VMEM(feed.shape, bf),
            pltpu.VMEM((2, half, rows, cols), bf), pltpu.VMEM((2, half, rows, cols), bf), pltpu.VMEM((2, half, rows, cols), bf),
            pltpu.VMEM((quarter, rows, cols), bf), pltpu.VMEM((quarter, rows, cols), bf),
            pltpu.VMEM((half, rows, wide), bf), pltpu.VMEM((half, rows, wide), bf), pltpu.VMEM((quarter, rows, wide), bf),
            pltpu.VMEM((quarter, rows, wide), bf), pltpu.VMEM((quarter, rows, wide), bf),
            pltpu.SemaphoreType.DMA((slots,)), pltpu.SemaphoreType.DMA((slots,))],
        compiler_params=pltpu.CompilerParams(collective_id=1, has_side_effects=True, vmem_limit_bytes=48 << 20),
    )(*own, *rest, *small, feed)


def add_low(*terms):
    out = terms[0].astype(f32)
    for term in terms[1:]:
        out = out + term.astype(f32)
    return out.astype(bf)


def order_matrix(owner, rows, width):
    place = lax.broadcasted_iota(jnp.int32, (1, width), 1)
    block = place // rows
    count = width // rows
    natural = place % rows
    for k, bit in enumerate([1 << b for b in range(count.bit_length() - 2, 1, -1)] + [2, 1]):
        on, base = (block // (1 << k)) % 2, (owner // bit) % 2
        natural = natural + (on + base - 2 * on * base) * (bit * rows)
    return (lax.broadcasted_iota(jnp.int32, (width, width), 0) == natural).astype(f32).astype(bf)


def norm_parts(values):
    centered = values - jnp.mean(values, axis=-1, keepdims=True)
    inverse = lax.rsqrt(jnp.mean(centered * centered, axis=-1, keepdims=True) + EPSILON)
    return centered * inverse, inverse


def norm_back(hat, inverse, gain, grad):
    scaled = grad * gain
    return inverse * (
        scaled - jnp.mean(scaled, axis=-1, keepdims=True) - hat * jnp.mean(scaled * hat, axis=-1, keepdims=True))


def over_rows(total, body, first=0):
    def step(k, _):
        body(pl.ds(pl.multiple_of(first + k * ROWS, ROWS), ROWS))
        return 0

    lax.fori_loop(0, total // ROWS, step, 0)


def column_sum(ref, row, values):
    ref[row : row + 1] += jnp.sum(values, axis=0, keepdims=True)


def bias_row(vec_nat, group, cols):
    lanes = pl.ds(pl.multiple_of(group * cols, 128), cols)
    q, v = vec_nat[6:7, lanes], vec_nat[7:8, lanes]
    parts = []
    for g in range(cols // 128):
        part = slice(g * 128, (g + 1) * 128)
        parts += [q[:, part], jnp.zeros((1, 128), f32), v[:, part]]
    return jnp.concatenate(parts, axis=1)


def fan_matrix(fan):
    row = lax.broadcasted_iota(jnp.int32, (128 * fan, 1), 0)
    unit = lax.broadcasted_iota(jnp.int32, (128 * fan, 128 * fan), 1)
    return (unit == (row % 128) * fan + row // 128).astype(f32).astype(bf)


def first_kernel(rows, fan, tokens, packs, weights, seg, seg_other, x_out, n1_out, own, recv, vec_rel, fc_bias, starts,
                 tok, pack, weight, send, vec_nat, order, fan_rows, send_sem, recv_sem, local_sem):
    dp, t = lax.axis_index("dp"), lax.axis_index("tensor")
    core = dp % 2
    away = core + t - 2 * core * t
    total, width = tok.shape
    cols = weight.shape[2] // 3
    partner = (flip(dp, (1,)), t)
    barrier = pltpu.get_barrier_semaphore()
    pl.semaphore_signal(barrier, inc=1, device_id=partner, device_id_type=MESH_ID)
    loads = [
        pltpu.make_async_copy(src, dst, local_sem.at[k])
        for k, (src, dst) in enumerate(((packs.at[0], pack), (tokens, tok), (weights.at[1], weight.at[1]), (weights.at[0], weight.at[0])))]
    for load in loads:
        load.start()
    order[...] = order_matrix(dp, rows, width)
    loads[0].wait()
    small = pack[:, cols:].astype(f32).T[:VECS]
    vec_rel[...] = small
    vec_nat[...] = lax.dot_general(small.astype(bf), order[...], NT, preferred_element_type=f32)
    send_bias, own_bias = bias_row(vec_nat, 1 - core, cols), bias_row(vec_nat, core, cols)
    for load in loads[1:3]:
        load.wait()
    pl.semaphore_wait(barrier, 1)
    parts, size = 2, total // 2
    copies = [
        pltpu.make_async_remote_copy(
            src_ref=send.at[pl.ds(k * size, size)], dst_ref=recv.at[pl.ds(k * size, size)], send_sem=send_sem.at[k],
            recv_sem=recv_sem.at[k], device_id=partner, device_id_type=MESH_ID)
        for k in range(parts)]

    def first(at):
        x = jnp.dot(tok[at], order[...], preferred_element_type=f32)
        hat, _ = norm_parts(x)
        n1 = (hat * vec_rel[0:1] + vec_rel[1:2]).astype(bf)
        x_out[at] = x.astype(bf)
        n1_out[at] = n1
        send[at] = (jnp.dot(n1, weight[1], preferred_element_type=f32) + send_bias).astype(bf)

    def second(at):
        own[at] = (jnp.dot(n1_out[at], weight[0], preferred_element_type=f32) + own_bias).astype(bf)

    for k in range(parts):
        over_rows(size, first, k * size)
        copies[k].start()
    loads[3].wait()
    over_rows(total, second)

    count = width // 128
    fan_rows[...] = jnp.zeros_like(fan_rows)
    for k in range(count):
        for m in range(fan):
            fan_rows[k : k + 1, m * 128 : (m + 1) * 128] = vec_nat[8 + m : 9 + m, k * 128 : (k + 1) * 128]
    bias = jnp.dot(fan_rows[...].astype(bf), fan_matrix(fan), preferred_element_type=f32)
    for k in range(count):
        fc_bias[:, k * 128 * fan : (k + 1) * 128 * fan] = bias[k : k + 1]
    docs = jnp.where(away == 0, seg[...], seg_other[...]).astype(f32)
    begin = jnp.zeros_like(docs)
    for d in range(1, 16):
        before = jnp.sum(jnp.where(docs < d, 1.0, 0.0), axis=1, keepdims=True)
        begin = jnp.where(docs == d, before, begin)
    starts[...] = begin.astype(jnp.int32)
    for copy in copies:
        copy.wait()


def picked(array, index):
    return pl.BlockSpec((1,) + array.shape[1:], lambda k, s: (index, 0, 0))


def whole(array):
    return pl.BlockSpec(array.shape, lambda k, s: (0,) * len(array.shape))


def like(shape, dtype):
    return jax.ShapeDtypeStruct(shape, dtype)


def by_rows(kernel, info, inputs, specs, outs, scratch=(), limit=60):
    total = inputs[0].shape[0]

    def spec(array, given=None):
        if given is not None:
            return given
        if array.shape[0] == total:
            return pl.BlockSpec((ROWS,) + array.shape[1:], lambda k, s: (k, 0))
        return whole(array)

    return pl.pallas_call(
        kernel,
        grid_spec=pltpu.PrefetchScalarGridSpec(
            num_scalar_prefetch=1, grid=(total // ROWS,), in_specs=[spec(a, g) for a, g in zip(inputs, specs)],
            out_specs=[spec(o) for o in outs], scratch_shapes=list(scratch)),
        out_shape=outs,
        cost_estimate=pl.CostEstimate(flops=1 << 22, bytes_accessed=1 << 18, transcendentals=0),
        compiler_params=pltpu.CompilerParams(vmem_limit_bytes=limit << 20),
    )(info, *inputs)


def project_first(rows, fan, tokens, packs, weights, seg, seg_other):
    n, width = tokens.shape
    qkv = like((n, weights.shape[2]), bf)
    return pl.pallas_call(
        functools.partial(first_kernel, rows, fan),
        in_specs=[ANY, ANY, ANY, VM, VM],
        out_specs=[VM, VM, VM, ANY, VM, VM, VM],
        out_shape=[
            like((n, width), bf), like((n, width), bf), qkv, qkv, like((VECS, width), f32), like((1, width * fan), f32),
            like(seg.shape, jnp.int32)],
        scratch_shapes=[
            pltpu.VMEM((n, width), bf), pltpu.VMEM(packs.shape[1:], bf), pltpu.VMEM(weights.shape, bf), pltpu.VMEM(qkv.shape, bf),
            pltpu.VMEM((VECS, width), f32), pltpu.VMEM((width, width), bf), pltpu.VMEM((8, 128 * fan), f32),
            pltpu.SemaphoreType.DMA((2,)), pltpu.SemaphoreType.DMA((2,)), pltpu.SemaphoreType.DMA((4,))],
        compiler_params=pltpu.CompilerParams(collective_id=3, has_side_effects=True, vmem_limit_bytes=60 << 20),
    )(tokens, packs, weights, seg, seg_other)


def middle_kernel(rows, x, o_own, o_send, cot, cot_recv, packs, vec_rel, fc00, fc01, fc10, fc11, pr0, pr1,
                  middle, n2, cot_rel, d_mlp, o_recv, fc_got, pr_got, order, send_sem, recv_sem):
    dp, t = lax.axis_index("dp"), lax.axis_index("tensor")
    core = dp % 2
    away = core + t - 2 * core * t
    partner = (flip(dp, (1,)), t)
    barrier = pltpu.get_barrier_semaphore()
    pl.semaphore_signal(barrier, inc=1, device_id=partner, device_id_type=MESH_ID)
    pl.semaphore_wait(barrier, 1)
    size = fc00.shape[0]
    copies = [
        pltpu.make_async_remote_copy(
            src_ref=src, dst_ref=dst, send_sem=send_sem.at[k], recv_sem=recv_sem.at[k], device_id=partner, device_id_type=MESH_ID)
        for k, (src, dst) in enumerate((
            (o_send, o_recv), (fc00, fc_got.at[0, pl.ds(0, size)]), (fc01, fc_got.at[0, pl.ds(size, size)]), (pr0, pr_got.at[0]),
            (fc10, fc_got.at[1, pl.ds(0, size)]), (fc11, fc_got.at[1, pl.ds(size, size)]), (pr1, pr_got.at[1])))]
    for copy in copies:
        copy.start()
    order[...] = order_matrix(dp, rows, x.shape[1])
    cols = o_own.shape[1]

    def cot_rows(at):
        grad = jnp.dot(jnp.where(away == 0, cot[at], cot_recv[at]), order[...], preferred_element_type=f32)
        cot_rel[at] = grad.astype(bf)
        d_mlp[at] = (BRANCH_SCALE * grad).astype(bf)

    over_rows(x.shape[0], cot_rows)
    copies[0].wait_recv()

    def body(at):
        branch = lax.dot_general(o_own[at], packs[0, :, :cols], NT, preferred_element_type=f32)
        branch = branch + lax.dot_general(o_recv[at], packs[1, :, :cols], NT, preferred_element_type=f32)
        mid = x[at].astype(f32) + BRANCH_SCALE * (branch + vec_rel[2:3])
        middle[at] = mid
        hat, _ = norm_parts(mid)
        n2[at] = (hat * vec_rel[3:4] + vec_rel[4:5]).astype(bf)

    over_rows(x.shape[0], body)
    for copy in copies[1:]:
        copy.wait_recv()
    for copy in copies:
        copy.wait_send()


def middle_part(rows, x, o_own, o_send, cot, cot_recv, packs, vec_rel, fc_parts, proj_parts):
    shape, half = x.shape, x.shape[1] // 2
    hidden = proj_parts[0].shape[1]
    got = like((2, half, hidden), bf)
    return pl.pallas_call(
        functools.partial(middle_kernel, rows),
        in_specs=[VM] * 7 + [HBM] * 6,
        out_specs=[VM] * 5 + [ANY] * 2,
        out_shape=[like(shape, f32), like(shape, bf), like(shape, bf), like(shape, bf), like(o_send.shape, bf), got, got],
        scratch_shapes=[
            pltpu.VMEM((shape[1], shape[1]), bf), pltpu.SemaphoreType.DMA((7,)), pltpu.SemaphoreType.DMA((7,))],
        compiler_params=pltpu.CompilerParams(collective_id=2, has_side_effects=True, vmem_limit_bytes=36 << 20),
    )(x, o_own, o_send, cot, cot_recv, packs, vec_rel, *fc_parts[0], *fc_parts[1], *proj_parts)


def after_kernel(rows, info, middle, mlp, back, cot, packs, vec_rel, block_out, d_middle, d_attn, do_own, do_send, sums, order):
    @pl.when(pl.program_id(0) == 0)
    def _():
        order[...] = order_matrix(info[1], rows, middle.shape[1])
        sums[...] = jnp.zeros_like(sums)

    cols = do_own.shape[1]
    mid = middle[...]
    out = (mid + BRANCH_SCALE * (mlp[...] + vec_rel[5:6])).astype(bf)
    block_out[...] = lax.dot_general(out, order[...], NT, preferred_element_type=f32).astype(bf)
    hat, inverse = norm_parts(mid)
    grad = back[...]
    out_grad = cot[...].astype(f32)
    entire = out_grad + norm_back(hat, inverse, vec_rel[3:4], grad)
    d_middle[...] = entire
    low = (BRANCH_SCALE * entire).astype(bf)
    d_attn[...] = low
    do_own[...] = jnp.dot(low, packs[0, :, :cols], preferred_element_type=f32).astype(bf)
    do_send[...] = jnp.dot(low, packs[1, :, :cols], preferred_element_type=f32).astype(bf)
    column_sum(sums, 0, BRANCH_SCALE * entire)
    column_sum(sums, 1, grad * hat)
    column_sum(sums, 2, grad)
    column_sum(sums, 3, BRANCH_SCALE * out_grad)


def after_part(info, rows, middle, mlp, back, cot, packs, vec_rel, cols):
    shape = middle.shape
    slim = like((shape[0], cols), bf)
    return by_rows(
        functools.partial(after_kernel, rows), info, (middle, mlp, back, cot, packs, vec_rel), (None,) * 6,
        [like(shape, bf), like(shape, f32), like(shape, bf), slim, slim, like((8, shape[1]), f32)],
        [pltpu.VMEM((shape[1], shape[1]), bf)])


def feed_kernel(info, n2, d_mlp, bias, fc_got, pr_got, fc00, fc01, fc10, fc11, pr0, pr1,
                acc, back, fc_lo, fc_hi, pr_lo, pr_hi, d_bias, n2_t, d_t, w_fc, w_pr, act, d_pre):
    step = pl.program_id(0)
    total, half = n2.shape[0], n2.shape[1] // 2

    @pl.when(step == 0)
    def _():
        acc[...] = jnp.zeros_like(acc)
        back[...] = jnp.zeros_like(back)
        n2_t[...] = n2[...].T
        d_t[...] = d_mlp[...].T

    @pl.when(step < pl.num_programs(0) // 2)
    def _():
        w_fc[: half // 2], w_fc[half // 2 : half], w_pr[:half] = fc00[...], fc01[...], pr0[...]

    @pl.when(step >= pl.num_programs(0) // 2)
    def _():
        w_fc[: half // 2], w_fc[half // 2 : half], w_pr[:half] = fc10[...], fc11[...], pr1[...]

    w_fc[half:], w_pr[half:] = fc_got[0], pr_got[0]
    root = 0.7978845608
    count = total // ROWS
    raw = {}
    grad_sum = jnp.zeros((1, w_fc.shape[1]), f32)

    def products(k):
        at = slice(k * ROWS, (k + 1) * ROWS)
        return (
            jnp.dot(n2[at], w_fc[...], preferred_element_type=f32) + bias[...],
            jnp.dot(d_mlp[at], w_pr[...], preferred_element_type=f32))

    def add_back(k):
        at = slice(k * ROWS, (k + 1) * ROWS)
        acc[at] += lax.dot_general(act[at], w_pr[...], NT, preferred_element_type=f32)
        back[at] += lax.dot_general(d_pre[at], w_fc[...], NT, preferred_element_type=f32)

    raw[0] = products(0)
    for k in range(count):
        at = slice(k * ROWS, (k + 1) * ROWS)
        if k + 1 < count:
            raw[k + 1] = products(k + 1)
        pre, d_act = raw.pop(k)
        square = pre * pre
        inner = jnp.tanh(pre * (root + root * 0.044715 * square))
        gate = 0.5 + 0.5 * inner
        act[at] = (pre * gate).astype(bf)
        slope = gate + pre * (0.5 - 0.5 * inner * inner) * (root + root * 3 * 0.044715 * square)
        grad = d_act * slope
        grad_sum = grad_sum + jnp.sum(grad, axis=0, keepdims=True)
        d_pre[at] = grad.astype(bf)
        if k > 0:
            add_back(k - 1)
    add_back(count - 1)
    d_bias[...] = grad_sum
    for out, left, right, low in (
        (fc_hi, n2_t, d_pre, half), (pr_hi, d_t, act, half), (fc_lo, n2_t, d_pre, 0), (pr_lo, d_t, act, 0)):
        out[0] = jnp.dot(left[low : low + half], right[...], preferred_element_type=f32).astype(bf)


def feed_part(info, n2, d_mlp, bias, fc_got, pr_got, fc_parts, proj_parts):
    (total, width), hidden, half = n2.shape, bias.shape[1] // 2, n2.shape[1] // 2
    steps = hidden // HIDDEN
    fixed = lambda a: pl.BlockSpec(a.shape, lambda k, s: (0,) * len(a.shape), pipeline_mode=pl.Buffered(1))
    early = lambda a: pl.BlockSpec((a.shape[0], HIDDEN), lambda k, s: (0, jnp.minimum(k, steps - 1)))
    late = lambda a: pl.BlockSpec((a.shape[0], HIDDEN), lambda k, s: (0, jnp.maximum(k - steps, 0)))
    two = lambda a: pl.BlockSpec((1, a.shape[1], HIDDEN), lambda k, s: (k // steps, 0, k % steps))
    unit = pl.BlockSpec((1, HIDDEN), lambda k, s: (0, (s[3] + (k // steps) * (1 - 2 * s[3])) * steps + k % steps))
    grad = like((2, half, hidden), bf)
    sums = [like((total, width), f32)] * 2
    return pl.pallas_call(
        feed_kernel,
        grid_spec=pltpu.PrefetchScalarGridSpec(
            num_scalar_prefetch=1,
            grid=(2 * steps,),
            in_specs=[fixed(n2), fixed(d_mlp), unit, two(fc_got), two(pr_got)]
            + [early(a) for a in fc_parts[0]] + [late(a) for a in fc_parts[1]] + [early(proj_parts[0]), late(proj_parts[1])],
            out_specs=[fixed(o) for o in sums] + [two(grad)] * 4 + [unit],
            scratch_shapes=[
                pltpu.VMEM((width, total), bf), pltpu.VMEM((width, total), bf), pltpu.VMEM((width, HIDDEN), bf),
                pltpu.VMEM((width, HIDDEN), bf), pltpu.VMEM((total, HIDDEN), bf), pltpu.VMEM((total, HIDDEN), bf)],
        ),
        out_shape=sums + [grad] * 4 + [like((1, 2 * hidden), f32)],
        cost_estimate=pl.CostEstimate(flops=1 << 22, bytes_accessed=1 << 18, transcendentals=0),
        compiler_params=pltpu.CompilerParams(vmem_limit_bytes=46 << 20),
    )(info, n2, d_mlp, bias, fc_got, pr_got, *fc_parts[0], *fc_parts[1], *proj_parts)


def weight_kernel(n1, d_attn, d_qkv, o, lo, hi, left_t):
    step, half = pl.program_id(0), left_t.shape[0] // 2

    @pl.when(step == 0)
    def _():
        left_t[...] = n1[...].T

    def products(right):
        for out, low in ((hi, half), (lo, 0)):
            out[...] = jnp.dot(left_t[low : low + half], right[...], preferred_element_type=f32).astype(bf)

    @pl.when(step < pl.num_programs(0) - 1)
    def _():
        products(d_qkv)

    @pl.when(step == pl.num_programs(0) - 1)
    def _():
        left_t[...] = d_attn[...].T
        products(o)


def weight_part(n1, d_attn, d_qkv, o):
    (n, width), cols = n1.shape, o.shape[1]
    steps = d_qkv.shape[1] // cols
    fixed = lambda a: pl.BlockSpec(a.shape, lambda k: (0, 0), pipeline_mode=pl.Buffered(1))
    out = pl.BlockSpec((width // 2, cols), lambda k: (0, k))
    grad = like((width // 2, d_qkv.shape[1] + cols), bf)
    return pl.pallas_call(
        weight_kernel,
        grid=(steps + 1,),
        in_specs=[fixed(n1), fixed(d_attn), pl.BlockSpec((n, cols), lambda k: (0, jnp.minimum(k, steps - 1))), fixed(o)],
        out_specs=[out, out],
        out_shape=[grad, grad],
        scratch_shapes=[pltpu.VMEM((width, n), bf)],
        cost_estimate=pl.CostEstimate(flops=1 << 22, bytes_accessed=1 << 18, transcendentals=0),
        compiler_params=pltpu.CompilerParams(vmem_limit_bytes=32 << 20),
    )(n1, d_attn, d_qkv, o)


def token_kernel(rows, fan, info, own, rest, x, d_middle, weights, vec_rel, mid_sums, fc_grad, grad_out, small, own_sums, rest_sums, vecs, nat, order, fan_rows):
    width, cols = x.shape[1], own.shape[1] // 3
    step = pl.program_id(0)

    @pl.when(step == 0)
    def _():
        order[...] = order_matrix(info[1], rows, width)
        for ref in (own_sums, rest_sums, vecs, nat, fan_rows):
            ref[...] = jnp.zeros_like(ref)

    grad = lax.dot_general(own[...], weights[0], NT, preferred_element_type=f32)
    grad = grad + lax.dot_general(rest[...], weights[1], NT, preferred_element_type=f32)
    hat, inverse = norm_parts(x[...].astype(f32))
    low = (d_middle[...] + norm_back(hat, inverse, vec_rel[0:1], grad)).astype(bf)
    grad_out[...] = lax.dot_general(low, order[...], NT, preferred_element_type=f32).astype(bf)
    column_sum(own_sums, 0, own[...].astype(f32))
    column_sum(rest_sums, 0, rest[...].astype(f32))
    column_sum(vecs, 0, grad * hat)
    column_sum(vecs, 1, grad)

    @pl.when(step == pl.num_programs(0) - 1)
    def _():
        for group, ref in ((info[0], own_sums), (1 - info[0], rest_sums)):
            for row, part_index in ((0, 0), (1, 2)):
                picks = [ref[0:1, (3 * g + part_index) * 128 : (3 * g + part_index + 1) * 128] for g in range(cols // 128)]
                nat[row : row + 1, pl.ds(pl.multiple_of(group * cols, 128), cols)] = jnp.concatenate(picks, axis=1)
        count = width // 128
        for k in range(count):
            fan_rows[k : k + 1] = fc_grad[:, k * 128 * fan : (k + 1) * 128 * fan]
        spread = lax.dot_general(fan_rows[...].astype(bf), fan_matrix(fan), NT, preferred_element_type=f32)
        for k in range(count):
            for m in range(fan):
                nat[2 + m : 3 + m, k * 128 : (k + 1) * 128] = spread[k : k + 1, m * 128 : (m + 1) * 128]
        moved = jnp.dot(nat[...].astype(bf), order[...], preferred_element_type=f32)
        vecs[2:4] = moved[0:2]
        vecs[4:8] = mid_sums[0:4]
        vecs[8 : 8 + fan] = moved[2 : 2 + fan]
        small[...] = vecs[...].T.astype(bf)


def token_part(info, rows, own, rest, x, d_middle, weights, vec_rel, mid_sums, fc_grad):
    n, width = x.shape
    wide, fan = own.shape[1], fc_grad.shape[1] // width
    return by_rows(
        functools.partial(token_kernel, rows, fan), info, (own, rest, x, d_middle, weights, vec_rel, mid_sums, fc_grad), (None,) * 8,
        [like((n, width), bf), like((width, SMALL), bf)],
        [pltpu.VMEM((8, wide), f32), pltpu.VMEM((8, wide), f32), pltpu.VMEM((SMALL, width), f32), pltpu.VMEM((8, width), f32),
         pltpu.VMEM((width, width), bf), pltpu.VMEM((8, 128 * fan), f32)], 32)


def on_device(
    tokens, segment_ids, ln1_gain, ln1_bias, w_qkv, b_qv, w_attn_out, b_attn_out,
    ln2_gain, ln2_bias, w_fc, b_fc, w_proj, b_proj, cotangent,
):
    dp_size = lax.axis_size("dp")
    dp_pos, t_pos = lax.axis_index("dp"), lax.axis_index("tensor")
    core = dp_pos % 2
    rows = ln1_gain.shape[0]
    width = tokens.shape[1]
    cols = w_qkv.shape[2]
    hidden = w_fc.shape[1]
    fan = b_fc.shape[0] // rows
    far = [1 << k for k in range(dp_size.bit_length() - 2, 1, -1)]
    swap = []
    for d in range(dp_size):
        for t in range(2):
            if d % 2 != t:
                swap.append((2 * d + t, 2 * (d - d % 2 + t) + d % 2))
    mine = core == t_pos

    pairs = cols // 128

    def by_pair(parts):
        parts = parts.reshape(-1, 3, pairs, 128)
        return jnp.swapaxes(parts, 1, 2).reshape(-1, 3 * cols)

    def by_part(columns):
        return jnp.swapaxes(columns.reshape(-1, pairs, 3, 128), 1, 2).reshape(-1, 3, cols)

    small = jnp.concatenate([jnp.stack([ln1_gain, ln1_bias, b_attn_out, ln2_gain, ln2_bias, b_proj]), b_qv], axis=0)
    small = jnp.concatenate([small.T, b_fc.reshape(rows, fan)], axis=1)
    small = jnp.pad(small, ((0, 0), (0, SMALL - small.shape[1])))
    out_pack = jnp.concatenate([w_attn_out.T, small], axis=1)
    tokens, seg_other, all_qkv, all_out, fc_far, proj_far = head(
        dp_size, tokens, segment_ids, (by_pair(w_qkv), out_pack, w_fc, w_proj.T), chunks_of(3 * cols, 0, 2) + chunks_of(cols + SMALL, 1, 1))
    all_qkv, all_out = (a.reshape(2, width, -1) for a in (all_qkv, all_out))
    fc_far, proj_far = fc_far.reshape(-1, hidden), proj_far.reshape(-1, hidden)
    fc_parts = [[fc_far], [exchange(fc_far, 0, dp_size)]]
    proj_half = exchange(proj_far, 2, dp_size)

    part = jnp.stack([core, dp_pos, jnp.where(mine, 1, 0), t_pos]).astype(jnp.int32)
    x, n1, qkv_own, qkv_recv, vec_rel, fc_bias, starts = project_first(
        rows, fan, tokens, all_out, all_qkv, segment_ids, seg_other)
    fc_parts, proj_half, qkv_own = lax.optimization_barrier((fc_parts, proj_half, qkv_own))
    fc_parts = [p + [exchange(p[0], 2, dp_size)] for p in fc_parts]
    proj_half = jnp.concatenate([proj_far, proj_half], axis=0)
    proj_parts = [proj_half, exchange(proj_half, 0, dp_size)]
    o_own, o_send, lse = attn_fwd(qkv_own, qkv_recv, starts, part)
    cot_recv = lax.ppermute(cotangent, BOTH, swap)
    half = width // 2
    middle, n2, cot, d_mlp, o_recv, fc_got, pr_got = middle_part(
        rows, x, o_own, o_send, cotangent, cot_recv, all_out, vec_rel, fc_parts, proj_parts)
    mlp, back, fc_lo, fc_hi, pr_lo, pr_hi, fc_grad = feed_part(
        part, n2, d_mlp, fc_bias, fc_got, pr_got, fc_parts, proj_parts)
    fc_got, pr_got = exchange(fc_hi, 1, dp_size), exchange(pr_hi, 1, dp_size)
    block_out, d_middle, d_attn, do_own, do_send, mid_sums = after_part(
        part, rows, middle, mlp, back, cot, all_out, vec_rel, cols)
    do_recv = exchange(do_send, 1, dp_size)

    near_size = half // 2
    fc_rest = add_low(fc_lo[1], fc_got[1])
    pr_rest = add_low(pr_lo[:, near_size:], pr_got[:, near_size:])
    last = (qkv_own, qkv_recv, do_own, do_recv, o_own, o_send)
    last, fc_rest, pr_rest = lax.optimization_barrier((last, fc_rest, pr_rest))
    fc_sent = exchange(fc_rest, 0, dp_size)
    pr_sent = exchange(pr_rest, 2, dp_size)
    block_recv = lax.ppermute(block_out, BOTH, swap)
    dq_own, dq_send = attn_bwd(*last, starts, lse, part)
    dq_recv = exchange(dq_send, 1, dp_size)
    dq_own, fc_sent, pr_sent = lax.optimization_barrier((dq_own, fc_sent, pr_sent))
    fc_rest = add_low(fc_lo[0, near_size:], fc_got[0, near_size:], fc_sent[near_size:])
    pr_rest = add_low(pr_lo[1, :near_size], pr_got[1, :near_size], pr_sent[1])
    dq_own, fc_rest, pr_rest = lax.optimization_barrier((dq_own, fc_rest, pr_rest))
    fc_near = exchange(fc_rest, 2, dp_size)
    pr_near = exchange(pr_rest, 0, dp_size)
    own_lo, own_hi = weight_part(n1, d_attn, dq_own, o_own)
    own_lo, dq_recv = lax.optimization_barrier((own_lo, dq_recv))
    grad_tokens, d_small = token_part(part, rows, dq_own, dq_recv, x, d_middle, all_qkv, vec_rel, mid_sums, fc_grad)
    grad_recv = lax.ppermute(grad_tokens, BOTH, swap)
    d_small, fc_near, pr_near = lax.optimization_barrier((d_small, fc_near, pr_near))
    sum_fc = add_low(fc_lo[0, :near_size], fc_got[0, :near_size], fc_sent[:near_size], fc_near)
    sum_proj = add_low(pr_lo[0, :near_size], pr_got[0, :near_size], pr_sent[0], pr_near)
    feed = jnp.concatenate([sum_fc, sum_proj], axis=1).reshape(-1, rows, 2 * hidden)
    dq_recv, d_small, feed = lax.optimization_barrier((dq_recv, d_small, feed))
    rest_lo, rest_hi = weight_part(n1, d_attn, dq_recv, o_recv)
    blocks = lambda arr: arr.reshape(dp_size // 2, rows, -1)
    sum_a, vecs, sum_feed = tail(
        dp_size, (blocks(own_lo), blocks(own_hi)), (blocks(rest_lo), blocks(rest_hi)),
        (blocks(d_small[:half]), blocks(d_small[half:])), feed)
    vecs, block_recv, grad_recv = lax.optimization_barrier((vecs, block_recv, grad_recv))
    block_out = jnp.where(mine, block_out, block_recv)
    grad_tokens = jnp.where(mine, grad_tokens, grad_recv)
    return (
        block_out,
        grad_tokens,
        vecs[:, 0],
        vecs[:, 1],
        by_part(sum_a[:, : 3 * cols]),
        vecs[:, 2:4].T,
        sum_a[:, 3 * cols :].T,
        vecs[:, 4],
        vecs[:, 5],
        vecs[:, 6],
        sum_feed[:, :hidden],
        vecs[:, 8 : 8 + fan].reshape(rows * fan),
        sum_feed[:, hidden:].T,
        vecs[:, 7],
    )


def solution(mesh):
    vec, tok = P("dp"), P(BOTH, None)
    in_specs = (
        tok, P("dp", None), vec, vec, P("dp", None, "tensor"), P(None, "dp"), P("tensor", "dp"),
        vec, vec, vec, P("dp", "tensor"), vec, P("tensor", "dp"), vec, tok,
    )
    out_specs = (
        tok, tok, vec, vec, P("dp", None, "tensor"), P(None, "dp"), P("tensor", "dp"),
        vec, vec, vec, P("dp", "tensor"), vec, P("tensor", "dp"), vec,
    )
    return jax.shard_map(on_device, mesh=mesh, in_specs=in_specs, out_specs=out_specs, check_vma=False)
```

```python
import functools

import jax
import jax.numpy as jnp
from jax import lax
from jax.experimental import pallas as pl
from jax.experimental.pallas import tpu as pltpu
from jax.sharding import PartitionSpec as P

HD = 64
QB = 256
NEG = -1e30
EPSILON = 1e-05
BRANCH_SCALE = 48.0 ** (-0.5)
SMALL = 128
VECS = 16
ROWS = 256
HIDDEN = 768
bf = jnp.bfloat16
f32 = jnp.float32
NT = (((1,), (1,)), ((), ()))
TN = (((0,), (0,)), ((), ()))
BOTH = ("dp", "tensor")
MESH_ID = pl.DeviceIdType.MESH
ANY = pl.BlockSpec(memory_space=pl.ANY)
VM = pl.BlockSpec(memory_space=pltpu.VMEM)
HBM = pl.BlockSpec(memory_space=pltpu.HBM)
SM = pl.BlockSpec(memory_space=pltpu.SMEM)


def attn_mask(kat, at, srow):
    keys = lax.broadcasted_iota(jnp.int32, (QB, QB), 0)
    rows = lax.broadcasted_iota(jnp.int32, (1, QB), 1) + (at - kat)
    return (keys >= srow - kat) & (keys <= rows)


def over_blocks(bounds, i, step, carry):
    low = bounds[0, i * QB] // QB
    mid = jnp.minimum((bounds[0, i * QB + QB - 1] + QB - 1) // QB, i)
    carry = lax.fori_loop(0, mid - low + 1, lambda k, c: step(True, jnp.where(k == 0, i, low + k - 1), c), carry)
    return lax.fori_loop(mid, i, functools.partial(step, False), carry)


def head_lanes(values):
    low = (lax.broadcasted_iota(jnp.int32, (1, values.shape[1]), 1) % 128) < HD
    zero = jnp.zeros((), bf)
    return jnp.where(low, values, zero), jnp.where(low, zero, values)


def fwd_kernel(info, bounds, own, recv, st_ref, okeep, osend, lse_ref, qm, ks, vt, osc, acc):
    half, cols = own.shape[0], own.shape[1] // 3
    n, nb, heads, pairs = 2 * half, 2 * half // QB, cols // HD, cols // 128
    c = info[0]
    for base, src in ((c * half, own), ((1 - c) * half, recv)):
        rows = pl.ds(pl.multiple_of(base, half), half)
        for g in range(pairs):
            lanes = slice(g * 128, (g + 1) * 128)
            part = lambda k: src[:, (3 * g + k) * 128 : (3 * g + k + 1) * 128]
            qm[0, rows, lanes], qm[1, rows, lanes] = head_lanes(part(0) * bf(HD**-0.5))
            ks[rows, lanes] = part(1)
            vt[lanes, rows] = part(2).T

    def qblock(i, _):
        at = pl.multiple_of(i * QB, QB)
        qr = pl.ds(at, QB)
        srow = st_ref[:, qr]
        acc[...] = jnp.zeros_like(acc)

        def step(masked, j, carry):
            kat = pl.multiple_of(j * QB, QB)
            kr = pl.ds(kat, QB)
            if masked:
                mask = attn_mask(kat, at, srow)
            scores, mixed = [], []
            for h in range(heads):
                lanes = slice(h // 2 * 128, h // 2 * 128 + 128)
                one = lax.dot_general(ks[kr, lanes], qm[h % 2, qr, lanes], NT, preferred_element_type=f32)
                scores.append(jnp.where(mask, one, NEG) if masked else one)
            for h in range(heads):
                top, total = carry[h]
                new = jnp.maximum(top, jnp.max(scores[h], axis=0, keepdims=True))
                weights = jnp.exp(scores[h] - new)
                fade = jnp.exp(top - new)
                total = fade * total + jnp.sum(weights, axis=0, keepdims=True)
                mixed.append((new, total, fade, weights.astype(bf)))
            for h in range(heads):
                sub = slice(h * HD, (h + 1) * HD)
                acc[sub] = mixed[h][2] * acc[sub] + jnp.dot(vt[sub, kr], mixed[h][3], preferred_element_type=f32)
            return tuple(m[:2] for m in mixed)

        carry = over_blocks(bounds, i, step, ((jnp.full((1, QB), NEG, f32), jnp.zeros((1, QB), f32)),) * heads)
        for h, (top, total) in enumerate(carry):
            sub = slice(h * HD, (h + 1) * HD)
            acc[sub] = acc[sub] / total
            lse_ref[h : h + 1, qr] = top + jnp.log(total)
        osc[qr] = acc[...].T.astype(bf)
        return 0

    lax.fori_loop(0, nb, qblock, 0)
    okeep[...] = osc[pl.ds(pl.multiple_of(c * half, half), half)]
    osend[...] = osc[pl.ds(pl.multiple_of((1 - c) * half, half), half)]


def attn_fwd(own, recv, starts, info):
    half, cols = own.shape[0], own.shape[1] // 3
    n = 2 * half
    return pl.pallas_call(
        fwd_kernel,
        in_specs=[SM, SM, VM, VM, VM],
        out_specs=[VM] * 3,
        scratch_shapes=[
            pltpu.VMEM((2, n, cols), bf), pltpu.VMEM((n, cols), bf), pltpu.VMEM((cols, n), bf),
            pltpu.VMEM((n, cols), bf), pltpu.VMEM((cols, QB), f32)],
        out_shape=[jax.ShapeDtypeStruct((half, cols), bf)] * 2 + [jax.ShapeDtypeStruct((cols // HD, n), f32)],
        cost_estimate=pl.CostEstimate(flops=n * n, bytes_accessed=n * 128, transcendentals=0),
        compiler_params=pltpu.CompilerParams(vmem_limit_bytes=30 << 20),
    )(info, starts, own, recv, starts)


def bwd_kernel(info, bounds, own, recv, doo, dor, oo, orr, st_ref, lse_ref, dkeep, dsend, qm, ks, vs, kt, dom, dlt, dqs, dks, dvs):
    half, cols = own.shape[0], own.shape[1] // 3
    n, nb, heads, pairs = 2 * half, 2 * half // QB, cols // HD, cols // 128
    c = info[0]
    lanes_of = lambda g: slice(g * 128, (g + 1) * 128)
    for base, src, do, o in ((c * half, own, doo, oo), ((1 - c) * half, recv, dor, orr)):
        rows = pl.ds(pl.multiple_of(base, half), half)
        for g in range(pairs):
            lanes = lanes_of(g)
            part = lambda k: src[:, (3 * g + k) * 128 : (3 * g + k + 1) * 128]
            qm[0, rows, lanes], qm[1, rows, lanes] = head_lanes(part(0) * bf(HD**-0.5))
            ks[rows, lanes] = part(1)
            vs[rows, lanes] = part(2)
            kt[lanes, rows] = part(1).T
            grad = do[:, lanes]
            dom[0, rows, lanes], dom[1, rows, lanes] = head_lanes(grad)
            prod = (grad.astype(f32) * o[:, lanes].astype(f32)).T
            for e in range(2):
                dlt[2 * g + e : 2 * g + e + 1, rows] = jnp.sum(prod[e * HD : (e + 1) * HD], axis=0, keepdims=True)
    dks[...] = jnp.zeros_like(dks)
    dvs[...] = jnp.zeros_like(dvs)

    def qblock(i, _):
        at = pl.multiple_of(i * QB, QB)
        qr = pl.ds(at, QB)
        srow = st_ref[:, qr]
        dqs[...] = jnp.zeros_like(dqs)

        def step(masked, j, carry):
            kat = pl.multiple_of(j * QB, QB)
            kr = pl.ds(kat, QB)
            if masked:
                mask = attn_mask(kat, at, srow)
            scores, softs, grads = [], [], []
            for h in range(heads):
                lanes = lanes_of(h // 2)
                one = lax.dot_general(ks[kr, lanes], qm[h % 2, qr, lanes], NT, preferred_element_type=f32)
                back = lax.dot_general(vs[kr, lanes], dom[h % 2, qr, lanes], NT, preferred_element_type=f32)
                scores.append((jnp.where(mask, one, NEG) if masked else one, back))
            for h in range(heads):
                soft = jnp.exp(scores[h][0] - lse_ref[h : h + 1, qr])
                grads.append((soft * (scores[h][1] - dlt[h : h + 1, qr])).astype(bf))
                softs.append(soft.astype(bf))
            for g in range(pairs):
                lanes = lanes_of(g)
                both = lambda ref: jnp.concatenate([ref[0, qr, lanes], ref[1, qr, lanes]], axis=0)
                two = slice(2 * g, 2 * g + 2)
                dvs[kr, lanes] += jnp.dot(jnp.concatenate(softs[two], axis=1), both(dom), preferred_element_type=f32)
                dks[kr, lanes] += jnp.dot(jnp.concatenate(grads[two], axis=1), both(qm), preferred_element_type=f32)
                for h in (2 * g, 2 * g + 1):
                    sub = slice(h * HD, (h + 1) * HD)
                    dqs[sub] += jnp.dot(kt[sub, kr], grads[h], preferred_element_type=f32)
            return carry

        over_blocks(bounds, i, step, 0)
        qm[0, qr] = (dqs[...] * (HD**-0.5)).T.astype(bf)
        return 0

    lax.fori_loop(0, nb, qblock, 0)
    for dst, base in ((dkeep, c * half), (dsend, (1 - c) * half)):
        rows = pl.ds(pl.multiple_of(base, half), half)
        for g in range(pairs):
            for k, value in enumerate((qm[0, rows, lanes_of(g)], dks[rows, lanes_of(g)], dvs[rows, lanes_of(g)])):
                dst[:, (3 * g + k) * 128 : (3 * g + k + 1) * 128] = value.astype(bf)


def attn_bwd(own, recv, do_own, do_recv, o_own, o_recv, starts, lse, info):
    half, cols = own.shape[0], own.shape[1] // 3
    n = 2 * half
    return pl.pallas_call(
        bwd_kernel,
        in_specs=[SM, SM] + [VM] * 8,
        out_specs=[VM] * 2,
        scratch_shapes=[
            pltpu.VMEM((2, n, cols), bf), pltpu.VMEM((n, cols), bf), pltpu.VMEM((n, cols), bf), pltpu.VMEM((cols, n), bf),
            pltpu.VMEM((2, n, cols), bf), pltpu.VMEM((cols // HD, n), f32), pltpu.VMEM((cols, QB), f32),
            pltpu.VMEM((n, cols), f32), pltpu.VMEM((n, cols), f32)],
        out_shape=[like((half, 3 * cols), bf)] * 2,
        cost_estimate=pl.CostEstimate(flops=n * n, bytes_accessed=n * 128, transcendentals=0),
        compiler_params=pltpu.CompilerParams(vmem_limit_bytes=56 << 20),
    )(info, starts, own, recv, do_own, do_recv, o_own, o_recv, starts, lse)


def dot(left, right, dims=(((1,), (0,)), ((), ()))):
    return lax.dot_general(left, right, dims, preferred_element_type=f32)


def exchange(value, bit, dp_size):
    if bit:
        return lax.ppermute(value, "dp", [(i, i ^ bit) for i in range(dp_size)])
    return lax.ppermute(value, "tensor", [(0, 1), (1, 0)])


def flip(index, bits):
    for bit in bits:
        index = index + bit * (1 - 2 * ((index // bit) % 2))
    return index

def far_groups(dp_size):
    far = [1 << k for k in range(dp_size.bit_length() - 2, 1, -1)]
    return [tuple(far[k : k + 2]) for k in range(0, len(far), 2)]

def group_moves(group):
    if len(group) == 1:
        return [(1, group)]
    return [(1, group[:1]), (2, group[1:]), (3, group)]

def chunks_of(cols, which, count, until=None):
    tiles = cols // 128
    cuts = [128 * ((tiles * k) // count) for k in range(count + 1)]
    arrays = range(which, until + 1) if until else (which,)
    return tuple(
        (array, low, high - low, 128 * ((high - low) // 256 + (high - low) // 128 % 2))
        for low, high in zip(cuts, cuts[1:]) for array in arrays)


def head_kernel(groups, chunks, tokens, seg, *refs):
    shards, x_out, seg_out, outs, nears, (send_sem, recv_sem, local_sem) = refs[:4], refs[4], refs[5], refs[6:10], refs[10:12], refs[12:]
    dp, t = lax.axis_index("dp"), lax.axis_index("tensor")
    core = dp % 2
    away = core + t - 2 * core * t
    near = {1: (flip(dp, (1,)), t), 2: (flip(dp, (2,)), t), 0: (dp, 1 - t)}
    distant = [bits for group in groups for _, bits in group_moves(group)]
    swap = (dp - core + t, core)
    barrier = pltpu.get_barrier_semaphore()
    for device in list(near.values()) + [(flip(dp, bits), t) for bits in distant]:
        pl.semaphore_signal(barrier, inc=1, device_id=device, device_id_type=MESH_ID)

    @pl.when(away == 1)
    def _():
        pl.semaphore_signal(barrier, inc=1, device_id=swap, device_id_type=MESH_ID)

    local = [
        pltpu.make_async_copy(shards[k], outs[k].at[away, 0] if k < 2 else outs[k].at[0], local_sem.at[k]) for k in range(4)]
    for copy in local:
        copy.start()
    pl.semaphore_wait(barrier, len(near) + len(distant) + away)
    count = [0]

    def remote(src, dst, device):
        slot = count[0]
        count[0] += 1
        return pltpu.make_async_remote_copy(
            src_ref=src, dst_ref=dst, send_sem=send_sem.at[slot], recv_sem=recv_sem.at[slot],
            device_id=device, device_id_type=MESH_ID)

    def blocks(ref, index, first, held, low, size):
        return ref.at[index, pl.ds(first, held), :, pl.ds(low, size)]

    plans = []
    for which, low, size, part in chunks:
        shard, out = shards[which], outs[which]
        steps, held = [], 1
        for group in groups:
            moves = []
            for place, bits in group_moves(group):
                src = shard.at[:, pl.ds(low, size)] if held == 1 else blocks(out, away, 0, held, low, size)
                dst = out.at[away, place, :, pl.ds(low, size)] if held == 1 else blocks(out, away, place * held, held, low, size)
                moves.append(remote(src, dst, (flip(dp, bits), t)))
            held *= len(group_moves(group)) + 1
            steps.append(moves)
        a, b = (low, part), (low + part, size - part)
        steps.append([
            remote(blocks(out, away, 0, held, *a), blocks(out, away, 0, held, *a), near[0]),
            remote(blocks(out, away, 0, held, *b), blocks(out, away, held, held, *b), near[2]),
        ])
        steps.append(
            [remote(blocks(out, k, 0, held, *a), blocks(out, k, held, held, *a), near[2]) for k in range(2)]
            + [remote(blocks(out, away, 0, 2 * held, *b), blocks(out, away, 0, 2 * held, *b), near[0])])
        steps.append([
            remote(blocks(out, k, 0, 2 * held, low, size),
                   blocks(out, 1 - k, 2 * held, 2 * held, low, size), near[1]) for k in range(2)])
        plans.append(steps)
    later = []
    held = 1
    for group in groups:
        moves = []
        for place, bits in group_moves(group):
            for shard, out in zip(shards[2:], outs[2:]):
                src = shard if held == 1 else out.at[pl.ds(0, held)]
                dst = out.at[place] if held == 1 else out.at[pl.ds(place * held, held)]
                moves.append(remote(src, dst, (flip(dp, bits), t)))
        held *= len(group_moves(group)) + 1
        later.append(moves)
    depth = len(plans[0])
    swap_copy = remote(tokens, x_out, swap)
    seg_copy = remote(seg, seg_out, near[1])
    near_copies = [remote(outs[2], nears[0], near[0]), remote(outs[3], nears[1], near[2])]
    stay_copy = pltpu.make_async_copy(tokens, x_out, local_sem.at[4])
    waited = set()

    def advance(number, phase):
        if number >= len(plans):
            return
        if phase > 0:
            for move in plans[number][phase - 1]:
                move.wait_recv()
        if phase == 1 and chunks[number][0] not in waited:
            waited.add(chunks[number][0])
            local[chunks[number][0]].wait()
        if phase < depth:
            for move in plans[number][phase]:
                move.start()

    advance(0, 0)
    seg_copy.start()

    @pl.when(away == 1)
    def _():
        swap_copy.start()

    @pl.when(away == 0)
    def _():
        stay_copy.start()

    far = len(groups)
    for number in range(len(plans)):
        if number == 0:
            for phase in range(1, far + 1):
                advance(0, phase)
            for k in range(1, len(plans)):
                advance(k, 0)
            for move in later[0]:
                move.start()
        advance(number, far + 1)
        for phase in range(1, far + 1):
            advance(number + 1, phase)
        advance(number, far + 2)
    for which in (2, 3):
        waited.add(which)
        local[which].wait()
    for k, moves in enumerate(later):
        for move in moves:
            if k > 0:
                move.start()
        for move in moves:
            move.wait()
    for copy in near_copies:
        copy.start()
    for number in range(len(plans)):
        advance(number, depth)

    @pl.when(away == 1)
    def _():
        swap_copy.wait()

    @pl.when(away == 0)
    def _():
        stay_copy.wait()

    seg_copy.wait()
    for which in sorted(set(range(4)) - waited):
        local[which].wait()
    for copy in near_copies:
        copy.wait()
    for steps in plans:
        for moves in steps:
            for move in moves:
                move.wait_send()


def head(dp_size, tokens, seg, shards, chunks):
    groups = far_groups(dp_size)
    partners = sum(len(group_moves(g)) for g in groups)
    slots = len(chunks) * (partners + 7) + 2 * partners + 4
    shapes = [(2, dp_size)] * 2 + [(dp_size // 4,)] * 4
    return pl.pallas_call(
        functools.partial(head_kernel, groups, chunks),
        in_specs=[VM] * 6,
        out_specs=[ANY] * 8,
        out_shape=[jax.ShapeDtypeStruct(a.shape, a.dtype) for a in (tokens, seg)]
        + [jax.ShapeDtypeStruct(lead + s.shape, s.dtype) for lead, s in zip(shapes, tuple(shards) + tuple(shards[2:]))],
        scratch_shapes=[pltpu.SemaphoreType.DMA((slots,)), pltpu.SemaphoreType.DMA((slots,)), pltpu.SemaphoreType.DMA((5,))],
        compiler_params=pltpu.CompilerParams(collective_id=0, has_side_effects=True),
    )(tokens, seg, *shards)


def tail_kernel(groups, own_lo, own_hi, rest_lo, rest_hi, small_lo, small_hi, feed, total, vecs, feed_total,
                feed_part, feed_got, part, got_core, got_near, got_last, got_far, vec, vec_core, vec_two, vec_one, vec_far, send_sem, recv_sem):
    dp, t = lax.axis_index("dp"), lax.axis_index("tensor")
    core = dp % 2
    away = core + t - 2 * core * t
    near = {1: (flip(dp, (1,)), t), 2: (flip(dp, (2,)), t), 0: (dp, 1 - t)}
    distant = [bits for group in groups for _, bits in group_moves(group)]
    barrier = pltpu.get_barrier_semaphore()
    for device in list(near.values()) + [(flip(dp, bits), t) for bits in distant]:
        pl.semaphore_signal(barrier, inc=1, device_id=device, device_id_type=MESH_ID)

    pl.semaphore_wait(barrier, len(near) + len(distant))
    count = [0]

    def remote(src, dst, device):
        slot = count[0]
        count[0] += 1
        return pltpu.make_async_remote_copy(
            src_ref=src, dst_ref=dst, send_sem=send_sem.at[slot], recv_sem=recv_sem.at[slot],
            device_id=device, device_id_type=MESH_ID)

    half, rows, cols = own_lo.shape
    quarter = half // 2
    chunks = [pl.ds(low, min(384, cols - low)) for low in range(0, cols, 384)]
    to_core = [[
        remote(rest_hi.at[:, :, c], got_core.at[0, :, :, c], near[1]),
        remote(own_hi.at[:, :, c], got_core.at[1, :, :, c], near[1])] for c in chunks]
    to_core[0].append(remote(small_hi, vec_core, near[1]))
    for moves in to_core:
        for move in moves:
            move.start()

    feed_steps = []
    held, used = feed.shape[0], 0
    for number, group in enumerate(reversed(groups)):
        moves = group_moves(group)
        held //= len(moves) + 1
        source, step = feed if number == 0 else feed_part, []
        for place, bits in moves:
            step.append(remote(source.at[pl.ds(place * held, held)], feed_got.at[pl.ds(used, held)], (flip(dp, bits), t)))
            used += held
        feed_steps.append((step, source, held, used - held * len(moves), len(moves)))
    for move in feed_steps[0][0]:
        move.start()

    def add(*terms):
        out = terms[0].astype(f32)
        for term in terms[1:]:
            out = out + term.astype(f32)
        return out.astype(bf)

    upper, lower = pl.ds(quarter, quarter), pl.ds(0, quarter)
    mine, other = away, 1 - away
    last = len(chunks) - 1
    steps, sent = {}, []

    def start(key, moves):
        steps[key] = moves
        sent.extend(moves)
        for move in moves:
            move.start()

    def arrive(key):
        for move in steps[key]:
            move.wait_recv()

    def core_stage(k):
        for move in to_core[k]:
            move.wait_recv()
        c = chunks[k]

        def body(q, _):
            part[0, q, :, c] = add(own_lo[q, :, c], got_core[0, q, :, c])
            part[1, q, :, c] = add(rest_lo[q, :, c], got_core[1, q, :, c])
            if k == 0:
                vec[q] = add(small_lo[q], vec_core[q])
            return 0

        lax.fori_loop(0, half, body, 0)
        if k % 2 == 1:
            start(("x", k), [remote(part.at[other, :, :, c], got_near.at[0, :, :, c], near[0])])
        else:
            start(("x", k), [
                remote(part.at[g, upper, :, c], got_near.at[g, lower, :, c], near[2]) for g in range(2)]
                + ([remote(vec.at[upper], vec_two, near[2])] if k == 0 else []))

    def x_stage(k):
        arrive(("x", k))
        c = chunks[k]

        def body(q, _):
            if k % 2 == 1:
                part[mine, q, :, c] = add(part[mine, q, :, c], got_near[0, q, :, c])
                return 0
            for g in range(2):
                part[g, q, :, c] = add(part[g, q, :, c], got_near[g, q, :, c])
            if k == 0:
                vec[q] = add(vec[q], vec_two[q])
            return 0

        lax.fori_loop(0, half if k % 2 == 1 else quarter, body, 0)
        if k % 2 == 1:
            start(("y", k), [remote(part.at[mine, upper, :, c], got_last.at[:, :, c], near[2])])
        else:
            start(("y", k), [remote(part.at[other, lower, :, c], got_last.at[:, :, c], near[0])]
                  + ([remote(vec.at[lower], vec_one, near[0])] if k == 0 else []))

    def far_moves(number, k):
        held, used = quarter, 0
        for index, group in enumerate(reversed(groups)):
            moves = group_moves(group)
            held //= len(moves) + 1
            if index == number:
                out = []
                for m, (place, bits) in enumerate(moves):
                    device, c = (flip(dp, bits), t), chunks[k]
                    out.append(remote(part.at[mine, pl.ds(place * held, held), :, c], got_far.at[pl.ds(used + m * held, held), :, c], device))
                    if k == 0:
                        out.append(remote(vec_one.at[pl.ds(place * held, held)], vec_far.at[pl.ds(used + m * held, held)], device))
                return out, held, used, len(moves)
            used += held * len(moves)

    def y_stage(k):
        arrive(("y", k))
        c = chunks[k]

        def body(q, _):
            part[mine, q, :, c] = add(part[mine, q, :, c], got_last[q, :, c])
            if k == 0:
                vec_one[q] = add(vec[q], vec_one[q])
            return 0

        lax.fori_loop(0, quarter, body, 0)
        start(("z", 0, k), far_moves(0, k)[0])

    far_shape = []
    held, used = quarter, 0
    for group in reversed(groups):
        moves = len(group_moves(group))
        held //= moves + 1
        far_shape.append((held, used, moves))
        used += held * moves

    def z_stage(number, k):
        arrive(("z", number, k))
        c = chunks[k]
        held, base, moves = far_shape[number]

        def body(q, _):
            part[mine, q, :, c] = add(part[mine, q, :, c], *[got_far[base + m * held + q, :, c] for m in range(moves)])
            if k == 0:
                vec_one[q] = add(vec_one[q], *[vec_far[base + m * held + q] for m in range(moves)])
            return 0

        lax.fori_loop(0, held, body, 0)
        if number + 1 < len(groups):
            start(("z", number + 1, k), far_moves(number + 1, k)[0])

    for k in range(last + 1):
        core_stage(k)
    for k in range(last + 1):
        x_stage(k)
        if k > 0:
            y_stage(k - 1)
    y_stage(last)
    for number in range(len(groups)):
        for k in range(last + 1):
            z_stage(number, k)
    to_far = []
    for number, (step, source, held, base, moves) in enumerate(feed_steps):
        if number > 0:
            for move in step:
                move.start()
        for move in step:
            move.wait_recv()

        def sum_feed(k, _, source=source, held=held, base=base, moves=moves):
            feed_part[k] = add(source[k], *[feed_got[base + m * held + k] for m in range(moves)])
            return 0

        if number + 1 < len(feed_steps):
            lax.fori_loop(0, held, sum_feed, 0)
        else:
            out = source[0].astype(f32)
            for m in range(moves):
                out = out + feed_got[base + m * held].astype(f32)
            feed_total[...] = out
        to_far += step
    total[...] = part[mine, 0].astype(f32)
    vecs[...] = vec_one[0].astype(f32)

    for move in sum(to_core, []) + sent + to_far:
        move.wait_send()


def tail(dp_size, own, rest, small, feed):
    groups = far_groups(dp_size)
    half, rows, cols = own[0].shape
    quarter = half // 2
    wide = small[0].shape[2]
    partners = sum(len(group_moves(g)) for g in groups)
    slots = (-(-cols // 384)) * (5 + partners) + 3 + 2 * partners
    return pl.pallas_call(
        functools.partial(tail_kernel, groups),
        in_specs=[VM] * 7,
        out_specs=[VM, VM, VM],
        out_shape=[
            jax.ShapeDtypeStruct((rows, cols), f32),
            jax.ShapeDtypeStruct((rows, wide), f32), jax.ShapeDtypeStruct(feed.shape[1:], f32)],
        scratch_shapes=[
            pltpu.VMEM(feed.shape, bf), pltpu.VMEM(feed.shape, bf),
            pltpu.VMEM((2, half, rows, cols), bf), pltpu.VMEM((2, half, rows, cols), bf), pltpu.VMEM((2, half, rows, cols), bf),
            pltpu.VMEM((quarter, rows, cols), bf), pltpu.VMEM((quarter, rows, cols), bf),
            pltpu.VMEM((half, rows, wide), bf), pltpu.VMEM((half, rows, wide), bf), pltpu.VMEM((quarter, rows, wide), bf),
            pltpu.VMEM((quarter, rows, wide), bf), pltpu.VMEM((quarter, rows, wide), bf),
            pltpu.SemaphoreType.DMA((slots,)), pltpu.SemaphoreType.DMA((slots,))],
        compiler_params=pltpu.CompilerParams(collective_id=1, has_side_effects=True, vmem_limit_bytes=48 << 20),
    )(*own, *rest, *small, feed)


def add_low(*terms):
    out = terms[0].astype(f32)
    for term in terms[1:]:
        out = out + term.astype(f32)
    return out.astype(bf)


def order_matrix(owner, rows, width):
    place = lax.broadcasted_iota(jnp.int32, (1, width), 1)
    block = place // rows
    count = width // rows
    natural = place % rows
    for k, bit in enumerate([1 << b for b in range(count.bit_length() - 2, 1, -1)] + [2, 1]):
        on, base = (block // (1 << k)) % 2, (owner // bit) % 2
        natural = natural + (on + base - 2 * on * base) * (bit * rows)
    return (lax.broadcasted_iota(jnp.int32, (width, width), 0) == natural).astype(f32).astype(bf)


def norm_parts(values):
    centered = values - jnp.mean(values, axis=-1, keepdims=True)
    inverse = lax.rsqrt(jnp.mean(centered * centered, axis=-1, keepdims=True) + EPSILON)
    return centered * inverse, inverse


def norm_back(hat, inverse, gain, grad):
    scaled = grad * gain
    return inverse * (
        scaled - jnp.mean(scaled, axis=-1, keepdims=True) - hat * jnp.mean(scaled * hat, axis=-1, keepdims=True))


def over_rows(total, body, first=0):
    def step(k, _):
        body(pl.ds(pl.multiple_of(first + k * ROWS, ROWS), ROWS))
        return 0

    lax.fori_loop(0, total // ROWS, step, 0)


def column_sum(ref, row, values):
    ref[row : row + 1] += jnp.sum(values, axis=0, keepdims=True)


def bias_row(vec_nat, group, cols):
    lanes = pl.ds(pl.multiple_of(group * cols, 128), cols)
    q, v = vec_nat[6:7, lanes], vec_nat[7:8, lanes]
    parts = []
    for g in range(cols // 128):
        part = slice(g * 128, (g + 1) * 128)
        parts += [q[:, part], jnp.zeros((1, 128), f32), v[:, part]]
    return jnp.concatenate(parts, axis=1)


def fan_matrix(fan):
    row = lax.broadcasted_iota(jnp.int32, (128 * fan, 1), 0)
    unit = lax.broadcasted_iota(jnp.int32, (128 * fan, 128 * fan), 1)
    return (unit == (row % 128) * fan + row // 128).astype(f32).astype(bf)


def first_kernel(rows, fan, tokens, packs, weights, seg, seg_other, x_out, n1_out, own, recv, vec_rel, fc_bias, starts,
                 tok, pack, weight, send, vec_nat, order, fan_rows, send_sem, recv_sem, local_sem):
    dp, t = lax.axis_index("dp"), lax.axis_index("tensor")
    core = dp % 2
    away = core + t - 2 * core * t
    total, width = tok.shape
    cols = weight.shape[2] // 3
    partner = (flip(dp, (1,)), t)
    barrier = pltpu.get_barrier_semaphore()
    pl.semaphore_signal(barrier, inc=1, device_id=partner, device_id_type=MESH_ID)
    loads = [
        pltpu.make_async_copy(src, dst, local_sem.at[k])
        for k, (src, dst) in enumerate(((packs.at[0], pack), (tokens, tok), (weights.at[1], weight.at[1]), (weights.at[0], weight.at[0])))]
    for load in loads:
        load.start()
    order[...] = order_matrix(dp, rows, width)
    loads[0].wait()
    small = pack[:, cols:].astype(f32).T[:VECS]
    vec_rel[...] = small
    vec_nat[...] = lax.dot_general(small.astype(bf), order[...], NT, preferred_element_type=f32)
    send_bias, own_bias = bias_row(vec_nat, 1 - core, cols), bias_row(vec_nat, core, cols)
    for load in loads[1:3]:
        load.wait()
    pl.semaphore_wait(barrier, 1)
    parts, size = 2, total // 2
    copies = [
        pltpu.make_async_remote_copy(
            src_ref=send.at[pl.ds(k * size, size)], dst_ref=recv.at[pl.ds(k * size, size)], send_sem=send_sem.at[k],
            recv_sem=recv_sem.at[k], device_id=partner, device_id_type=MESH_ID)
        for k in range(parts)]

    def first(at):
        x = jnp.dot(tok[at], order[...], preferred_element_type=f32)
        hat, _ = norm_parts(x)
        n1 = (hat * vec_rel[0:1] + vec_rel[1:2]).astype(bf)
        x_out[at] = x.astype(bf)
        n1_out[at] = n1
        send[at] = (jnp.dot(n1, weight[1], preferred_element_type=f32) + send_bias).astype(bf)

    def second(at):
        own[at] = (jnp.dot(n1_out[at], weight[0], preferred_element_type=f32) + own_bias).astype(bf)

    for k in range(parts):
        over_rows(size, first, k * size)
        copies[k].start()
    loads[3].wait()
    over_rows(total, second)

    count = width // 128
    fan_rows[...] = jnp.zeros_like(fan_rows)
    for k in range(count):
        for m in range(fan):
            fan_rows[k : k + 1, m * 128 : (m + 1) * 128] = vec_nat[8 + m : 9 + m, k * 128 : (k + 1) * 128]
    bias = jnp.dot(fan_rows[...].astype(bf), fan_matrix(fan), preferred_element_type=f32)
    for k in range(count):
        fc_bias[:, k * 128 * fan : (k + 1) * 128 * fan] = bias[k : k + 1]
    docs = jnp.where(away == 0, seg[...], seg_other[...]).astype(f32)
    begin = jnp.zeros_like(docs)
    for d in range(1, 16):
        before = jnp.sum(jnp.where(docs < d, 1.0, 0.0), axis=1, keepdims=True)
        begin = jnp.where(docs == d, before, begin)
    starts[...] = begin.astype(jnp.int32)
    for copy in copies:
        copy.wait()


def picked(array, index):
    return pl.BlockSpec((1,) + array.shape[1:], lambda k, s: (index, 0, 0))


def whole(array):
    return pl.BlockSpec(array.shape, lambda k, s: (0,) * len(array.shape))


def like(shape, dtype):
    return jax.ShapeDtypeStruct(shape, dtype)


def by_rows(kernel, info, inputs, specs, outs, scratch=(), limit=60):
    total = inputs[0].shape[0]

    def spec(array, given=None):
        if given is not None:
            return given
        if array.shape[0] == total:
            return pl.BlockSpec((ROWS,) + array.shape[1:], lambda k, s: (k, 0))
        return whole(array)

    return pl.pallas_call(
        kernel,
        grid_spec=pltpu.PrefetchScalarGridSpec(
            num_scalar_prefetch=1, grid=(total // ROWS,), in_specs=[spec(a, g) for a, g in zip(inputs, specs)],
            out_specs=[spec(o) for o in outs], scratch_shapes=list(scratch)),
        out_shape=outs,
        cost_estimate=pl.CostEstimate(flops=1 << 22, bytes_accessed=1 << 18, transcendentals=0),
        compiler_params=pltpu.CompilerParams(vmem_limit_bytes=limit << 20),
    )(info, *inputs)


def project_first(rows, fan, tokens, packs, weights, seg, seg_other):
    n, width = tokens.shape
    qkv = like((n, weights.shape[2]), bf)
    return pl.pallas_call(
        functools.partial(first_kernel, rows, fan),
        in_specs=[ANY, ANY, ANY, VM, VM],
        out_specs=[VM, VM, VM, ANY, VM, VM, VM],
        out_shape=[
            like((n, width), bf), like((n, width), bf), qkv, qkv, like((VECS, width), f32), like((1, width * fan), f32),
            like(seg.shape, jnp.int32)],
        scratch_shapes=[
            pltpu.VMEM((n, width), bf), pltpu.VMEM(packs.shape[1:], bf), pltpu.VMEM(weights.shape, bf), pltpu.VMEM(qkv.shape, bf),
            pltpu.VMEM((VECS, width), f32), pltpu.VMEM((width, width), bf), pltpu.VMEM((8, 128 * fan), f32),
            pltpu.SemaphoreType.DMA((2,)), pltpu.SemaphoreType.DMA((2,)), pltpu.SemaphoreType.DMA((4,))],
        compiler_params=pltpu.CompilerParams(collective_id=3, has_side_effects=True, vmem_limit_bytes=60 << 20),
    )(tokens, packs, weights, seg, seg_other)


def middle_kernel(rows, x, o_own, o_send, cot, cot_recv, packs, vec_rel, fc00, fc01, fc10, fc11, pr0, pr1,
                  middle, n2, cot_rel, d_mlp, o_recv, fc_got, pr_got, order, send_sem, recv_sem):
    dp, t = lax.axis_index("dp"), lax.axis_index("tensor")
    core = dp % 2
    away = core + t - 2 * core * t
    partner = (flip(dp, (1,)), t)
    barrier = pltpu.get_barrier_semaphore()
    pl.semaphore_signal(barrier, inc=1, device_id=partner, device_id_type=MESH_ID)
    pl.semaphore_wait(barrier, 1)
    size = fc00.shape[0]
    copies = [
        pltpu.make_async_remote_copy(
            src_ref=src, dst_ref=dst, send_sem=send_sem.at[k], recv_sem=recv_sem.at[k], device_id=partner, device_id_type=MESH_ID)
        for k, (src, dst) in enumerate((
            (o_send, o_recv), (fc00, fc_got.at[0, pl.ds(0, size)]), (fc01, fc_got.at[0, pl.ds(size, size)]), (pr0, pr_got.at[0]),
            (fc10, fc_got.at[1, pl.ds(0, size)]), (fc11, fc_got.at[1, pl.ds(size, size)]), (pr1, pr_got.at[1])))]
    for copy in copies:
        copy.start()
    order[...] = order_matrix(dp, rows, x.shape[1])
    cols = o_own.shape[1]

    def cot_rows(at):
        grad = jnp.dot(jnp.where(away == 0, cot[at], cot_recv[at]), order[...], preferred_element_type=f32)
        cot_rel[at] = grad.astype(bf)
        d_mlp[at] = (BRANCH_SCALE * grad).astype(bf)

    over_rows(x.shape[0], cot_rows)
    copies[0].wait_recv()

    def body(at):
        branch = lax.dot_general(o_own[at], packs[0, :, :cols], NT, preferred_element_type=f32)
        branch = branch + lax.dot_general(o_recv[at], packs[1, :, :cols], NT, preferred_element_type=f32)
        mid = x[at].astype(f32) + BRANCH_SCALE * (branch + vec_rel[2:3])
        middle[at] = mid
        hat, _ = norm_parts(mid)
        n2[at] = (hat * vec_rel[3:4] + vec_rel[4:5]).astype(bf)

    over_rows(x.shape[0], body)
    for copy in copies[1:]:
        copy.wait_recv()
    for copy in copies:
        copy.wait_send()


def middle_part(rows, x, o_own, o_send, cot, cot_recv, packs, vec_rel, fc_parts, proj_parts):
    shape, half = x.shape, x.shape[1] // 2
    hidden = proj_parts[0].shape[1]
    got = like((2, half, hidden), bf)
    return pl.pallas_call(
        functools.partial(middle_kernel, rows),
        in_specs=[VM] * 7 + [HBM] * 6,
        out_specs=[VM] * 5 + [ANY] * 2,
        out_shape=[like(shape, f32), like(shape, bf), like(shape, bf), like(shape, bf), like(o_send.shape, bf), got, got],
        scratch_shapes=[
            pltpu.VMEM((shape[1], shape[1]), bf), pltpu.SemaphoreType.DMA((7,)), pltpu.SemaphoreType.DMA((7,))],
        compiler_params=pltpu.CompilerParams(collective_id=2, has_side_effects=True, vmem_limit_bytes=36 << 20),
    )(x, o_own, o_send, cot, cot_recv, packs, vec_rel, *fc_parts[0], *fc_parts[1], *proj_parts)


def after_kernel(rows, info, middle, mlp, back, cot, packs, vec_rel, block_out, d_middle, d_attn, do_own, do_send, sums, order):
    @pl.when(pl.program_id(0) == 0)
    def _():
        order[...] = order_matrix(info[1], rows, middle.shape[1])
        sums[...] = jnp.zeros_like(sums)

    cols = do_own.shape[1]
    mid = middle[...]
    out = (mid + BRANCH_SCALE * (mlp[...] + vec_rel[5:6])).astype(bf)
    block_out[...] = lax.dot_general(out, order[...], NT, preferred_element_type=f32).astype(bf)
    hat, inverse = norm_parts(mid)
    grad = back[...]
    out_grad = cot[...].astype(f32)
    entire = out_grad + norm_back(hat, inverse, vec_rel[3:4], grad)
    d_middle[...] = entire
    low = (BRANCH_SCALE * entire).astype(bf)
    d_attn[...] = low
    do_own[...] = jnp.dot(low, packs[0, :, :cols], preferred_element_type=f32).astype(bf)
    do_send[...] = jnp.dot(low, packs[1, :, :cols], preferred_element_type=f32).astype(bf)
    column_sum(sums, 0, BRANCH_SCALE * entire)
    column_sum(sums, 1, grad * hat)
    column_sum(sums, 2, grad)
    column_sum(sums, 3, BRANCH_SCALE * out_grad)


def after_part(info, rows, middle, mlp, back, cot, packs, vec_rel, cols):
    shape = middle.shape
    slim = like((shape[0], cols), bf)
    return by_rows(
        functools.partial(after_kernel, rows), info, (middle, mlp, back, cot, packs, vec_rel), (None,) * 6,
        [like(shape, bf), like(shape, f32), like(shape, bf), slim, slim, like((8, shape[1]), f32)],
        [pltpu.VMEM((shape[1], shape[1]), bf)])


def feed_kernel(info, n2, d_mlp, bias, fc_got, pr_got, fc00, fc01, fc10, fc11, pr0, pr1,
                acc, back, fc_lo, fc_hi, pr_lo, pr_hi, d_bias, n2_t, d_t, w_fc, w_pr, act, d_pre):
    step = pl.program_id(0)
    total, half = n2.shape[0], n2.shape[1] // 2

    @pl.when(step == 0)
    def _():
        acc[...] = jnp.zeros_like(acc)
        back[...] = jnp.zeros_like(back)
        n2_t[...] = n2[...].T
        d_t[...] = d_mlp[...].T

    @pl.when(step < pl.num_programs(0) // 2)
    def _():
        w_fc[: half // 2], w_fc[half // 2 : half], w_pr[:half] = fc00[...], fc01[...], pr0[...]

    @pl.when(step >= pl.num_programs(0) // 2)
    def _():
        w_fc[: half // 2], w_fc[half // 2 : half], w_pr[:half] = fc10[...], fc11[...], pr1[...]

    w_fc[half:], w_pr[half:] = fc_got[0], pr_got[0]
    root = 0.7978845608
    count = total // ROWS
    raw = {}
    grad_sum = jnp.zeros((1, w_fc.shape[1]), f32)

    def products(k):
        at = slice(k * ROWS, (k + 1) * ROWS)
        return (
            jnp.dot(n2[at], w_fc[...], preferred_element_type=f32) + bias[...],
            jnp.dot(d_mlp[at], w_pr[...], preferred_element_type=f32))

    def add_back(k):
        at = slice(k * ROWS, (k + 1) * ROWS)
        acc[at] += lax.dot_general(act[at], w_pr[...], NT, preferred_element_type=f32)
        back[at] += lax.dot_general(d_pre[at], w_fc[...], NT, preferred_element_type=f32)

    raw[0] = products(0)
    for k in range(count):
        at = slice(k * ROWS, (k + 1) * ROWS)
        if k + 1 < count:
            raw[k + 1] = products(k + 1)
        pre, d_act = raw.pop(k)
        square = pre * pre
        inner = jnp.tanh(pre * (root + root * 0.044715 * square))
        gate = 0.5 + 0.5 * inner
        act[at] = (pre * gate).astype(bf)
        slope = gate + pre * (0.5 - 0.5 * inner * inner) * (root + root * 3 * 0.044715 * square)
        grad = d_act * slope
        grad_sum = grad_sum + jnp.sum(grad, axis=0, keepdims=True)
        d_pre[at] = grad.astype(bf)
        if k > 0:
            add_back(k - 1)
    add_back(count - 1)
    d_bias[...] = grad_sum
    for out, left, right, low in (
        (fc_hi, n2_t, d_pre, half), (pr_hi, d_t, act, half), (fc_lo, n2_t, d_pre, 0), (pr_lo, d_t, act, 0)):
        out[0] = jnp.dot(left[low : low + half], right[...], preferred_element_type=f32).astype(bf)


def feed_part(info, n2, d_mlp, bias, fc_got, pr_got, fc_parts, proj_parts):
    (total, width), hidden, half = n2.shape, bias.shape[1] // 2, n2.shape[1] // 2
    steps = hidden // HIDDEN
    fixed = lambda a: pl.BlockSpec(a.shape, lambda k, s: (0,) * len(a.shape), pipeline_mode=pl.Buffered(1))
    early = lambda a: pl.BlockSpec((a.shape[0], HIDDEN), lambda k, s: (0, jnp.minimum(k, steps - 1)))
    late = lambda a: pl.BlockSpec((a.shape[0], HIDDEN), lambda k, s: (0, jnp.maximum(k - steps, 0)))
    two = lambda a: pl.BlockSpec((1, a.shape[1], HIDDEN), lambda k, s: (k // steps, 0, k % steps))
    unit = pl.BlockSpec((1, HIDDEN), lambda k, s: (0, (s[3] + (k // steps) * (1 - 2 * s[3])) * steps + k % steps))
    grad = like((2, half, hidden), bf)
    sums = [like((total, width), f32)] * 2
    return pl.pallas_call(
        feed_kernel,
        grid_spec=pltpu.PrefetchScalarGridSpec(
            num_scalar_prefetch=1,
            grid=(2 * steps,),
            in_specs=[fixed(n2), fixed(d_mlp), unit, two(fc_got), two(pr_got)]
            + [early(a) for a in fc_parts[0]] + [late(a) for a in fc_parts[1]] + [early(proj_parts[0]), late(proj_parts[1])],
            out_specs=[fixed(o) for o in sums] + [two(grad)] * 4 + [unit],
            scratch_shapes=[
                pltpu.VMEM((width, total), bf), pltpu.VMEM((width, total), bf), pltpu.VMEM((width, HIDDEN), bf),
                pltpu.VMEM((width, HIDDEN), bf), pltpu.VMEM((total, HIDDEN), bf), pltpu.VMEM((total, HIDDEN), bf)],
        ),
        out_shape=sums + [grad] * 4 + [like((1, 2 * hidden), f32)],
        cost_estimate=pl.CostEstimate(flops=1 << 22, bytes_accessed=1 << 18, transcendentals=0),
        compiler_params=pltpu.CompilerParams(vmem_limit_bytes=46 << 20),
    )(info, n2, d_mlp, bias, fc_got, pr_got, *fc_parts[0], *fc_parts[1], *proj_parts)


def weight_kernel(n1, d_attn, d_qkv, o, lo, hi, left_t):
    step, half = pl.program_id(0), left_t.shape[0] // 2

    @pl.when(step == 0)
    def _():
        left_t[...] = n1[...].T

    def products(right):
        for out, low in ((hi, half), (lo, 0)):
            out[...] = jnp.dot(left_t[low : low + half], right[...], preferred_element_type=f32).astype(bf)

    @pl.when(step < pl.num_programs(0) - 1)
    def _():
        products(d_qkv)

    @pl.when(step == pl.num_programs(0) - 1)
    def _():
        left_t[...] = d_attn[...].T
        products(o)


def weight_part(n1, d_attn, d_qkv, o):
    (n, width), cols = n1.shape, o.shape[1]
    steps = d_qkv.shape[1] // cols
    fixed = lambda a: pl.BlockSpec(a.shape, lambda k: (0, 0), pipeline_mode=pl.Buffered(1))
    out = pl.BlockSpec((width // 2, cols), lambda k: (0, k))
    grad = like((width // 2, d_qkv.shape[1] + cols), bf)
    return pl.pallas_call(
        weight_kernel,
        grid=(steps + 1,),
        in_specs=[fixed(n1), fixed(d_attn), pl.BlockSpec((n, cols), lambda k: (0, jnp.minimum(k, steps - 1))), fixed(o)],
        out_specs=[out, out],
        out_shape=[grad, grad],
        scratch_shapes=[pltpu.VMEM((width, n), bf)],
        cost_estimate=pl.CostEstimate(flops=1 << 22, bytes_accessed=1 << 18, transcendentals=0),
        compiler_params=pltpu.CompilerParams(vmem_limit_bytes=32 << 20),
    )(n1, d_attn, d_qkv, o)


def token_kernel(rows, fan, info, own, rest, x, d_middle, weights, vec_rel, mid_sums, fc_grad, grad_out, small, own_sums, rest_sums, vecs, nat, order, fan_rows):
    width, cols = x.shape[1], own.shape[1] // 3
    step = pl.program_id(0)

    @pl.when(step == 0)
    def _():
        order[...] = order_matrix(info[1], rows, width)
        for ref in (own_sums, rest_sums, vecs, nat, fan_rows):
            ref[...] = jnp.zeros_like(ref)

    grad = lax.dot_general(own[...], weights[0], NT, preferred_element_type=f32)
    grad = grad + lax.dot_general(rest[...], weights[1], NT, preferred_element_type=f32)
    hat, inverse = norm_parts(x[...].astype(f32))
    low = (d_middle[...] + norm_back(hat, inverse, vec_rel[0:1], grad)).astype(bf)
    grad_out[...] = lax.dot_general(low, order[...], NT, preferred_element_type=f32).astype(bf)
    column_sum(own_sums, 0, own[...].astype(f32))
    column_sum(rest_sums, 0, rest[...].astype(f32))
    column_sum(vecs, 0, grad * hat)
    column_sum(vecs, 1, grad)

    @pl.when(step == pl.num_programs(0) - 1)
    def _():
        for group, ref in ((info[0], own_sums), (1 - info[0], rest_sums)):
            for row, part_index in ((0, 0), (1, 2)):
                picks = [ref[0:1, (3 * g + part_index) * 128 : (3 * g + part_index + 1) * 128] for g in range(cols // 128)]
                nat[row : row + 1, pl.ds(pl.multiple_of(group * cols, 128), cols)] = jnp.concatenate(picks, axis=1)
        count = width // 128
        for k in range(count):
            fan_rows[k : k + 1] = fc_grad[:, k * 128 * fan : (k + 1) * 128 * fan]
        spread = lax.dot_general(fan_rows[...].astype(bf), fan_matrix(fan), NT, preferred_element_type=f32)
        for k in range(count):
            for m in range(fan):
                nat[2 + m : 3 + m, k * 128 : (k + 1) * 128] = spread[k : k + 1, m * 128 : (m + 1) * 128]
        moved = jnp.dot(nat[...].astype(bf), order[...], preferred_element_type=f32)
        vecs[2:4] = moved[0:2]
        vecs[4:8] = mid_sums[0:4]
        vecs[8 : 8 + fan] = moved[2 : 2 + fan]
        small[...] = vecs[...].T.astype(bf)


def token_part(info, rows, own, rest, x, d_middle, weights, vec_rel, mid_sums, fc_grad):
    n, width = x.shape
    wide, fan = own.shape[1], fc_grad.shape[1] // width
    return by_rows(
        functools.partial(token_kernel, rows, fan), info, (own, rest, x, d_middle, weights, vec_rel, mid_sums, fc_grad), (None,) * 8,
        [like((n, width), bf), like((width, SMALL), bf)],
        [pltpu.VMEM((8, wide), f32), pltpu.VMEM((8, wide), f32), pltpu.VMEM((SMALL, width), f32), pltpu.VMEM((8, width), f32),
         pltpu.VMEM((width, width), bf), pltpu.VMEM((8, 128 * fan), f32)], 32)


def on_device(
    tokens, segment_ids, ln1_gain, ln1_bias, w_qkv, b_qv, w_attn_out, b_attn_out,
    ln2_gain, ln2_bias, w_fc, b_fc, w_proj, b_proj, cotangent,
):
    dp_size = lax.axis_size("dp")
    dp_pos, t_pos = lax.axis_index("dp"), lax.axis_index("tensor")
    core = dp_pos % 2
    rows = ln1_gain.shape[0]
    width = tokens.shape[1]
    cols = w_qkv.shape[2]
    hidden = w_fc.shape[1]
    fan = b_fc.shape[0] // rows
    far = [1 << k for k in range(dp_size.bit_length() - 2, 1, -1)]
    swap = []
    for d in range(dp_size):
        for t in range(2):
            if d % 2 != t:
                swap.append((2 * d + t, 2 * (d - d % 2 + t) + d % 2))
    mine = core == t_pos

    pairs = cols // 128

    def by_pair(parts):
        parts = parts.reshape(-1, 3, pairs, 128)
        return jnp.swapaxes(parts, 1, 2).reshape(-1, 3 * cols)

    def by_part(columns):
        return jnp.swapaxes(columns.reshape(-1, pairs, 3, 128), 1, 2).reshape(-1, 3, cols)

    small = jnp.concatenate([jnp.stack([ln1_gain, ln1_bias, b_attn_out, ln2_gain, ln2_bias, b_proj]), b_qv], axis=0)
    small = jnp.concatenate([small.T, b_fc.reshape(rows, fan)], axis=1)
    small = jnp.pad(small, ((0, 0), (0, SMALL - small.shape[1])))
    out_pack = jnp.concatenate([w_attn_out.T, small], axis=1)
    tokens, seg_other, all_qkv, all_out, fc_far, proj_far, fc_near, proj_near = head(
        dp_size, tokens, segment_ids, (by_pair(w_qkv), out_pack, w_fc, w_proj.T), chunks_of(3 * cols, 0, 2) + chunks_of(cols + SMALL, 1, 1))
    all_qkv, all_out = (a.reshape(2, width, -1) for a in (all_qkv, all_out))
    fc_far, proj_far, fc_near, proj_near = (a.reshape(-1, hidden) for a in (fc_far, proj_far, fc_near, proj_near))
    fc_parts = [[p, exchange(p, 2, dp_size)] for p in (fc_far, fc_near)]
    proj_half = jnp.concatenate([proj_far, proj_near], axis=0)
    proj_parts = [proj_half, exchange(proj_half, 0, dp_size)]

    part = jnp.stack([core, dp_pos, jnp.where(mine, 1, 0), t_pos]).astype(jnp.int32)
    x, n1, qkv_own, qkv_recv, vec_rel, fc_bias, starts = project_first(
        rows, fan, tokens, all_out, all_qkv, segment_ids, seg_other)
    o_own, o_send, lse = attn_fwd(qkv_own, qkv_recv, starts, part)
    cot_sent, _ = lax.optimization_barrier((cotangent, proj_half))
    cot_recv = lax.ppermute(cot_sent, BOTH, swap)
    half = width // 2
    middle, n2, cot, d_mlp, o_recv, fc_got, pr_got = middle_part(
        rows, x, o_own, o_send, cotangent, cot_recv, all_out, vec_rel, fc_parts, proj_parts)
    mlp, back, fc_lo, fc_hi, pr_lo, pr_hi, fc_grad = feed_part(
        part, n2, d_mlp, fc_bias, fc_got, pr_got, fc_parts, proj_parts)
    fc_got, pr_got = exchange(fc_hi, 1, dp_size), exchange(pr_hi, 1, dp_size)
    block_out, d_middle, d_attn, do_own, do_send, mid_sums = after_part(
        part, rows, middle, mlp, back, cot, all_out, vec_rel, cols)
    do_recv = exchange(do_send, 1, dp_size)

    near_size = half // 2
    fc_rest = add_low(fc_lo[1], fc_got[1])
    pr_rest = add_low(pr_lo[:, near_size:], pr_got[:, near_size:])
    last = (qkv_own, qkv_recv, do_own, do_recv, o_own, o_send)
    last, fc_rest, pr_rest = lax.optimization_barrier((last, fc_rest, pr_rest))
    fc_sent = exchange(fc_rest, 0, dp_size)
    pr_sent = exchange(pr_rest, 2, dp_size)
    block_recv = lax.ppermute(block_out, BOTH, swap)
    dq_own, dq_send = attn_bwd(*last, starts, lse, part)
    dq_recv = exchange(dq_send, 1, dp_size)
    dq_own, fc_sent, pr_sent = lax.optimization_barrier((dq_own, fc_sent, pr_sent))
    fc_rest = add_low(fc_lo[0, near_size:], fc_got[0, near_size:], fc_sent[near_size:])
    pr_rest = add_low(pr_lo[1, :near_size], pr_got[1, :near_size], pr_sent[1])
    dq_own, fc_rest, pr_rest = lax.optimization_barrier((dq_own, fc_rest, pr_rest))
    fc_near = exchange(fc_rest, 2, dp_size)
    pr_near = exchange(pr_rest, 0, dp_size)
    own_lo, own_hi = weight_part(n1, d_attn, dq_own, o_own)
    own_lo, dq_recv = lax.optimization_barrier((own_lo, dq_recv))
    grad_tokens, d_small = token_part(part, rows, dq_own, dq_recv, x, d_middle, all_qkv, vec_rel, mid_sums, fc_grad)
    grad_recv = lax.ppermute(grad_tokens, BOTH, swap)
    d_small, fc_near, pr_near = lax.optimization_barrier((d_small, fc_near, pr_near))
    sum_fc = add_low(fc_lo[0, :near_size], fc_got[0, :near_size], fc_sent[:near_size], fc_near)
    sum_proj = add_low(pr_lo[0, :near_size], pr_got[0, :near_size], pr_sent[0], pr_near)
    feed = jnp.concatenate([sum_fc, sum_proj], axis=1).reshape(-1, rows, 2 * hidden)
    dq_recv, d_small, feed = lax.optimization_barrier((dq_recv, d_small, feed))
    rest_lo, rest_hi = weight_part(n1, d_attn, dq_recv, o_recv)
    blocks = lambda arr: arr.reshape(dp_size // 2, rows, -1)
    sum_a, vecs, sum_feed = tail(
        dp_size, (blocks(own_lo), blocks(own_hi)), (blocks(rest_lo), blocks(rest_hi)),
        (blocks(d_small[:half]), blocks(d_small[half:])), feed)
    vecs, block_recv, grad_recv = lax.optimization_barrier((vecs, block_recv, grad_recv))
    block_out = jnp.where(mine, block_out, block_recv)
    grad_tokens = jnp.where(mine, grad_tokens, grad_recv)
    return (
        block_out,
        grad_tokens,
        vecs[:, 0],
        vecs[:, 1],
        by_part(sum_a[:, : 3 * cols]),
        vecs[:, 2:4].T,
        sum_a[:, 3 * cols :].T,
        vecs[:, 4],
        vecs[:, 5],
        vecs[:, 6],
        sum_feed[:, :hidden],
        vecs[:, 8 : 8 + fan].reshape(rows * fan),
        sum_feed[:, hidden:].T,
        vecs[:, 7],
    )


def solution(mesh):
    vec, tok = P("dp"), P(BOTH, None)
    in_specs = (
        tok, P("dp", None), vec, vec, P("dp", None, "tensor"), P(None, "dp"), P("tensor", "dp"),
        vec, vec, vec, P("dp", "tensor"), vec, P("tensor", "dp"), vec, tok,
    )
    out_specs = (
        tok, tok, vec, vec, P("dp", None, "tensor"), P(None, "dp"), P("tensor", "dp"),
        vec, vec, vec, P("dp", "tensor"), vec, P("tensor", "dp"), vec,
    )
    return jax.shard_map(on_device, mesh=mesh, in_specs=in_specs, out_specs=out_specs, check_vma=False)
```

```python
import functools

import jax
import jax.numpy as jnp
from jax import lax
from jax.experimental import pallas as pl
from jax.experimental.pallas import tpu as pltpu
from jax.sharding import PartitionSpec as P

HD = 64
QB = 256
NEG = -1e30
EPSILON = 1e-05
BRANCH_SCALE = 48.0 ** (-0.5)
SMALL = 128
VECS = 16
ROWS = 256
HIDDEN = 768
bf = jnp.bfloat16
f32 = jnp.float32
NT = (((1,), (1,)), ((), ()))
TN = (((0,), (0,)), ((), ()))
BOTH = ("dp", "tensor")
MESH_ID = pl.DeviceIdType.MESH
ANY = pl.BlockSpec(memory_space=pl.ANY)
VM = pl.BlockSpec(memory_space=pltpu.VMEM)
HBM = pl.BlockSpec(memory_space=pltpu.HBM)
SM = pl.BlockSpec(memory_space=pltpu.SMEM)


def attn_mask(kat, at, srow):
    keys = lax.broadcasted_iota(jnp.int32, (QB, QB), 0)
    rows = lax.broadcasted_iota(jnp.int32, (1, QB), 1) + (at - kat)
    return (keys >= srow - kat) & (keys <= rows)


def over_blocks(bounds, i, step, carry):
    low = bounds[0, i * QB] // QB
    mid = jnp.minimum((bounds[0, i * QB + QB - 1] + QB - 1) // QB, i)
    carry = lax.fori_loop(0, mid - low + 1, lambda k, c: step(True, jnp.where(k == 0, i, low + k - 1), c), carry)
    return lax.fori_loop(mid, i, functools.partial(step, False), carry)


def head_lanes(values):
    low = (lax.broadcasted_iota(jnp.int32, (1, values.shape[1]), 1) % 128) < HD
    zero = jnp.zeros((), bf)
    return jnp.where(low, values, zero), jnp.where(low, zero, values)


def fwd_kernel(info, bounds, own, recv, st_ref, okeep, osend, lse_ref, qm, ks, vt, osc, acc):
    half, cols = own.shape[0], own.shape[1] // 3
    n, nb, heads, pairs = 2 * half, 2 * half // QB, cols // HD, cols // 128
    c = info[0]
    for base, src in ((c * half, own), ((1 - c) * half, recv)):
        rows = pl.ds(pl.multiple_of(base, half), half)
        for g in range(pairs):
            lanes = slice(g * 128, (g + 1) * 128)
            part = lambda k: src[:, (3 * g + k) * 128 : (3 * g + k + 1) * 128]
            qm[0, rows, lanes], qm[1, rows, lanes] = head_lanes(part(0) * bf(HD**-0.5))
            ks[rows, lanes] = part(1)
            vt[lanes, rows] = part(2).T

    def qblock(i, _):
        at = pl.multiple_of(i * QB, QB)
        qr = pl.ds(at, QB)
        srow = st_ref[:, qr]
        acc[...] = jnp.zeros_like(acc)

        def step(masked, j, carry):
            kat = pl.multiple_of(j * QB, QB)
            kr = pl.ds(kat, QB)
            if masked:
                mask = attn_mask(kat, at, srow)
            scores, mixed = [], []
            for h in range(heads):
                lanes = slice(h // 2 * 128, h // 2 * 128 + 128)
                one = lax.dot_general(ks[kr, lanes], qm[h % 2, qr, lanes], NT, preferred_element_type=f32)
                scores.append(jnp.where(mask, one, NEG) if masked else one)
            for h in range(heads):
                top, total = carry[h]
                new = jnp.maximum(top, jnp.max(scores[h], axis=0, keepdims=True))
                weights = jnp.exp(scores[h] - new)
                fade = jnp.exp(top - new)
                total = fade * total + jnp.sum(weights, axis=0, keepdims=True)
                mixed.append((new, total, fade, weights.astype(bf)))
            for h in range(heads):
                sub = slice(h * HD, (h + 1) * HD)
                acc[sub] = mixed[h][2] * acc[sub] + jnp.dot(vt[sub, kr], mixed[h][3], preferred_element_type=f32)
            return tuple(m[:2] for m in mixed)

        carry = over_blocks(bounds, i, step, ((jnp.full((1, QB), NEG, f32), jnp.zeros((1, QB), f32)),) * heads)
        for h, (top, total) in enumerate(carry):
            sub = slice(h * HD, (h + 1) * HD)
            acc[sub] = acc[sub] / total
            lse_ref[h : h + 1, qr] = top + jnp.log(total)
        osc[qr] = acc[...].T.astype(bf)
        return 0

    lax.fori_loop(0, nb, qblock, 0)
    okeep[...] = osc[pl.ds(pl.multiple_of(c * half, half), half)]
    osend[...] = osc[pl.ds(pl.multiple_of((1 - c) * half, half), half)]


def attn_fwd(own, recv, starts, info):
    half, cols = own.shape[0], own.shape[1] // 3
    n = 2 * half
    return pl.pallas_call(
        fwd_kernel,
        in_specs=[SM, SM, VM, VM, VM],
        out_specs=[VM] * 3,
        scratch_shapes=[
            pltpu.VMEM((2, n, cols), bf), pltpu.VMEM((n, cols), bf), pltpu.VMEM((cols, n), bf),
            pltpu.VMEM((n, cols), bf), pltpu.VMEM((cols, QB), f32)],
        out_shape=[jax.ShapeDtypeStruct((half, cols), bf)] * 2 + [jax.ShapeDtypeStruct((cols // HD, n), f32)],
        cost_estimate=pl.CostEstimate(flops=n * n, bytes_accessed=n * 128, transcendentals=0),
        compiler_params=pltpu.CompilerParams(vmem_limit_bytes=30 << 20),
    )(info, starts, own, recv, starts)


def bwd_kernel(info, bounds, own, recv, doo, dor, oo, orr, st_ref, lse_ref, dkeep, dsend, qm, ks, vs, kt, dom, dlt, dqs, dks, dvs):
    half, cols = own.shape[0], own.shape[1] // 3
    n, nb, heads, pairs = 2 * half, 2 * half // QB, cols // HD, cols // 128
    c = info[0]
    lanes_of = lambda g: slice(g * 128, (g + 1) * 128)
    for base, src, do, o in ((c * half, own, doo, oo), ((1 - c) * half, recv, dor, orr)):
        rows = pl.ds(pl.multiple_of(base, half), half)
        for g in range(pairs):
            lanes = lanes_of(g)
            part = lambda k: src[:, (3 * g + k) * 128 : (3 * g + k + 1) * 128]
            qm[0, rows, lanes], qm[1, rows, lanes] = head_lanes(part(0) * bf(HD**-0.5))
            ks[rows, lanes] = part(1)
            vs[rows, lanes] = part(2)
            kt[lanes, rows] = part(1).T
            grad = do[:, lanes]
            dom[0, rows, lanes], dom[1, rows, lanes] = head_lanes(grad)
            prod = (grad.astype(f32) * o[:, lanes].astype(f32)).T
            for e in range(2):
                dlt[2 * g + e : 2 * g + e + 1, rows] = jnp.sum(prod[e * HD : (e + 1) * HD], axis=0, keepdims=True)
    dks[...] = jnp.zeros_like(dks)
    dvs[...] = jnp.zeros_like(dvs)

    def qblock(i, _):
        at = pl.multiple_of(i * QB, QB)
        qr = pl.ds(at, QB)
        srow = st_ref[:, qr]
        dqs[...] = jnp.zeros_like(dqs)

        def step(masked, j, carry):
            kat = pl.multiple_of(j * QB, QB)
            kr = pl.ds(kat, QB)
            if masked:
                mask = attn_mask(kat, at, srow)
            scores, softs, grads = [], [], []
            for h in range(heads):
                lanes = lanes_of(h // 2)
                one = lax.dot_general(ks[kr, lanes], qm[h % 2, qr, lanes], NT, preferred_element_type=f32)
                back = lax.dot_general(vs[kr, lanes], dom[h % 2, qr, lanes], NT, preferred_element_type=f32)
                scores.append((jnp.where(mask, one, NEG) if masked else one, back))
            for h in range(heads):
                soft = jnp.exp(scores[h][0] - lse_ref[h : h + 1, qr])
                grads.append((soft * (scores[h][1] - dlt[h : h + 1, qr])).astype(bf))
                softs.append(soft.astype(bf))
            for g in range(pairs):
                lanes = lanes_of(g)
                both = lambda ref: jnp.concatenate([ref[0, qr, lanes], ref[1, qr, lanes]], axis=0)
                two = slice(2 * g, 2 * g + 2)
                dvs[kr, lanes] += jnp.dot(jnp.concatenate(softs[two], axis=1), both(dom), preferred_element_type=f32)
                dks[kr, lanes] += jnp.dot(jnp.concatenate(grads[two], axis=1), both(qm), preferred_element_type=f32)
                for h in (2 * g, 2 * g + 1):
                    sub = slice(h * HD, (h + 1) * HD)
                    dqs[sub] += jnp.dot(kt[sub, kr], grads[h], preferred_element_type=f32)
            return carry

        over_blocks(bounds, i, step, 0)
        qm[0, qr] = (dqs[...] * (HD**-0.5)).T.astype(bf)
        return 0

    lax.fori_loop(0, nb, qblock, 0)
    for dst, base in ((dkeep, c * half), (dsend, (1 - c) * half)):
        rows = pl.ds(pl.multiple_of(base, half), half)
        for g in range(pairs):
            for k, value in enumerate((qm[0, rows, lanes_of(g)], dks[rows, lanes_of(g)], dvs[rows, lanes_of(g)])):
                dst[:, (3 * g + k) * 128 : (3 * g + k + 1) * 128] = value.astype(bf)


def attn_bwd(own, recv, do_own, do_recv, o_own, o_recv, starts, lse, info):
    half, cols = own.shape[0], own.shape[1] // 3
    n = 2 * half
    return pl.pallas_call(
        bwd_kernel,
        in_specs=[SM, SM] + [VM] * 8,
        out_specs=[VM] * 2,
        scratch_shapes=[
            pltpu.VMEM((2, n, cols), bf), pltpu.VMEM((n, cols), bf), pltpu.VMEM((n, cols), bf), pltpu.VMEM((cols, n), bf),
            pltpu.VMEM((2, n, cols), bf), pltpu.VMEM((cols // HD, n), f32), pltpu.VMEM((cols, QB), f32),
            pltpu.VMEM((n, cols), f32), pltpu.VMEM((n, cols), f32)],
        out_shape=[like((half, 3 * cols), bf)] * 2,
        cost_estimate=pl.CostEstimate(flops=n * n, bytes_accessed=n * 128, transcendentals=0),
        compiler_params=pltpu.CompilerParams(vmem_limit_bytes=56 << 20),
    )(info, starts, own, recv, do_own, do_recv, o_own, o_recv, starts, lse)


def dot(left, right, dims=(((1,), (0,)), ((), ()))):
    return lax.dot_general(left, right, dims, preferred_element_type=f32)


def exchange(value, bit, dp_size):
    if bit:
        return lax.ppermute(value, "dp", [(i, i ^ bit) for i in range(dp_size)])
    return lax.ppermute(value, "tensor", [(0, 1), (1, 0)])


def flip(index, bits):
    for bit in bits:
        index = index + bit * (1 - 2 * ((index // bit) % 2))
    return index

def far_groups(dp_size):
    far = [1 << k for k in range(dp_size.bit_length() - 2, 1, -1)]
    return [tuple(far[k : k + 2]) for k in range(0, len(far), 2)]

def group_moves(group):
    if len(group) == 1:
        return [(1, group)]
    return [(1, group[:1]), (2, group[1:]), (3, group)]

def chunks_of(cols, which, count, until=None):
    tiles = cols // 128
    cuts = [128 * ((tiles * k) // count) for k in range(count + 1)]
    arrays = range(which, until + 1) if until else (which,)
    return tuple(
        (array, low, high - low, 128 * ((high - low) // 256 + (high - low) // 128 % 2))
        for low, high in zip(cuts, cuts[1:]) for array in arrays)


def head_kernel(groups, chunks, tokens, seg, cot, *refs):
    shards, x_out, seg_out, cot_out, outs, (send_sem, recv_sem, local_sem) = refs[:4], refs[4], refs[5], refs[6], refs[7:11], refs[11:]
    dp, t = lax.axis_index("dp"), lax.axis_index("tensor")
    core = dp % 2
    away = core + t - 2 * core * t
    near = {1: (flip(dp, (1,)), t), 2: (flip(dp, (2,)), t), 0: (dp, 1 - t)}
    distant = [bits for group in groups for _, bits in group_moves(group)]
    swap = (dp - core + t, core)
    barrier = pltpu.get_barrier_semaphore()
    for device in list(near.values()) + [(flip(dp, bits), t) for bits in distant]:
        pl.semaphore_signal(barrier, inc=1, device_id=device, device_id_type=MESH_ID)

    @pl.when(away == 1)
    def _():
        pl.semaphore_signal(barrier, inc=1, device_id=swap, device_id_type=MESH_ID)

    local = [
        pltpu.make_async_copy(shards[k], outs[k].at[away, 0] if k < 2 else outs[k].at[0], local_sem.at[k]) for k in range(4)]
    for copy in local:
        copy.start()
    pl.semaphore_wait(barrier, len(near) + len(distant) + away)
    count = [0]

    def remote(src, dst, device):
        slot = count[0]
        count[0] += 1
        return pltpu.make_async_remote_copy(
            src_ref=src, dst_ref=dst, send_sem=send_sem.at[slot], recv_sem=recv_sem.at[slot],
            device_id=device, device_id_type=MESH_ID)

    def blocks(ref, index, first, held, low, size):
        return ref.at[index, pl.ds(first, held), :, pl.ds(low, size)]

    plans = []
    for which, low, size, part in chunks:
        shard, out = shards[which], outs[which]
        steps, held = [], 1
        for group in groups:
            moves = []
            for place, bits in group_moves(group):
                src = shard.at[:, pl.ds(low, size)] if held == 1 else blocks(out, away, 0, held, low, size)
                dst = out.at[away, place, :, pl.ds(low, size)] if held == 1 else blocks(out, away, place * held, held, low, size)
                moves.append(remote(src, dst, (flip(dp, bits), t)))
            held *= len(group_moves(group)) + 1
            steps.append(moves)
        a, b = (low, part), (low + part, size - part)
        steps.append([
            remote(blocks(out, away, 0, held, *a), blocks(out, away, 0, held, *a), near[0]),
            remote(blocks(out, away, 0, held, *b), blocks(out, away, held, held, *b), near[2]),
        ])
        steps.append(
            [remote(blocks(out, k, 0, held, *a), blocks(out, k, held, held, *a), near[2]) for k in range(2)]
            + [remote(blocks(out, away, 0, 2 * held, *b), blocks(out, away, 0, 2 * held, *b), near[0])])
        steps.append([
            remote(blocks(out, k, 0, 2 * held, low, size),
                   blocks(out, 1 - k, 2 * held, 2 * held, low, size), near[1]) for k in range(2)])
        plans.append(steps)
    later = []
    held = 1
    for group in groups:
        moves = []
        for place, bits in group_moves(group):
            for shard, out in zip(shards[2:], outs[2:]):
                src = shard if held == 1 else out.at[pl.ds(0, held)]
                dst = out.at[place] if held == 1 else out.at[pl.ds(place * held, held)]
                moves.append(remote(src, dst, (flip(dp, bits), t)))
        held *= len(group_moves(group)) + 1
        later.append(moves)
    depth = len(plans[0])
    swap_copy = remote(tokens, x_out, swap)
    seg_copy = remote(seg, seg_out, near[1])
    cot_copy = remote(cot, cot_out, swap)
    stay_copy = pltpu.make_async_copy(tokens, x_out, local_sem.at[4])
    waited = set()

    def advance(number, phase):
        if number >= len(plans):
            return
        if phase > 0:
            for move in plans[number][phase - 1]:
                move.wait_recv()
        if phase == 1 and chunks[number][0] not in waited:
            waited.add(chunks[number][0])
            local[chunks[number][0]].wait()
        if phase < depth:
            for move in plans[number][phase]:
                move.start()

    advance(0, 0)
    seg_copy.start()

    @pl.when(away == 1)
    def _():
        swap_copy.start()

    @pl.when(away == 0)
    def _():
        stay_copy.start()

    far = len(groups)
    for number in range(len(plans)):
        if number == 0:
            for phase in range(1, far + 1):
                advance(0, phase)
            for k in range(1, len(plans)):
                advance(k, 0)
            for move in later[0]:
                move.start()
        advance(number, far + 1)
        if number == len(plans) - 1:

            @pl.when(away == 1)
            def _():
                cot_copy.start()

        for phase in range(1, far + 1):
            advance(number + 1, phase)
        advance(number, far + 2)
    for number in range(len(plans)):
        advance(number, depth)

    @pl.when(away == 1)
    def _():
        swap_copy.wait()

    @pl.when(away == 0)
    def _():
        stay_copy.wait()

    seg_copy.wait()

    @pl.when(away == 1)
    def _():
        cot_copy.wait()

    for which in sorted(set(range(4)) - waited):
        local[which].wait()
    for k, moves in enumerate(later):
        if k > 0:
            for move in moves:
                move.start()
        for move in moves:
            move.wait()
    for steps in plans:
        for moves in steps:
            for move in moves:
                move.wait_send()


def head(dp_size, tokens, seg, cot, shards, chunks):
    groups = far_groups(dp_size)
    partners = sum(len(group_moves(g)) for g in groups)
    slots = len(chunks) * (partners + 7) + 2 * partners + 3
    shapes = [(2, dp_size)] * 2 + [(dp_size // 4,)] * 2
    return pl.pallas_call(
        functools.partial(head_kernel, groups, chunks),
        in_specs=[VM] * 2 + [ANY] + [VM] * 4,
        out_specs=[ANY] * 7,
        out_shape=[jax.ShapeDtypeStruct(a.shape, a.dtype) for a in (tokens, seg, cot)]
        + [jax.ShapeDtypeStruct(lead + s.shape, s.dtype) for lead, s in zip(shapes, shards)],
        scratch_shapes=[pltpu.SemaphoreType.DMA((slots,)), pltpu.SemaphoreType.DMA((slots,)), pltpu.SemaphoreType.DMA((5,))],
        compiler_params=pltpu.CompilerParams(collective_id=0, has_side_effects=True),
    )(tokens, seg, cot, *shards)


def tail_kernel(groups, own_lo, own_hi, rest_lo, rest_hi, small_lo, small_hi, feed, total, vecs, feed_total,
                feed_part, feed_got, part, got_core, got_near, got_last, got_far, vec, vec_core, vec_two, vec_one, vec_far, send_sem, recv_sem):
    dp, t = lax.axis_index("dp"), lax.axis_index("tensor")
    core = dp % 2
    away = core + t - 2 * core * t
    near = {1: (flip(dp, (1,)), t), 2: (flip(dp, (2,)), t), 0: (dp, 1 - t)}
    distant = [bits for group in groups for _, bits in group_moves(group)]
    barrier = pltpu.get_barrier_semaphore()
    for device in list(near.values()) + [(flip(dp, bits), t) for bits in distant]:
        pl.semaphore_signal(barrier, inc=1, device_id=device, device_id_type=MESH_ID)

    pl.semaphore_wait(barrier, len(near) + len(distant))
    count = [0]

    def remote(src, dst, device):
        slot = count[0]
        count[0] += 1
        return pltpu.make_async_remote_copy(
            src_ref=src, dst_ref=dst, send_sem=send_sem.at[slot], recv_sem=recv_sem.at[slot],
            device_id=device, device_id_type=MESH_ID)

    half, rows, cols = own_lo.shape
    quarter = half // 2
    chunks = [pl.ds(low, min(384, cols - low)) for low in range(0, cols, 384)]
    to_core = [[
        remote(rest_hi.at[:, :, c], got_core.at[0, :, :, c], near[1]),
        remote(own_hi.at[:, :, c], got_core.at[1, :, :, c], near[1])] for c in chunks]
    to_core[0].append(remote(small_hi, vec_core, near[1]))
    for moves in to_core:
        for move in moves:
            move.start()

    feed_steps = []
    held, used = feed.shape[0], 0
    for number, group in enumerate(reversed(groups)):
        moves = group_moves(group)
        held //= len(moves) + 1
        source, step = feed if number == 0 else feed_part, []
        for place, bits in moves:
            step.append(remote(source.at[pl.ds(place * held, held)], feed_got.at[pl.ds(used, held)], (flip(dp, bits), t)))
            used += held
        feed_steps.append((step, source, held, used - held * len(moves), len(moves)))
    for move in feed_steps[0][0]:
        move.start()

    def add(*terms):
        out = terms[0].astype(f32)
        for term in terms[1:]:
            out = out + term.astype(f32)
        return out.astype(bf)

    upper, lower = pl.ds(quarter, quarter), pl.ds(0, quarter)
    mine, other = away, 1 - away
    last = len(chunks) - 1
    steps, sent = {}, []

    def start(key, moves):
        steps[key] = moves
        sent.extend(moves)
        for move in moves:
            move.start()

    def arrive(key):
        for move in steps[key]:
            move.wait_recv()

    def core_stage(k):
        for move in to_core[k]:
            move.wait_recv()
        c = chunks[k]

        def body(q, _):
            part[0, q, :, c] = add(own_lo[q, :, c], got_core[0, q, :, c])
            part[1, q, :, c] = add(rest_lo[q, :, c], got_core[1, q, :, c])
            if k == 0:
                vec[q] = add(small_lo[q], vec_core[q])
            return 0

        lax.fori_loop(0, half, body, 0)
        if k % 2 == 1:
            start(("x", k), [remote(part.at[other, :, :, c], got_near.at[0, :, :, c], near[0])])
        else:
            start(("x", k), [
                remote(part.at[g, upper, :, c], got_near.at[g, lower, :, c], near[2]) for g in range(2)]
                + ([remote(vec.at[upper], vec_two, near[2])] if k == 0 else []))

    def x_stage(k):
        arrive(("x", k))
        c = chunks[k]

        def body(q, _):
            if k % 2 == 1:
                part[mine, q, :, c] = add(part[mine, q, :, c], got_near[0, q, :, c])
                return 0
            for g in range(2):
                part[g, q, :, c] = add(part[g, q, :, c], got_near[g, q, :, c])
            if k == 0:
                vec[q] = add(vec[q], vec_two[q])
            return 0

        lax.fori_loop(0, half if k % 2 == 1 else quarter, body, 0)
        if k % 2 == 1:
            start(("y", k), [remote(part.at[mine, upper, :, c], got_last.at[:, :, c], near[2])])
        else:
            start(("y", k), [remote(part.at[other, lower, :, c], got_last.at[:, :, c], near[0])]
                  + ([remote(vec.at[lower], vec_one, near[0])] if k == 0 else []))

    def far_moves(number, k):
        held, used = quarter, 0
        for index, group in enumerate(reversed(groups)):
            moves = group_moves(group)
            held //= len(moves) + 1
            if index == number:
                out = []
                for m, (place, bits) in enumerate(moves):
                    device, c = (flip(dp, bits), t), chunks[k]
                    out.append(remote(part.at[mine, pl.ds(place * held, held), :, c], got_far.at[pl.ds(used + m * held, held), :, c], device))
                    if k == 0:
                        out.append(remote(vec_one.at[pl.ds(place * held, held)], vec_far.at[pl.ds(used + m * held, held)], device))
                return out, held, used, len(moves)
            used += held * len(moves)

    def y_stage(k):
        arrive(("y", k))
        c = chunks[k]

        def body(q, _):
            part[mine, q, :, c] = add(part[mine, q, :, c], got_last[q, :, c])
            if k == 0:
                vec_one[q] = add(vec[q], vec_one[q])
            return 0

        lax.fori_loop(0, quarter, body, 0)
        start(("z", 0, k), far_moves(0, k)[0])

    far_shape = []
    held, used = quarter, 0
    for group in reversed(groups):
        moves = len(group_moves(group))
        held //= moves + 1
        far_shape.append((held, used, moves))
        used += held * moves

    def z_stage(number, k):
        arrive(("z", number, k))
        c = chunks[k]
        held, base, moves = far_shape[number]

        def body(q, _):
            part[mine, q, :, c] = add(part[mine, q, :, c], *[got_far[base + m * held + q, :, c] for m in range(moves)])
            if k == 0:
                vec_one[q] = add(vec_one[q], *[vec_far[base + m * held + q] for m in range(moves)])
            return 0

        lax.fori_loop(0, held, body, 0)
        if number + 1 < len(groups):
            start(("z", number + 1, k), far_moves(number + 1, k)[0])

    for k in range(last + 1):
        core_stage(k)
    for k in range(last + 1):
        x_stage(k)
        if k > 0:
            y_stage(k - 1)
    y_stage(last)
    for number in range(len(groups)):
        for k in range(last + 1):
            z_stage(number, k)
    to_far = []
    for number, (step, source, held, base, moves) in enumerate(feed_steps):
        if number > 0:
            for move in step:
                move.start()
        for move in step:
            move.wait_recv()

        def sum_feed(k, _, source=source, held=held, base=base, moves=moves):
            feed_part[k] = add(source[k], *[feed_got[base + m * held + k] for m in range(moves)])
            return 0

        if number + 1 < len(feed_steps):
            lax.fori_loop(0, held, sum_feed, 0)
        else:
            out = source[0].astype(f32)
            for m in range(moves):
                out = out + feed_got[base + m * held].astype(f32)
            feed_total[...] = out
        to_far += step
    total[...] = part[mine, 0].astype(f32)
    vecs[...] = vec_one[0].astype(f32)

    for move in sum(to_core, []) + sent + to_far:
        move.wait_send()


def tail(dp_size, own, rest, small, feed):
    groups = far_groups(dp_size)
    half, rows, cols = own[0].shape
    quarter = half // 2
    wide = small[0].shape[2]
    partners = sum(len(group_moves(g)) for g in groups)
    slots = (-(-cols // 384)) * (5 + partners) + 3 + 2 * partners
    return pl.pallas_call(
        functools.partial(tail_kernel, groups),
        in_specs=[VM] * 7,
        out_specs=[VM, VM, VM],
        out_shape=[
            jax.ShapeDtypeStruct((rows, cols), f32),
            jax.ShapeDtypeStruct((rows, wide), f32), jax.ShapeDtypeStruct(feed.shape[1:], f32)],
        scratch_shapes=[
            pltpu.VMEM(feed.shape, bf), pltpu.VMEM(feed.shape, bf),
            pltpu.VMEM((2, half, rows, cols), bf), pltpu.VMEM((2, half, rows, cols), bf), pltpu.VMEM((2, half, rows, cols), bf),
            pltpu.VMEM((quarter, rows, cols), bf), pltpu.VMEM((quarter, rows, cols), bf),
            pltpu.VMEM((half, rows, wide), bf), pltpu.VMEM((half, rows, wide), bf), pltpu.VMEM((quarter, rows, wide), bf),
            pltpu.VMEM((quarter, rows, wide), bf), pltpu.VMEM((quarter, rows, wide), bf),
            pltpu.SemaphoreType.DMA((slots,)), pltpu.SemaphoreType.DMA((slots,))],
        compiler_params=pltpu.CompilerParams(collective_id=1, has_side_effects=True, vmem_limit_bytes=48 << 20),
    )(*own, *rest, *small, feed)


def add_low(*terms):
    out = terms[0].astype(f32)
    for term in terms[1:]:
        out = out + term.astype(f32)
    return out.astype(bf)


def order_matrix(owner, rows, width):
    place = lax.broadcasted_iota(jnp.int32, (1, width), 1)
    block = place // rows
    count = width // rows
    natural = place % rows
    for k, bit in enumerate([1 << b for b in range(count.bit_length() - 2, 1, -1)] + [2, 1]):
        on, base = (block // (1 << k)) % 2, (owner // bit) % 2
        natural = natural + (on + base - 2 * on * base) * (bit * rows)
    return (lax.broadcasted_iota(jnp.int32, (width, width), 0) == natural).astype(f32).astype(bf)


def norm_parts(values):
    centered = values - jnp.mean(values, axis=-1, keepdims=True)
    inverse = lax.rsqrt(jnp.mean(centered * centered, axis=-1, keepdims=True) + EPSILON)
    return centered * inverse, inverse


def norm_back(hat, inverse, gain, grad):
    scaled = grad * gain
    return inverse * (
        scaled - jnp.mean(scaled, axis=-1, keepdims=True) - hat * jnp.mean(scaled * hat, axis=-1, keepdims=True))


def over_rows(total, body, first=0):
    def step(k, _):
        body(pl.ds(pl.multiple_of(first + k * ROWS, ROWS), ROWS))
        return 0

    lax.fori_loop(0, total // ROWS, step, 0)


def column_sum(ref, row, values):
    ref[row : row + 1] += jnp.sum(values, axis=0, keepdims=True)


def bias_row(vec_nat, group, cols):
    lanes = pl.ds(pl.multiple_of(group * cols, 128), cols)
    q, v = vec_nat[6:7, lanes], vec_nat[7:8, lanes]
    parts = []
    for g in range(cols // 128):
        part = slice(g * 128, (g + 1) * 128)
        parts += [q[:, part], jnp.zeros((1, 128), f32), v[:, part]]
    return jnp.concatenate(parts, axis=1)


def fan_matrix(fan):
    row = lax.broadcasted_iota(jnp.int32, (128 * fan, 1), 0)
    unit = lax.broadcasted_iota(jnp.int32, (128 * fan, 128 * fan), 1)
    return (unit == (row % 128) * fan + row // 128).astype(f32).astype(bf)


def first_kernel(rows, fan, tokens, packs, weights, seg, seg_other, x_out, n1_out, own, recv, vec_rel, fc_bias, starts,
                 tok, pack, weight, send, vec_nat, order, fan_rows, send_sem, recv_sem, local_sem):
    dp, t = lax.axis_index("dp"), lax.axis_index("tensor")
    core = dp % 2
    away = core + t - 2 * core * t
    total, width = tok.shape
    cols = weight.shape[2] // 3
    partner = (flip(dp, (1,)), t)
    barrier = pltpu.get_barrier_semaphore()
    pl.semaphore_signal(barrier, inc=1, device_id=partner, device_id_type=MESH_ID)
    loads = [
        pltpu.make_async_copy(src, dst, local_sem.at[k])
        for k, (src, dst) in enumerate(((packs.at[0], pack), (tokens, tok), (weights.at[1], weight.at[1]), (weights.at[0], weight.at[0])))]
    for load in loads:
        load.start()
    order[...] = order_matrix(dp, rows, width)
    loads[0].wait()
    small = pack[:, cols:].astype(f32).T[:VECS]
    vec_rel[...] = small
    vec_nat[...] = lax.dot_general(small.astype(bf), order[...], NT, preferred_element_type=f32)
    send_bias, own_bias = bias_row(vec_nat, 1 - core, cols), bias_row(vec_nat, core, cols)
    for load in loads[1:3]:
        load.wait()
    pl.semaphore_wait(barrier, 1)
    parts, size = 2, total // 2
    copies = [
        pltpu.make_async_remote_copy(
            src_ref=send.at[pl.ds(k * size, size)], dst_ref=recv.at[pl.ds(k * size, size)], send_sem=send_sem.at[k],
            recv_sem=recv_sem.at[k], device_id=partner, device_id_type=MESH_ID)
        for k in range(parts)]

    def first(at):
        x = jnp.dot(tok[at], order[...], preferred_element_type=f32)
        hat, _ = norm_parts(x)
        n1 = (hat * vec_rel[0:1] + vec_rel[1:2]).astype(bf)
        x_out[at] = x.astype(bf)
        n1_out[at] = n1
        send[at] = (jnp.dot(n1, weight[1], preferred_element_type=f32) + send_bias).astype(bf)

    def second(at):
        own[at] = (jnp.dot(n1_out[at], weight[0], preferred_element_type=f32) + own_bias).astype(bf)

    for k in range(parts):
        over_rows(size, first, k * size)
        copies[k].start()
    loads[3].wait()
    over_rows(total, second)

    count = width // 128
    fan_rows[...] = jnp.zeros_like(fan_rows)
    for k in range(count):
        for m in range(fan):
            fan_rows[k : k + 1, m * 128 : (m + 1) * 128] = vec_nat[8 + m : 9 + m, k * 128 : (k + 1) * 128]
    bias = jnp.dot(fan_rows[...].astype(bf), fan_matrix(fan), preferred_element_type=f32)
    for k in range(count):
        fc_bias[:, k * 128 * fan : (k + 1) * 128 * fan] = bias[k : k + 1]
    docs = jnp.where(away == 0, seg[...], seg_other[...]).astype(f32)
    begin = jnp.zeros_like(docs)
    for d in range(1, 16):
        before = jnp.sum(jnp.where(docs < d, 1.0, 0.0), axis=1, keepdims=True)
        begin = jnp.where(docs == d, before, begin)
    starts[...] = begin.astype(jnp.int32)
    for copy in copies:
        copy.wait()


def picked(array, index):
    return pl.BlockSpec((1,) + array.shape[1:], lambda k, s: (index, 0, 0))


def whole(array):
    return pl.BlockSpec(array.shape, lambda k, s: (0,) * len(array.shape))


def like(shape, dtype):
    return jax.ShapeDtypeStruct(shape, dtype)


def by_rows(kernel, info, inputs, specs, outs, scratch=(), limit=60):
    total = inputs[0].shape[0]

    def spec(array, given=None):
        if given is not None:
            return given
        if array.shape[0] == total:
            return pl.BlockSpec((ROWS,) + array.shape[1:], lambda k, s: (k, 0))
        return whole(array)

    return pl.pallas_call(
        kernel,
        grid_spec=pltpu.PrefetchScalarGridSpec(
            num_scalar_prefetch=1, grid=(total // ROWS,), in_specs=[spec(a, g) for a, g in zip(inputs, specs)],
            out_specs=[spec(o) for o in outs], scratch_shapes=list(scratch)),
        out_shape=outs,
        cost_estimate=pl.CostEstimate(flops=1 << 22, bytes_accessed=1 << 18, transcendentals=0),
        compiler_params=pltpu.CompilerParams(vmem_limit_bytes=limit << 20),
    )(info, *inputs)


def project_first(rows, fan, tokens, packs, weights, seg, seg_other):
    n, width = tokens.shape
    qkv = like((n, weights.shape[2]), bf)
    return pl.pallas_call(
        functools.partial(first_kernel, rows, fan),
        in_specs=[ANY, ANY, ANY, VM, VM],
        out_specs=[VM, VM, VM, ANY, VM, VM, VM],
        out_shape=[
            like((n, width), bf), like((n, width), bf), qkv, qkv, like((VECS, width), f32), like((1, width * fan), f32),
            like(seg.shape, jnp.int32)],
        scratch_shapes=[
            pltpu.VMEM((n, width), bf), pltpu.VMEM(packs.shape[1:], bf), pltpu.VMEM(weights.shape, bf), pltpu.VMEM(qkv.shape, bf),
            pltpu.VMEM((VECS, width), f32), pltpu.VMEM((width, width), bf), pltpu.VMEM((8, 128 * fan), f32),
            pltpu.SemaphoreType.DMA((2,)), pltpu.SemaphoreType.DMA((2,)), pltpu.SemaphoreType.DMA((4,))],
        compiler_params=pltpu.CompilerParams(collective_id=3, has_side_effects=True, vmem_limit_bytes=60 << 20),
    )(tokens, packs, weights, seg, seg_other)


def middle_kernel(rows, x, o_own, o_send, cot, cot_recv, packs, vec_rel, fc00, fc01, fc10, fc11, pr0, pr1,
                  middle, n2, cot_rel, d_mlp, o_recv, fc_got, pr_got, order, send_sem, recv_sem):
    dp, t = lax.axis_index("dp"), lax.axis_index("tensor")
    core = dp % 2
    away = core + t - 2 * core * t
    partner = (flip(dp, (1,)), t)
    barrier = pltpu.get_barrier_semaphore()
    pl.semaphore_signal(barrier, inc=1, device_id=partner, device_id_type=MESH_ID)
    pl.semaphore_wait(barrier, 1)
    size = fc00.shape[0]
    copies = [
        pltpu.make_async_remote_copy(
            src_ref=src, dst_ref=dst, send_sem=send_sem.at[k], recv_sem=recv_sem.at[k], device_id=partner, device_id_type=MESH_ID)
        for k, (src, dst) in enumerate((
            (o_send, o_recv), (fc00, fc_got.at[0, pl.ds(0, size)]), (fc01, fc_got.at[0, pl.ds(size, size)]), (pr0, pr_got.at[0]),
            (fc10, fc_got.at[1, pl.ds(0, size)]), (fc11, fc_got.at[1, pl.ds(size, size)]), (pr1, pr_got.at[1])))]
    for copy in copies:
        copy.start()
    order[...] = order_matrix(dp, rows, x.shape[1])
    cols = o_own.shape[1]

    def cot_rows(at):
        grad = jnp.dot(jnp.where(away == 0, cot[at], cot_recv[at]), order[...], preferred_element_type=f32)
        cot_rel[at] = grad.astype(bf)
        d_mlp[at] = (BRANCH_SCALE * grad).astype(bf)

    over_rows(x.shape[0], cot_rows)
    copies[0].wait_recv()

    def body(at):
        branch = lax.dot_general(o_own[at], packs[0, :, :cols], NT, preferred_element_type=f32)
        branch = branch + lax.dot_general(o_recv[at], packs[1, :, :cols], NT, preferred_element_type=f32)
        mid = x[at].astype(f32) + BRANCH_SCALE * (branch + vec_rel[2:3])
        middle[at] = mid
        hat, _ = norm_parts(mid)
        n2[at] = (hat * vec_rel[3:4] + vec_rel[4:5]).astype(bf)

    over_rows(x.shape[0], body)
    for copy in copies[1:]:
        copy.wait_recv()
    for copy in copies:
        copy.wait_send()


def middle_part(rows, x, o_own, o_send, cot, cot_recv, packs, vec_rel, fc_parts, proj_parts):
    shape, half = x.shape, x.shape[1] // 2
    hidden = proj_parts[0].shape[1]
    got = like((2, half, hidden), bf)
    return pl.pallas_call(
        functools.partial(middle_kernel, rows),
        in_specs=[VM] * 7 + [HBM] * 6,
        out_specs=[VM] * 5 + [ANY] * 2,
        out_shape=[like(shape, f32), like(shape, bf), like(shape, bf), like(shape, bf), like(o_send.shape, bf), got, got],
        scratch_shapes=[
            pltpu.VMEM((shape[1], shape[1]), bf), pltpu.SemaphoreType.DMA((7,)), pltpu.SemaphoreType.DMA((7,))],
        compiler_params=pltpu.CompilerParams(collective_id=2, has_side_effects=True, vmem_limit_bytes=36 << 20),
    )(x, o_own, o_send, cot, cot_recv, packs, vec_rel, *fc_parts[0], *fc_parts[1], *proj_parts)


def after_kernel(rows, info, middle, mlp, back, cot, packs, vec_rel, block_out, d_middle, d_attn, do_own, do_send, sums, order):
    @pl.when(pl.program_id(0) == 0)
    def _():
        order[...] = order_matrix(info[1], rows, middle.shape[1])
        sums[...] = jnp.zeros_like(sums)

    cols = do_own.shape[1]
    mid = middle[...]
    out = (mid + BRANCH_SCALE * (mlp[...] + vec_rel[5:6])).astype(bf)
    block_out[...] = lax.dot_general(out, order[...], NT, preferred_element_type=f32).astype(bf)
    hat, inverse = norm_parts(mid)
    grad = back[...]
    out_grad = cot[...].astype(f32)
    entire = out_grad + norm_back(hat, inverse, vec_rel[3:4], grad)
    d_middle[...] = entire
    low = (BRANCH_SCALE * entire).astype(bf)
    d_attn[...] = low
    do_own[...] = jnp.dot(low, packs[0, :, :cols], preferred_element_type=f32).astype(bf)
    do_send[...] = jnp.dot(low, packs[1, :, :cols], preferred_element_type=f32).astype(bf)
    column_sum(sums, 0, BRANCH_SCALE * entire)
    column_sum(sums, 1, grad * hat)
    column_sum(sums, 2, grad)
    column_sum(sums, 3, BRANCH_SCALE * out_grad)


def after_part(info, rows, middle, mlp, back, cot, packs, vec_rel, cols):
    shape = middle.shape
    slim = like((shape[0], cols), bf)
    return by_rows(
        functools.partial(after_kernel, rows), info, (middle, mlp, back, cot, packs, vec_rel), (None,) * 6,
        [like(shape, bf), like(shape, f32), like(shape, bf), slim, slim, like((8, shape[1]), f32)],
        [pltpu.VMEM((shape[1], shape[1]), bf)])


def feed_kernel(info, n2, d_mlp, bias, fc_got, pr_got, fc00, fc01, fc10, fc11, pr0, pr1,
                acc, back, fc_lo, fc_hi, pr_lo, pr_hi, d_bias, n2_t, d_t, w_fc, w_pr, act, d_pre):
    step = pl.program_id(0)
    total, half = n2.shape[0], n2.shape[1] // 2

    @pl.when(step == 0)
    def _():
        acc[...] = jnp.zeros_like(acc)
        back[...] = jnp.zeros_like(back)
        n2_t[...] = n2[...].T
        d_t[...] = d_mlp[...].T

    @pl.when(step < pl.num_programs(0) // 2)
    def _():
        w_fc[: half // 2], w_fc[half // 2 : half], w_pr[:half] = fc00[...], fc01[...], pr0[...]

    @pl.when(step >= pl.num_programs(0) // 2)
    def _():
        w_fc[: half // 2], w_fc[half // 2 : half], w_pr[:half] = fc10[...], fc11[...], pr1[...]

    w_fc[half:], w_pr[half:] = fc_got[0], pr_got[0]
    root = 0.7978845608
    count = total // ROWS
    raw = {}
    grad_sum = jnp.zeros((1, w_fc.shape[1]), f32)

    def products(k):
        at = slice(k * ROWS, (k + 1) * ROWS)
        return (
            jnp.dot(n2[at], w_fc[...], preferred_element_type=f32) + bias[...],
            jnp.dot(d_mlp[at], w_pr[...], preferred_element_type=f32))

    def add_back(k):
        at = slice(k * ROWS, (k + 1) * ROWS)
        acc[at] += lax.dot_general(act[at], w_pr[...], NT, preferred_element_type=f32)
        back[at] += lax.dot_general(d_pre[at], w_fc[...], NT, preferred_element_type=f32)

    raw[0] = products(0)
    for k in range(count):
        at = slice(k * ROWS, (k + 1) * ROWS)
        if k + 1 < count:
            raw[k + 1] = products(k + 1)
        pre, d_act = raw.pop(k)
        square = pre * pre
        inner = jnp.tanh(pre * (root + root * 0.044715 * square))
        gate = 0.5 + 0.5 * inner
        act[at] = (pre * gate).astype(bf)
        slope = gate + pre * (0.5 - 0.5 * inner * inner) * (root + root * 3 * 0.044715 * square)
        grad = d_act * slope
        grad_sum = grad_sum + jnp.sum(grad, axis=0, keepdims=True)
        d_pre[at] = grad.astype(bf)
        if k > 0:
            add_back(k - 1)
    add_back(count - 1)
    d_bias[...] = grad_sum
    for out, left, right, low in (
        (fc_hi, n2_t, d_pre, half), (pr_hi, d_t, act, half), (fc_lo, n2_t, d_pre, 0), (pr_lo, d_t, act, 0)):
        out[0] = jnp.dot(left[low : low + half], right[...], preferred_element_type=f32).astype(bf)


def feed_part(info, n2, d_mlp, bias, fc_got, pr_got, fc_parts, proj_parts):
    (total, width), hidden, half = n2.shape, bias.shape[1] // 2, n2.shape[1] // 2
    steps = hidden // HIDDEN
    fixed = lambda a: pl.BlockSpec(a.shape, lambda k, s: (0,) * len(a.shape), pipeline_mode=pl.Buffered(1))
    early = lambda a: pl.BlockSpec((a.shape[0], HIDDEN), lambda k, s: (0, jnp.minimum(k, steps - 1)))
    late = lambda a: pl.BlockSpec((a.shape[0], HIDDEN), lambda k, s: (0, jnp.maximum(k - steps, 0)))
    two = lambda a: pl.BlockSpec((1, a.shape[1], HIDDEN), lambda k, s: (k // steps, 0, k % steps))
    unit = pl.BlockSpec((1, HIDDEN), lambda k, s: (0, (s[3] + (k // steps) * (1 - 2 * s[3])) * steps + k % steps))
    grad = like((2, half, hidden), bf)
    sums = [like((total, width), f32)] * 2
    return pl.pallas_call(
        feed_kernel,
        grid_spec=pltpu.PrefetchScalarGridSpec(
            num_scalar_prefetch=1,
            grid=(2 * steps,),
            in_specs=[fixed(n2), fixed(d_mlp), unit, two(fc_got), two(pr_got)]
            + [early(a) for a in fc_parts[0]] + [late(a) for a in fc_parts[1]] + [early(proj_parts[0]), late(proj_parts[1])],
            out_specs=[fixed(o) for o in sums] + [two(grad)] * 4 + [unit],
            scratch_shapes=[
                pltpu.VMEM((width, total), bf), pltpu.VMEM((width, total), bf), pltpu.VMEM((width, HIDDEN), bf),
                pltpu.VMEM((width, HIDDEN), bf), pltpu.VMEM((total, HIDDEN), bf), pltpu.VMEM((total, HIDDEN), bf)],
        ),
        out_shape=sums + [grad] * 4 + [like((1, 2 * hidden), f32)],
        cost_estimate=pl.CostEstimate(flops=1 << 22, bytes_accessed=1 << 18, transcendentals=0),
        compiler_params=pltpu.CompilerParams(vmem_limit_bytes=46 << 20),
    )(info, n2, d_mlp, bias, fc_got, pr_got, *fc_parts[0], *fc_parts[1], *proj_parts)


def weight_kernel(n1, d_attn, d_qkv, o, lo, hi, left_t):
    step, half = pl.program_id(0), left_t.shape[0] // 2

    @pl.when(step == 0)
    def _():
        left_t[...] = n1[...].T

    def products(right):
        for out, low in ((hi, half), (lo, 0)):
            out[...] = jnp.dot(left_t[low : low + half], right[...], preferred_element_type=f32).astype(bf)

    @pl.when(step < pl.num_programs(0) - 1)
    def _():
        products(d_qkv)

    @pl.when(step == pl.num_programs(0) - 1)
    def _():
        left_t[...] = d_attn[...].T
        products(o)


def weight_part(n1, d_attn, d_qkv, o):
    (n, width), cols = n1.shape, o.shape[1]
    steps = d_qkv.shape[1] // cols
    fixed = lambda a: pl.BlockSpec(a.shape, lambda k: (0, 0), pipeline_mode=pl.Buffered(1))
    out = pl.BlockSpec((width // 2, cols), lambda k: (0, k))
    grad = like((width // 2, d_qkv.shape[1] + cols), bf)
    return pl.pallas_call(
        weight_kernel,
        grid=(steps + 1,),
        in_specs=[fixed(n1), fixed(d_attn), pl.BlockSpec((n, cols), lambda k: (0, jnp.minimum(k, steps - 1))), fixed(o)],
        out_specs=[out, out],
        out_shape=[grad, grad],
        scratch_shapes=[pltpu.VMEM((width, n), bf)],
        cost_estimate=pl.CostEstimate(flops=1 << 22, bytes_accessed=1 << 18, transcendentals=0),
        compiler_params=pltpu.CompilerParams(vmem_limit_bytes=32 << 20),
    )(n1, d_attn, d_qkv, o)


def token_kernel(rows, fan, info, own, rest, x, d_middle, weights, vec_rel, mid_sums, fc_grad, grad_out, small, own_sums, rest_sums, vecs, nat, order, fan_rows):
    width, cols = x.shape[1], own.shape[1] // 3
    step = pl.program_id(0)

    @pl.when(step == 0)
    def _():
        order[...] = order_matrix(info[1], rows, width)
        for ref in (own_sums, rest_sums, vecs, nat, fan_rows):
            ref[...] = jnp.zeros_like(ref)

    grad = lax.dot_general(own[...], weights[0], NT, preferred_element_type=f32)
    grad = grad + lax.dot_general(rest[...], weights[1], NT, preferred_element_type=f32)
    hat, inverse = norm_parts(x[...].astype(f32))
    low = (d_middle[...] + norm_back(hat, inverse, vec_rel[0:1], grad)).astype(bf)
    grad_out[...] = lax.dot_general(low, order[...], NT, preferred_element_type=f32).astype(bf)
    column_sum(own_sums, 0, own[...].astype(f32))
    column_sum(rest_sums, 0, rest[...].astype(f32))
    column_sum(vecs, 0, grad * hat)
    column_sum(vecs, 1, grad)

    @pl.when(step == pl.num_programs(0) - 1)
    def _():
        for group, ref in ((info[0], own_sums), (1 - info[0], rest_sums)):
            for row, part_index in ((0, 0), (1, 2)):
                picks = [ref[0:1, (3 * g + part_index) * 128 : (3 * g + part_index + 1) * 128] for g in range(cols // 128)]
                nat[row : row + 1, pl.ds(pl.multiple_of(group * cols, 128), cols)] = jnp.concatenate(picks, axis=1)
        count = width // 128
        for k in range(count):
            fan_rows[k : k + 1] = fc_grad[:, k * 128 * fan : (k + 1) * 128 * fan]
        spread = lax.dot_general(fan_rows[...].astype(bf), fan_matrix(fan), NT, preferred_element_type=f32)
        for k in range(count):
            for m in range(fan):
                nat[2 + m : 3 + m, k * 128 : (k + 1) * 128] = spread[k : k + 1, m * 128 : (m + 1) * 128]
        moved = jnp.dot(nat[...].astype(bf), order[...], preferred_element_type=f32)
        vecs[2:4] = moved[0:2]
        vecs[4:8] = mid_sums[0:4]
        vecs[8 : 8 + fan] = moved[2 : 2 + fan]
        small[...] = vecs[...].T.astype(bf)


def token_part(info, rows, own, rest, x, d_middle, weights, vec_rel, mid_sums, fc_grad):
    n, width = x.shape
    wide, fan = own.shape[1], fc_grad.shape[1] // width
    return by_rows(
        functools.partial(token_kernel, rows, fan), info, (own, rest, x, d_middle, weights, vec_rel, mid_sums, fc_grad), (None,) * 8,
        [like((n, width), bf), like((width, SMALL), bf)],
        [pltpu.VMEM((8, wide), f32), pltpu.VMEM((8, wide), f32), pltpu.VMEM((SMALL, width), f32), pltpu.VMEM((8, width), f32),
         pltpu.VMEM((width, width), bf), pltpu.VMEM((8, 128 * fan), f32)], 32)


def on_device(
    tokens, segment_ids, ln1_gain, ln1_bias, w_qkv, b_qv, w_attn_out, b_attn_out,
    ln2_gain, ln2_bias, w_fc, b_fc, w_proj, b_proj, cotangent,
):
    dp_size = lax.axis_size("dp")
    dp_pos, t_pos = lax.axis_index("dp"), lax.axis_index("tensor")
    core = dp_pos % 2
    rows = ln1_gain.shape[0]
    width = tokens.shape[1]
    cols = w_qkv.shape[2]
    hidden = w_fc.shape[1]
    fan = b_fc.shape[0] // rows
    far = [1 << k for k in range(dp_size.bit_length() - 2, 1, -1)]
    swap = []
    for d in range(dp_size):
        for t in range(2):
            if d % 2 != t:
                swap.append((2 * d + t, 2 * (d - d % 2 + t) + d % 2))
    mine = core == t_pos

    pairs = cols // 128

    def by_pair(parts):
        parts = parts.reshape(-1, 3, pairs, 128)
        return jnp.swapaxes(parts, 1, 2).reshape(-1, 3 * cols)

    def by_part(columns):
        return jnp.swapaxes(columns.reshape(-1, pairs, 3, 128), 1, 2).reshape(-1, 3, cols)

    small = jnp.concatenate([jnp.stack([ln1_gain, ln1_bias, b_attn_out, ln2_gain, ln2_bias, b_proj]), b_qv], axis=0)
    small = jnp.concatenate([small.T, b_fc.reshape(rows, fan)], axis=1)
    small = jnp.pad(small, ((0, 0), (0, SMALL - small.shape[1])))
    out_pack = jnp.concatenate([w_attn_out.T, small], axis=1)
    tokens, seg_other, cot_recv, all_qkv, all_out, fc_far, proj_far = head(
        dp_size, tokens, segment_ids, cotangent, (by_pair(w_qkv), out_pack, w_fc, w_proj.T), chunks_of(3 * cols, 0, 2) + chunks_of(cols + SMALL, 1, 1))
    all_qkv, all_out = (a.reshape(2, width, -1) for a in (all_qkv, all_out))
    fc_far, proj_far = fc_far.reshape(-1, hidden), proj_far.reshape(-1, hidden)
    fc_parts = [[fc_far], [exchange(fc_far, 0, dp_size)]]
    proj_half = exchange(proj_far, 2, dp_size)

    part = jnp.stack([core, dp_pos, jnp.where(mine, 1, 0), t_pos]).astype(jnp.int32)
    x, n1, qkv_own, qkv_recv, vec_rel, fc_bias, starts = project_first(
        rows, fan, tokens, all_out, all_qkv, segment_ids, seg_other)
    fc_parts, proj_half, qkv_own = lax.optimization_barrier((fc_parts, proj_half, qkv_own))
    fc_parts = [p + [exchange(p[0], 2, dp_size)] for p in fc_parts]
    proj_half = jnp.concatenate([proj_far, proj_half], axis=0)
    proj_parts = [proj_half, exchange(proj_half, 0, dp_size)]
    o_own, o_send, lse = attn_fwd(qkv_own, qkv_recv, starts, part)
    half = width // 2
    middle, n2, cot, d_mlp, o_recv, fc_got, pr_got = middle_part(
        rows, x, o_own, o_send, cotangent, cot_recv, all_out, vec_rel, fc_parts, proj_parts)
    mlp, back, fc_lo, fc_hi, pr_lo, pr_hi, fc_grad = feed_part(
        part, n2, d_mlp, fc_bias, fc_got, pr_got, fc_parts, proj_parts)
    fc_got, pr_got = exchange(fc_hi, 1, dp_size), exchange(pr_hi, 1, dp_size)
    block_out, d_middle, d_attn, do_own, do_send, mid_sums = after_part(
        part, rows, middle, mlp, back, cot, all_out, vec_rel, cols)
    do_recv = exchange(do_send, 1, dp_size)

    near_size = half // 2
    fc_rest = add_low(fc_lo[1], fc_got[1])
    pr_rest = add_low(pr_lo[:, near_size:], pr_got[:, near_size:])
    last = (qkv_own, qkv_recv, do_own, do_recv, o_own, o_send)
    last, fc_rest, pr_rest = lax.optimization_barrier((last, fc_rest, pr_rest))
    fc_sent = exchange(fc_rest, 0, dp_size)
    pr_sent = exchange(pr_rest, 2, dp_size)
    block_recv = lax.ppermute(block_out, BOTH, swap)
    dq_own, dq_send = attn_bwd(*last, starts, lse, part)
    dq_recv = exchange(dq_send, 1, dp_size)
    dq_own, fc_sent, pr_sent = lax.optimization_barrier((dq_own, fc_sent, pr_sent))
    fc_rest = add_low(fc_lo[0, near_size:], fc_got[0, near_size:], fc_sent[near_size:])
    pr_rest = add_low(pr_lo[1, :near_size], pr_got[1, :near_size], pr_sent[1])
    dq_own, fc_rest, pr_rest = lax.optimization_barrier((dq_own, fc_rest, pr_rest))
    fc_near = exchange(fc_rest, 2, dp_size)
    pr_near = exchange(pr_rest, 0, dp_size)
    own_lo, own_hi = weight_part(n1, d_attn, dq_own, o_own)
    own_lo, dq_recv = lax.optimization_barrier((own_lo, dq_recv))
    grad_tokens, d_small = token_part(part, rows, dq_own, dq_recv, x, d_middle, all_qkv, vec_rel, mid_sums, fc_grad)
    grad_recv = lax.ppermute(grad_tokens, BOTH, swap)
    d_small, fc_near, pr_near = lax.optimization_barrier((d_small, fc_near, pr_near))
    sum_fc = add_low(fc_lo[0, :near_size], fc_got[0, :near_size], fc_sent[:near_size], fc_near)
    sum_proj = add_low(pr_lo[0, :near_size], pr_got[0, :near_size], pr_sent[0], pr_near)
    feed = jnp.concatenate([sum_fc, sum_proj], axis=1).reshape(-1, rows, 2 * hidden)
    dq_recv, d_small, feed = lax.optimization_barrier((dq_recv, d_small, feed))
    rest_lo, rest_hi = weight_part(n1, d_attn, dq_recv, o_recv)
    blocks = lambda arr: arr.reshape(dp_size // 2, rows, -1)
    sum_a, vecs, sum_feed = tail(
        dp_size, (blocks(own_lo), blocks(own_hi)), (blocks(rest_lo), blocks(rest_hi)),
        (blocks(d_small[:half]), blocks(d_small[half:])), feed)
    vecs, block_recv, grad_recv = lax.optimization_barrier((vecs, block_recv, grad_recv))
    block_out = jnp.where(mine, block_out, block_recv)
    grad_tokens = jnp.where(mine, grad_tokens, grad_recv)
    return (
        block_out,
        grad_tokens,
        vecs[:, 0],
        vecs[:, 1],
        by_part(sum_a[:, : 3 * cols]),
        vecs[:, 2:4].T,
        sum_a[:, 3 * cols :].T,
        vecs[:, 4],
        vecs[:, 5],
        vecs[:, 6],
        sum_feed[:, :hidden],
        vecs[:, 8 : 8 + fan].reshape(rows * fan),
        sum_feed[:, hidden:].T,
        vecs[:, 7],
    )


def solution(mesh):
    vec, tok = P("dp"), P(BOTH, None)
    in_specs = (
        tok, P("dp", None), vec, vec, P("dp", None, "tensor"), P(None, "dp"), P("tensor", "dp"),
        vec, vec, vec, P("dp", "tensor"), vec, P("tensor", "dp"), vec, tok,
    )
    out_specs = (
        tok, tok, vec, vec, P("dp", None, "tensor"), P(None, "dp"), P("tensor", "dp"),
        vec, vec, vec, P("dp", "tensor"), vec, P("tensor", "dp"), vec,
    )
    return jax.shard_map(on_device, mesh=mesh, in_specs=in_specs, out_specs=out_specs, check_vma=False)
```

```python
import functools

import jax
import jax.numpy as jnp
from jax import lax
from jax.experimental import pallas as pl
from jax.experimental.pallas import tpu as pltpu
from jax.sharding import PartitionSpec as P

HD = 64
QB = 256
NEG = -1e30
EPSILON = 1e-05
BRANCH_SCALE = 48.0 ** (-0.5)
SMALL = 128
VECS = 16
ROWS = 256
HIDDEN = 768
bf = jnp.bfloat16
f32 = jnp.float32
NT = (((1,), (1,)), ((), ()))
TN = (((0,), (0,)), ((), ()))
BOTH = ("dp", "tensor")
MESH_ID = pl.DeviceIdType.MESH
ANY = pl.BlockSpec(memory_space=pl.ANY)
VM = pl.BlockSpec(memory_space=pltpu.VMEM)
HBM = pl.BlockSpec(memory_space=pltpu.HBM)
SM = pl.BlockSpec(memory_space=pltpu.SMEM)


def attn_mask(kat, at, srow):
    keys = lax.broadcasted_iota(jnp.int32, (QB, QB), 0)
    rows = lax.broadcasted_iota(jnp.int32, (1, QB), 1) + (at - kat)
    return (keys >= srow - kat) & (keys <= rows)


def over_blocks(bounds, i, step, carry):
    low = bounds[0, i * QB] // QB
    mid = jnp.minimum((bounds[0, i * QB + QB - 1] + QB - 1) // QB, i)
    carry = lax.fori_loop(0, mid - low + 1, lambda k, c: step(True, jnp.where(k == 0, i, low + k - 1), c), carry)
    return lax.fori_loop(mid, i, functools.partial(step, False), carry)


def head_lanes(values):
    low = (lax.broadcasted_iota(jnp.int32, (1, values.shape[1]), 1) % 128) < HD
    zero = jnp.zeros((), bf)
    return jnp.where(low, values, zero), jnp.where(low, zero, values)


def fwd_kernel(info, bounds, own_far, recv_far, st_ref, okeep, osend, lse_ref, qm, ks, vt, osc, acc, own, recv, load_sem):
    loads = [pltpu.make_async_copy(src, dst, load_sem.at[k]) for k, (src, dst) in enumerate(((own_far, own), (recv_far, recv)))]
    for load in loads:
        load.start()
    half, cols = own.shape[0], own.shape[1] // 3
    n, nb, heads, pairs = 2 * half, 2 * half // QB, cols // HD, cols // 128
    c = info[0]
    for load, base, src in ((loads[0], c * half, own), (loads[1], (1 - c) * half, recv)):
        load.wait()
        rows = pl.ds(pl.multiple_of(base, half), half)
        for g in range(pairs):
            lanes = slice(g * 128, (g + 1) * 128)
            part = lambda k: src[:, (3 * g + k) * 128 : (3 * g + k + 1) * 128]
            qm[0, rows, lanes], qm[1, rows, lanes] = head_lanes(part(0) * bf(HD**-0.5))
            ks[rows, lanes] = part(1)
            vt[lanes, rows] = part(2).T

    def qblock(i, _):
        at = pl.multiple_of(i * QB, QB)
        qr = pl.ds(at, QB)
        srow = st_ref[:, qr]
        acc[...] = jnp.zeros_like(acc)

        def step(masked, j, carry):
            kat = pl.multiple_of(j * QB, QB)
            kr = pl.ds(kat, QB)
            if masked:
                mask = attn_mask(kat, at, srow)
            scores, mixed = [], []
            for h in range(heads):
                lanes = slice(h // 2 * 128, h // 2 * 128 + 128)
                one = lax.dot_general(ks[kr, lanes], qm[h % 2, qr, lanes], NT, preferred_element_type=f32)
                scores.append(jnp.where(mask, one, NEG) if masked else one)
            for h in range(heads):
                top, total = carry[h]
                new = jnp.maximum(top, jnp.max(scores[h], axis=0, keepdims=True))
                weights = jnp.exp(scores[h] - new)
                fade = jnp.exp(top - new)
                total = fade * total + jnp.sum(weights, axis=0, keepdims=True)
                mixed.append((new, total, fade, weights.astype(bf)))
            for h in range(heads):
                sub = slice(h * HD, (h + 1) * HD)
                acc[sub] = mixed[h][2] * acc[sub] + jnp.dot(vt[sub, kr], mixed[h][3], preferred_element_type=f32)
            return tuple(m[:2] for m in mixed)

        carry = over_blocks(bounds, i, step, ((jnp.full((1, QB), NEG, f32), jnp.zeros((1, QB), f32)),) * heads)
        for h, (top, total) in enumerate(carry):
            sub = slice(h * HD, (h + 1) * HD)
            acc[sub] = acc[sub] / total
            lse_ref[h : h + 1, qr] = top + jnp.log(total)
        osc[qr] = acc[...].T.astype(bf)
        return 0

    lax.fori_loop(0, nb, qblock, 0)
    okeep[...] = osc[pl.ds(pl.multiple_of(c * half, half), half)]
    osend[...] = osc[pl.ds(pl.multiple_of((1 - c) * half, half), half)]


def attn_fwd(own, recv, starts, info):
    half, cols = own.shape[0], own.shape[1] // 3
    n = 2 * half
    return pl.pallas_call(
        fwd_kernel,
        in_specs=[SM, SM, ANY, ANY, VM],
        out_specs=[VM] * 3,
        scratch_shapes=[
            pltpu.VMEM((2, n, cols), bf), pltpu.VMEM((n, cols), bf), pltpu.VMEM((cols, n), bf),
            pltpu.VMEM((n, cols), bf), pltpu.VMEM((cols, QB), f32), pltpu.VMEM(own.shape, bf), pltpu.VMEM(own.shape, bf),
            pltpu.SemaphoreType.DMA((2,))],
        out_shape=[jax.ShapeDtypeStruct((half, cols), bf)] * 2 + [jax.ShapeDtypeStruct((cols // HD, n), f32)],
        cost_estimate=pl.CostEstimate(flops=n * n, bytes_accessed=n * 128, transcendentals=0),
        compiler_params=pltpu.CompilerParams(vmem_limit_bytes=60 << 20),
    )(info, starts, own, recv, starts)


def bwd_kernel(info, bounds, own, recv, doo, dor, oo, orr, st_ref, lse_ref, dkeep, dsend, qm, ks, vs, kt, dom, dlt, dqs, dks, dvs):
    half, cols = own.shape[0], own.shape[1] // 3
    n, nb, heads, pairs = 2 * half, 2 * half // QB, cols // HD, cols // 128
    c = info[0]
    lanes_of = lambda g: slice(g * 128, (g + 1) * 128)
    for base, src, do, o in ((c * half, own, doo, oo), ((1 - c) * half, recv, dor, orr)):
        rows = pl.ds(pl.multiple_of(base, half), half)
        for g in range(pairs):
            lanes = lanes_of(g)
            part = lambda k: src[:, (3 * g + k) * 128 : (3 * g + k + 1) * 128]
            qm[0, rows, lanes], qm[1, rows, lanes] = head_lanes(part(0) * bf(HD**-0.5))
            ks[rows, lanes] = part(1)
            vs[rows, lanes] = part(2)
            kt[lanes, rows] = part(1).T
            grad = do[:, lanes]
            dom[0, rows, lanes], dom[1, rows, lanes] = head_lanes(grad)
            prod = (grad.astype(f32) * o[:, lanes].astype(f32)).T
            for e in range(2):
                dlt[2 * g + e : 2 * g + e + 1, rows] = jnp.sum(prod[e * HD : (e + 1) * HD], axis=0, keepdims=True)
    dks[...] = jnp.zeros_like(dks)
    dvs[...] = jnp.zeros_like(dvs)

    def qblock(i, _):
        at = pl.multiple_of(i * QB, QB)
        qr = pl.ds(at, QB)
        srow = st_ref[:, qr]
        dqs[...] = jnp.zeros_like(dqs)

        def step(masked, j, carry):
            kat = pl.multiple_of(j * QB, QB)
            kr = pl.ds(kat, QB)
            if masked:
                mask = attn_mask(kat, at, srow)
            scores, softs, grads = [], [], []
            for h in range(heads):
                lanes = lanes_of(h // 2)
                one = lax.dot_general(ks[kr, lanes], qm[h % 2, qr, lanes], NT, preferred_element_type=f32)
                back = lax.dot_general(vs[kr, lanes], dom[h % 2, qr, lanes], NT, preferred_element_type=f32)
                scores.append((jnp.where(mask, one, NEG) if masked else one, back))
            for h in range(heads):
                soft = jnp.exp(scores[h][0] - lse_ref[h : h + 1, qr])
                grads.append((soft * (scores[h][1] - dlt[h : h + 1, qr])).astype(bf))
                softs.append(soft.astype(bf))
            for g in range(pairs):
                lanes = lanes_of(g)
                both = lambda ref: jnp.concatenate([ref[0, qr, lanes], ref[1, qr, lanes]], axis=0)
                two = slice(2 * g, 2 * g + 2)
                dvs[kr, lanes] += jnp.dot(jnp.concatenate(softs[two], axis=1), both(dom), preferred_element_type=f32)
                dks[kr, lanes] += jnp.dot(jnp.concatenate(grads[two], axis=1), both(qm), preferred_element_type=f32)
                for h in (2 * g, 2 * g + 1):
                    sub = slice(h * HD, (h + 1) * HD)
                    dqs[sub] += jnp.dot(kt[sub, kr], grads[h], preferred_element_type=f32)
            return carry

        over_blocks(bounds, i, step, 0)
        qm[0, qr] = (dqs[...] * (HD**-0.5)).T.astype(bf)
        return 0

    lax.fori_loop(0, nb, qblock, 0)
    for dst, base in ((dkeep, c * half), (dsend, (1 - c) * half)):
        rows = pl.ds(pl.multiple_of(base, half), half)
        for g in range(pairs):
            for k, value in enumerate((qm[0, rows, lanes_of(g)], dks[rows, lanes_of(g)], dvs[rows, lanes_of(g)])):
                dst[:, (3 * g + k) * 128 : (3 * g + k + 1) * 128] = value.astype(bf)


def attn_bwd(own, recv, do_own, do_recv, o_own, o_recv, starts, lse, info):
    half, cols = own.shape[0], own.shape[1] // 3
    n = 2 * half
    return pl.pallas_call(
        bwd_kernel,
        in_specs=[SM, SM] + [VM] * 8,
        out_specs=[VM] * 2,
        scratch_shapes=[
            pltpu.VMEM((2, n, cols), bf), pltpu.VMEM((n, cols), bf), pltpu.VMEM((n, cols), bf), pltpu.VMEM((cols, n), bf),
            pltpu.VMEM((2, n, cols), bf), pltpu.VMEM((cols // HD, n), f32), pltpu.VMEM((cols, QB), f32),
            pltpu.VMEM((n, cols), f32), pltpu.VMEM((n, cols), f32)],
        out_shape=[like((half, 3 * cols), bf)] * 2,
        cost_estimate=pl.CostEstimate(flops=n * n, bytes_accessed=n * 128, transcendentals=0),
        compiler_params=pltpu.CompilerParams(vmem_limit_bytes=56 << 20),
    )(info, starts, own, recv, do_own, do_recv, o_own, o_recv, starts, lse)


def dot(left, right, dims=(((1,), (0,)), ((), ()))):
    return lax.dot_general(left, right, dims, preferred_element_type=f32)


def exchange(value, bit, dp_size):
    if bit:
        return lax.ppermute(value, "dp", [(i, i ^ bit) for i in range(dp_size)])
    return lax.ppermute(value, "tensor", [(0, 1), (1, 0)])


def flip(index, bits):
    for bit in bits:
        index = index + bit * (1 - 2 * ((index // bit) % 2))
    return index

def far_groups(dp_size):
    far = [1 << k for k in range(dp_size.bit_length() - 2, 1, -1)]
    return [tuple(far[k : k + 2]) for k in range(0, len(far), 2)]

def group_moves(group):
    if len(group) == 1:
        return [(1, group)]
    return [(1, group[:1]), (2, group[1:]), (3, group)]

def chunks_of(cols, which, count, until=None):
    tiles = cols // 128
    cuts = [128 * ((tiles * k) // count) for k in range(count + 1)]
    arrays = range(which, until + 1) if until else (which,)
    return tuple(
        (array, low, high - low, 128 * ((high - low) // 256 + (high - low) // 128 % 2))
        for low, high in zip(cuts, cuts[1:]) for array in arrays)


def head_kernel(groups, chunks, tokens, seg, *refs):
    shards, x_out, seg_out, outs, (send_sem, recv_sem, local_sem) = refs[:4], refs[4], refs[5], refs[6:10], refs[10:]
    dp, t = lax.axis_index("dp"), lax.axis_index("tensor")
    core = dp % 2
    away = core + t - 2 * core * t
    near = {1: (flip(dp, (1,)), t), 2: (flip(dp, (2,)), t), 0: (dp, 1 - t)}
    distant = [bits for group in groups for _, bits in group_moves(group)]
    swap = (dp - core + t, core)
    barrier = pltpu.get_barrier_semaphore()
    for device in list(near.values()) + [(flip(dp, bits), t) for bits in distant]:
        pl.semaphore_signal(barrier, inc=1, device_id=device, device_id_type=MESH_ID)

    @pl.when(away == 1)
    def _():
        pl.semaphore_signal(barrier, inc=1, device_id=swap, device_id_type=MESH_ID)

    local = [
        pltpu.make_async_copy(shards[k], outs[k].at[away, 0] if k < 2 else outs[k].at[0], local_sem.at[k]) for k in range(4)]
    for copy in local:
        copy.start()
    pl.semaphore_wait(barrier, len(near) + len(distant) + away)
    count = [0]

    def remote(src, dst, device):
        slot = count[0]
        count[0] += 1
        return pltpu.make_async_remote_copy(
            src_ref=src, dst_ref=dst, send_sem=send_sem.at[slot], recv_sem=recv_sem.at[slot],
            device_id=device, device_id_type=MESH_ID)

    def blocks(ref, index, first, held, low, size):
        return ref.at[index, pl.ds(first, held), :, pl.ds(low, size)]

    plans = []
    for which, low, size, part in chunks:
        shard, out = shards[which], outs[which]
        steps, held = [], 1
        for group in groups:
            moves = []
            for place, bits in group_moves(group):
                src = shard.at[:, pl.ds(low, size)] if held == 1 else blocks(out, away, 0, held, low, size)
                dst = out.at[away, place, :, pl.ds(low, size)] if held == 1 else blocks(out, away, place * held, held, low, size)
                moves.append(remote(src, dst, (flip(dp, bits), t)))
            held *= len(group_moves(group)) + 1
            steps.append(moves)
        a, b = (low, part), (low + part, size - part)
        steps.append([
            remote(blocks(out, away, 0, held, *a), blocks(out, away, 0, held, *a), near[0]),
            remote(blocks(out, away, 0, held, *b), blocks(out, away, held, held, *b), near[2]),
        ])
        steps.append(
            [remote(blocks(out, k, 0, held, *a), blocks(out, k, held, held, *a), near[2]) for k in range(2)]
            + [remote(blocks(out, away, 0, 2 * held, *b), blocks(out, away, 0, 2 * held, *b), near[0])])
        steps.append([
            remote(blocks(out, k, 0, 2 * held, low, size),
                   blocks(out, 1 - k, 2 * held, 2 * held, low, size), near[1]) for k in range(2)])
        plans.append(steps)
    later = []
    held = 1
    for group in groups:
        moves = []
        for place, bits in group_moves(group):
            for shard, out in zip(shards[2:], outs[2:]):
                src = shard if held == 1 else out.at[pl.ds(0, held)]
                dst = out.at[place] if held == 1 else out.at[pl.ds(place * held, held)]
                moves.append(remote(src, dst, (flip(dp, bits), t)))
        held *= len(group_moves(group)) + 1
        later.append(moves)
    depth = len(plans[0])
    swap_copy = remote(tokens, x_out, swap)
    seg_copy = remote(seg, seg_out, near[1])
    stay_copy = pltpu.make_async_copy(tokens, x_out, local_sem.at[4])
    waited = set()

    def advance(number, phase):
        if number >= len(plans):
            return
        if phase > 0:
            for move in plans[number][phase - 1]:
                move.wait_recv()
        if phase == 1 and chunks[number][0] not in waited:
            waited.add(chunks[number][0])
            local[chunks[number][0]].wait()
        if phase < depth:
            for move in plans[number][phase]:
                move.start()

    advance(0, 0)
    seg_copy.start()

    @pl.when(away == 1)
    def _():
        swap_copy.start()

    @pl.when(away == 0)
    def _():
        stay_copy.start()

    far = len(groups)
    for number in range(len(plans)):
        if number == 0:
            for phase in range(1, far + 1):
                advance(0, phase)
            for k in range(1, len(plans)):
                advance(k, 0)
            for move in later[0]:
                move.start()
        advance(number, far + 1)
        for phase in range(1, far + 1):
            advance(number + 1, phase)
        advance(number, far + 2)
    for number in range(len(plans)):
        advance(number, depth)

    @pl.when(away == 1)
    def _():
        swap_copy.wait()

    @pl.when(away == 0)
    def _():
        stay_copy.wait()

    seg_copy.wait()
    for which in sorted(set(range(4)) - waited):
        local[which].wait()
    for k, moves in enumerate(later):
        if k > 0:
            for move in moves:
                move.start()
        for move in moves:
            move.wait()
    for steps in plans:
        for moves in steps:
            for move in moves:
                move.wait_send()


def head(dp_size, tokens, seg, shards, chunks):
    groups = far_groups(dp_size)
    partners = sum(len(group_moves(g)) for g in groups)
    slots = len(chunks) * (partners + 7) + 2 * partners + 2
    shapes = [(2, dp_size)] * 2 + [(dp_size // 4,)] * 2
    return pl.pallas_call(
        functools.partial(head_kernel, groups, chunks),
        in_specs=[VM] * 6,
        out_specs=[ANY] * 6,
        out_shape=[jax.ShapeDtypeStruct(a.shape, a.dtype) for a in (tokens, seg)]
        + [jax.ShapeDtypeStruct(lead + s.shape, s.dtype) for lead, s in zip(shapes, shards)],
        scratch_shapes=[pltpu.SemaphoreType.DMA((slots,)), pltpu.SemaphoreType.DMA((slots,)), pltpu.SemaphoreType.DMA((5,))],
        compiler_params=pltpu.CompilerParams(collective_id=0, has_side_effects=True),
    )(tokens, seg, *shards)


def tail_kernel(groups, own_lo, own_hi, rest_lo, rest_hi, small_lo, small_hi, feed, total, vecs, feed_total,
                feed_part, feed_got, part, got_core, got_near, got_last, got_far, vec, vec_core, vec_two, vec_one, vec_far, send_sem, recv_sem):
    dp, t = lax.axis_index("dp"), lax.axis_index("tensor")
    core = dp % 2
    away = core + t - 2 * core * t
    near = {1: (flip(dp, (1,)), t), 2: (flip(dp, (2,)), t), 0: (dp, 1 - t)}
    distant = [bits for group in groups for _, bits in group_moves(group)]
    barrier = pltpu.get_barrier_semaphore()
    for device in list(near.values()) + [(flip(dp, bits), t) for bits in distant]:
        pl.semaphore_signal(barrier, inc=1, device_id=device, device_id_type=MESH_ID)

    pl.semaphore_wait(barrier, len(near) + len(distant))
    count = [0]

    def remote(src, dst, device):
        slot = count[0]
        count[0] += 1
        return pltpu.make_async_remote_copy(
            src_ref=src, dst_ref=dst, send_sem=send_sem.at[slot], recv_sem=recv_sem.at[slot],
            device_id=device, device_id_type=MESH_ID)

    half, rows, cols = own_lo.shape
    quarter = half // 2
    chunks = [pl.ds(low, min(384, cols - low)) for low in range(0, cols, 384)]
    to_core = [[
        remote(rest_hi.at[:, :, c], got_core.at[0, :, :, c], near[1]),
        remote(own_hi.at[:, :, c], got_core.at[1, :, :, c], near[1])] for c in chunks]
    to_core[0].append(remote(small_hi, vec_core, near[1]))
    for moves in to_core:
        for move in moves:
            move.start()

    feed_steps = []
    held, used = feed.shape[0], 0
    for number, group in enumerate(reversed(groups)):
        moves = group_moves(group)
        held //= len(moves) + 1
        source, step = feed if number == 0 else feed_part, []
        for place, bits in moves:
            step.append(remote(source.at[pl.ds(place * held, held)], feed_got.at[pl.ds(used, held)], (flip(dp, bits), t)))
            used += held
        feed_steps.append((step, source, held, used - held * len(moves), len(moves)))
    for move in feed_steps[0][0]:
        move.start()

    def add(*terms):
        out = terms[0].astype(f32)
        for term in terms[1:]:
            out = out + term.astype(f32)
        return out.astype(bf)

    upper, lower = pl.ds(quarter, quarter), pl.ds(0, quarter)
    mine, other = away, 1 - away
    last = len(chunks) - 1
    steps, sent = {}, []

    def start(key, moves):
        steps[key] = moves
        sent.extend(moves)
        for move in moves:
            move.start()

    def arrive(key):
        for move in steps[key]:
            move.wait_recv()

    def core_stage(k):
        for move in to_core[k]:
            move.wait_recv()
        c = chunks[k]

        def body(q, _):
            part[0, q, :, c] = add(own_lo[q, :, c], got_core[0, q, :, c])
            part[1, q, :, c] = add(rest_lo[q, :, c], got_core[1, q, :, c])
            if k == 0:
                vec[q] = add(small_lo[q], vec_core[q])
            return 0

        lax.fori_loop(0, half, body, 0)
        if k % 2 == 1:
            start(("x", k), [remote(part.at[other, :, :, c], got_near.at[0, :, :, c], near[0])])
        else:
            start(("x", k), [
                remote(part.at[g, upper, :, c], got_near.at[g, lower, :, c], near[2]) for g in range(2)]
                + ([remote(vec.at[upper], vec_two, near[2])] if k == 0 else []))

    def x_stage(k):
        arrive(("x", k))
        c = chunks[k]

        def body(q, _):
            if k % 2 == 1:
                part[mine, q, :, c] = add(part[mine, q, :, c], got_near[0, q, :, c])
                return 0
            for g in range(2):
                part[g, q, :, c] = add(part[g, q, :, c], got_near[g, q, :, c])
            if k == 0:
                vec[q] = add(vec[q], vec_two[q])
            return 0

        lax.fori_loop(0, half if k % 2 == 1 else quarter, body, 0)
        if k % 2 == 1:
            start(("y", k), [remote(part.at[mine, upper, :, c], got_last.at[:, :, c], near[2])])
        else:
            start(("y", k), [remote(part.at[other, lower, :, c], got_last.at[:, :, c], near[0])]
                  + ([remote(vec.at[lower], vec_one, near[0])] if k == 0 else []))

    def far_moves(number, k):
        held, used = quarter, 0
        for index, group in enumerate(reversed(groups)):
            moves = group_moves(group)
            held //= len(moves) + 1
            if index == number:
                out = []
                for m, (place, bits) in enumerate(moves):
                    device, c = (flip(dp, bits), t), chunks[k]
                    out.append(remote(part.at[mine, pl.ds(place * held, held), :, c], got_far.at[pl.ds(used + m * held, held), :, c], device))
                    if k == 0:
                        out.append(remote(vec_one.at[pl.ds(place * held, held)], vec_far.at[pl.ds(used + m * held, held)], device))
                return out, held, used, len(moves)
            used += held * len(moves)

    def y_stage(k):
        arrive(("y", k))
        c = chunks[k]

        def body(q, _):
            part[mine, q, :, c] = add(part[mine, q, :, c], got_last[q, :, c])
            if k == 0:
                vec_one[q] = add(vec[q], vec_one[q])
            return 0

        lax.fori_loop(0, quarter, body, 0)
        start(("z", 0, k), far_moves(0, k)[0])

    far_shape = []
    held, used = quarter, 0
    for group in reversed(groups):
        moves = len(group_moves(group))
        held //= moves + 1
        far_shape.append((held, used, moves))
        used += held * moves

    def z_stage(number, k):
        arrive(("z", number, k))
        c = chunks[k]
        held, base, moves = far_shape[number]

        def body(q, _):
            part[mine, q, :, c] = add(part[mine, q, :, c], *[got_far[base + m * held + q, :, c] for m in range(moves)])
            if k == 0:
                vec_one[q] = add(vec_one[q], *[vec_far[base + m * held + q] for m in range(moves)])
            return 0

        lax.fori_loop(0, held, body, 0)
        if number + 1 < len(groups):
            start(("z", number + 1, k), far_moves(number + 1, k)[0])

    for k in range(last + 1):
        core_stage(k)
    for k in range(last + 1):
        x_stage(k)
        if k > 0:
            y_stage(k - 1)
    y_stage(last)
    for number in range(len(groups)):
        for k in range(last + 1):
            z_stage(number, k)
    to_far = []
    for number, (step, source, held, base, moves) in enumerate(feed_steps):
        if number > 0:
            for move in step:
                move.start()
        for move in step:
            move.wait_recv()

        def sum_feed(k, _, source=source, held=held, base=base, moves=moves):
            feed_part[k] = add(source[k], *[feed_got[base + m * held + k] for m in range(moves)])
            return 0

        if number + 1 < len(feed_steps):
            lax.fori_loop(0, held, sum_feed, 0)
        else:
            out = source[0].astype(f32)
            for m in range(moves):
                out = out + feed_got[base + m * held].astype(f32)
            feed_total[...] = out
        to_far += step
    total[...] = part[mine, 0].astype(f32)
    vecs[...] = vec_one[0].astype(f32)

    for move in sum(to_core, []) + sent + to_far:
        move.wait_send()


def tail(dp_size, own, rest, small, feed):
    groups = far_groups(dp_size)
    half, rows, cols = own[0].shape
    quarter = half // 2
    wide = small[0].shape[2]
    partners = sum(len(group_moves(g)) for g in groups)
    slots = (-(-cols // 384)) * (5 + partners) + 3 + 2 * partners
    return pl.pallas_call(
        functools.partial(tail_kernel, groups),
        in_specs=[VM] * 7,
        out_specs=[VM, VM, VM],
        out_shape=[
            jax.ShapeDtypeStruct((rows, cols), f32),
            jax.ShapeDtypeStruct((rows, wide), f32), jax.ShapeDtypeStruct(feed.shape[1:], f32)],
        scratch_shapes=[
            pltpu.VMEM(feed.shape, bf), pltpu.VMEM(feed.shape, bf),
            pltpu.VMEM((2, half, rows, cols), bf), pltpu.VMEM((2, half, rows, cols), bf), pltpu.VMEM((2, half, rows, cols), bf),
            pltpu.VMEM((quarter, rows, cols), bf), pltpu.VMEM((quarter, rows, cols), bf),
            pltpu.VMEM((half, rows, wide), bf), pltpu.VMEM((half, rows, wide), bf), pltpu.VMEM((quarter, rows, wide), bf),
            pltpu.VMEM((quarter, rows, wide), bf), pltpu.VMEM((quarter, rows, wide), bf),
            pltpu.SemaphoreType.DMA((slots,)), pltpu.SemaphoreType.DMA((slots,))],
        compiler_params=pltpu.CompilerParams(collective_id=1, has_side_effects=True, vmem_limit_bytes=48 << 20),
    )(*own, *rest, *small, feed)


def add_low(*terms):
    out = terms[0].astype(f32)
    for term in terms[1:]:
        out = out + term.astype(f32)
    return out.astype(bf)


def order_matrix(owner, rows, width):
    place = lax.broadcasted_iota(jnp.int32, (1, width), 1)
    block = place // rows
    count = width // rows
    natural = place % rows
    for k, bit in enumerate([1 << b for b in range(count.bit_length() - 2, 1, -1)] + [2, 1]):
        on, base = (block // (1 << k)) % 2, (owner // bit) % 2
        natural = natural + (on + base - 2 * on * base) * (bit * rows)
    return (lax.broadcasted_iota(jnp.int32, (width, width), 0) == natural).astype(f32).astype(bf)


def norm_parts(values):
    centered = values - jnp.mean(values, axis=-1, keepdims=True)
    inverse = lax.rsqrt(jnp.mean(centered * centered, axis=-1, keepdims=True) + EPSILON)
    return centered * inverse, inverse


def norm_back(hat, inverse, gain, grad):
    scaled = grad * gain
    return inverse * (
        scaled - jnp.mean(scaled, axis=-1, keepdims=True) - hat * jnp.mean(scaled * hat, axis=-1, keepdims=True))


def over_rows(total, body, first=0):
    def step(k, _):
        body(pl.ds(pl.multiple_of(first + k * ROWS, ROWS), ROWS))
        return 0

    lax.fori_loop(0, total // ROWS, step, 0)


def column_sum(ref, row, values):
    ref[row : row + 1] += jnp.sum(values, axis=0, keepdims=True)


def bias_row(vec_nat, group, cols):
    lanes = pl.ds(pl.multiple_of(group * cols, 128), cols)
    q, v = vec_nat[6:7, lanes], vec_nat[7:8, lanes]
    parts = []
    for g in range(cols // 128):
        part = slice(g * 128, (g + 1) * 128)
        parts += [q[:, part], jnp.zeros((1, 128), f32), v[:, part]]
    return jnp.concatenate(parts, axis=1)


def fan_matrix(fan):
    row = lax.broadcasted_iota(jnp.int32, (128 * fan, 1), 0)
    unit = lax.broadcasted_iota(jnp.int32, (128 * fan, 128 * fan), 1)
    return (unit == (row % 128) * fan + row // 128).astype(f32).astype(bf)


def first_kernel(rows, fan, tokens, packs, weights, seg, seg_other, x_out, n1_out, own, recv, vec_rel, fc_bias, starts,
                 tok, pack, weight, send, vec_nat, order, fan_rows, send_sem, recv_sem, local_sem):
    dp, t = lax.axis_index("dp"), lax.axis_index("tensor")
    core = dp % 2
    away = core + t - 2 * core * t
    total, width = tok.shape
    cols = weight.shape[2] // 3
    partner = (flip(dp, (1,)), t)
    barrier = pltpu.get_barrier_semaphore()
    pl.semaphore_signal(barrier, inc=1, device_id=partner, device_id_type=MESH_ID)
    loads = [
        pltpu.make_async_copy(src, dst, local_sem.at[k])
        for k, (src, dst) in enumerate(((packs.at[0], pack), (tokens, tok), (weights.at[1], weight.at[1]), (weights.at[0], weight.at[0])))]
    for load in loads:
        load.start()
    order[...] = order_matrix(dp, rows, width)
    loads[0].wait()
    small = pack[:, cols:].astype(f32).T[:VECS]
    vec_rel[...] = small
    vec_nat[...] = lax.dot_general(small.astype(bf), order[...], NT, preferred_element_type=f32)
    send_bias, own_bias = bias_row(vec_nat, 1 - core, cols), bias_row(vec_nat, core, cols)
    for load in loads[1:3]:
        load.wait()
    pl.semaphore_wait(barrier, 1)
    parts, size = 2, total // 2
    copies = [
        pltpu.make_async_remote_copy(
            src_ref=send.at[pl.ds(k * size, size)], dst_ref=recv.at[pl.ds(k * size, size)], send_sem=send_sem.at[k],
            recv_sem=recv_sem.at[k], device_id=partner, device_id_type=MESH_ID)
        for k in range(parts)]

    def first(at):
        x = jnp.dot(tok[at], order[...], preferred_element_type=f32)
        hat, _ = norm_parts(x)
        n1 = (hat * vec_rel[0:1] + vec_rel[1:2]).astype(bf)
        x_out[at] = x.astype(bf)
        n1_out[at] = n1
        send[at] = (jnp.dot(n1, weight[1], preferred_element_type=f32) + send_bias).astype(bf)

    def second(at):
        own[at] = (jnp.dot(n1_out[at], weight[0], preferred_element_type=f32) + own_bias).astype(bf)

    for k in range(parts):
        over_rows(size, first, k * size)
        copies[k].start()
    loads[3].wait()
    over_rows(total, second)

    count = width // 128
    fan_rows[...] = jnp.zeros_like(fan_rows)
    for k in range(count):
        for m in range(fan):
            fan_rows[k : k + 1, m * 128 : (m + 1) * 128] = vec_nat[8 + m : 9 + m, k * 128 : (k + 1) * 128]
    bias = jnp.dot(fan_rows[...].astype(bf), fan_matrix(fan), preferred_element_type=f32)
    for k in range(count):
        fc_bias[:, k * 128 * fan : (k + 1) * 128 * fan] = bias[k : k + 1]
    docs = jnp.where(away == 0, seg[...], seg_other[...]).astype(f32)
    begin = jnp.zeros_like(docs)
    for d in range(1, 16):
        before = jnp.sum(jnp.where(docs < d, 1.0, 0.0), axis=1, keepdims=True)
        begin = jnp.where(docs == d, before, begin)
    starts[...] = begin.astype(jnp.int32)
    for copy in copies:
        copy.wait()


def picked(array, index):
    return pl.BlockSpec((1,) + array.shape[1:], lambda k, s: (index, 0, 0))


def whole(array):
    return pl.BlockSpec(array.shape, lambda k, s: (0,) * len(array.shape))


def like(shape, dtype):
    return jax.ShapeDtypeStruct(shape, dtype)


def by_rows(kernel, info, inputs, specs, outs, scratch=(), limit=60):
    total = inputs[0].shape[0]

    def spec(array, given=None):
        if given is not None:
            return given
        if array.shape[0] == total:
            return pl.BlockSpec((ROWS,) + array.shape[1:], lambda k, s: (k, 0))
        return whole(array)

    return pl.pallas_call(
        kernel,
        grid_spec=pltpu.PrefetchScalarGridSpec(
            num_scalar_prefetch=1, grid=(total // ROWS,), in_specs=[spec(a, g) for a, g in zip(inputs, specs)],
            out_specs=[spec(o) for o in outs], scratch_shapes=list(scratch)),
        out_shape=outs,
        cost_estimate=pl.CostEstimate(flops=1 << 22, bytes_accessed=1 << 18, transcendentals=0),
        compiler_params=pltpu.CompilerParams(vmem_limit_bytes=limit << 20),
    )(info, *inputs)


def project_first(rows, fan, tokens, packs, weights, seg, seg_other):
    n, width = tokens.shape
    qkv = like((n, weights.shape[2]), bf)
    return pl.pallas_call(
        functools.partial(first_kernel, rows, fan),
        in_specs=[ANY, ANY, ANY, VM, VM],
        out_specs=[VM, VM, VM, ANY, VM, VM, VM],
        out_shape=[
            like((n, width), bf), like((n, width), bf), qkv, qkv, like((VECS, width), f32), like((1, width * fan), f32),
            like(seg.shape, jnp.int32)],
        scratch_shapes=[
            pltpu.VMEM((n, width), bf), pltpu.VMEM(packs.shape[1:], bf), pltpu.VMEM(weights.shape, bf), pltpu.VMEM(qkv.shape, bf),
            pltpu.VMEM((VECS, width), f32), pltpu.VMEM((width, width), bf), pltpu.VMEM((8, 128 * fan), f32),
            pltpu.SemaphoreType.DMA((2,)), pltpu.SemaphoreType.DMA((2,)), pltpu.SemaphoreType.DMA((4,))],
        compiler_params=pltpu.CompilerParams(collective_id=3, has_side_effects=True, vmem_limit_bytes=60 << 20),
    )(tokens, packs, weights, seg, seg_other)


def middle_kernel(rows, x, o_own, o_send, cot, cot_recv, packs, vec_rel, fc00, fc01, fc10, fc11, pr0, pr1,
                  middle, n2, cot_rel, d_mlp, o_recv, fc_got, pr_got, order, send_sem, recv_sem):
    dp, t = lax.axis_index("dp"), lax.axis_index("tensor")
    core = dp % 2
    away = core + t - 2 * core * t
    partner = (flip(dp, (1,)), t)
    barrier = pltpu.get_barrier_semaphore()
    pl.semaphore_signal(barrier, inc=1, device_id=partner, device_id_type=MESH_ID)
    pl.semaphore_wait(barrier, 1)
    size = fc00.shape[0]
    copies = [
        pltpu.make_async_remote_copy(
            src_ref=src, dst_ref=dst, send_sem=send_sem.at[k], recv_sem=recv_sem.at[k], device_id=partner, device_id_type=MESH_ID)
        for k, (src, dst) in enumerate((
            (o_send, o_recv), (fc00, fc_got.at[0, pl.ds(0, size)]), (fc01, fc_got.at[0, pl.ds(size, size)]), (pr0, pr_got.at[0]),
            (fc10, fc_got.at[1, pl.ds(0, size)]), (fc11, fc_got.at[1, pl.ds(size, size)]), (pr1, pr_got.at[1])))]
    for copy in copies:
        copy.start()
    order[...] = order_matrix(dp, rows, x.shape[1])
    cols = o_own.shape[1]

    def cot_rows(at):
        grad = jnp.dot(jnp.where(away == 0, cot[at], cot_recv[at]), order[...], preferred_element_type=f32)
        cot_rel[at] = grad.astype(bf)
        d_mlp[at] = (BRANCH_SCALE * grad).astype(bf)

    over_rows(x.shape[0], cot_rows)
    copies[0].wait_recv()

    def body(at):
        branch = lax.dot_general(o_own[at], packs[0, :, :cols], NT, preferred_element_type=f32)
        branch = branch + lax.dot_general(o_recv[at], packs[1, :, :cols], NT, preferred_element_type=f32)
        mid = x[at].astype(f32) + BRANCH_SCALE * (branch + vec_rel[2:3])
        middle[at] = mid
        hat, _ = norm_parts(mid)
        n2[at] = (hat * vec_rel[3:4] + vec_rel[4:5]).astype(bf)

    over_rows(x.shape[0], body)
    for copy in copies[1:]:
        copy.wait_recv()
    for copy in copies:
        copy.wait_send()


def middle_part(rows, x, o_own, o_send, cot, cot_recv, packs, vec_rel, fc_parts, proj_parts):
    shape, half = x.shape, x.shape[1] // 2
    hidden = proj_parts[0].shape[1]
    got = like((2, half, hidden), bf)
    return pl.pallas_call(
        functools.partial(middle_kernel, rows),
        in_specs=[VM] * 7 + [HBM] * 6,
        out_specs=[VM] * 5 + [ANY] * 2,
        out_shape=[like(shape, f32), like(shape, bf), like(shape, bf), like(shape, bf), like(o_send.shape, bf), got, got],
        scratch_shapes=[
            pltpu.VMEM((shape[1], shape[1]), bf), pltpu.SemaphoreType.DMA((7,)), pltpu.SemaphoreType.DMA((7,))],
        compiler_params=pltpu.CompilerParams(collective_id=2, has_side_effects=True, vmem_limit_bytes=36 << 20),
    )(x, o_own, o_send, cot, cot_recv, packs, vec_rel, *fc_parts[0], *fc_parts[1], *proj_parts)


def after_kernel(rows, info, middle, mlp, back, cot, packs, vec_rel, block_out, d_middle, d_attn, do_own, do_send, sums, order):
    @pl.when(pl.program_id(0) == 0)
    def _():
        order[...] = order_matrix(info[1], rows, middle.shape[1])
        sums[...] = jnp.zeros_like(sums)

    cols = do_own.shape[1]
    mid = middle[...]
    out = (mid + BRANCH_SCALE * (mlp[...] + vec_rel[5:6])).astype(bf)
    block_out[...] = lax.dot_general(out, order[...], NT, preferred_element_type=f32).astype(bf)
    hat, inverse = norm_parts(mid)
    grad = back[...]
    out_grad = cot[...].astype(f32)
    entire = out_grad + norm_back(hat, inverse, vec_rel[3:4], grad)
    d_middle[...] = entire
    low = (BRANCH_SCALE * entire).astype(bf)
    d_attn[...] = low
    do_own[...] = jnp.dot(low, packs[0, :, :cols], preferred_element_type=f32).astype(bf)
    do_send[...] = jnp.dot(low, packs[1, :, :cols], preferred_element_type=f32).astype(bf)
    column_sum(sums, 0, BRANCH_SCALE * entire)
    column_sum(sums, 1, grad * hat)
    column_sum(sums, 2, grad)
    column_sum(sums, 3, BRANCH_SCALE * out_grad)


def after_part(info, rows, middle, mlp, back, cot, packs, vec_rel, cols):
    shape = middle.shape
    slim = like((shape[0], cols), bf)
    return by_rows(
        functools.partial(after_kernel, rows), info, (middle, mlp, back, cot, packs, vec_rel), (None,) * 6,
        [like(shape, bf), like(shape, f32), like(shape, bf), slim, slim, like((8, shape[1]), f32)],
        [pltpu.VMEM((shape[1], shape[1]), bf)])


def feed_kernel(info, n2, d_mlp, bias, fc_got, pr_got, fc00, fc01, fc10, fc11, pr0, pr1,
                acc, back, fc_lo, fc_hi, pr_lo, pr_hi, d_bias, n2_t, d_t, w_fc, w_pr, act, d_pre):
    step = pl.program_id(0)
    total, half = n2.shape[0], n2.shape[1] // 2

    @pl.when(step == 0)
    def _():
        acc[...] = jnp.zeros_like(acc)
        back[...] = jnp.zeros_like(back)
        n2_t[...] = n2[...].T
        d_t[...] = d_mlp[...].T

    @pl.when(step < pl.num_programs(0) // 2)
    def _():
        w_fc[: half // 2], w_fc[half // 2 : half], w_pr[:half] = fc00[...], fc01[...], pr0[...]

    @pl.when(step >= pl.num_programs(0) // 2)
    def _():
        w_fc[: half // 2], w_fc[half // 2 : half], w_pr[:half] = fc10[...], fc11[...], pr1[...]

    w_fc[half:], w_pr[half:] = fc_got[0], pr_got[0]
    root = 0.7978845608
    count = total // ROWS
    raw = {}
    grad_sum = jnp.zeros((1, w_fc.shape[1]), f32)

    def products(k):
        at = slice(k * ROWS, (k + 1) * ROWS)
        return (
            jnp.dot(n2[at], w_fc[...], preferred_element_type=f32) + bias[...],
            jnp.dot(d_mlp[at], w_pr[...], preferred_element_type=f32))

    def add_back(k):
        at = slice(k * ROWS, (k + 1) * ROWS)
        acc[at] += lax.dot_general(act[at], w_pr[...], NT, preferred_element_type=f32)
        back[at] += lax.dot_general(d_pre[at], w_fc[...], NT, preferred_element_type=f32)

    raw[0] = products(0)
    for k in range(count):
        at = slice(k * ROWS, (k + 1) * ROWS)
        if k + 1 < count:
            raw[k + 1] = products(k + 1)
        pre, d_act = raw.pop(k)
        square = pre * pre
        inner = jnp.tanh(pre * (root + root * 0.044715 * square))
        gate = 0.5 + 0.5 * inner
        act[at] = (pre * gate).astype(bf)
        slope = gate + pre * (0.5 - 0.5 * inner * inner) * (root + root * 3 * 0.044715 * square)
        grad = d_act * slope
        grad_sum = grad_sum + jnp.sum(grad, axis=0, keepdims=True)
        d_pre[at] = grad.astype(bf)
        if k > 0:
            add_back(k - 1)
    add_back(count - 1)
    d_bias[...] = grad_sum
    for out, left, right, low in (
        (fc_hi, n2_t, d_pre, half), (pr_hi, d_t, act, half), (fc_lo, n2_t, d_pre, 0), (pr_lo, d_t, act, 0)):
        out[0] = jnp.dot(left[low : low + half], right[...], preferred_element_type=f32).astype(bf)


def feed_part(info, n2, d_mlp, bias, fc_got, pr_got, fc_parts, proj_parts):
    (total, width), hidden, half = n2.shape, bias.shape[1] // 2, n2.shape[1] // 2
    steps = hidden // HIDDEN
    fixed = lambda a: pl.BlockSpec(a.shape, lambda k, s: (0,) * len(a.shape), pipeline_mode=pl.Buffered(1))
    early = lambda a: pl.BlockSpec((a.shape[0], HIDDEN), lambda k, s: (0, jnp.minimum(k, steps - 1)))
    late = lambda a: pl.BlockSpec((a.shape[0], HIDDEN), lambda k, s: (0, jnp.maximum(k - steps, 0)))
    two = lambda a: pl.BlockSpec((1, a.shape[1], HIDDEN), lambda k, s: (k // steps, 0, k % steps))
    unit = pl.BlockSpec((1, HIDDEN), lambda k, s: (0, (s[3] + (k // steps) * (1 - 2 * s[3])) * steps + k % steps))
    grad = like((2, half, hidden), bf)
    sums = [like((total, width), f32)] * 2
    return pl.pallas_call(
        feed_kernel,
        grid_spec=pltpu.PrefetchScalarGridSpec(
            num_scalar_prefetch=1,
            grid=(2 * steps,),
            in_specs=[fixed(n2), fixed(d_mlp), unit, two(fc_got), two(pr_got)]
            + [early(a) for a in fc_parts[0]] + [late(a) for a in fc_parts[1]] + [early(proj_parts[0]), late(proj_parts[1])],
            out_specs=[fixed(o) for o in sums] + [two(grad)] * 4 + [unit],
            scratch_shapes=[
                pltpu.VMEM((width, total), bf), pltpu.VMEM((width, total), bf), pltpu.VMEM((width, HIDDEN), bf),
                pltpu.VMEM((width, HIDDEN), bf), pltpu.VMEM((total, HIDDEN), bf), pltpu.VMEM((total, HIDDEN), bf)],
        ),
        out_shape=sums + [grad] * 4 + [like((1, 2 * hidden), f32)],
        cost_estimate=pl.CostEstimate(flops=1 << 22, bytes_accessed=1 << 18, transcendentals=0),
        compiler_params=pltpu.CompilerParams(vmem_limit_bytes=46 << 20),
    )(info, n2, d_mlp, bias, fc_got, pr_got, *fc_parts[0], *fc_parts[1], *proj_parts)


def weight_kernel(n1, d_attn, d_qkv, o, lo, hi, left_t):
    step, half = pl.program_id(0), left_t.shape[0] // 2

    @pl.when(step == 0)
    def _():
        left_t[...] = n1[...].T

    def products(right):
        for out, low in ((hi, half), (lo, 0)):
            out[...] = jnp.dot(left_t[low : low + half], right[...], preferred_element_type=f32).astype(bf)

    @pl.when(step < pl.num_programs(0) - 1)
    def _():
        products(d_qkv)

    @pl.when(step == pl.num_programs(0) - 1)
    def _():
        left_t[...] = d_attn[...].T
        products(o)


def weight_part(n1, d_attn, d_qkv, o):
    (n, width), cols = n1.shape, o.shape[1]
    steps = d_qkv.shape[1] // cols
    fixed = lambda a: pl.BlockSpec(a.shape, lambda k: (0, 0), pipeline_mode=pl.Buffered(1))
    out = pl.BlockSpec((width // 2, cols), lambda k: (0, k))
    grad = like((width // 2, d_qkv.shape[1] + cols), bf)
    return pl.pallas_call(
        weight_kernel,
        grid=(steps + 1,),
        in_specs=[fixed(n1), fixed(d_attn), pl.BlockSpec((n, cols), lambda k: (0, jnp.minimum(k, steps - 1))), fixed(o)],
        out_specs=[out, out],
        out_shape=[grad, grad],
        scratch_shapes=[pltpu.VMEM((width, n), bf)],
        cost_estimate=pl.CostEstimate(flops=1 << 22, bytes_accessed=1 << 18, transcendentals=0),
        compiler_params=pltpu.CompilerParams(vmem_limit_bytes=32 << 20),
    )(n1, d_attn, d_qkv, o)


def token_kernel(rows, fan, info, own, rest, x, d_middle, weights, vec_rel, mid_sums, fc_grad, grad_out, small, own_sums, rest_sums, vecs, nat, order, fan_rows):
    width, cols = x.shape[1], own.shape[1] // 3
    step = pl.program_id(0)

    @pl.when(step == 0)
    def _():
        order[...] = order_matrix(info[1], rows, width)
        for ref in (own_sums, rest_sums, vecs, nat, fan_rows):
            ref[...] = jnp.zeros_like(ref)

    grad = lax.dot_general(own[...], weights[0], NT, preferred_element_type=f32)
    grad = grad + lax.dot_general(rest[...], weights[1], NT, preferred_element_type=f32)
    hat, inverse = norm_parts(x[...].astype(f32))
    low = (d_middle[...] + norm_back(hat, inverse, vec_rel[0:1], grad)).astype(bf)
    grad_out[...] = lax.dot_general(low, order[...], NT, preferred_element_type=f32).astype(bf)
    column_sum(own_sums, 0, own[...].astype(f32))
    column_sum(rest_sums, 0, rest[...].astype(f32))
    column_sum(vecs, 0, grad * hat)
    column_sum(vecs, 1, grad)

    @pl.when(step == pl.num_programs(0) - 1)
    def _():
        for group, ref in ((info[0], own_sums), (1 - info[0], rest_sums)):
            for row, part_index in ((0, 0), (1, 2)):
                picks = [ref[0:1, (3 * g + part_index) * 128 : (3 * g + part_index + 1) * 128] for g in range(cols // 128)]
                nat[row : row + 1, pl.ds(pl.multiple_of(group * cols, 128), cols)] = jnp.concatenate(picks, axis=1)
        count = width // 128
        for k in range(count):
            fan_rows[k : k + 1] = fc_grad[:, k * 128 * fan : (k + 1) * 128 * fan]
        spread = lax.dot_general(fan_rows[...].astype(bf), fan_matrix(fan), NT, preferred_element_type=f32)
        for k in range(count):
            for m in range(fan):
                nat[2 + m : 3 + m, k * 128 : (k + 1) * 128] = spread[k : k + 1, m * 128 : (m + 1) * 128]
        moved = jnp.dot(nat[...].astype(bf), order[...], preferred_element_type=f32)
        vecs[2:4] = moved[0:2]
        vecs[4:8] = mid_sums[0:4]
        vecs[8 : 8 + fan] = moved[2 : 2 + fan]
        small[...] = vecs[...].T.astype(bf)


def token_part(info, rows, own, rest, x, d_middle, weights, vec_rel, mid_sums, fc_grad):
    n, width = x.shape
    wide, fan = own.shape[1], fc_grad.shape[1] // width
    return by_rows(
        functools.partial(token_kernel, rows, fan), info, (own, rest, x, d_middle, weights, vec_rel, mid_sums, fc_grad), (None,) * 8,
        [like((n, width), bf), like((width, SMALL), bf)],
        [pltpu.VMEM((8, wide), f32), pltpu.VMEM((8, wide), f32), pltpu.VMEM((SMALL, width), f32), pltpu.VMEM((8, width), f32),
         pltpu.VMEM((width, width), bf), pltpu.VMEM((8, 128 * fan), f32)], 32)


def on_device(
    tokens, segment_ids, ln1_gain, ln1_bias, w_qkv, b_qv, w_attn_out, b_attn_out,
    ln2_gain, ln2_bias, w_fc, b_fc, w_proj, b_proj, cotangent,
):
    dp_size = lax.axis_size("dp")
    dp_pos, t_pos = lax.axis_index("dp"), lax.axis_index("tensor")
    core = dp_pos % 2
    rows = ln1_gain.shape[0]
    width = tokens.shape[1]
    cols = w_qkv.shape[2]
    hidden = w_fc.shape[1]
    fan = b_fc.shape[0] // rows
    far = [1 << k for k in range(dp_size.bit_length() - 2, 1, -1)]
    swap = []
    for d in range(dp_size):
        for t in range(2):
            if d % 2 != t:
                swap.append((2 * d + t, 2 * (d - d % 2 + t) + d % 2))
    mine = core == t_pos

    pairs = cols // 128

    def by_pair(parts):
        parts = parts.reshape(-1, 3, pairs, 128)
        return jnp.swapaxes(parts, 1, 2).reshape(-1, 3 * cols)

    def by_part(columns):
        return jnp.swapaxes(columns.reshape(-1, pairs, 3, 128), 1, 2).reshape(-1, 3, cols)

    small = jnp.concatenate([jnp.stack([ln1_gain, ln1_bias, b_attn_out, ln2_gain, ln2_bias, b_proj]), b_qv], axis=0)
    small = jnp.concatenate([small.T, b_fc.reshape(rows, fan)], axis=1)
    small = jnp.pad(small, ((0, 0), (0, SMALL - small.shape[1])))
    out_pack = jnp.concatenate([w_attn_out.T, small], axis=1)
    tokens, seg_other, all_qkv, all_out, fc_far, proj_far = head(
        dp_size, tokens, segment_ids, (by_pair(w_qkv), out_pack, w_fc, w_proj.T), chunks_of(3 * cols, 0, 2) + chunks_of(cols + SMALL, 1, 1))
    all_qkv, all_out = (a.reshape(2, width, -1) for a in (all_qkv, all_out))
    fc_far, proj_far = fc_far.reshape(-1, hidden), proj_far.reshape(-1, hidden)
    fc_parts = [[fc_far], [exchange(fc_far, 0, dp_size)]]
    proj_half = exchange(proj_far, 2, dp_size)

    part = jnp.stack([core, dp_pos, jnp.where(mine, 1, 0), t_pos]).astype(jnp.int32)
    x, n1, qkv_own, qkv_recv, vec_rel, fc_bias, starts = project_first(
        rows, fan, tokens, all_out, all_qkv, segment_ids, seg_other)
    fc_parts, proj_half, qkv_own = lax.optimization_barrier((fc_parts, proj_half, qkv_own))
    fc_parts = [p + [exchange(p[0], 2, dp_size)] for p in fc_parts]
    proj_half = jnp.concatenate([proj_far, proj_half], axis=0)
    proj_parts = [proj_half, exchange(proj_half, 0, dp_size)]
    o_own, o_send, lse = attn_fwd(qkv_own, qkv_recv, starts, part)
    cot_recv = lax.ppermute(cotangent, BOTH, swap)
    half = width // 2
    middle, n2, cot, d_mlp, o_recv, fc_got, pr_got = middle_part(
        rows, x, o_own, o_send, cotangent, cot_recv, all_out, vec_rel, fc_parts, proj_parts)
    mlp, back, fc_lo, fc_hi, pr_lo, pr_hi, fc_grad = feed_part(
        part, n2, d_mlp, fc_bias, fc_got, pr_got, fc_parts, proj_parts)
    fc_got, pr_got = exchange(fc_hi, 1, dp_size), exchange(pr_hi, 1, dp_size)
    block_out, d_middle, d_attn, do_own, do_send, mid_sums = after_part(
        part, rows, middle, mlp, back, cot, all_out, vec_rel, cols)
    do_recv = exchange(do_send, 1, dp_size)

    near_size = half // 2
    fc_rest = add_low(fc_lo[1], fc_got[1])
    pr_rest = add_low(pr_lo[:, near_size:], pr_got[:, near_size:])
    last = (qkv_own, qkv_recv, do_own, do_recv, o_own, o_send)
    last, fc_rest, pr_rest = lax.optimization_barrier((last, fc_rest, pr_rest))
    fc_sent = exchange(fc_rest, 0, dp_size)
    pr_sent = exchange(pr_rest, 2, dp_size)
    block_recv = lax.ppermute(block_out, BOTH, swap)
    dq_own, dq_send = attn_bwd(*last, starts, lse, part)
    dq_recv = exchange(dq_send, 1, dp_size)
    dq_own, fc_sent, pr_sent = lax.optimization_barrier((dq_own, fc_sent, pr_sent))
    fc_rest = add_low(fc_lo[0, near_size:], fc_got[0, near_size:], fc_sent[near_size:])
    pr_rest = add_low(pr_lo[1, :near_size], pr_got[1, :near_size], pr_sent[1])
    dq_own, fc_rest, pr_rest = lax.optimization_barrier((dq_own, fc_rest, pr_rest))
    fc_near = exchange(fc_rest, 2, dp_size)
    pr_near = exchange(pr_rest, 0, dp_size)
    own_lo, own_hi = weight_part(n1, d_attn, dq_own, o_own)
    own_lo, dq_recv = lax.optimization_barrier((own_lo, dq_recv))
    grad_tokens, d_small = token_part(part, rows, dq_own, dq_recv, x, d_middle, all_qkv, vec_rel, mid_sums, fc_grad)
    grad_recv = lax.ppermute(grad_tokens, BOTH, swap)
    d_small, fc_near, pr_near = lax.optimization_barrier((d_small, fc_near, pr_near))
    sum_fc = add_low(fc_lo[0, :near_size], fc_got[0, :near_size], fc_sent[:near_size], fc_near)
    sum_proj = add_low(pr_lo[0, :near_size], pr_got[0, :near_size], pr_sent[0], pr_near)
    feed = jnp.concatenate([sum_fc, sum_proj], axis=1).reshape(-1, rows, 2 * hidden)
    dq_recv, d_small, feed = lax.optimization_barrier((dq_recv, d_small, feed))
    rest_lo, rest_hi = weight_part(n1, d_attn, dq_recv, o_recv)
    blocks = lambda arr: arr.reshape(dp_size // 2, rows, -1)
    sum_a, vecs, sum_feed = tail(
        dp_size, (blocks(own_lo), blocks(own_hi)), (blocks(rest_lo), blocks(rest_hi)),
        (blocks(d_small[:half]), blocks(d_small[half:])), feed)
    vecs, block_recv, grad_recv = lax.optimization_barrier((vecs, block_recv, grad_recv))
    block_out = jnp.where(mine, block_out, block_recv)
    grad_tokens = jnp.where(mine, grad_tokens, grad_recv)
    return (
        block_out,
        grad_tokens,
        vecs[:, 0],
        vecs[:, 1],
        by_part(sum_a[:, : 3 * cols]),
        vecs[:, 2:4].T,
        sum_a[:, 3 * cols :].T,
        vecs[:, 4],
        vecs[:, 5],
        vecs[:, 6],
        sum_feed[:, :hidden],
        vecs[:, 8 : 8 + fan].reshape(rows * fan),
        sum_feed[:, hidden:].T,
        vecs[:, 7],
    )


def solution(mesh):
    vec, tok = P("dp"), P(BOTH, None)
    in_specs = (
        tok, P("dp", None), vec, vec, P("dp", None, "tensor"), P(None, "dp"), P("tensor", "dp"),
        vec, vec, vec, P("dp", "tensor"), vec, P("tensor", "dp"), vec, tok,
    )
    out_specs = (
        tok, tok, vec, vec, P("dp", None, "tensor"), P(None, "dp"), P("tensor", "dp"),
        vec, vec, vec, P("dp", "tensor"), vec, P("tensor", "dp"), vec,
    )
    return jax.shard_map(on_device, mesh=mesh, in_specs=in_specs, out_specs=out_specs, check_vma=False)
```
